32 devices in a mesh: fsdp: 4 (over x, core), ctx: 4 (over z), tp: 2 (over y).
Axes of the slice: x: 2, y: 2, z: 4, core: 2. Of those that a mesh axis runs over, the one named last changes fastest.
Arguments:
- tokens: bfloat16 [4, 2048, 1536], P('fsdp', 'ctx'), may hold values from -6 to 6
- segments: int32 [4, 2048], P('fsdp', 'ctx'), may hold values from 0 to 7, never falling along the last dimension, each value on 1 to 800 neighbouring positions
- adapter_index: int32 [4], P('fsdp'), may hold values from 0 to 7
- w_qkv: bfloat16 [1536, 3, 1536], P('fsdp', None, 'tp'), may hold values from -0.15625 to 0.15625
- w_forget: bfloat16 [1536, 24], P('fsdp', 'tp'), may hold values from -0.4375 to 0.4375
- forget_bias: bfloat16 [24], P('tp'), may hold values from -2 to 8
- w_out: bfloat16 [1536, 1536], P('tp', 'fsdp'), may hold values from -0.625 to 0.625
- w_gate_up: bfloat16 [1536, 2, 4096], P('fsdp', None, 'tp'), may hold values from -0.15625 to 0.15625
- w_down: bfloat16 [4096, 1536], P('tp', 'fsdp'), may hold values from -0.09375 to 0.09375
- gain_attn: bfloat16 [1536], replicated, may hold values from 0.5 to 1.5
- gain_ffn: bfloat16 [1536], replicated, may hold values from 0.5 to 1.5
- a_qkv: bfloat16 [8, 1536, 16], replicated, may hold values from -0.15625 to 0.15625
- b_qkv: bfloat16 [8, 16, 3, 1536], replicated, may hold values from -1.5 to 1.5
- a_out: bfloat16 [8, 1536, 16], replicated, may hold values from -0.625 to 0.625
- b_out: bfloat16 [8, 16, 1536], replicated, may hold values from -1.5 to 1.5
- a_gate_up: bfloat16 [8, 1536, 16], replicated, may hold values from -0.15625 to 0.15625
- b_gate_up: bfloat16 [8, 16, 2, 4096], replicated, may hold values from -1.5 to 1.5
- a_down: bfloat16 [8, 4096, 16], replicated, may hold values from -0.09375 to 0.09375
- b_down: bfloat16 [8, 16, 1536], replicated, may hold values from -1.5 to 1.5
- cotangent: bfloat16 [4, 2048, 1536], P('fsdp', 'ctx'), may hold values from -6 to 6
Outputs:
- block_output: bfloat16 [4, 2048, 1536], P('fsdp', 'ctx')
- grad_tokens: float32 [4, 2048, 1536], P('fsdp', 'ctx')
- grad_a_qkv: float32 [8, 1536, 16], P(None, ('fsdp', 'ctx', 'tp'))
- grad_b_qkv: float32 [8, 16, 3, 1536], P(None, None, None, ('fsdp', 'ctx', 'tp'))
- grad_a_out: float32 [8, 1536, 16], P(None, ('fsdp', 'ctx', 'tp'))
- grad_b_out: float32 [8, 16, 1536], P(None, None, ('fsdp', 'ctx', 'tp'))
- grad_a_gate_up: float32 [8, 1536, 16], P(None, ('fsdp', 'ctx', 'tp'))
- grad_b_gate_up: float32 [8, 16, 2, 4096], P(None, None, None, ('fsdp', 'ctx', 'tp'))
- grad_a_down: float32 [8, 4096, 16], P(None, ('fsdp', 'ctx', 'tp'))
- grad_b_down: float32 [8, 16, 1536], P(None, None, ('fsdp', 'ctx', 'tp'))
The draws below stay inside these ranges and needn't reach their ends.
Inputs may be any that keep to these rules, and one draw needn't show every extreme that they name: `segments`: document numbers never fall along a sequence; every document of 0 to 7 is present with 1 to 800 tokens, and one has exactly 800.
All inputs are finite; a program needn't handle non-finite values.
Results may differ from the reference program's by a relative error of at most 0.01575.
The reference program's roundings to bfloat16 on the way count: a program that leaves them out, or rounds other values in their place, can miss the bound.
Values may be sent and summed in bfloat16 or wider, within the bound.
No kernel may reach another device: no remote copies, remote signals or barrier semaphores. Data moves between devices by JAX's collectives and lax.ppermute only.
A program may use at most 576 MiB of HBM per device.

```python
import math
import jax
import jax.numpy as jnp
import numpy as np
from jax import lax

D = 1536
H = 24
HD = 64
FF = 4096
R = 16
ADAPTERS = 8
LEN = 2048
HH = 1536
SEQS = 4
DOCS = 8
DOC_MOST = 800


def place_ends(drawn, key, least, top_value):
    index_at = [jax.random.randint(jax.random.fold_in(key, axis), (), 0, length) for axis, length in enumerate(drawn.shape)]
    widest = drawn.shape.index(max(drawn.shape))
    next_to = index_at[:widest] + [(index_at[widest] + 1) % drawn.shape[widest]] + index_at[widest + 1:]
    return drawn.at[tuple(index_at)].set(least).at[tuple(next_to)].set(top_value)


def levels(own_key, shape, shards, least, high):
    factor_of = 1.0
    for dim, blocks in shards:
        steps = jax.random.uniform(jax.random.fold_in(jax.random.fold_in(own_key, 6), dim), (blocks,), jnp.float32, least / len(shards), high / len(shards))
        factor_of = factor_of * jnp.repeat(jnp.exp(steps), shape[dim] // blocks).reshape((-1,) + (1,) * (len(shape) - 1 - dim))
    return factor_of


def profile(count, total, bound, slope):
    portions = [(1 << 20) // math.isqrt(standing ** slope) + 1 for standing in range(2, count + 1)]
    surplus, counts = total - bound - (count - 1), [1] * (count - 1)
    while surplus > 0:
        candidates = [i for i in range(count - 1) if counts[i] < bound]
        whole, left = sum([portions[i] for i in candidates]), surplus
        for i in candidates:
            extra = min(bound - counts[i], max(1, left * portions[i] // whole), surplus)
            counts[i] = counts[i] + extra
            surplus = surplus - extra
    return np.array([bound] + counts)


def ragged_sizes(stream_key, amount, total, reach, lean):
    if amount == 2:
        one = jax.random.randint(stream_key, (), max(1, total - reach), min(reach, total - 1) + 1)
        return jnp.stack([one, total - one])
    lengths = jnp.asarray(profile(amount, total, reach, lean), jnp.int32)
    pairs = (amount - 1) // 2
    source_of, receiver = lengths[1:1 + 2 * pairs:2], lengths[2:2 + 2 * pairs:2]
    room = jnp.minimum(source_of - 1, reach - receiver)
    moved = jax.random.randint(jax.random.fold_in(stream_key, 1), (pairs,), 0, 1 << 20) % (room + 1)
    lengths = lengths.at[1:1 + 2 * pairs:2].set(source_of - moved).at[2:2 + 2 * pairs:2].set(receiver + moved)
    return lengths[jax.random.permutation(jax.random.fold_in(stream_key, 2), amount)]


def scatter_about(key, dims, scale, limit, cuts=(), dtype=jnp.bfloat16):
    values = scale * jax.random.normal(key, dims, jnp.float32)
    if cuts:
        values = values * levels(key, dims, cuts, -0.22, 0.18)
    return jnp.clip(values, -limit, limit).astype(dtype)


def setup_inputs(seed: int = 0) -> dict:
    key_of = jax.random.split(jax.random.key(seed), 21)
    tokens = scatter_about(key_of[0], (SEQS, LEN, D), 1.0, 6.0, ((0, 4), (1, 4)))
    segments = jax.vmap(lambda own: jnp.searchsorted(jnp.cumsum(ragged_sizes(own, DOCS, LEN, DOC_MOST, 1)), jnp.arange(LEN), side="right"))(jax.random.split(key_of[1], SEQS)).reshape((SEQS, LEN)).astype(jnp.int32)
    adapter_index = place_ends(jax.random.randint(key_of[2], (SEQS,), 0, ADAPTERS), jax.random.fold_in(key_of[2], 1), 0, ADAPTERS - 1).astype(jnp.int32)
    w_qkv = scatter_about(key_of[3], (D, 3, HH), D ** -0.5, 0.15625, ((0, 4), (2, 2)))
    w_forget = scatter_about(key_of[4], (D, H), (D // 8) ** -0.5, 0.4375, ((0, 4), (1, 2)))
    forget_bias = jnp.clip(-2.0 + 10.0 * jax.random.uniform(key_of[5], (H,), jnp.float32) ** levels(key_of[5], (H,), ((0, 2),), -0.2, 0.2), -2.0, 8.0).astype(jnp.bfloat16)
    w_out = scatter_about(key_of[6], (HH, D), (HH // 16) ** -0.5, 0.625, ((0, 2), (1, 4)))
    w_gate_up = scatter_about(key_of[7], (D, 2, FF), D ** -0.5, 0.15625, ((0, 4), (2, 2)))
    w_down = scatter_about(key_of[8], (FF, D), FF ** -0.5, 0.09375, ((0, 2), (1, 4)))
    gain_attn = jnp.clip(1.0 + 0.1 * jax.random.normal(key_of[9], (D,), jnp.float32), 0.5, 1.5).astype(jnp.bfloat16)
    gain_ffn = jnp.clip(1.0 + 0.1 * jax.random.normal(key_of[10], (D,), jnp.float32), 0.5, 1.5).astype(jnp.bfloat16)
    a_qkv = scatter_about(key_of[11], (ADAPTERS, D, R), D ** -0.5, 0.15625)
    b_qkv = scatter_about(key_of[12], (ADAPTERS, R, 3, HH), R ** -0.5, 1.5)
    a_out = scatter_about(key_of[13], (ADAPTERS, HH, R), (HH // 16) ** -0.5, 0.625)
    b_out = scatter_about(key_of[14], (ADAPTERS, R, D), R ** -0.5, 1.5)
    a_gate_up = scatter_about(key_of[15], (ADAPTERS, D, R), D ** -0.5, 0.15625)
    b_gate_up = scatter_about(key_of[16], (ADAPTERS, R, 2, FF), R ** -0.5, 1.5)
    a_down = scatter_about(key_of[17], (ADAPTERS, FF, R), FF ** -0.5, 0.09375)
    b_down = scatter_about(key_of[18], (ADAPTERS, R, D), R ** -0.5, 1.5)
    cotangent = scatter_about(key_of[19], (SEQS, LEN, D), 1.0, 6.0, ((0, 4), (1, 4)))
    return {"tokens": tokens, "segments": segments, "adapter_index": adapter_index, "w_qkv": w_qkv, "w_forget": w_forget, "forget_bias": forget_bias, "w_out": w_out, "w_gate_up": w_gate_up, "w_down": w_down, "gain_attn": gain_attn, "gain_ffn": gain_ffn, "a_qkv": a_qkv, "b_qkv": b_qkv, "a_out": a_out, "b_out": b_out, "a_gate_up": a_gate_up, "b_gate_up": b_gate_up, "a_down": a_down, "b_down": b_down, "cotangent": cotangent}


@jax.custom_vjp
def low(v):
    return lax.optimization_barrier(v.astype(jnp.bfloat16)).astype(jnp.float32)

@jax.custom_vjp
def low_back(v):
    return v

def low_keep(v):
    return (low(v), None)

def low_pass(kept, grad):
    return (grad,)

def back_keep(v):
    return (v, None)

def back_low(kept, grad):
    return (low(grad),)
low.defvjp(low_keep, low_pass)
low_back.defvjp(back_keep, back_low)

def matmul(left, right):
    return jnp.dot(left, right, precision=lax.Precision.HIGHEST, preferred_element_type=jnp.float32)

def rms_norm(values, gain_vec):
    return values * lax.rsqrt(lax.optimization_barrier(jnp.mean(values * values, axis=-1, keepdims=True)) + 1e-05) * gain_vec

def seg_combine(earlier, subsequent):
    early_first, early_last, early_tail = earlier
    late_first, late_last, late_tail = subsequent
    first_seg = jnp.where(early_first < 0, late_first, early_first)
    last_seg = jnp.where(late_last < 0, early_last, late_last)
    joined = (late_first == late_last) & (early_last == late_first)
    tail_sum = jnp.where(late_last < 0, early_tail, late_tail + jnp.where(joined, early_tail, 0.0))
    return (first_seg, last_seg, tail_sum)

def head_attention(head_item, allowed):
    queries, key_part, value_part, gate_part = head_item
    scores = low_back(matmul(queries, key_part.T) * HD ** (-0.5) + gate_part[:, None] - gate_part[None, :])
    scores = jnp.where(allowed, scores, -1e+30)
    top_score = lax.optimization_barrier(jnp.max(scores, axis=-1, keepdims=True))
    weights = jnp.exp(scores - top_score)
    weights = weights / lax.optimization_barrier(jnp.sum(weights, axis=-1, keepdims=True))
    return matmul(low(weights), value_part)

def block_layer(seq_tokens, seq_segs, index, frozen, adapter_set):
    w_qkv, w_forget, forget_bias, w_out, w_gate_up, w_down, gain_attn, gain_ffn = frozen
    a_qkv, b_qkv, a_out, b_out, a_gate_up, b_gate_up, a_down, b_down = adapter_set
    length = seq_tokens.shape[0]
    normed = low(rms_norm(seq_tokens, gain_attn))
    low_qkv = low_back(low(matmul(normed, a_qkv[index])))
    projected = low_back(matmul(normed, w_qkv.reshape(D, 3 * HH)) + matmul(low_qkv, b_qkv[index].reshape(R, 3 * HH)))
    projected = projected.reshape(length, 3, H, HD)
    queries = low(projected[:, 0]).transpose(1, 0, 2)
    key_all = low(projected[:, 1]).transpose(1, 0, 2)
    value_all = low(projected[:, 2]).transpose(1, 0, 2)
    logits = low_back(matmul(normed, w_forget) + forget_bias)
    log_forget = jax.nn.log_sigmoid(logits)
    seg_col = seq_segs[:, None]
    gates = lax.associative_scan(seg_combine, (seg_col, seg_col, log_forget), axis=0)[2]
    position = jnp.arange(length)
    allowed = (seq_segs[:, None] == seq_segs[None, :]) & (position[None, :] <= position[:, None])
    mixed = lax.map(jax.checkpoint(lambda head_item: head_attention(head_item, allowed)), (queries, key_all, value_all, gates.T))
    mixed = low(low_back(mixed.transpose(1, 0, 2).reshape(length, HH)))
    low_out = low_back(low(matmul(mixed, a_out[index])))
    attended = low_back(matmul(mixed, w_out) + matmul(low_out, b_out[index]))
    hidden_in = seq_tokens + attended
    normed_ffn = low(rms_norm(hidden_in, gain_ffn))
    low_ffn = low_back(low(matmul(normed_ffn, a_gate_up[index])))
    both = matmul(normed_ffn, w_gate_up.reshape(D, 2 * FF)) + matmul(low_ffn, b_gate_up[index].reshape(R, 2 * FF))
    both = both.reshape(length, 2, FF)
    gate_val = low_back(both[:, 0])
    up_val = low_back(both[:, 1])
    units = low(jax.nn.silu(gate_val) * up_val)
    low_down = low_back(low(matmul(units, a_down[index])))
    ffn_out = low_back(matmul(units, w_down) + matmul(low_down, b_down[index]))
    return hidden_in + ffn_out

def reference(tokens, segments, adapter_index, w_qkv, w_forget, forget_bias, w_out, w_gate_up, w_down, gain_attn, gain_ffn, a_qkv, b_qkv, a_out, b_out, a_gate_up, b_gate_up, a_down, b_down, cotangent):
    frozen = tuple((item.astype(jnp.float32) for item in (w_qkv, w_forget, forget_bias, w_out, w_gate_up, w_down, gain_attn, gain_ffn)))
    adapters = tuple((item.astype(jnp.float32) for item in (a_qkv, b_qkv, a_out, b_out, a_gate_up, b_gate_up, a_down, b_down)))
    seg_float = segments.astype(jnp.float32)

    def forward(inputs, adapter_set):

        def step(carry, scan_item):
            seq_tokens, seq_segs, index = scan_item
            return (carry, block_layer(seq_tokens, seq_segs, index, frozen, adapter_set))
        return lax.scan(step, jnp.zeros((), jnp.float32), (inputs, seg_float, adapter_index))[1]
    result, pullback = jax.vjp(forward, tokens.astype(jnp.float32), adapters)
    grad_inputs, grad_set = pullback(cotangent.astype(jnp.float32))
    return (result.astype(jnp.bfloat16), grad_inputs, grad_set[0], grad_set[1], grad_set[2], grad_set[3], grad_set[4], grad_set[5], grad_set[6], grad_set[7])
```

```python
import jax
import jax.numpy as jnp
from jax import lax
from jax.sharding import PartitionSpec as P

HD = 64
DOC_MOST = 800
DOCS = 8
BF = jnp.bfloat16
F32 = jnp.float32
HI = lax.Precision.HIGHEST


def dot(a, b):
    return jnp.dot(a, b, preferred_element_type=F32)


def dot_t(a, b):
    return lax.dot_general(a, b, (((1,), (1,)), ((), ())), preferred_element_type=F32)


def t_dot(a, b):
    return lax.dot_general(a, b, (((0,), (0,)), ((), ())), preferred_element_type=F32)


def xor_order(size):
    order, bit = [0], size // 2
    while bit:
        order, bit = order + [step ^ bit for step in order], bit // 2
    return order


def gather_blocks(shard, axis_name, dim):
    size = lax.axis_size(axis_name)
    pieces, bit = [shard], size // 2
    while bit:
        pairs = [(i, i ^ bit) for i in range(size)]
        pieces = pieces + [lax.ppermute(part, axis_name, pairs) for part in pieces]
        bit //= 2
    return jnp.concatenate(pieces, axis=dim)


def to_xor(values, dim, size, rank):
    block = values.shape[dim] // size
    return jnp.concatenate(
        [lax.dynamic_slice_in_dim(values, (rank ^ step) * block, block, dim) for step in xor_order(size)],
        axis=dim,
    )


def from_xor(values, dim, size, rank):
    block = values.shape[dim] // size
    bits = size.bit_length() - 1
    pieces = []
    for natural in range(size):
        mixed = rank ^ natural
        place = sum(((mixed >> j) & 1) << (bits - 1 - j) for j in range(bits))
        pieces.append(lax.dynamic_slice_in_dim(values, place * block, block, dim))
    return jnp.concatenate(pieces, axis=dim)


def rms_factor(values):
    return lax.rsqrt(jnp.mean(values * values, axis=-1, keepdims=True) + 1e-05)


def rms_back(values, gain_vec, incoming):
    factor = rms_factor(values)
    scaled = incoming * gain_vec
    return factor * scaled - values * factor**3 * jnp.mean(values * scaled, axis=-1, keepdims=True)


def heads(values):
    return values.reshape(values.shape[0], -1, HD)


def shift(values, hop, size):
    pairs = [(i, i + hop) for i in range(size) if 0 <= i + hop < size]
    return lax.ppermute(values, "ctx", pairs)


def body(
    tokens, segments, adapter_index, w_qkv, w_forget, forget_bias, w_out, w_gate_up, w_down,
    gain_attn, gain_ffn, a_qkv, b_qkv, a_out, b_out, a_gate_up, b_gate_up, a_down, b_down, cotangent,
):
    count, rows, width = tokens.shape
    assert count == 1
    head_cols = w_qkv.shape[2]
    local_heads = w_forget.shape[1]
    unit_cols = w_gate_up.shape[2]
    rank_r = a_qkv.shape[2]
    n_f, n_c, n_t = (lax.axis_size("fsdp"), lax.axis_size("ctx"), lax.axis_size("tp"))
    assert n_t == 2
    f_rank, c_rank, t_rank = (lax.axis_index("fsdp"), lax.axis_index("ctx"), lax.axis_index("tp"))
    hops = -(-(DOC_MOST - 1) // rows)
    assert hops == 2 and n_c > 1
    tail = -(-(DOC_MOST - 1 - rows) // 32) * 32
    before = hops * rows
    half = rows // 2
    swap_t = [(0, 1), (1, 0)]

    def other(values):
        return lax.ppermute(values, "tp", swap_t)

    tok_raw = tokens[0]
    prev_one = shift(tok_raw, 1, n_c)
    prev_two = shift(prev_one[rows - tail :], 1, n_c)
    tok_prev = jnp.concatenate([jnp.zeros((rows - tail, width), BF), prev_two, prev_one], axis=0)

    pick = adapter_index[0]
    take = lambda table: lax.dynamic_index_in_dim(table, pick, 0, keepdims=False)
    mix = lambda values, dim: to_xor(values, dim, n_f, f_rank)
    qkv_a, ffn_a = (mix(take(a_qkv), 0), mix(take(a_gate_up), 0))
    out_b, down_b = (mix(take(b_out), 1), mix(take(b_down), 1))
    qkv_b = lax.dynamic_slice_in_dim(take(b_qkv), t_rank * head_cols, head_cols, 2).reshape(rank_r, 3 * head_cols)
    out_a = take(a_out)
    ffn_b = lax.dynamic_slice_in_dim(take(b_gate_up), t_rank * unit_cols, unit_cols, 2).reshape(rank_r, 2 * unit_cols)
    down_a = lax.dynamic_slice_in_dim(take(a_down), t_rank * unit_cols, unit_cols, 0)
    gain_one = mix(gain_attn.astype(F32), 0)
    gain_two = mix(gain_ffn.astype(F32), 0)
    bias = forget_bias.astype(F32)

    qkv_w = gather_blocks(w_qkv.reshape(-1, 3 * head_cols), "fsdp", 0)
    forget_w = gather_blocks(w_forget, "fsdp", 0)
    out_w_own = gather_blocks(w_out, "fsdp", 1)
    out_w_other = other(out_w_own)
    first = t_rank == 0
    out_w = jnp.concatenate(
        [jnp.where(first, out_w_own, out_w_other), jnp.where(first, out_w_other, out_w_own)], axis=0
    )
    gate_up_w = gather_blocks(w_gate_up.reshape(-1, 2 * unit_cols), "fsdp", 0)
    down_w = gather_blocks(w_down, "fsdp", 1)

    seg_all = lax.all_gather(segments[0], "ctx", tiled=True)
    full = seg_all.shape[0]
    starts_of = jnp.sum(seg_all[None, :] < jnp.arange(DOCS)[:, None], axis=1)
    starts = jnp.sum(jnp.where(seg_all[:, None] == jnp.arange(DOCS)[None, :], starts_of[None, :], 0), axis=1)
    starts = jnp.concatenate([starts, jnp.full((before,), 2 * full, starts.dtype)])
    base = c_rank * rows
    start_own = lax.dynamic_slice_in_dim(starts, base, rows)
    start_next = lax.dynamic_slice_in_dim(starts, base + rows, before)
    pos_own = base + jnp.arange(rows)
    pos_keys = base - before + jnp.arange(before + rows)
    pos_next = base + rows + jnp.arange(before)
    allowed = (pos_keys[None, :] >= start_own[:, None]) & (pos_keys[None, :] <= pos_own[:, None])
    allowed_next = pos_own[None, :] >= start_next[:, None]

    def project(tok, cols_from):
        values = tok.astype(F32)
        normed = (values * rms_factor(values) * gain_one).astype(BF)
        low = dot(normed, qkv_a).astype(BF)
        proj = (dot(normed, qkv_w[:, cols_from:]) + dot(low, qkv_b[:, cols_from:])).astype(BF)
        logits = dot(normed, forget_w) + bias
        return normed, low, proj, logits

    tok_own = mix(tok_raw, 1)
    normed, low_qkv, proj, logits = project(tok_own, 0)
    _, _, proj_prev, logits_prev = project(mix(tok_prev, 1), head_cols)
    query = (proj[:, :head_cols].astype(F32) * HD ** (-0.5)).astype(BF)
    keys = jnp.concatenate([proj_prev[:, :head_cols], proj[:, head_cols : 2 * head_cols]], axis=0)
    vals = jnp.concatenate([proj_prev[:, head_cols:], proj[:, 2 * head_cols :]], axis=0)
    forget = jax.nn.log_sigmoid(logits)
    forget_prev = jax.nn.log_sigmoid(logits_prev)
    same_own = allowed[:, before:].astype(F32)
    after_own = (jnp.arange(rows)[None, :] > jnp.arange(rows)[:, None]).astype(F32)
    after_prev = (jnp.arange(before)[None, :] > jnp.arange(before)[:, None]).astype(F32)
    exact = lambda a, b: jnp.dot(a, b, precision=HI, preferred_element_type=F32)
    gates = exact(same_own, forget)
    key_gates = jnp.concatenate([-exact(after_prev, forget_prev), gates], axis=0)
    total_one = jnp.sum(forget_prev[before - rows :], axis=0)
    key_gates_next = -exact(after_own, forget)

    q_h, k_h, v_h = (heads(query), heads(keys), heads(vals))

    def score(q, k, gq, gk, ok):
        s = jnp.einsum("qhd,khd->hqk", q, k, preferred_element_type=F32)
        return jnp.where(ok[None], s + gq.T[:, :, None] - gk.T[:, None, :], -1e30)

    s = score(q_h, k_h, gates, key_gates, allowed)
    top = jnp.max(s, axis=-1, keepdims=True)
    w = jnp.exp(s - top)
    total = jnp.sum(w, axis=-1, keepdims=True)
    w = w / total
    mixed_f = jnp.einsum("hqk,khd->qhd", w.astype(BF), v_h, preferred_element_type=F32)
    log_total = (top + jnp.log(total))[:, :, 0].T
    mixed_own = mixed_f.reshape(rows, head_cols).astype(BF)
    mixed_other = other(mixed_own)
    mixed = jnp.concatenate(
        [jnp.where(first, mixed_own, mixed_other), jnp.where(first, mixed_other, mixed_own)], axis=1
    )
    q_gate = gates - log_total
    q_gate_two = (q_gate + total_one[None, :])[:tail]
    send_q1 = shift(query, -1, n_c)
    send_q2 = shift(query[:tail], -2, n_c)
    send_g1 = shift(q_gate, -1, n_c)
    send_g2 = shift(q_gate_two, -2, n_c)

    low_out = dot(mixed, out_a).astype(BF)
    hidden = tok_own.astype(F32) + dot(mixed, out_w) + dot(low_out, out_b)
    normed_ffn = (hidden * rms_factor(hidden) * gain_two).astype(BF)
    low_ffn = dot(normed_ffn, ffn_a).astype(BF)
    both = dot(normed_ffn, gate_up_w) + dot(low_ffn, ffn_b)
    gate_val, up_val = both[:, :unit_cols], both[:, unit_cols:]
    sig = jax.nn.sigmoid(gate_val)
    units = (gate_val * sig * up_val).astype(BF)
    cot = mix(cotangent[0], 1)
    grad_low_down = dot_t(cot, down_b).astype(BF)
    grad_units = dot_t(cot, down_w) + dot_t(grad_low_down, down_a)
    grad_gate = (grad_units * up_val * sig * (1.0 + gate_val * (1.0 - sig))).astype(BF)
    grad_up = (grad_units * gate_val * sig).astype(BF)
    grad_both = jnp.concatenate([grad_gate, grad_up], axis=1)
    part = dot_t(grad_both, gate_up_w)
    part_low = dot_t(grad_both, ffn_b)
    mine = t_rank * half
    theirs = (1 - t_rank) * half
    own_rows = lambda values: lax.dynamic_slice_in_dim(values, mine, half, 0)
    far_rows = lambda values: lax.dynamic_slice_in_dim(values, theirs, half, 0)
    got = other(far_rows(part).astype(BF))
    got_low = other(far_rows(part_low))
    grad_low_ffn = (own_rows(part_low) + got_low).astype(BF)
    grad_normed_ffn = own_rows(part) + got.astype(F32) + dot_t(grad_low_ffn, ffn_a)
    hidden_half = own_rows(hidden)
    grad_hidden = own_rows(cot).astype(F32) + rms_back(hidden_half, gain_two, grad_normed_ffn)
    grad_hidden_b = grad_hidden.astype(BF)
    grad_low_out = dot_t(grad_hidden_b, out_b).astype(BF)
    grad_mixed_half = (dot_t(grad_hidden_b, out_w) + dot_t(grad_low_out, out_a)).astype(BF)
    gm_own = lax.dynamic_slice_in_dim(grad_mixed_half, t_rank * head_cols, head_cols, 1)
    gm_far = other(lax.dynamic_slice_in_dim(grad_mixed_half, (1 - t_rank) * head_cols, head_cols, 1))
    grad_mixed = jnp.concatenate([jnp.where(first, gm_own, gm_far), jnp.where(first, gm_far, gm_own)], axis=0)

    d_h = heads(grad_mixed)
    delta = jnp.sum(d_h.astype(F32) * mixed_f, axis=-1)
    send_d1 = shift(grad_mixed, -1, n_c)
    send_d2 = shift(grad_mixed[:tail], -2, n_c)
    send_e1 = shift(delta, -1, n_c)
    send_e2 = shift(delta[:tail], -2, n_c)
    pad = lambda values: jnp.pad(values, ((0, rows - tail), (0, 0)))
    q_next = jnp.concatenate([send_q1, pad(send_q2)], axis=0)
    g_next = jnp.concatenate([send_g1, pad(send_g2)], axis=0)
    d_next = jnp.concatenate([send_d1, pad(send_d2)], axis=0)
    e_next = jnp.concatenate([send_e1, pad(send_e2)], axis=0)

    def back(q, k, v, d, gq, gk, e, ok):
        p = jnp.exp(score(q, k, gq, gk, ok))
        dp = jnp.einsum("qhd,khd->hqk", d, v, preferred_element_type=F32)
        return p.astype(BF), (p * (dp - e.T[:, :, None])).astype(BF)

    p_own, ds_own = back(q_h, k_h, v_h, d_h, q_gate, key_gates, delta, allowed)
    qn_h, dn_h = (heads(q_next), heads(d_next))
    p_nxt, ds_nxt = back(qn_h, k_h[before:], v_h[before:], dn_h, g_next, key_gates_next, e_next, allowed_next)
    grad_q = jnp.einsum("hqk,khd->qhd", ds_own, k_h, preferred_element_type=F32) * HD ** (-0.5)
    grad_k = jnp.einsum("hqk,qhd->khd", ds_own[:, :, before:], q_h, preferred_element_type=F32)
    grad_k = grad_k + jnp.einsum("hqk,qhd->khd", ds_nxt, qn_h, preferred_element_type=F32)
    grad_v = jnp.einsum("hqk,qhd->khd", p_own[:, :, before:], d_h, preferred_element_type=F32)
    grad_v = grad_v + jnp.einsum("hqk,qhd->khd", p_nxt, dn_h, preferred_element_type=F32)
    row_sum = jnp.sum(ds_own.astype(F32), axis=2).T
    col_own = jnp.sum(ds_own[:, :, before:].astype(F32), axis=1).T
    col_next = jnp.sum(ds_nxt.astype(F32), axis=1).T
    across = jnp.sum(ds_own[:, :, : before - rows].astype(F32), axis=(1, 2))[None, :]
    across = shift(across, -1, n_c)
    grad_forget = (
        lax.dot_general(same_own, row_sum - col_own, (((0,), (0,)), ((), ())), precision=HI, preferred_element_type=F32)
        + lax.dot_general(after_own, col_next, (((0,), (0,)), ((), ())), precision=HI, preferred_element_type=F32)
        + across
    )
    grad_logits = (grad_forget * jax.nn.sigmoid(-logits)).astype(BF)
    grad_proj = jnp.concatenate(
        [grad_q.reshape(rows, head_cols), grad_k.reshape(rows, head_cols), grad_v.reshape(rows, head_cols)], axis=1
    ).astype(BF)

    part_low_qkv = dot_t(grad_proj, qkv_b)
    grad_low_qkv = (part_low_qkv + other(part_low_qkv)).astype(BF)
    part_in = dot_t(grad_proj, qkv_w) + dot_t(grad_logits, forget_w)
    got_in = other(far_rows(part_in).astype(BF))
    grad_normed = own_rows(part_in) + got_in.astype(F32) + dot_t(own_rows(grad_low_qkv), qkv_a)
    grad_tok = (grad_hidden + rms_back(own_rows(tok_own).astype(F32), gain_one, grad_normed)).astype(BF)
    tok_far = other(grad_tok)
    grad_tok = jnp.concatenate([jnp.where(first, grad_tok, tok_far), jnp.where(first, tok_far, grad_tok)], axis=0)
    grad_tokens = from_xor(grad_tok, 1, n_f, f_rank).astype(F32)

    part_low_down = dot(units, down_a)
    low_down = (part_low_down + other(part_low_down)).astype(BF)
    part_down = dot(units, down_w).astype(BF)
    ffn_out = part_down.astype(F32) + other(part_down).astype(F32)
    block_output = from_xor((hidden + ffn_out + dot(low_down, down_b)).astype(BF), 1, n_f, f_rank)

    own_part = lambda values, n: values * (lax.broadcasted_iota(jnp.int32, (1, n), 1) // (n // 2) == t_rank)
    natural = lambda values: from_xor(values, 1, n_f, f_rank)
    place = lambda values: jnp.concatenate([jnp.where(first, values, 0.0), jnp.where(first, 0.0, values)], axis=1)
    g_b_qkv = t_dot(low_qkv, grad_proj)
    g_b_ffn = t_dot(low_ffn, grad_both)
    tables = [
        own_part(natural(t_dot(grad_low_qkv, normed)), width),
        *[place(g_b_qkv[:, i * head_cols : (i + 1) * head_cols]) for i in range(3)],
        t_dot(grad_low_out, own_rows(mixed)),
        natural(t_dot(own_rows(low_out), grad_hidden_b)),
        natural(t_dot(grad_low_ffn, own_rows(normed_ffn))),
        *[place(g_b_ffn[:, i * unit_cols : (i + 1) * unit_cols]) for i in range(2)],
        place(t_dot(grad_low_down, units)),
        own_part(natural(t_dot(low_down, cot)), width),
    ]
    packed = jnp.concatenate([t.reshape(rank_r, n_f, n_c, n_t, -1) for t in tables], axis=4)
    block = packed.shape[4]
    packed = packed.transpose(2, 1, 3, 0, 4)
    by_ctx = jnp.sum(lax.all_to_all(packed, "ctx", 0, 0, tiled=True).reshape(n_c, n_f * n_t, rank_r, block), axis=0)
    landed = lax.all_to_all(by_ctx, ("fsdp", "tp"), 0, 0, tiled=True)
    by_seq = jnp.sum(landed.reshape(n_f, n_t, rank_r, block), axis=1)
    every = lax.all_gather(adapter_index, "fsdp", tiled=True)
    onehot = (jnp.arange(a_qkv.shape[0])[:, None] == every[None, :]).astype(F32)
    spread = jnp.einsum("as,srk->ark", onehot, by_seq, precision=HI, preferred_element_type=F32)
    sizes = [t.shape[1] // (n_f * n_c * n_t) for t in tables]
    outs, at = [], 0
    for size in sizes:
        outs.append(spread[:, :, at : at + size])
        at += size
    swap = lambda values: values.transpose(0, 2, 1)
    return (
        block_output[None],
        grad_tokens[None],
        swap(outs[0]),
        jnp.stack(outs[1:4], axis=2),
        swap(outs[4]),
        outs[5],
        swap(outs[6]),
        jnp.stack(outs[7:9], axis=2),
        swap(outs[9]),
        outs[10],
    )


def solution(mesh):
    in_specs = (
        P("fsdp", "ctx", None), P("fsdp", "ctx"), P("fsdp"), P("fsdp", None, "tp"), P("fsdp", "tp"), P("tp"),
        P("tp", "fsdp"), P("fsdp", None, "tp"), P("tp", "fsdp"),
        P(), P(), P(), P(), P(), P(), P(), P(), P(), P(),
        P("fsdp", "ctx", None),
    )
    out_specs = (
        P("fsdp", "ctx", None),
        P("fsdp", "ctx", None),
        P(None, ("fsdp", "ctx", "tp"), None),
        P(None, None, None, ("fsdp", "ctx", "tp")),
        P(None, ("fsdp", "ctx", "tp"), None),
        P(None, None, ("fsdp", "ctx", "tp")),
        P(None, ("fsdp", "ctx", "tp"), None),
        P(None, None, None, ("fsdp", "ctx", "tp")),
        P(None, ("fsdp", "ctx", "tp"), None),
        P(None, None, ("fsdp", "ctx", "tp")),
    )
    return jax.shard_map(body, mesh=mesh, in_specs=in_specs, out_specs=out_specs, check_vma=False)
```

```python
import jax
import jax.numpy as jnp
from jax import lax
from jax.experimental import pallas as pl
from jax.experimental.pallas import tpu as pltpu
from jax.sharding import PartitionSpec as P

HD = 64
DOC_MOST = 800
DOCS = 8
BF = jnp.bfloat16
F32 = jnp.float32
HI = lax.Precision.HIGHEST


def dot(a, b):
    return jnp.dot(a, b, preferred_element_type=F32)


def dot_t(a, b):
    return lax.dot_general(a, b, (((1,), (1,)), ((), ())), preferred_element_type=F32)


def t_dot(a, b):
    return lax.dot_general(a, b, (((0,), (0,)), ((), ())), preferred_element_type=F32)


def xor_order(size):
    order, bit = [0], size // 2
    while bit:
        order, bit = order + [step ^ bit for step in order], bit // 2
    return order


def after(values, *done):
    return lax.optimization_barrier((values, *done))[0]


def far_blocks(shard, dim):
    size = lax.axis_size("fsdp")
    own, bit = shard, size // 2
    while True:
        got = lax.ppermute(own, "fsdp", [(i, i ^ bit) for i in range(size)])
        if bit == 2:
            return own, got
        own, bit = jnp.concatenate([own, got], axis=dim), bit // 2


def near_blocks(own, got, dim):
    both = jnp.concatenate([own, got], axis=dim)
    size = lax.axis_size("fsdp")
    return [both, lax.ppermute(both, "fsdp", [(i, i ^ 1) for i in range(size)])]


def to_xor(values, dim, size, rank):
    block = values.shape[dim] // size
    return jnp.concatenate(
        [lax.dynamic_slice_in_dim(values, (rank ^ step) * block, block, dim) for step in xor_order(size)],
        axis=dim,
    )


def from_xor(values, dim, size, rank):
    block = values.shape[dim] // size
    bits = size.bit_length() - 1
    pieces = []
    for natural in range(size):
        mixed = rank ^ natural
        place = sum(((mixed >> j) & 1) << (bits - 1 - j) for j in range(bits))
        pieces.append(lax.dynamic_slice_in_dim(values, place * block, block, dim))
    return jnp.concatenate(pieces, axis=dim)


def shift(values, hop, size):
    pairs = [(i, i + hop) for i in range(size) if 0 <= i + hop < size]
    return lax.ppermute(values, "ctx", pairs)


LANES = 128
BLK = 256
BIG = -1e30


def spec(shape, index):
    return pl.BlockSpec(shape, index)


def call(kernel, grid, ins, in_specs, outs, out_specs, scratch=(), prefetch=0, flops=0, nbytes=0, exps=0, aliases=None):
    return pl.pallas_call(
        kernel,
        out_shape=outs,
        grid_spec=pltpu.PrefetchScalarGridSpec(
            num_scalar_prefetch=prefetch, grid=grid, in_specs=in_specs, out_specs=out_specs, scratch_shapes=list(scratch)
        ),
        compiler_params=pltpu.CompilerParams(
            dimension_semantics=("arbitrary",) * len(grid), vmem_limit_bytes=56 * 2**20
        ),
        input_output_aliases=aliases or {},
        cost_estimate=pl.CostEstimate(flops=1, bytes_accessed=1, transcendentals=0),
    )(*ins)


def spread_lanes(side, head, n_heads, keys):
    base = HD * (1 - side)
    to = lax.broadcasted_iota(jnp.int32, (LANES, LANES), 1) - base
    one = 3 * n_heads + DOCS
    parts = jnp.where((to >= 3) & (to < 6), one, -1)
    gate_at = 0
    if keys:
        parts = jnp.where((to >= 0) & (to < 3), one, -1)
        gate_at = 3
    part = to - gate_at
    parts = jnp.where((part >= 0) & (part < 3), part * n_heads + head, parts)
    parts = jnp.where((to >= 8) & (to < 8 + DOCS), to - 8 + 3 * n_heads, parts)
    return (lax.broadcasted_iota(jnp.int32, (LANES, LANES), 0) == parts).astype(BF)


def spread_parts(side, head, n_heads):
    base = HD * (1 - side)
    to = lax.broadcasted_iota(jnp.int32, (LANES, LANES), 1) - base
    parts = jnp.where((to >= 0) & (to < 3), to * n_heads + head, -1)
    return (lax.broadcasted_iota(jnp.int32, (LANES, LANES), 0) == parts).astype(BF)


def data_lanes(side, rows):
    lane = lax.broadcasted_iota(jnp.int32, (rows, LANES), 1)
    return (lane < HD) if side == 0 else (lane >= HD)


def with_gates(values, gate_parts, side, select):
    extra = dot(gate_parts, select).astype(BF)
    return jnp.where(data_lanes(side, values.shape[0]), values, extra)


def attention_forward(bounds, q, k, v, gq, gk, gates, total, n_heads):
    rows, keys = q.shape[0], k.shape[0]
    n_q, n_before = rows // BLK, (keys - rows) // BLK
    pairs = n_heads // 2

    def kernel(lo_ref, q_ref, k_ref, v_ref, gq_ref, gk_ref, gate_ref, tot_ref, mixed_ref, float_ref, one_ref, two_ref, kx, log_ref):
        pair = pl.program_id(0)
        lane = lax.broadcasted_iota(jnp.int32, (BLK, LANES), 1)
        causal = lax.broadcasted_iota(jnp.int32, (BLK, BLK), 0) >= lax.broadcasted_iota(jnp.int32, (BLK, BLK), 1)
        for side in range(2):
            kx[side] = with_gates(k_ref[...], gk_ref[...], side, spread_lanes(side, 2 * pair + side, n_heads, True))
        for qb in range(n_q):
            at = slice(qb * BLK, (qb + 1) * BLK)
            qx = [
                with_gates(q_ref[at, :], gq_ref[at, :], side, spread_lanes(side, 2 * pair + side, n_heads, False))
                for side in range(2)
            ]
            diag = n_before + qb
            state = []
            for side in range(2):
                s = jnp.where(causal, dot_t(qx[side], kx[side, diag * BLK : (diag + 1) * BLK, :]), BIG)
                top = jnp.max(s, axis=1, keepdims=True)
                w = jnp.exp(s - top)
                part = w[:, :LANES] + w[:, LANES:]
                state += [top, part, dot(w.astype(BF), v_ref[diag * BLK : (diag + 1) * BLK, :])]

            def step(kb, state):
                here = pl.ds(pl.multiple_of(kb * BLK, BLK), BLK)
                new = []
                for side in range(2):
                    top, part, acc = state[3 * side : 3 * side + 3]
                    s = dot_t(qx[side], kx[side, here, :])
                    higher = jnp.maximum(top, jnp.max(s, axis=1, keepdims=True))
                    keep = jnp.exp(top - higher)
                    w = jnp.exp(s - higher)
                    part = part * keep + (w[:, :LANES] + w[:, LANES:])
                    acc = acc * keep + dot(w.astype(BF), v_ref[here, :])
                    new += [higher, part, acc]
                return tuple(new)

            state = lax.fori_loop(lo_ref[qb], diag, step, tuple(state))
            results, logs = [], jnp.zeros((BLK, LANES), F32)
            for side in range(2):
                top, part, acc = state[3 * side : 3 * side + 3]
                total = jnp.sum(part, axis=1, keepdims=True)
                results.append(acc / total)
                logs = jnp.where(lane == 2 * pair + side, top + jnp.log(total), logs)
            out = jnp.where(lane < HD, results[0], results[1])
            mixed_ref[at, :] = out.astype(BF)
            float_ref[at, :] = out

            @pl.when(pair == 0)
            def _():
                log_ref[at, :] = logs

            @pl.when(pair > 0)
            def _():
                log_ref[at, :] = jnp.where((lane >> 1) == pair, logs, log_ref[at, :])

            @pl.when(pair == pairs - 1)
            def _():
                values = gate_ref[at, :] - log_ref[at, :]
                rest = gq_ref[at, :].astype(F32)
                one_ref[at, :] = jnp.where(lane < 3 * n_heads, split_lanes(values, n_heads), rest).astype(BF)
                values = values + tot_ref[:1, :]
                two_ref[at, :] = jnp.where(lane < 3 * n_heads, split_lanes(values, n_heads), rest).astype(BF)

    return call(
        kernel,
        (pairs,),
        (bounds, q, k, v, gq, gk, gates, total),
        [
            spec((rows, LANES), lambda i, *_: (0, i)),
            spec((keys, LANES), lambda i, *_: (0, i)),
            spec((keys, LANES), lambda i, *_: (0, i)),
            spec((rows, LANES), lambda i, *_: (0, 0)),
            spec((keys, LANES), lambda i, *_: (0, 0)),
            spec((rows, LANES), lambda i, *_: (0, 0)),
            spec((8, LANES), lambda i, *_: (0, 0)),
        ],
        (
            jax.ShapeDtypeStruct(q.shape, BF),
            jax.ShapeDtypeStruct(q.shape, F32),
            jax.ShapeDtypeStruct((rows, LANES), BF),
            jax.ShapeDtypeStruct((rows, LANES), BF),
        ),
        (
            spec((rows, LANES), lambda i, *_: (0, i)),
            spec((rows, LANES), lambda i, *_: (0, i)),
            spec((rows, LANES), lambda i, *_: (0, 0)),
            spec((rows, LANES), lambda i, *_: (0, 0)),
        ),
        [pltpu.VMEM((2, keys, LANES), BF), pltpu.VMEM((rows, LANES), F32)],
        prefetch=1,
        flops=8 * rows * 768 * LANES * n_heads,
        nbytes=3 * keys * 2 * HD * n_heads,
        exps=rows * 768 * n_heads,
    )


def attention_dq(bounds, q, k, v, d, gq, gk, n_heads, n_far):
    rows, keys = q.shape[0], k.shape[0]
    n_q, n_before = rows // BLK, (keys - rows) // BLK
    pairs = n_heads // 2

    def kernel(lo_ref, q_ref, k_ref, v_ref, d_ref, gq_ref, gk_ref, gd_ref, dq_ref, row_ref, far_ref, kx):
        pair = pl.program_id(0)
        lane = lax.broadcasted_iota(jnp.int32, (BLK, LANES), 1)
        causal = lax.broadcasted_iota(jnp.int32, (BLK, BLK), 0) >= lax.broadcasted_iota(jnp.int32, (BLK, BLK), 1)
        for side in range(2):
            kx[side] = with_gates(k_ref[...], gk_ref[...], side, spread_lanes(side, 2 * pair + side, n_heads, True))

        @pl.when(pair == 0)
        def _():
            far_ref[...] = jnp.zeros_like(far_ref)
            row_ref[...] = jnp.zeros_like(row_ref)

        for qb in range(n_q):
            at = slice(qb * BLK, (qb + 1) * BLK)
            qx, dx = [], []
            for side in range(2):
                head = 2 * pair + side
                qx.append(with_gates(q_ref[at, :], gq_ref[at, :], side, spread_lanes(side, head, n_heads, False)))
                dx.append(with_gates(d_ref[at, :], gd_ref[at, :], side, spread_parts(side, head, n_heads)))
            diag = n_before + qb

            def block(here, accs, masked):
                new = []
                for side in range(2):
                    keys_x = kx[side, here, :]
                    s = dot_t(qx[side], keys_x)
                    if masked:
                        s = jnp.where(causal, s, BIG)
                    vx = jnp.where(data_lanes(side, BLK), v_ref[here, :], jnp.ones((), BF))
                    ds = (jnp.exp(s) * dot_t(dx[side], vx)).astype(BF)
                    new.append(accs[side] + dot(ds, keys_x))
                return tuple(new)

            def step(kb, accs):
                return block(pl.ds(pl.multiple_of(kb * BLK, BLK), BLK), accs, False)

            lo = lo_ref[qb]
            accs = (jnp.zeros((BLK, LANES), F32),) * 2
            accs = lax.fori_loop(lo, n_far, step, accs)

            @pl.when(lo < n_far)
            def _():
                for side in range(2):
                    base = HD * (1 - side)
                    moved = jnp.sum(jnp.where(lane == base, accs[side], 0.0))
                    far_ref[...] += jnp.where(lane[:8] == 2 * pair + side, moved, 0.0)

            accs = lax.fori_loop(jnp.maximum(lo, n_far), diag, step, accs)
            accs = block(slice(diag * BLK, (diag + 1) * BLK), accs, True)
            dq_ref[at, :] = (jnp.where(lane < HD, accs[0], accs[1]) * HD ** (-0.5)).astype(BF)
            for side in range(2):
                base = HD * (1 - side)
                total = jnp.sum(jnp.where(lane == base, accs[side], 0.0), axis=1, keepdims=True)
                row_ref[at, :] = jnp.where(lane == 2 * pair + side, total, row_ref[at, :])

    return call(
        kernel,
        (pairs,),
        (bounds, q, k, v, d, gq, gk, d),
        [
            spec((rows, LANES), lambda i, *_: (0, i)),
            spec((keys, LANES), lambda i, *_: (0, i)),
            spec((keys, LANES), lambda i, *_: (0, i)),
            spec((rows, LANES), lambda i, *_: (0, i)),
            spec((rows, LANES), lambda i, *_: (0, 0)),
            spec((keys, LANES), lambda i, *_: (0, 0)),
            spec((rows, LANES), lambda i, *_: (0, pairs)),
        ],
        (
            jax.ShapeDtypeStruct(q.shape, BF),
            jax.ShapeDtypeStruct((rows, LANES), F32),
            jax.ShapeDtypeStruct((8, LANES), F32),
        ),
        (
            spec((rows, LANES), lambda i, *_: (0, i)),
            spec((rows, LANES), lambda i, *_: (0, 0)),
            spec((8, LANES), lambda i, *_: (0, 0)),
        ),
        [pltpu.VMEM((2, keys, LANES), BF)],
        prefetch=1,
        flops=6 * rows * 768 * LANES * n_heads,
        nbytes=3 * keys * 2 * HD * n_heads,
        exps=rows * 768 * n_heads,
    )


def attention_dkv(bounds, k, v, q, d, gq, q_one, q_two, d_one, d_two, gk, gkn, n_heads):
    rows, tail = q.shape[0], q_two.shape[0]
    later = 2 * rows
    place = k.shape[0] // rows - 1
    n_k = rows // BLK
    pairs = n_heads // 2

    def kernel(
        hi_ref, k_ref, v_ref, q_ref, d_ref, gq_ref, gd_ref, q1_ref, d1_ref, gq1_ref, gd1_ref,
        q2_ref, d2_ref, gq2_ref, gd2_ref, gk_ref, gkn_ref,
        dk_ref, dv_ref, own_ref, next_ref, qx, dx, qnx, dnx,
    ):
        pair = pl.program_id(0)
        lane = lax.broadcasted_iota(jnp.int32, (BLK, LANES), 1)
        causal = lax.broadcasted_iota(jnp.int32, (BLK, BLK), 1) >= lax.broadcasted_iota(jnp.int32, (BLK, BLK), 0)
        for side in range(2):
            head = 2 * pair + side
            pick_q, pick_d = (spread_lanes(side, head, n_heads, False), spread_parts(side, head, n_heads))
            qx[side] = with_gates(q_ref[...], gq_ref[...], side, pick_q)
            dx[side] = with_gates(d_ref[...], gd_ref[...], side, pick_d)
            qnx[side, :rows, :] = with_gates(q1_ref[...], gq1_ref[...], side, pick_q)
            dnx[side, :rows, :] = with_gates(d1_ref[...], gd1_ref[...], side, pick_d)
            qnx[side, rows : rows + tail, :] = with_gates(q2_ref[...], gq2_ref[...], side, pick_q)
            dnx[side, rows : rows + tail, :] = with_gates(d2_ref[...], gd2_ref[...], side, pick_d)
            qnx[side, rows + tail :, :] = jnp.zeros((rows - tail, LANES), BF)
            dnx[side, rows + tail :, :] = jnp.zeros((rows - tail, LANES), BF)

        @pl.when(pair == 0)
        def _():
            own_ref[...] = jnp.zeros_like(own_ref)
            next_ref[...] = jnp.zeros_like(next_ref)

        for kb in range(n_k):
            at = slice(kb * BLK, (kb + 1) * BLK)
            kx, kxn, vx = [], [], []
            for side in range(2):
                pick = spread_lanes(side, 2 * pair + side, n_heads, True)
                kx.append(with_gates(k_ref[at, :], gk_ref[at, :], side, pick))
                kxn.append(with_gates(k_ref[at, :], gkn_ref[at, :], side, pick))
                vx.append(jnp.where(data_lanes(side, BLK), v_ref[at, :], jnp.ones((), BF)))

            def block(keys_x, q_all, d_all, here, accs, masked):
                new = []
                for side in range(2):
                    queries = q_all[side, here, :]
                    s = dot_t(keys_x[side], queries)
                    if masked:
                        s = jnp.where(causal, s, BIG)
                    w = jnp.exp(s)
                    grads = d_all[side, here, :]
                    ds = (w * dot_t(vx[side], grads)).astype(BF)
                    new += [accs[2 * side] + dot(ds, queries), accs[2 * side + 1] + dot(w.astype(BF), grads)]
                return tuple(new)

            accs = (jnp.zeros((BLK, LANES), F32),) * 4
            for qb in range(kb, n_k):
                accs = block(kx, qx, dx, slice(qb * BLK, (qb + 1) * BLK), accs, qb == kb)

            def column(acc, side):
                base = HD * (1 - side) + 3
                return jnp.sum(jnp.where(lane == base, acc, 0.0), axis=1, keepdims=True)

            own = [column(accs[2 * side], side) for side in range(2)]

            def step(qb, accs):
                return block(kxn, qnx, dnx, pl.ds(pl.multiple_of(qb * BLK, BLK), BLK), accs, False)

            accs = lax.fori_loop(0, hi_ref[kb], step, accs)
            dk_ref[at, :] = jnp.where(lane < HD, accs[0], accs[2]).astype(BF)
            dv_ref[at, :] = jnp.where(lane < HD, accs[1], accs[3]).astype(BF)
            for side in range(2):
                there = lane == 2 * pair + side
                own_ref[at, :] = jnp.where(there, own[side], own_ref[at, :])
                next_ref[at, :] = jnp.where(there, column(accs[2 * side], side) - own[side], next_ref[at, :])

    heads_spec = lambda n: spec((n, LANES), lambda i, *_: (0, i))
    shared = lambda n: spec((n, LANES), lambda i, *_: (0, 0))
    last = lambda n: spec((n, LANES), lambda i, *_: (0, pairs))
    keys_spec = spec((rows, LANES), lambda i, *_: (place, i))
    sizes = [jax.ShapeDtypeStruct(q.shape, BF)] * 2 + [jax.ShapeDtypeStruct((rows, LANES), F32)] * 2
    return call(
        kernel,
        (pairs,),
        (bounds, k, v, q, d, gq, d, q_one, d_one, q_one, d_one, q_two, d_two, q_two, d_two, gk, gkn),
        [
            keys_spec, keys_spec, heads_spec(rows), heads_spec(rows), shared(rows), last(rows),
            heads_spec(rows), heads_spec(rows), last(rows), last(rows),
            heads_spec(tail), heads_spec(tail), last(tail), last(tail),
            spec((rows, LANES), lambda i, *_: (place, 0)), shared(rows),
        ],
        tuple(sizes),
        (heads_spec(rows), heads_spec(rows), shared(rows), shared(rows)),
        [pltpu.VMEM((2, rows, LANES), BF)] * 2 + [pltpu.VMEM((2, later, LANES), BF)] * 2,
        prefetch=1,
        flops=8 * rows * 768 * LANES * n_heads,
        nbytes=6 * rows * 2 * HD * n_heads,
        exps=rows * 768 * n_heads,
    )


def whole(values):
    return spec(values.shape, lambda *_: (0,) * len(values.shape))


def lane_ids(rows):
    return lax.broadcasted_iota(jnp.int32, (rows, LANES), 1)


def split3(values):
    high = values.astype(BF)
    rest = values - high.astype(F32)
    mid = rest.astype(BF)
    return high, mid, (rest - mid.astype(F32)).astype(BF)


def split_lanes(values, n):
    lane = lane_ids(values.shape[0])
    values = jnp.where(lane < n, values, 0.0)
    high, mid, low = (part.astype(F32) for part in split3(values))
    return high + pltpu.roll(mid, n, 1) + pltpu.roll(low, 2 * n, 1)


def exact_dot(mask, values):
    high, mid, low = split3(values)
    return dot(mask, high) + dot(mask, mid) + dot(mask, low)


def norm_terms(blocks):
    width = sum(b.shape[1] for b in blocks)
    total = sum(jnp.sum(b * b, axis=1, keepdims=True) for b in blocks)
    return lax.rsqrt(total / width + 1e-05)


def project(offs, x, x_far, tail, gain, w, side_w, qkv_b, bias, cols, rank_r, filled=None, before=0):
    width = gain.shape[1]
    block = width // 4
    own = filled is None
    n_far = 0 if own else -(-tail // BLK)
    rows = x.shape[0] // BLK * BLK
    grid = rows // BLK + n_far
    base = before // BLK if own else 0

    def kernel(*refs):
        offs_ref, x_ref = refs[0], refs[1]
        at = 2
        if not own:
            far_ref, at = refs[2], 3
        gain_ref, w0, w1, side_ref, b_ref, bias_ref = refs[at : at + 6]
        at += 6 + (0 if own else 3)
        outs, scr = refs[at:-1], refs[-1]
        step = pl.program_id(0)
        blocks = []
        for k in range(4):
            here = pl.ds(pl.multiple_of(offs_ref[k], LANES), block)
            value = x_ref[:, here]
            if not own:
                start = pl.multiple_of(jnp.minimum(step * BLK, tail + 32 - BLK), 32)
                far = far_ref[pl.ds(start, BLK), here]
                value = jnp.where(step < n_far, far, value)
            blocks.append(value.astype(F32))
        factor = norm_terms(blocks)
        for k in range(4):
            here = pl.ds(pl.multiple_of(offs_ref[k], LANES), block)
            scr[:, k * block : (k + 1) * block] = (blocks[k] * factor * gain_ref[:, here]).astype(BF)
        left, right = scr[:, : 2 * block], scr[:, 2 * block :]
        side = dot(left, side_ref[: 2 * block, :]) + dot(right, side_ref[2 * block :, :])
        low = side[:, LANES - rank_r :].astype(BF)
        full = lambda a, b: dot(left, w0[:, a:b]) + dot(right, w1[:, a:b]) + dot(low, b_ref[:, a:b])
        if own:
            n_ref, low_ref, q_ref, k_ref, v_ref, logit_ref = outs
            n_ref[...] = scr[...]
            low_ref[...] = low
            q_ref[...] = (full(0, cols).astype(BF).astype(F32) * HD ** (-0.5)).astype(BF)
        else:
            k_ref, v_ref, logit_ref = outs
        k_ref[...] = full(cols, 2 * cols).astype(BF)
        v_ref[...] = full(2 * cols, 3 * cols).astype(BF)
        logit_ref[...] = side + bias_ref[...]

    keys = before + rows if own else filled[0].shape[0]
    ins = [offs, x] + ([] if own else [x_far]) + [gain, w[0], w[1], side_w, qkv_b, bias] + ([] if own else list(filled))
    row_spec = spec((BLK, width), (lambda i, *_: (i, 0)) if own else (lambda i, *_: (jnp.maximum(i - n_far, 0), 0)))
    in_specs = [row_spec] + ([] if own else [whole(x_far)])
    in_specs += [whole(v) for v in (gain, w[0], w[1], side_w, qkv_b, bias)]
    if not own:
        in_specs += [pl.BlockSpec(memory_space=pl.ANY)] * 3
    at_keys = lambda n: spec((BLK, n), lambda i, *_: (i + base, 0))
    outs = [jax.ShapeDtypeStruct((keys, cols), BF)] * 2 + [jax.ShapeDtypeStruct((keys, LANES), F32)]
    out_specs = [at_keys(cols), at_keys(cols), at_keys(LANES)]
    if own:
        here = lambda n: spec((BLK, n), lambda i, *_: (i, 0))
        outs = [
            jax.ShapeDtypeStruct((rows, width), BF),
            jax.ShapeDtypeStruct((rows, rank_r), BF),
            jax.ShapeDtypeStruct((rows, cols), BF),
        ] + outs
        out_specs = [here(width), here(rank_r), here(cols)] + out_specs
    n_cols = 3 * cols if own else 2 * cols
    return call(
        kernel, (grid,), ins, in_specs, tuple(outs), tuple(out_specs), [pltpu.VMEM((BLK, width), BF)], prefetch=1,
        aliases={} if own else {9: 0, 10: 1, 11: 2},
        flops=2 * grid * BLK * width * n_cols, nbytes=2 * width * 3 * cols,
    )


def gate_tables(logits, seg_keys, seg_row, n_heads, rows):
    keys = logits.shape[0]
    before = keys - rows
    one = 3 * n_heads + DOCS

    def kernel(logit_ref, seg_ref, row_ref, gq_ref, gk_ref, gkn_ref, gate_ref, tot_ref):
        lane = lane_ids(BLK)
        doc = lane - 3 * n_heads + 1
        doc_lane = (doc > 0) & (doc <= DOCS)
        inner = lax.broadcasted_iota(jnp.int32, (BLK, BLK), 1) > lax.broadcasted_iota(jnp.int32, (BLK, BLK), 0)
        later = inner.astype(BF)

        def forget(at):
            value = logit_ref[at, :]
            value = jnp.minimum(value, 0.0) - jnp.log(1.0 + jnp.exp(-jnp.abs(value)))
            return jnp.where((lane < n_heads) & (seg_ref[at, :] > 0), value, 0.0)

        def lanes(values, docs):
            return (split_lanes(values, n_heads) + docs + jnp.where(lane == one, 1.0, 0.0)).astype(BF)

        def docs_k(at):
            return jnp.where(doc_lane & (doc != seg_ref[at, :]), BIG, 0.0)

        def suffix(first, last, carry, out_ref, base):
            for b in range(last - 1, first - 1, -1):
                at = slice(b * BLK, (b + 1) * BLK)
                values = forget(at)
                sums = exact_dot(later, values) + carry
                out_ref[b * BLK - base : (b + 1) * BLK - base, :] = lanes(sums, docs_k(at))
                carry = carry + jnp.sum(values, axis=0, keepdims=True)
            return carry

        n_before, n_all = before // BLK, keys // BLK
        zero = jnp.zeros((1, LANES), F32)
        near = suffix((before - rows) // BLK, n_before, zero, gk_ref, 0)
        tot_ref[...] = jnp.broadcast_to(near, tot_ref.shape)
        suffix(0, (before - rows) // BLK, near, gk_ref, 0)
        suffix(n_before, n_all, zero, gkn_ref, before)
        own = jnp.concatenate([forget(slice(b * BLK, (b + 1) * BLK)) for b in range(n_before, n_all)], axis=0)
        for b in range(rows // BLK):
            at = slice(before + b * BLK, before + (b + 1) * BLK)
            here = slice(b * BLK, (b + 1) * BLK)
            q_pos = lax.broadcasted_iota(jnp.int32, (BLK, rows), 0) + b * BLK
            k_pos = lax.broadcasted_iota(jnp.int32, (BLK, rows), 1)
            same = (row_ref[...] == seg_ref[at, :]) & (k_pos <= q_pos)
            sums = exact_dot(same.astype(BF), own)
            gate_ref[here, :] = sums
            gq_ref[here, :] = lanes(sums, jnp.where(doc_lane & (doc == seg_ref[at, :]), 1.0, 0.0))
            gk_ref[at, :] = lanes(-sums, docs_k(at))

    shape = lambda n, t: jax.ShapeDtypeStruct((n, LANES), t)
    outs = (shape(rows, BF), shape(keys, BF), shape(rows, BF), shape(rows, F32), shape(8, F32))
    return call(
        kernel, (1,), (logits, seg_keys, seg_row), [whole(logits), whole(seg_keys), whole(seg_row)],
        outs, tuple(whole(o) for o in outs), flops=10**8, nbytes=4 * 10**6,
    )


def out_projection(offs, rank, x, mixed_own, mixed_far, w_own, w_far, a_own, a_far, out_b, gain, ffn_a):
    rows, width = x.shape
    block = width // 4
    rank_r = a_own.shape[1]

    def kernel(
        offs_ref, rank_ref, x_ref, mo, mf, wo0, wo1, wf0, wf1, ao, af, b_ref, gain_ref, fa, h_ref, n_ref, low_ref, lo_ref
    ):
        def run(m0, m1, w0, w1, a0, a1):
            low = (dot(m0[...], a0[...]) + dot(m1[...], a1[...])).astype(BF)
            lo_ref[...] = low
            for half in range(2):
                both = dot(m0[...], w0[half][...]) + dot(m1[...], w1[half][...])
                both = both + dot(low, b_ref[:, 2 * half * block : 2 * (half + 1) * block])
                for j in range(2):
                    k = 2 * half + j
                    here = pl.ds(pl.multiple_of(offs_ref[k], LANES), block)
                    value = x_ref[:, here].astype(F32) + both[:, j * block : (j + 1) * block]
                    h_ref[:, k * block : (k + 1) * block] = value

        pl.when(rank_ref[0] == 0)(lambda: run(mo, mf, (wo0, wo1), (wf0, wf1), ao, af))
        pl.when(rank_ref[0] != 0)(lambda: run(mf, mo, (wf0, wf1), (wo0, wo1), af, ao))
        value = h_ref[...]
        normed = (value * norm_terms([value]) * gain_ref[...]).astype(BF)
        n_ref[...] = normed
        low_ref[...] = dot(normed, fa[...]).astype(BF)

    rowed = lambda v: spec((BLK, v.shape[1]), lambda i, *_: (i, 0))
    outs = (
        jax.ShapeDtypeStruct((rows, width), F32), jax.ShapeDtypeStruct((rows, width), BF),
        jax.ShapeDtypeStruct((rows, rank_r), BF), jax.ShapeDtypeStruct((rows, rank_r), BF),
    )
    ins = (offs, rank, x, mixed_own, mixed_far, *w_own, *w_far, a_own, a_far, out_b, gain, ffn_a)
    return call(
        kernel, (rows // BLK,), ins,
        [rowed(x), rowed(mixed_own), rowed(mixed_far)] + [whole(v) for v in ins[5:]],
        outs, tuple(rowed(o) for o in outs), prefetch=2, flops=4 * rows * width * mixed_own.shape[1],
        nbytes=4 * width * mixed_own.shape[1] + 8 * rows * width,
    )


def feed_forward(rank, normed, low, cot, grad_low, weights, ffn_b, down_a, earlier=None):
    rows, width = normed.shape
    depth = width // 2
    half = rows // 2
    rank_r = low.shape[1]
    unit_cols = down_a.shape[0]
    final = earlier is not None
    tile = 512 if unit_cols % 512 == 0 else unit_cols
    tiles = unit_cols // tile

    def kernel(
        rank_ref, x_ref, low_ref, cot_ref, gl_ref, wg0, wg1, wu0, wu1, wd0, wd1, bg_ref, bu_ref, ad_ref, *rest,
    ):
        step = pl.program_id(0)
        if final:
            begin, begin_low, units_ref, gg_ref, gu_ref, far_ref, own_ref, own_low_ref, part_ref, part_low_ref = rest
        else:
            units_ref, gg_ref, gu_ref, part_ref, part_low_ref = rest

        @pl.when(step == 0)
        def _():
            part_ref[...] = begin[...] if final else jnp.zeros_like(part_ref)
            part_low_ref[...] = begin_low[...] if final else jnp.zeros_like(part_low_ref)

        left, right = slice(0, depth), slice(depth, width)
        gate = dot(x_ref[:, left], wg0[...]) + dot(x_ref[:, right], wg1[...]) + dot(low_ref[...], bg_ref[...])
        up = dot(x_ref[:, left], wu0[...]) + dot(x_ref[:, right], wu1[...]) + dot(low_ref[...], bu_ref[...])
        grad = dot(cot_ref[:, left], wd0[...]) + dot(cot_ref[:, right], wd1[...]) + dot_t(gl_ref[...], ad_ref[...])
        sig = jax.nn.sigmoid(gate)
        act = gate * sig
        units_ref[...] = (act * up).astype(BF)
        gg = (grad * up * sig * (1.0 + gate * (1.0 - sig))).astype(BF)
        gu = (grad * act).astype(BF)
        gg_ref[...] = gg
        gu_ref[...] = gu
        part_low_ref[:, :rank_r] += dot_t(gg, bg_ref[...]) + dot_t(gu, bu_ref[...])
        part_ref[:, left] += dot_t(gg, wg0[...]) + dot_t(gu, wu0[...])
        part_ref[:, right] += dot_t(gg, wg1[...]) + dot_t(gu, wu1[...])

        @pl.when((step == tiles - 1) & final)
        def _():
            if not final:
                return
            mine = pl.ds(pl.multiple_of(rank_ref[0] * half, half), half)
            theirs = pl.ds(pl.multiple_of((1 - rank_ref[0]) * half, half), half)
            far_ref[:, :width] = part_ref[theirs, :].astype(BF)
            far_ref[:, width:] = split_lanes(part_low_ref[theirs, :], rank_r).astype(BF)
            own_ref[...] = part_ref[mine, :]
            own_low_ref[...] = part_low_ref[mine, :]

    out = jax.ShapeDtypeStruct((rows, unit_cols), BF)
    out_spec = spec((rows, tile), lambda i, *_: (0, i))
    sums = (jax.ShapeDtypeStruct((rows, width), F32), jax.ShapeDtypeStruct((rows, LANES), F32))
    ends = sums
    if final:
        ends = (
            jax.ShapeDtypeStruct((half, width + LANES), BF), jax.ShapeDtypeStruct((half, width), F32),
            jax.ShapeDtypeStruct((half, LANES), F32),
        )
    return call(
        kernel,
        (tiles,),
        (rank, normed, low, cot, grad_low, *weights, *weights, *weights, ffn_b, ffn_b, down_a, *(earlier or ())),
        [
            whole(normed), whole(low), whole(cot), whole(grad_low),
            *[spec((depth, tile), lambda i, *_: (0, i)) for _ in range(2)],
            *[spec((depth, tile), lambda i, *_: (0, i + tiles)) for _ in range(2)],
            *[spec((depth, tile), lambda i, *_: (0, i + 2 * tiles)) for _ in range(2)],
            spec((rank_r, tile), lambda i, *_: (0, i)),
            spec((rank_r, tile), lambda i, *_: (0, i + tiles)),
            spec((tile, rank_r), lambda i, *_: (i, 0)),
            *[whole(e) for e in earlier or ()],
        ],
        (out, out, out, *ends),
        (out_spec, out_spec, out_spec, *[whole(e) for e in ends]),
        [pltpu.VMEM(e.shape, F32) for e in sums] if final else [],
        prefetch=1,
    )


def whole_low(parts, n):
    parts = parts.astype(F32)
    return parts[:, :n] + parts[:, n : 2 * n] + parts[:, 2 * n : 3 * n]


def middle(rank, own, got, own_low, hidden, cot, gain, ffn_a, out_b, w_own, w_far, a_own, a_far):
    half, width = own.shape
    depth = width // 2
    rank_r = out_b.shape[0]
    cols = a_own.shape[0]

    def kernel(
        rank_ref, own_ref, got_ref, low_ref, h_ref, cot_ref, gain_ref, fa, b_ref, wo0, wo1, wf0, wf1, ao, af,
        gh_ref, ghb_ref, glf_ref, glo_ref, mine_ref, far_ref,
    ):
        ffn_low = (low_ref[:, :rank_r] + whole_low(got_ref[:, width:], rank_r)).astype(BF)
        glf_ref[...] = ffn_low
        incoming = own_ref[...] + got_ref[:, :width].astype(F32) + dot_t(ffn_low, fa[...])
        value = h_ref[...]
        factor = norm_terms([value])
        scaled = incoming * gain_ref[...]
        mean = jnp.mean(value * scaled, axis=1, keepdims=True)
        grad = cot_ref[...].astype(F32) + (factor * scaled - value * (factor * factor * factor * mean))
        gh_ref[...] = grad
        low_precision = grad.astype(BF)
        ghb_ref[...] = low_precision
        left, right = low_precision[:, :depth], low_precision[:, depth:]
        out_low = dot_t(low_precision, b_ref[...]).astype(BF)
        glo_ref[...] = out_low
        mine_ref[...] = (dot_t(left, wo0[...]) + dot_t(right, wo1[...]) + dot_t(out_low, ao[...])).astype(BF)
        far_ref[...] = (dot_t(left, wf0[...]) + dot_t(right, wf1[...]) + dot_t(out_low, af[...])).astype(BF)

    outs = (
        jax.ShapeDtypeStruct((half, width), F32), jax.ShapeDtypeStruct((half, width), BF),
        jax.ShapeDtypeStruct((half, rank_r), BF), jax.ShapeDtypeStruct((half, rank_r), BF),
        jax.ShapeDtypeStruct((half, cols), BF), jax.ShapeDtypeStruct((half, cols), BF),
    )
    ins = (rank, own, got, own_low, hidden, cot, gain, ffn_a, out_b, *w_own, *w_far, a_own, a_far)
    mine = lambda v: spec((half, v.shape[1]), lambda i, r: (r[0], 0))
    in_specs = [whole(own), whole(got), whole(own_low), mine(hidden), mine(cot)] + [whole(v) for v in ins[6:]]
    return call(
        kernel, (1,), ins, in_specs, outs, tuple(whole(o) for o in outs), prefetch=1,
        flops=4 * half * width * cols, nbytes=4 * width * cols + 16 * half * width,
    )


def mixed_gradient(rank, own, far, mixed, n_heads):
    half, cols = own.shape

    def kernel(rank_ref, own_ref, far_ref, mixed_ref, out_ref):
        lane = lane_ids(half)
        for ref, first in ((own_ref, rank_ref[0]), (far_ref, 1 - rank_ref[0])):
            at = pl.ds(pl.multiple_of(first * half, half), half)
            sums = jnp.zeros((half, LANES), F32)
            for pair in range(n_heads // 2):
                here = slice(pair * LANES, (pair + 1) * LANES)
                product = ref[:, here].astype(F32) * mixed_ref[at, here]
                a = jnp.sum(jnp.where(lane < HD, product, 0.0), axis=1, keepdims=True)
                b = jnp.sum(jnp.where(lane < HD, 0.0, product), axis=1, keepdims=True)
                sums = jnp.where(lane == 2 * pair, -a, jnp.where(lane == 2 * pair + 1, -b, sums))
            out_ref[at, :cols] = ref[...]
            out_ref[at, cols:] = split_lanes(sums, n_heads).astype(BF)

    out = jax.ShapeDtypeStruct((2 * half, cols + LANES), BF)
    return call(
        kernel, (1,), (rank, own, far, mixed), [whole(own), whole(far), whole(mixed)], out, whole(out), prefetch=1,
        flops=4 * half * cols, nbytes=16 * half * cols,
    )


def input_gradient(rank, grads, logits, seg_keys, seg_row, row_lanes, own_lanes, next_lanes, across, w, side_w, qkv_b, n_heads):
    rows, cols = grads[0].shape
    depth = w[0].shape[0]
    half = rows // 2
    rank_r = qkv_b.shape[0]
    before = logits.shape[0] - rows
    steps = 3
    chunk = 2 * depth // (2 * steps)

    def kernel(
        rank_ref, q_ref, k_ref, v_ref, logit_ref, seg_ref, seg_row_ref, r_ref, o_ref, n_ref, a_ref, w0, w1, s0, s1, b_ref,
        far_ref, own_ref, low_ref, gl_ref,
    ):
        @pl.when(pl.program_id(0) == 0)
        def _():
            lane = lane_ids(rows)
            t = lax.broadcasted_iota(jnp.int32, (rows, rows), 0)
            i = lax.broadcasted_iota(jnp.int32, (rows, rows), 1)
            same = ((seg_row_ref[...] == seg_ref[...]) & (i >= t)).astype(BF)
            total = exact_dot(same, r_ref[...] - o_ref[...]) + exact_dot((i < t).astype(BF), n_ref[...])
            total = total + a_ref[:1, :]
            value = jnp.where(lane < n_heads, total * jax.nn.sigmoid(-logit_ref[...]), 0.0)
            gl_ref[...] = value.astype(BF)
            low = dot_t(q_ref[...], b_ref[:, :cols]) + dot_t(k_ref[...], b_ref[:, cols : 2 * cols])
            low_ref[...] = low + dot_t(v_ref[...], b_ref[:, 2 * cols :])

        mine = pl.ds(pl.multiple_of(rank_ref[0] * half, half), half)
        theirs = pl.ds(pl.multiple_of((1 - rank_ref[0]) * half, half), half)
        for p, (w_ref, s_ref) in enumerate(((w0, s0), (w1, s1))):
            def part(at):
                value = dot_t(q_ref[at, :], w_ref[:, :cols]) + dot_t(k_ref[at, :], w_ref[:, cols : 2 * cols])
                return value + dot_t(v_ref[at, :], w_ref[:, 2 * cols :]) + dot_t(gl_ref[at, :], s_ref[...])

            far_ref[p] = part(theirs).astype(BF)
            own_ref[p] = part(mine)

    ins = (rank, *grads, logits, seg_keys, seg_row, row_lanes, own_lanes, next_lanes, across, w[0], w[1], side_w, side_w, qkv_b)
    at_own = lambda v: spec((rows, v.shape[1]), lambda i, *_: (before // rows, 0))
    in_specs = [whole(g) for g in grads] + [at_own(logits), at_own(seg_keys)]
    in_specs += [whole(v) for v in (seg_row, row_lanes, own_lanes, next_lanes, across)]
    n_col = w[0].shape[1]
    in_specs += [spec((chunk, n_col), lambda i, *_: (i, 0))] * 2
    in_specs += [spec((chunk, LANES), lambda i, *_: (i, 0)), spec((chunk, LANES), lambda i, *_: (i + steps, 0))]
    in_specs += [whole(qkv_b)]
    outs = (
        jax.ShapeDtypeStruct((2, half, depth), BF), jax.ShapeDtypeStruct((2, half, depth), F32),
        jax.ShapeDtypeStruct((rows, rank_r), F32),
    )
    halves = spec((2, half, chunk), lambda i, *_: (0, 0, i))
    return call(
        kernel, (steps,), ins, in_specs, outs, (halves, halves, whole(outs[2])), [pltpu.VMEM((rows, LANES), BF)],
        prefetch=1, flops=2 * rows * 2 * depth * 3 * cols, nbytes=4 * depth * 3 * cols,
    )


def token_gradient(offs, rank, own, got, grad_low, a, x, gain, grad_hidden):
    half, width = grad_hidden.shape
    block = width // 4

    def kernel(offs_ref, rank_ref, own_ref, got_ref, low_ref, a_ref, x_ref, gain_ref, gh_ref, out_ref):
        blocks, scaled, product = [], [], 0.0
        for k in range(4):
            here = pl.ds(pl.multiple_of(offs_ref[k], LANES), block)
            cols = slice(k % 2 * block, (k % 2 + 1) * block)
            value = own_ref[k // 2][:, cols] + got_ref[k // 2][:, cols].astype(F32)
            value = value + dot_t(low_ref[...], a_ref[k * block : (k + 1) * block, :])
            blocks.append(x_ref[:, here].astype(F32))
            scaled.append(value * gain_ref[:, here])
            product = product + jnp.sum(blocks[k] * scaled[k], axis=1, keepdims=True)
        factor = norm_terms(blocks)
        mean = product / width
        for k in range(4):
            here = pl.ds(pl.multiple_of(offs_ref[k], LANES), block)
            back = factor * scaled[k] - blocks[k] * (factor * factor * factor * mean)
            out_ref[:, here] = (gh_ref[:, k * block : (k + 1) * block] + back).astype(BF)

    mine = lambda v: spec((half, v.shape[1]), lambda i, o, r: (r[0], 0))
    out = jax.ShapeDtypeStruct((half, width), BF)
    return call(
        kernel, (1,), (offs, rank, own, got, grad_low, a, x, gain, grad_hidden),
        [whole(own), whole(got), mine(grad_low), whole(a), mine(x), whole(gain), whole(grad_hidden)],
        out, whole(out), prefetch=2, nbytes=20 * half * width,
    )


def both_halves(rank, own, far):
    half, width = own.shape

    def kernel(rank_ref, own_ref, far_ref, out_ref):
        @pl.when(pl.program_id(0) == rank_ref[0])
        def _():
            out_ref[...] = own_ref[...].astype(F32)

        @pl.when(pl.program_id(0) != rank_ref[0])
        def _():
            out_ref[...] = far_ref[...].astype(F32)

    return call(
        kernel, (2,), (rank, own, far), [whole(own), whole(far)], jax.ShapeDtypeStruct((2 * half, width), F32),
        spec((half, width), lambda i, *_: (i, 0)), prefetch=1, nbytes=16 * half * width,
    )


def down_partial(units, weights, down_a):
    rows, unit_cols = units[0].shape
    depth = weights[0][0].shape[0]
    rank_r = down_a[0].shape[1]

    def kernel(u0, u1, w00, w01, w10, w11, a0, a1, out_ref, low_ref):
        low_ref[...] = jnp.zeros_like(low_ref)
        low_ref[:, :rank_r] = dot(u0[...], a0[...]) + dot(u1[...], a1[...])
        out_ref[:, :depth] = (dot_t(u0[...], w00[...]) + dot_t(u1[...], w10[...])).astype(BF)
        out_ref[:, depth : 2 * depth] = (dot_t(u0[...], w01[...]) + dot_t(u1[...], w11[...])).astype(BF)
        out_ref[:, 2 * depth :] = split_lanes(low_ref[...], rank_r).astype(BF)

    rowed = lambda n: spec((BLK, n), lambda i: (i, 0))
    ins = (*units, *weights[0], *weights[1], *down_a)
    down_spec = spec((depth, unit_cols), lambda i: (0, 2))
    return call(
        kernel, (rows // BLK,), ins, [rowed(unit_cols)] * 2 + [down_spec] * 4 + [whole(v) for v in down_a],
        jax.ShapeDtypeStruct((rows, 2 * depth + LANES), BF), rowed(2 * depth + LANES), [pltpu.VMEM((BLK, LANES), F32)],
    )


def block_result(offs, hidden, own, got, down_b):
    rows, width = hidden.shape
    block = width // 4
    rank_r = down_b.shape[0]

    def kernel(offs_ref, h_ref, own_ref, got_ref, b_ref, out_ref, sum_ref):
        low = (whole_low(own_ref[:, width:], rank_r) + whole_low(got_ref[:, width:], rank_r)).astype(BF)
        sum_ref[...] = low
        for k in range(4):
            here = pl.ds(pl.multiple_of(offs_ref[k], LANES), block)
            cols = slice(k * block, (k + 1) * block)
            both = own_ref[:, cols].astype(F32) + got_ref[:, cols].astype(F32)
            out_ref[:, here] = (h_ref[:, cols] + both + dot(low, b_ref[:, cols])).astype(BF)

    rowed = lambda v: spec((BLK, v.shape[1]), lambda i, *_: (i, 0))
    outs = (jax.ShapeDtypeStruct((rows, width), BF), jax.ShapeDtypeStruct((rows, rank_r), BF))
    return call(
        kernel, (rows // BLK,), (offs, hidden, own, got, down_b),
        [rowed(hidden), rowed(own), rowed(got), whole(down_b)], outs, tuple(rowed(o) for o in outs),
        prefetch=1, nbytes=12 * rows * width,
    )


def body(
    tokens, segments, adapter_index, w_qkv, w_forget, forget_bias, w_out, w_gate_up, w_down,
    gain_attn, gain_ffn, a_qkv, b_qkv, a_out, b_out, a_gate_up, b_gate_up, a_down, b_down, cotangent,
):
    count, rows, width = tokens.shape
    assert count == 1
    head_cols = w_qkv.shape[2]
    n_heads = w_forget.shape[1]
    unit_cols = w_gate_up.shape[2]
    rank_r = a_qkv.shape[2]
    n_f, n_c, n_t = (lax.axis_size("fsdp"), lax.axis_size("ctx"), lax.axis_size("tp"))
    f_rank, t_rank = (lax.axis_index("fsdp"), lax.axis_index("tp"))
    hops = -(-(DOC_MOST - 1) // rows)
    assert hops == 2 and n_c > 2 and n_t == 2 and n_f % 4 == 0
    tail = -(-(DOC_MOST - 1 - rows) // 32) * 32
    before = hops * rows
    half = rows // 2
    block = width // 4
    first = t_rank == 0
    rank = t_rank.astype(jnp.int32)[None]

    def other(values):
        return lax.ppermute(values, "tp", [(0, 1), (1, 0)])

    mix = lambda values, dim: to_xor(values, dim, n_f, f_rank)
    direct = n_f == 4 and block % LANES == 0
    if direct:
        offs = jnp.stack([(f_rank ^ step) * block for step in xor_order(4)]).astype(jnp.int32)
        lay = lambda values, dim: values
    else:
        offs = jnp.arange(4, dtype=jnp.int32) * block
        lay = mix

    pick = adapter_index[0]
    tok = lay(tokens[0], 1)
    seg_one = segments[0] + 1
    note = jnp.zeros((32, width), BF).at[0, :rows].set(seg_one.astype(BF))
    qkv_far = far_blocks(w_qkv.reshape(-1, 3 * head_cols), 0)
    prev_one = shift(jnp.concatenate([tok, note], axis=0), 1, n_c)
    side = jnp.broadcast_to(pick.astype(BF), (w_forget.shape[0], 1))
    side_far = far_blocks(jnp.concatenate([w_forget, side], axis=1), 0)
    take = lambda table: lax.dynamic_index_in_dim(table, pick, 0, keepdims=False)
    mine = lambda values, n, dim: lax.dynamic_slice_in_dim(values, t_rank * n, n, dim)
    theirs = lambda values, n, dim: lax.dynamic_slice_in_dim(values, (1 - t_rank) * n, n, dim)
    qkv_a, ffn_a = (mix(take(a_qkv), 0), mix(take(a_gate_up), 0))
    out_b, down_b = (mix(take(b_out), 1), mix(take(b_down), 1))
    qkv_b = mine(take(b_qkv), head_cols, 2).reshape(rank_r, 3 * head_cols)
    out_a = take(a_out)
    out_a_own, out_a_far = (mine(out_a, head_cols, 0), theirs(out_a, head_cols, 0))
    ffn_b = mine(take(b_gate_up), unit_cols, 2).reshape(rank_r, 2 * unit_cols)
    down_a = mine(take(a_down), unit_cols, 0)
    gain_one = lay(gain_attn.astype(F32), 0)[None]
    gain_two = mix(gain_ffn.astype(F32), 0)[None]
    bias = jnp.pad(forget_bias.astype(F32), (0, LANES - n_heads))[None]
    cot = mix(cotangent[0], 1)
    grad_low_down = dot_t(cot, down_b).astype(BF)

    units_half = unit_cols // 2
    halves = [slice(0, units_half), slice(units_half, unit_cols)]
    ffn_own = [
        jnp.concatenate([w_gate_up[:, 0, at], w_gate_up[:, 1, at], w_down[at].T], axis=1) for at in halves
    ]
    ffn_b_half = [ffn_b.reshape(rank_r, 2, unit_cols)[:, :, at].reshape(rank_r, -1) for at in halves]
    down_a_half = [down_a[at] for at in halves]
    (
        prev_one, qkv_far, side_far, qkv_a, ffn_a, out_b, down_b, qkv_b, out_a_own, out_a_far, ffn_b_half, down_a_half,
        gain_one, gain_two, bias, cot, grad_low_down, ffn_own, w_out,
    ) = lax.optimization_barrier((
        prev_one, qkv_far, side_far, qkv_a, ffn_a, out_b, down_b, qkv_b, out_a_own, out_a_far, ffn_b_half, down_a_half,
        gain_one, gain_two, bias, cot, grad_low_down, ffn_own, w_out,
    ))
    out_far = far_blocks(w_out, 1)
    prev_two = shift(prev_one[rows - tail :], 1, n_c)
    qkv_w = near_blocks(*qkv_far, 0)
    side_all = jnp.concatenate(near_blocks(*side_far, 0), axis=0)
    every = from_xor(side_all[:: w_forget.shape[0], n_heads], 0, n_f, f_rank).astype(jnp.int32)
    side_w = jnp.concatenate([side_all, jnp.zeros((width, LANES - n_heads - 1 - rank_r), BF), qkv_a], axis=1)
    ffn_far = [far_blocks(after(ffn_own[0], out_far[1]), 0)]

    args = (gain_one, qkv_w, side_w, qkv_b, bias, head_cols, rank_r)
    out_w_own = near_blocks(*out_far, 1)
    normed, low_qkv, query, *filled = project(offs, tok, None, tail, *args, None, before)
    prev_two = after(prev_two, query)
    seg_two = prev_two[tail, :rows].astype(jnp.int32)
    seg_far = []
    for b in range(-(-tail // BLK)):
        start, end = min(b * BLK, tail + 32 - BLK), min((b + 1) * BLK, tail)
        known = seg_two[rows - tail + b * BLK : rows - tail + end]
        seg_far.append(jnp.pad(known, (b * BLK - start, BLK - (end - start))))
    seg_keys = jnp.concatenate(seg_far + [prev_one[rows, :rows].astype(jnp.int32), seg_one])
    last_keys = jnp.max(seg_keys.reshape(-1, BLK), axis=1)
    lows = jnp.sum(last_keys[None, :] < seg_one[::BLK][:, None], axis=1).astype(jnp.int32)

    keys, vals, logits = project(offs, prev_one, prev_two, tail, *args, filled)
    out_w_far = [other(part) for part in out_w_own]
    seg_col, seg_row = (seg_keys[:, None], seg_one[None, :])
    logits, *out_w_far = lax.optimization_barrier((logits, *out_w_far))
    gq, gk, gk_next, gates, total = gate_tables(logits, seg_col, seg_row, n_heads, rows)
    mixed_own, mixed_f, gq_one, gq_two = attention_forward(lows, query, keys, vals, gq, gk, gates, total, n_heads)
    mixed_far = other(mixed_own)
    ffn_w = [near_blocks(ffn_far[0][0], after(ffn_far[0][1], mixed_far), 0)]
    ffn_far.append(far_blocks(after(ffn_own[1], ffn_far[0][1], mixed_own), 0))
    sent_q1 = jnp.concatenate([query, gq_one], axis=1)
    sent_q2 = jnp.concatenate([query[:tail], gq_two[:tail]], axis=1)
    mixed_far, sent_q1, sent_q2 = lax.optimization_barrier((mixed_far, sent_q1, sent_q2))
    next_q1 = shift(sent_q1, -1, n_c)
    next_q2 = shift(sent_q2, -2, n_c)

    hidden, normed_ffn, low_ffn, low_out = out_projection(
        offs, rank, tok, mixed_own, mixed_far, out_w_own, out_w_far, out_a_own, out_a_far, out_b, gain_two, ffn_a
    )
    ffn_in = (rank, normed_ffn, low_ffn, cot, grad_low_down)
    units_a, gate_a, up_a, *sums = feed_forward(*ffn_in, ffn_w[0], ffn_b_half[0], down_a_half[0])
    ffn_w.append(near_blocks(ffn_far[1][0], after(ffn_far[1][1], units_a), 0))
    units_b, gate_b, up_b, far, own, own_low = feed_forward(
        *ffn_in, ffn_w[1], ffn_b_half[1], down_a_half[1], sums
    )
    units, grad_gate, grad_up = ((units_a, units_b), (gate_a, gate_b), (up_a, up_b))
    got = other(far)
    down_own = down_partial((units_a, after(units_b, far)), ffn_w, down_a_half)
    got, down_own = lax.optimization_barrier((got, down_own))
    grad_hidden, grad_hidden_b, grad_low_ffn, grad_low_out, gm_own, gm_send = middle(
        rank, own, got, own_low, hidden, cot, gain_two, ffn_a, out_b, out_w_own, out_w_far, out_a_own, out_a_far
    )
    grad_mixed = mixed_gradient(rank, gm_own, other(gm_send), mixed_f, n_heads)

    sent_d2 = grad_mixed[:tail]
    next_d1 = shift(grad_mixed, -1, n_c)
    next_d2 = shift(sent_d2, -2, n_c)
    grad_q, row_lanes, across = attention_dq(
        lows, query, keys, vals, grad_mixed, gq_one, gk, n_heads, (before - rows) // BLK
    )
    across = shift(across, -1, n_c)
    docs_at = head_cols + 3 * n_heads
    next_q1, next_q2, next_d1, next_d2, _ = lax.optimization_barrier((next_q1, next_q2, next_d1, next_d2, grad_q))
    next_docs = jnp.concatenate([next_q1[::BLK, docs_at : docs_at + DOCS], next_q2[::BLK, docs_at : docs_at + DOCS]])
    next_docs = next_docs.astype(F32)
    ids = jnp.arange(1, DOCS + 1).astype(F32)
    next_first = jnp.where(jnp.sum(next_docs, 1) > 0, jnp.sum(next_docs * ids[None, :], 1), 99.0)
    last_rows = seg_one[BLK - 1 :: BLK].astype(F32)
    highs = jnp.sum(next_first[None, :] <= last_rows[:, None], axis=1).astype(jnp.int32)
    grad_k, grad_v, own_lanes, next_lanes = attention_dkv(
        highs, keys, vals, query, grad_mixed, gq_one, next_q1, next_q2, next_d1, next_d2, gk, gk_next, n_heads
    )
    down_got = other(after(down_own, grad_mixed))

    lane = lax.broadcasted_iota(jnp.int32, (1, width), 1)
    own_part = lambda values: values * (lane // (width // 2) == t_rank)
    natural = lambda values: from_xor(values, 1, n_f, f_rank)
    by_tp = lambda a, b: jnp.concatenate([jnp.where(first, a, b), jnp.where(first, b, a)], axis=1)
    place = lambda values: by_tp(values, jnp.zeros_like(values))
    rows_of = lambda values: lax.dynamic_slice_in_dim(values, t_rank * half, half, 0)
    onehot = (jnp.arange(a_qkv.shape[0])[:, None] == every[None, :]).astype(F32)
    onehot = jnp.repeat(onehot, n_c * n_t, axis=1)

    owners = n_f * n_c * n_t

    def to_owners(tables, *done):
        packed = jnp.concatenate([t.reshape(rank_r, owners, -1) for t in tables], axis=2).transpose(1, 0, 2)
        packed = packed.reshape(owners, -1)
        landed = lax.all_to_all(after(packed, *done), ("fsdp", "ctx", "tp"), 0, 0, tiled=True)
        return landed, [t.shape[1] // owners for t in tables]

    def spread_out(landed, sizes):
        spread = jnp.dot(onehot, landed, precision=HI, preferred_element_type=F32).reshape(-1, rank_r, sum(sizes))
        outs, at = [], 0
        for size in sizes:
            outs.append(spread[:, :, at : at + size])
            at += size
        return outs

    early, early_sizes = to_owners([
        by_tp(t_dot(grad_low_out, rows_of(mixed_own)), t_dot(grad_low_out, rows_of(mixed_far))),
        natural(t_dot(rows_of(low_out), grad_hidden_b)),
        natural(t_dot(grad_low_ffn, rows_of(normed_ffn))),
        place(jnp.concatenate([t_dot(low_ffn, part) for part in grad_gate], axis=1)),
        place(jnp.concatenate([t_dot(low_ffn, part) for part in grad_up], axis=1)),
        place(jnp.concatenate([t_dot(grad_low_down, part) for part in units], axis=1)),
    ], next_d2)
    grad_q, early = lax.optimization_barrier((grad_q, early))

    grads = (grad_q, grad_k, grad_v)
    far_in, own_in, part_low_qkv = input_gradient(
        rank, grads, logits, seg_col, seg_row, row_lanes, own_lanes, next_lanes, across, qkv_w, side_w, qkv_b, n_heads
    )
    grad_low_qkv = (part_low_qkv + other(part_low_qkv)).astype(BF)
    got_in = other(far_in)
    block_output, low_down = block_result(offs, hidden, down_own, after(down_got, far_in), down_b)
    early = spread_out(after(early, far_in), early_sizes)
    grad_tok = token_gradient(offs, rank, own_in, got_in, grad_low_qkv, qkv_a, tok, gain_one, grad_hidden)
    grad_tokens = both_halves(rank, grad_tok, other(grad_tok))
    if not direct:
        block_output = from_xor(block_output, 1, n_f, f_rank)
        grad_tokens = from_xor(grad_tokens, 1, n_f, f_rank)

    late = spread_out(*to_owners(
        [own_part(natural(t_dot(grad_low_qkv, normed)))]
        + [place(t_dot(low_qkv, grad)) for grad in grads]
        + [own_part(natural(t_dot(low_down, cot)))],
        grad_tok,
    ))
    swap = lambda values: values.transpose(0, 2, 1)
    return (
        block_output[None],
        grad_tokens[None],
        swap(late[0]),
        jnp.stack(late[1:4], axis=2),
        swap(early[0]),
        early[1],
        swap(early[2]),
        jnp.stack(early[3:5], axis=2),
        swap(early[5]),
        late[4],
    )


def solution(mesh):
    in_specs = (
        P("fsdp", "ctx", None), P("fsdp", "ctx"), P("fsdp"), P("fsdp", None, "tp"), P("fsdp", "tp"), P("tp"),
        P("tp", "fsdp"), P("fsdp", None, "tp"), P("tp", "fsdp"),
        P(), P(), P(), P(), P(), P(), P(), P(), P(), P(),
        P("fsdp", "ctx", None),
    )
    out_specs = (
        P("fsdp", "ctx", None),
        P("fsdp", "ctx", None),
        P(None, ("fsdp", "ctx", "tp"), None),
        P(None, None, None, ("fsdp", "ctx", "tp")),
        P(None, ("fsdp", "ctx", "tp"), None),
        P(None, None, ("fsdp", "ctx", "tp")),
        P(None, ("fsdp", "ctx", "tp"), None),
        P(None, None, None, ("fsdp", "ctx", "tp")),
        P(None, ("fsdp", "ctx", "tp"), None),
        P(None, None, ("fsdp", "ctx", "tp")),
    )
    return jax.shard_map(body, mesh=mesh, in_specs=in_specs, out_specs=out_specs, check_vma=False)
```

```python
import jax
import jax.numpy as jnp
from jax import lax
from jax.experimental import pallas as pl
from jax.experimental.pallas import tpu as pltpu
from jax.sharding import PartitionSpec as P

HD = 64
DOC_MOST = 800
DOCS = 8
BF = jnp.bfloat16
F32 = jnp.float32
HI = lax.Precision.HIGHEST


def dot(a, b):
    return jnp.dot(a, b, preferred_element_type=F32)


def dot_t(a, b):
    return lax.dot_general(a, b, (((1,), (1,)), ((), ())), preferred_element_type=F32)


def t_dot(a, b):
    return lax.dot_general(a, b, (((0,), (0,)), ((), ())), preferred_element_type=F32)


def xor_order(size):
    order, bit = [0], size // 2
    while bit:
        order, bit = order + [step ^ bit for step in order], bit // 2
    return order


def after(values, *done):
    return lax.optimization_barrier((values, *done))[0]


def far_blocks(shard, dim):
    size = lax.axis_size("fsdp")
    own, bit = shard, size // 2
    while True:
        got = lax.ppermute(own, "fsdp", [(i, i ^ bit) for i in range(size)])
        if bit == 2:
            return own, got
        own, bit = jnp.concatenate([own, got], axis=dim), bit // 2


def near_blocks(own, got, dim):
    both = jnp.concatenate([own, got], axis=dim)
    size = lax.axis_size("fsdp")
    return [both, lax.ppermute(both, "fsdp", [(i, i ^ 1) for i in range(size)])]


def to_xor(values, dim, size, rank):
    block = values.shape[dim] // size
    return jnp.concatenate(
        [lax.dynamic_slice_in_dim(values, (rank ^ step) * block, block, dim) for step in xor_order(size)],
        axis=dim,
    )


def from_xor(values, dim, size, rank):
    block = values.shape[dim] // size
    bits = size.bit_length() - 1
    pieces = []
    for natural in range(size):
        mixed = rank ^ natural
        place = sum(((mixed >> j) & 1) << (bits - 1 - j) for j in range(bits))
        pieces.append(lax.dynamic_slice_in_dim(values, place * block, block, dim))
    return jnp.concatenate(pieces, axis=dim)


def shift(values, hop, size):
    pairs = [(i, i + hop) for i in range(size) if 0 <= i + hop < size]
    return lax.ppermute(values, "ctx", pairs)


LANES = 128
BLK = 256
BIG = -1e30


def spec(shape, index):
    return pl.BlockSpec(shape, index)


def call(kernel, grid, ins, in_specs, outs, out_specs, scratch=(), prefetch=0, flops=0, nbytes=0, exps=0, aliases=None):
    return pl.pallas_call(
        kernel,
        out_shape=outs,
        grid_spec=pltpu.PrefetchScalarGridSpec(
            num_scalar_prefetch=prefetch, grid=grid, in_specs=in_specs, out_specs=out_specs, scratch_shapes=list(scratch)
        ),
        compiler_params=pltpu.CompilerParams(
            dimension_semantics=("arbitrary",) * len(grid), vmem_limit_bytes=56 * 2**20
        ),
        input_output_aliases=aliases or {},
        cost_estimate=pl.CostEstimate(flops=1, bytes_accessed=1, transcendentals=0),
    )(*ins)


def whole(values):
    return spec(values.shape, lambda *_: (0,) * len(values.shape))


def lane_ids(rows):
    return lax.broadcasted_iota(jnp.int32, (rows, LANES), 1)


def split3(values):
    high = values.astype(BF)
    rest = values - high.astype(F32)
    mid = rest.astype(BF)
    return high, mid, (rest - mid.astype(F32)).astype(BF)


def split_lanes(values, n):
    lane = lane_ids(values.shape[0])
    values = jnp.where(lane < n, values, 0.0)
    high, mid, low = (part.astype(F32) for part in split3(values))
    return high + pltpu.roll(mid, n, 1) + pltpu.roll(low, 2 * n, 1)


def exact_dot(mask, values):
    high, mid, low = split3(values)
    return dot(mask, high) + dot(mask, mid) + dot(mask, low)


def norm_terms(blocks):
    width = sum(b.shape[1] for b in blocks)
    total = sum(jnp.sum(b * b, axis=1, keepdims=True) for b in blocks)
    return lax.rsqrt(total / width + 1e-05)


def pair_lanes(pair, n_heads, kind):
    lane = lax.broadcasted_iota(jnp.int32, (LANES, LANES), 1)
    to = lane & (HD - 1)
    head = jnp.where(lane >= HD, 2 * pair, 2 * pair + 1)
    gate_at = 3 if kind == "k" else 0
    part = to - gate_at
    source = jnp.where((part >= 0) & (part < 3), part * n_heads + head, -1)
    if kind != "d":
        ones = to - (3 - gate_at)
        source = jnp.where((ones >= 0) & (ones < 3), 3 * n_heads + DOCS, source)
        source = jnp.where((to >= 8) & (to < 8 + DOCS), to - 8 + 3 * n_heads, source)
    return (lax.broadcasted_iota(jnp.int32, (LANES, LANES), 0) == source).astype(BF)


def pair_of(values, gate_parts, select):
    extra = dot(gate_parts, select).astype(BF)
    low = lane_ids(values.shape[0]) < HD
    return jnp.where(low, values, extra), jnp.where(low, extra, values)


def pair_ones(values):
    low = lane_ids(values.shape[0]) < HD
    one = jnp.ones((), BF)
    return jnp.where(low, values, one), jnp.where(low, one, values)


def block_at(index):
    return pl.ds(pl.multiple_of(index * BLK, BLK), BLK)


def causal_from(rows, first):
    row = lax.broadcasted_iota(jnp.int32, (rows, BLK), 0)
    return row + first >= lax.broadcasted_iota(jnp.int32, (rows, BLK), 1)


def lane_column(acc, lane_at):
    return jnp.sum(jnp.where(lane_ids(acc.shape[0]) == lane_at, acc, 0.0), axis=1, keepdims=True)


def attention_forward(bounds, q, k, v, gq, gk, gates, total, n_heads):
    rows, keys = q.shape[0], k.shape[0]
    n_before = (keys - rows) // BLK
    pairs = n_heads // 2
    assert rows == 2 * BLK

    def kernel(
        lo_ref, q_ref, k_ref, v_ref, gq_ref, gk_ref, gate_ref, tot_ref, mixed_ref, float_ref, one_ref, two_ref,
        qx, scores, tops, parts, accs, log_ref,
    ):
        pair = pl.program_id(0)
        pick_k = pair_lanes(pair, n_heads, "k")
        for side, value in enumerate(pair_of(q_ref[...], gq_ref[...], pair_lanes(pair, n_heads, "q"))):
            qx[side] = value
        both, late, early = slice(0, rows), slice(BLK, rows), slice(0, BLK)

        def score(kb, here, at, mask=None, first=False):
            for side, key in enumerate(pair_of(k_ref[here, :], gk_ref[here, :], pick_k)):
                s = dot_t(qx[side, at, :], key)
                if mask is not None:
                    s = jnp.where(mask, s, BIG)
                scores[side, at, here] = s
                top = jnp.maximum(s[:, :LANES], s[:, LANES:])
                tops[side, at, :] = top if first else jnp.maximum(tops[side, at, :], top)

        def gather(here, at, first=False):
            for side in range(2):
                w = jnp.exp(scores[side, at, here] - tops[side, at, :1])
                part = w[:, :LANES] + w[:, LANES:]
                acc = dot(w.astype(BF), v_ref[here, :])
                parts[side, at, :] = part if first else parts[side, at, :] + part
                accs[side, at, :] = acc if first else accs[side, at, :] + acc

        own = [slice(b * BLK, (b + 1) * BLK) for b in (n_before, n_before + 1)]
        low, high = lo_ref[0], jnp.minimum(lo_ref[1], n_before)
        score(n_before, own[0], both, causal_from(rows, 0), True)
        score(n_before + 1, own[1], late, causal_from(BLK, 0))
        pl.loop(high, n_before)(lambda kb: score(kb, block_at(kb), both))
        pl.loop(low, high)(lambda kb: score(kb, block_at(kb), early))
        for side in range(2):
            tops[side] = jnp.broadcast_to(jnp.max(tops[side], axis=1, keepdims=True), (rows, LANES))
        gather(own[0], both, True)
        gather(own[1], late)
        pl.loop(high, n_before)(lambda kb: gather(block_at(kb), both))
        pl.loop(low, high)(lambda kb: gather(block_at(kb), early))
        lane = lane_ids(rows)
        results, logs = [], jnp.zeros((rows, LANES), F32)
        for side in range(2):
            row_total = jnp.sum(parts[side], axis=1, keepdims=True)
            results.append(accs[side] / row_total)
            logs = jnp.where(lane == 2 * pair + side, tops[side] + jnp.log(row_total), logs)
        out = jnp.where(lane < HD, results[0], results[1])
        mixed_ref[...] = out.astype(BF)
        float_ref[...] = out

        @pl.when(pair == 0)
        def _():
            log_ref[...] = logs

        @pl.when(pair > 0)
        def _():
            log_ref[...] = jnp.where((lane >> 1) == pair, logs, log_ref[...])

        @pl.when(pair == pairs - 1)
        def _():
            values = gate_ref[...] - log_ref[...]
            rest = gq_ref[...].astype(F32)
            one_ref[...] = jnp.where(lane < 3 * n_heads, split_lanes(values, n_heads), rest).astype(BF)
            values = values + tot_ref[:1, :]
            two_ref[...] = jnp.where(lane < 3 * n_heads, split_lanes(values, n_heads), rest).astype(BF)

    here = lambda n: spec((n, LANES), lambda i, *_: (0, i))
    shared = lambda n: spec((n, LANES), lambda i, *_: (0, 0))
    return call(
        kernel,
        (pairs,),
        (bounds, q, k, v, gq, gk, gates, total),
        [here(rows), here(keys), here(keys), shared(rows), shared(keys), shared(rows), shared(8)],
        (
            jax.ShapeDtypeStruct(q.shape, BF), jax.ShapeDtypeStruct(q.shape, F32),
            jax.ShapeDtypeStruct((rows, LANES), BF), jax.ShapeDtypeStruct((rows, LANES), BF),
        ),
        (here(rows), here(rows), shared(rows), shared(rows)),
        [pltpu.VMEM((2, rows, LANES), BF), pltpu.VMEM((2, rows, keys), F32)]
        + [pltpu.VMEM((2, rows, LANES), F32)] * 3 + [pltpu.VMEM((rows, LANES), F32)],
        prefetch=1,
    )


def attention_dq(bounds, q, k, v, d, gq, gk, n_heads, n_far):
    rows, keys = q.shape[0], k.shape[0]
    n_before = (keys - rows) // BLK
    pairs = n_heads // 2

    def kernel(lo_ref, q_ref, k_ref, v_ref, d_ref, gq_ref, gk_ref, gd_ref, dq_ref, row_ref, far_ref, qx, dx, accs):
        pair = pl.program_id(0)
        lane = lane_ids(rows)
        pick_k = pair_lanes(pair, n_heads, "k")
        for side, value in enumerate(pair_of(q_ref[...], gq_ref[...], pair_lanes(pair, n_heads, "q"))):
            qx[side] = value
        for side, value in enumerate(pair_of(d_ref[...], gd_ref[...], pair_lanes(pair, n_heads, "d"))):
            dx[side] = value
        both, late, early = slice(0, rows), slice(BLK, rows), slice(0, BLK)

        @pl.when(pair == 0)
        def _():
            far_ref[...] = jnp.zeros_like(far_ref)
            row_ref[...] = jnp.zeros_like(row_ref)

        def block(here, at, mask=None, first=False):
            values = pair_ones(v_ref[here, :])
            for side, key in enumerate(pair_of(k_ref[here, :], gk_ref[here, :], pick_k)):
                s = dot_t(qx[side, at, :], key)
                if mask is not None:
                    s = jnp.where(mask, s, BIG)
                ds = (jnp.exp(s) * dot_t(dx[side, at, :], values[side])).astype(BF)
                acc = dot(ds, key)
                accs[side, at, :] = acc if first else accs[side, at, :] + acc

        low, high = lo_ref[0], jnp.minimum(lo_ref[1], n_before)

        @pl.when(low < n_far)
        def _():
            accs[...] = jnp.zeros_like(accs)
            pl.loop(high, n_far)(lambda kb: block(block_at(kb), both))
            pl.loop(low, jnp.minimum(high, n_far))(lambda kb: block(block_at(kb), early))
            for side in range(2):
                moved = jnp.sum(jnp.where(lane == HD * (1 - side), accs[side], 0.0))
                far_ref[...] += jnp.where(lane[:8] == 2 * pair + side, moved, 0.0)
            block(slice(n_before * BLK, (n_before + 1) * BLK), both, causal_from(rows, 0))

        @pl.when(low >= n_far)
        def _():
            block(slice(n_before * BLK, (n_before + 1) * BLK), both, causal_from(rows, 0), True)

        block(slice((n_before + 1) * BLK, (n_before + 2) * BLK), late, causal_from(BLK, 0))
        pl.loop(jnp.maximum(high, n_far), n_before)(lambda kb: block(block_at(kb), both))
        pl.loop(jnp.maximum(low, n_far), high)(lambda kb: block(block_at(kb), early))
        dq_ref[...] = (jnp.where(lane < HD, accs[0], accs[1]) * HD ** (-0.5)).astype(BF)
        for side in range(2):
            total = lane_column(accs[side], HD * (1 - side))
            row_ref[...] = jnp.where(lane == 2 * pair + side, total, row_ref[...])

    here = lambda n: spec((n, LANES), lambda i, *_: (0, i))
    shared = lambda n: spec((n, LANES), lambda i, *_: (0, 0))
    return call(
        kernel,
        (pairs,),
        (bounds, q, k, v, d, gq, gk, d),
        [here(rows), here(keys), here(keys), here(rows), shared(rows), shared(keys), spec((rows, LANES), lambda i, *_: (0, pairs))],
        (
            jax.ShapeDtypeStruct(q.shape, BF), jax.ShapeDtypeStruct((rows, LANES), F32),
            jax.ShapeDtypeStruct((8, LANES), F32),
        ),
        (here(rows), shared(rows), shared(8)),
        [pltpu.VMEM((2, rows, LANES), BF)] * 2 + [pltpu.VMEM((2, rows, LANES), F32)],
        prefetch=1,
    )


def score_block(kx, vx, queries, grads, at, dks, dvs, mask=None, first=False):
    for side in range(2):
        s = dot_t(kx[side, at, :], queries[side])
        if mask is not None:
            s = jnp.where(mask, s, BIG)
        w = jnp.exp(s)
        ds = (w * dot_t(vx[side, at, :], grads[side])).astype(BF)
        dk, dv = dot(ds, queries[side]), dot(w.astype(BF), grads[side])
        dks[side, at, :] = dk if first else dks[side, at, :] + dk
        dvs[side, at, :] = dv if first else dvs[side, at, :] + dv


def attention_dkv_own(k, v, q, d, gq, gk, n_heads):
    rows = q.shape[0]
    place = k.shape[0] // rows - 1
    pairs = n_heads // 2

    def kernel(k_ref, v_ref, q_ref, d_ref, gq_ref, gd_ref, gk_ref, dk_ref, dv_ref, own_ref, kx, vx, dks, dvs):
        pair = pl.program_id(0)
        lane = lane_ids(rows)
        pick_q, pick_d = (pair_lanes(pair, n_heads, "q"), pair_lanes(pair, n_heads, "d"))
        for side, value in enumerate(pair_of(k_ref[...], gk_ref[...], pair_lanes(pair, n_heads, "k"))):
            kx[side] = value
        for side, value in enumerate(pair_ones(v_ref[...])):
            vx[side] = value
        both, late, early = slice(0, rows), slice(BLK, rows), slice(0, BLK)

        @pl.when(pair == 0)
        def _():
            own_ref[...] = jnp.zeros_like(own_ref)

        def load(here):
            return pair_of(q_ref[here, :], gq_ref[here, :], pick_q), pair_of(d_ref[here, :], gd_ref[here, :], pick_d)

        keep = lax.broadcasted_iota(jnp.int32, (rows, BLK), 0) - BLK <= lax.broadcasted_iota(jnp.int32, (rows, BLK), 1)
        first_keep = lax.broadcasted_iota(jnp.int32, (BLK, BLK), 0) <= lax.broadcasted_iota(jnp.int32, (BLK, BLK), 1)
        score_block(kx, vx, *load(late), both, dks, dvs, keep, True)
        score_block(kx, vx, *load(early), early, dks, dvs, first_keep)
        for side in range(2):
            column = lane_column(dks[side], HD * (1 - side) + 3)
            own_ref[...] = jnp.where(lane == 2 * pair + side, column, own_ref[...])
        dk_ref[...] = jnp.where(lane < HD, dks[0], dks[1])
        dv_ref[...] = jnp.where(lane < HD, dvs[0], dvs[1])

    heads_spec = lambda n: spec((n, LANES), lambda i, *_: (0, i))
    shared = lambda n: spec((n, LANES), lambda i, *_: (0, 0))
    keys_spec = spec((rows, LANES), lambda i, *_: (place, i))
    return call(
        kernel, (pairs,), (k, v, q, d, gq, d, gk),
        [
            keys_spec, keys_spec, heads_spec(rows), heads_spec(rows), shared(rows),
            spec((rows, LANES), lambda i, *_: (0, pairs)), spec((rows, LANES), lambda i, *_: (place, 0)),
        ],
        (jax.ShapeDtypeStruct(q.shape, F32), jax.ShapeDtypeStruct(q.shape, F32), jax.ShapeDtypeStruct((rows, LANES), F32)),
        (heads_spec(rows), heads_spec(rows), shared(rows)),
        [pltpu.VMEM((2, rows, LANES), BF)] * 2 + [pltpu.VMEM((2, rows, LANES), F32)] * 2,
    )


def attention_dkv_next(bounds, k, v, q_one, q_two, d_one, d_two, gkn, dk, dv, n_heads):
    rows, tail = q_one.shape[0], q_two.shape[0]
    place = k.shape[0] // rows - 1
    pairs = n_heads // 2
    assert 0 < tail - BLK <= BLK

    def kernel(
        hi_ref, k_ref, v_ref, q1_ref, d1_ref, gq1_ref, gd1_ref, q2_ref, d2_ref, gq2_ref, gd2_ref, gkn_ref,
        dk_own, dv_own, dk_ref, dv_ref, next_ref, kx, vx, dks, dvs,
    ):
        pair = pl.program_id(0)
        lane = lane_ids(rows)
        both, late, early = slice(0, rows), slice(BLK, rows), slice(0, BLK)
        few, many = hi_ref[0], hi_ref[1]

        @pl.when(pair == 0)
        def _():
            next_ref[...] = jnp.zeros_like(next_ref)

        @pl.when(many > 0)
        def _():
            pick_q, pick_d = (pair_lanes(pair, n_heads, "q"), pair_lanes(pair, n_heads, "d"))
            for side, value in enumerate(pair_of(k_ref[...], gkn_ref[...], pair_lanes(pair, n_heads, "k"))):
                kx[side] = value
            for side, value in enumerate(pair_ones(v_ref[...])):
                vx[side] = value
            dks[...] = jnp.zeros_like(dks)
            dvs[...] = jnp.zeros_like(dvs)

            def block(refs, here, at):
                q_ref, gq_ref, d_ref, gd_ref = refs
                queries = pair_of(q_ref[here, :], gq_ref[here, :], pick_q)
                score_block(kx, vx, queries, pair_of(d_ref[here, :], gd_ref[here, :], pick_d), at, dks, dvs)

            one, two = (q1_ref, gq1_ref, d1_ref, gd1_ref), (q2_ref, gq2_ref, d2_ref, gd2_ref)
            pl.loop(0, jnp.minimum(few, 2))(lambda j: block(one, block_at(j), both))
            pl.loop(few, jnp.minimum(many, 2))(lambda j: block(one, block_at(j), late))
            pl.when(few > 2)(lambda: block(two, early, both))
            pl.when((few <= 2) & (many > 2))(lambda: block(two, early, late))
            pl.when(many > 3)(lambda: block(two, slice(BLK, tail), both))
            for side in range(2):
                value = lane_column(dks[side], HD * (1 - side) + 3)
                next_ref[...] = jnp.where(lane == 2 * pair + side, value, next_ref[...])
            dk_ref[...] = (dk_own[...] + jnp.where(lane < HD, dks[0], dks[1])).astype(BF)
            dv_ref[...] = (dv_own[...] + jnp.where(lane < HD, dvs[0], dvs[1])).astype(BF)

        @pl.when(many == 0)
        def _():
            dk_ref[...] = dk_own[...].astype(BF)
            dv_ref[...] = dv_own[...].astype(BF)

    heads_spec = lambda n: spec((n, LANES), lambda i, *_: (0, i))
    shared = lambda n: spec((n, LANES), lambda i, *_: (0, 0))
    last = lambda n: spec((n, LANES), lambda i, *_: (0, pairs))
    keys_spec = spec((rows, LANES), lambda i, *_: (place, i))
    return call(
        kernel, (pairs,), (bounds, k, v, q_one, d_one, q_one, d_one, q_two, d_two, q_two, d_two, gkn, dk, dv),
        [
            keys_spec, keys_spec, heads_spec(rows), heads_spec(rows), last(rows), last(rows),
            heads_spec(tail), heads_spec(tail), last(tail), last(tail), shared(rows), heads_spec(rows), heads_spec(rows),
        ],
        (jax.ShapeDtypeStruct(dk.shape, BF), jax.ShapeDtypeStruct(dk.shape, BF), jax.ShapeDtypeStruct((rows, LANES), F32)),
        (heads_spec(rows), heads_spec(rows), shared(rows)),
        [pltpu.VMEM((2, rows, LANES), BF)] * 2 + [pltpu.VMEM((2, rows, LANES), F32)] * 2,
        prefetch=1,
    )


def project(offs, x, x_far, tail, gain, w, side_w, qkv_b, bias, cols, rank_r, filled=None, before=0):
    width = gain.shape[1]
    block = width // 4
    own = filled is None
    rows = x.shape[0] // (2 * BLK) * 2 * BLK
    row_steps = 1 if own else 2
    parts = ("q", "k", "v") if own else ("k", "v")
    assert rows == 2 * BLK and BLK <= tail <= rows - 32

    def kernel(*refs):
        offs_ref, x_ref = refs[0], refs[1]
        at = 2
        if not own:
            far_ref, at = refs[2], 3
        gain_ref, *pieces, side_ref, b_ref, bias_ref = refs[at : at + 8]
        at += 8 + (0 if own else 3)
        outs, scr = refs[at:-3], refs[-3:]
        part, step = pl.program_id(0), pl.program_id(1)
        n_outs = dict(zip(("n", "low", "q", "k", "v", "logits") if own else ("k", "v", "logits"), outs))
        scr, low_scr, joint = scr
        at_rows = pl.ds(pl.multiple_of(step * rows, rows), rows)

        @pl.when(part == 0)
        def _():
            blocks = []
            for k in range(4):
                here = pl.ds(pl.multiple_of(offs_ref[k], LANES), block)
                value = x_ref[:, here]
                if not own:
                    far = jnp.concatenate([far_ref[:BLK, here], far_ref[tail + 32 - BLK : tail + 32, here]], axis=0)
                    value = jnp.where(step == 0, far, value)
                blocks.append(value.astype(F32))
            factor = norm_terms(blocks)
            for k in range(4):
                here = pl.ds(pl.multiple_of(offs_ref[k], LANES), block)
                scr[at_rows, k * block : (k + 1) * block] = (blocks[k] * factor * gain_ref[:, here]).astype(BF)
            side = dot(scr[at_rows, :], side_ref[...])
            low = side[:, LANES - rank_r :].astype(BF)
            low_scr[at_rows, :rank_r] = low
            n_outs["logits"][at_rows, :] = side + bias_ref[...]
            if own:
                n_outs["n"][...] = scr[...]
                n_outs["low"][...] = low

        @pl.when(step == 0)
        def _():
            for k in range(4):
                joint[k * block : (k + 1) * block, :] = pieces[k][...]

        value = dot(scr[at_rows, :], joint[...])
        value = (value + dot(low_scr[at_rows, :rank_r], b_ref[...])).astype(BF)
        for n, name in enumerate(parts):
            @pl.when(part == n)
            def _(name=name):
                out = n_outs[name]
                out[at_rows, :] = (value.astype(F32) * HD ** (-0.5)).astype(BF) if name == "q" else value

    keys = before + rows if own else filled[0].shape[0]
    ins = [offs, x] + ([] if own else [x_far]) + [gain, *w, side_w, qkv_b, bias] + ([] if own else list(filled))
    row_spec = spec((rows, width), lambda i, *_: (0, 0))
    in_specs = [row_spec] + ([] if own else [whole(x_far)])
    first = 0 if own else 1
    column = lambda n: spec((n, cols), lambda j, *_: (0, j + first))
    in_specs += [whole(gain), *[column(block)] * 4, whole(side_w), column(rank_r), whole(bias)]
    if not own:
        in_specs += [pl.BlockSpec(memory_space=pl.ANY)] * 3
    some = row_steps * rows
    at_keys = lambda n: spec((some, n), lambda *_: (before // some if own else 0, 0))
    outs = [jax.ShapeDtypeStruct((keys, cols), BF)] * 2 + [jax.ShapeDtypeStruct((keys, LANES), F32)]
    out_specs = [at_keys(cols), at_keys(cols), at_keys(LANES)]
    if own:
        here = lambda n: spec((rows, n), lambda *_: (0, 0))
        outs = [
            jax.ShapeDtypeStruct((rows, width), BF),
            jax.ShapeDtypeStruct((rows, rank_r), BF),
            jax.ShapeDtypeStruct((rows, cols), BF),
        ] + outs
        out_specs = [here(width), here(rank_r), here(cols)] + out_specs
    return call(
        kernel, (len(parts), row_steps), ins, in_specs, tuple(outs), tuple(out_specs),
        [pltpu.VMEM((some, width), BF), pltpu.VMEM((some, LANES), BF), pltpu.VMEM((width, cols), BF)], prefetch=1,
        aliases={} if own else {11: 0, 12: 1, 13: 2},
    )


def gate_tables(logits, seg_keys, seg_row, n_heads, rows):
    keys = logits.shape[0]
    before = keys - rows
    one = 3 * n_heads + DOCS

    def kernel(logit_ref, seg_ref, row_ref, gq_ref, gk_ref, gkn_ref, gate_ref, tot_ref):
        lane = lane_ids(BLK)
        doc = lane - 3 * n_heads + 1
        doc_lane = (doc > 0) & (doc <= DOCS)
        inner = lax.broadcasted_iota(jnp.int32, (BLK, BLK), 1) > lax.broadcasted_iota(jnp.int32, (BLK, BLK), 0)
        later = inner.astype(BF)

        def forget(at):
            value = logit_ref[at, :]
            value = jnp.minimum(value, 0.0) - jnp.log(1.0 + jnp.exp(-jnp.abs(value)))
            return jnp.where((lane < n_heads) & (seg_ref[at, :] > 0), value, 0.0)

        def lanes(values, docs):
            return (split_lanes(values, n_heads) + docs + jnp.where(lane == one, 1.0, 0.0)).astype(BF)

        def docs_k(at):
            return jnp.where(doc_lane & (doc != seg_ref[at, :]), BIG, 0.0)

        def suffix(first, last, carry, out_ref, base):
            for b in range(last - 1, first - 1, -1):
                at = slice(b * BLK, (b + 1) * BLK)
                values = forget(at)
                sums = exact_dot(later, values) + carry
                out_ref[b * BLK - base : (b + 1) * BLK - base, :] = lanes(sums, docs_k(at))
                carry = carry + jnp.sum(values, axis=0, keepdims=True)
            return carry

        n_before, n_all = before // BLK, keys // BLK
        zero = jnp.zeros((1, LANES), F32)
        near = suffix((before - rows) // BLK, n_before, zero, gk_ref, 0)
        tot_ref[...] = jnp.broadcast_to(near, tot_ref.shape)
        suffix(0, (before - rows) // BLK, near, gk_ref, 0)
        suffix(n_before, n_all, zero, gkn_ref, before)
        own = jnp.concatenate([forget(slice(b * BLK, (b + 1) * BLK)) for b in range(n_before, n_all)], axis=0)
        for b in range(rows // BLK):
            at = slice(before + b * BLK, before + (b + 1) * BLK)
            here = slice(b * BLK, (b + 1) * BLK)
            q_pos = lax.broadcasted_iota(jnp.int32, (BLK, rows), 0) + b * BLK
            k_pos = lax.broadcasted_iota(jnp.int32, (BLK, rows), 1)
            same = (row_ref[...] == seg_ref[at, :]) & (k_pos <= q_pos)
            sums = exact_dot(same.astype(BF), own)
            gate_ref[here, :] = sums
            gq_ref[here, :] = lanes(sums, jnp.where(doc_lane & (doc == seg_ref[at, :]), 1.0, 0.0))
            gk_ref[at, :] = lanes(-sums, docs_k(at))

    shape = lambda n, t: jax.ShapeDtypeStruct((n, LANES), t)
    outs = (shape(rows, BF), shape(keys, BF), shape(rows, BF), shape(rows, F32), shape(8, F32))
    return call(
        kernel, (1,), (logits, seg_keys, seg_row), [whole(logits), whole(seg_keys), whole(seg_row)],
        outs, tuple(whole(o) for o in outs), flops=10**8, nbytes=4 * 10**6,
    )


def weight_halves(w):
    half = w[0].shape[0] // 2
    at = lambda row: spec((half, w[0].shape[1]), lambda *_: (row, 0))
    return [at(0), at(0), at(1), at(1)]


def out_projection(offs, rank, x, mixed_own, mixed_far, w, a_own, a_far, out_b, gain, ffn_a):
    rows, width = x.shape
    block = width // 4
    rank_r = a_own.shape[1]

    def kernel(
        offs_ref, rank_ref, x_ref, mo, mf, wo0, wo1, wf0, wf1, ao, af, b_ref, gain_ref, fa, h_ref, n_ref, low_ref, lo_ref
    ):
        def run(m0, m1, w0, w1, a0, a1):
            low = (dot(m0[...], a0[...]) + dot(m1[...], a1[...])).astype(BF)
            lo_ref[...] = low
            for half in range(2):
                both = dot(m0[...], w0[half][...]) + dot(m1[...], w1[half][...])
                both = both + dot(low, b_ref[:, 2 * half * block : 2 * (half + 1) * block])
                for j in range(2):
                    k = 2 * half + j
                    here = pl.ds(pl.multiple_of(offs_ref[k], LANES), block)
                    value = x_ref[:, here].astype(F32) + both[:, j * block : (j + 1) * block]
                    h_ref[:, k * block : (k + 1) * block] = value

        pl.when(rank_ref[0] == 0)(lambda: run(mo, mf, (wo0, wo1), (wf0, wf1), ao, af))
        pl.when(rank_ref[0] != 0)(lambda: run(mf, mo, (wf0, wf1), (wo0, wo1), af, ao))
        value = h_ref[...]
        normed = (value * norm_terms([value]) * gain_ref[...]).astype(BF)
        n_ref[...] = normed
        low_ref[...] = dot(normed, fa[...]).astype(BF)

    rowed = whole
    outs = (
        jax.ShapeDtypeStruct((rows, width), F32), jax.ShapeDtypeStruct((rows, width), BF),
        jax.ShapeDtypeStruct((rows, rank_r), BF), jax.ShapeDtypeStruct((rows, rank_r), BF),
    )
    ins = (offs, rank, x, mixed_own, mixed_far, *w, *w, a_own, a_far, out_b, gain, ffn_a)
    return call(
        kernel, (1,), ins,
        [rowed(x), rowed(mixed_own), rowed(mixed_far)] + weight_halves(w) + [whole(v) for v in ins[9:]],
        outs, tuple(rowed(o) for o in outs), prefetch=2, flops=4 * rows * width * mixed_own.shape[1],
        nbytes=4 * width * mixed_own.shape[1] + 8 * rows * width,
    )


def feed_forward(rank, normed, low, cot, grad_low, gate_up, down, ffn_b, down_a):
    rows, width = normed.shape
    block = width // 4
    half = rows // 2
    rank_r = low.shape[1]
    unit_cols = down_a.shape[0]
    tile = 512 if unit_cols % 512 == 0 else unit_cols
    tiles = unit_cols // tile
    down_at = down[0].shape[1] // tile - tiles

    def kernel(
        rank_ref, x_ref, low_ref, cot_ref, gl_ref, *rest,
    ):
        pieces, rest = rest[:12], rest[12:]
        bg_ref, bu_ref, ad_ref, *rest, wg, wu, wd = rest
        step = pl.program_id(0)
        units_ref, gg_ref, gu_ref, far_ref, own_ref, own_low_ref, part_ref, part_low_ref = rest

        @pl.when(step == 0)
        def _():
            part_ref[...] = jnp.zeros_like(part_ref)
            part_low_ref[...] = jnp.zeros_like(part_low_ref)

        for n, joint in enumerate((wg, wu, wd)):
            for k in range(4):
                joint[k * block : (k + 1) * block, :] = pieces[4 * n + k][...]
        gate = dot(x_ref[...], wg[...]) + dot(low_ref[...], bg_ref[...])
        up = dot(x_ref[...], wu[...]) + dot(low_ref[...], bu_ref[...])
        grad = dot(cot_ref[...], wd[...]) + dot_t(gl_ref[...], ad_ref[...])
        sig = jax.nn.sigmoid(gate)
        act = gate * sig
        units_ref[...] = (act * up).astype(BF)
        gg = (grad * up * sig * (1.0 + gate * (1.0 - sig))).astype(BF)
        gu = (grad * act).astype(BF)
        gg_ref[...] = gg
        gu_ref[...] = gu
        part_low_ref[:, :rank_r] += dot_t(gg, bg_ref[...]) + dot_t(gu, bu_ref[...])
        part_ref[...] += dot_t(gg, wg[...]) + dot_t(gu, wu[...])

        @pl.when(step == tiles - 1)
        def _():
            mine = pl.ds(pl.multiple_of(rank_ref[0] * half, half), half)
            theirs = pl.ds(pl.multiple_of((1 - rank_ref[0]) * half, half), half)
            far_ref[:, :width] = part_ref[theirs, :].astype(BF)
            far_ref[:, width:] = split_lanes(part_low_ref[theirs, :], rank_r).astype(BF)
            own_ref[...] = part_ref[mine, :]
            own_low_ref[...] = part_low_ref[mine, :]

    out = jax.ShapeDtypeStruct((rows, unit_cols), BF)
    out_spec = spec((rows, tile), lambda i, *_: (0, i))
    sums = (jax.ShapeDtypeStruct((rows, width), F32), jax.ShapeDtypeStruct((rows, LANES), F32))
    ends = (
        jax.ShapeDtypeStruct((half, width + LANES), BF), jax.ShapeDtypeStruct((half, width), F32),
        jax.ShapeDtypeStruct((half, LANES), F32),
    )
    return call(
        kernel,
        (tiles,),
        (rank, normed, low, cot, grad_low, *gate_up, *gate_up, *down, ffn_b, ffn_b, down_a),
        [
            whole(normed), whole(low), whole(cot), whole(grad_low),
            *[spec((block, tile), lambda i, *_: (0, i)) for _ in range(4)],
            *[spec((block, tile), lambda i, *_: (0, i + tiles)) for _ in range(4)],
            *[spec((block, tile), lambda i, *_: (0, i + down_at)) for _ in range(4)],
            spec((rank_r, tile), lambda i, *_: (0, i)),
            spec((rank_r, tile), lambda i, *_: (0, i + tiles)),
            spec((tile, rank_r), lambda i, *_: (i, 0)),
        ],
        (out, out, out, *ends),
        (out_spec, out_spec, out_spec, *[whole(e) for e in ends]),
        [pltpu.VMEM(e.shape, F32) for e in sums] + [pltpu.VMEM((width, tile), BF)] * 3,
        prefetch=1,
    )


def whole_low(parts, n):
    parts = parts.astype(F32)
    return parts[:, :n] + parts[:, n : 2 * n] + parts[:, 2 * n : 3 * n]


def middle(rank, own, got, own_low, hidden, cot, gain, ffn_a, out_b, w, a_own, a_far):
    half, width = own.shape
    depth = width // 2
    rank_r = out_b.shape[0]
    cols = a_own.shape[0]

    def kernel(
        rank_ref, own_ref, got_ref, low_ref, h_ref, cot_ref, gain_ref, fa, b_ref, wo0, wo1, wf0, wf1, ao, af,
        gh_ref, ghb_ref, glf_ref, glo_ref, mine_ref, far_ref,
    ):
        ffn_low = (low_ref[:, :rank_r] + whole_low(got_ref[:, width:], rank_r)).astype(BF)
        glf_ref[...] = ffn_low
        incoming = own_ref[...] + got_ref[:, :width].astype(F32) + dot_t(ffn_low, fa[...])
        value = h_ref[...]
        factor = norm_terms([value])
        scaled = incoming * gain_ref[...]
        mean = jnp.mean(value * scaled, axis=1, keepdims=True)
        grad = cot_ref[...].astype(F32) + (factor * scaled - value * (factor * factor * factor * mean))
        gh_ref[...] = grad
        low_precision = grad.astype(BF)
        ghb_ref[...] = low_precision
        left, right = low_precision[:, :depth], low_precision[:, depth:]
        out_low = dot_t(low_precision, b_ref[...]).astype(BF)
        glo_ref[...] = out_low
        mine_ref[...] = (dot_t(left, wo0[...]) + dot_t(right, wo1[...]) + dot_t(out_low, ao[...])).astype(BF)
        far_ref[...] = (dot_t(left, wf0[...]) + dot_t(right, wf1[...]) + dot_t(out_low, af[...])).astype(BF)

    outs = (
        jax.ShapeDtypeStruct((half, width), F32), jax.ShapeDtypeStruct((half, width), BF),
        jax.ShapeDtypeStruct((half, rank_r), BF), jax.ShapeDtypeStruct((half, rank_r), BF),
        jax.ShapeDtypeStruct((half, cols), BF), jax.ShapeDtypeStruct((half, cols), BF),
    )
    ins = (rank, own, got, own_low, hidden, cot, gain, ffn_a, out_b, *w, *w, a_own, a_far)
    mine = lambda v: spec((half, v.shape[1]), lambda i, r: (r[0], 0))
    in_specs = [whole(own), whole(got), whole(own_low), mine(hidden), mine(cot)] + [whole(v) for v in ins[6:9]]
    in_specs += weight_halves(w) + [whole(a_own), whole(a_far)]
    return call(
        kernel, (1,), ins, in_specs, outs, tuple(whole(o) for o in outs), prefetch=1,
        flops=4 * half * width * cols, nbytes=4 * width * cols + 16 * half * width,
    )


def mixed_gradient(rank, own, far, mixed, n_heads, tail):
    half, cols = own.shape

    def kernel(rank_ref, own_ref, far_ref, mixed_ref, out_ref, tail_ref):
        lane = lane_ids(half)
        for ref, first in ((own_ref, rank_ref[0]), (far_ref, 1 - rank_ref[0])):
            at = pl.ds(pl.multiple_of(first * half, half), half)
            sums = jnp.zeros((half, LANES), F32)
            for pair in range(n_heads // 2):
                here = slice(pair * LANES, (pair + 1) * LANES)
                product = ref[:, here].astype(F32) * mixed_ref[at, here]
                a = jnp.sum(jnp.where(lane < HD, product, 0.0), axis=1, keepdims=True)
                b = jnp.sum(jnp.where(lane < HD, 0.0, product), axis=1, keepdims=True)
                sums = jnp.where(lane == 2 * pair, -a, jnp.where(lane == 2 * pair + 1, -b, sums))
            out_ref[at, :cols] = ref[...]
            out_ref[at, cols:] = split_lanes(sums, n_heads).astype(BF)
        tail_ref[...] = out_ref[:tail, :]

    outs = [jax.ShapeDtypeStruct((n, cols + LANES), BF) for n in (2 * half, tail)]
    return call(
        kernel, (1,), (rank, own, far, mixed), [whole(own), whole(far), whole(mixed)],
        tuple(outs), tuple(whole(o) for o in outs), prefetch=1,
        flops=4 * half * cols, nbytes=16 * half * cols,
    )


def input_gradient(rank, grads, logits, seg_keys, seg_row, row_lanes, own_lanes, next_lanes, across, w, side_w, qkv_b, low_qkv, n_heads):
    rows, cols = grads[0].shape
    depth = w[0].shape[0]
    half = rows // 2
    rank_r = qkv_b.shape[0]
    before = logits.shape[0] - rows
    steps = 3
    chunk = 2 * depth // (2 * steps)

    def kernel(
        rank_ref, q_ref, k_ref, v_ref, logit_ref, seg_ref, seg_row_ref, r_ref, o_ref, n_ref, a_ref, w0, w1, s0, s1, b_ref,
        lq_ref, far_ref, own_ref, low_ref, tq_ref, tk_ref, tv_ref, gl_ref,
    ):
        @pl.when(pl.program_id(0) == 0)
        def _():
            lane = lane_ids(rows)
            t = lax.broadcasted_iota(jnp.int32, (rows, rows), 0)
            i = lax.broadcasted_iota(jnp.int32, (rows, rows), 1)
            same = ((seg_row_ref[...] == seg_ref[...]) & (i >= t)).astype(BF)
            total = exact_dot(same, r_ref[...] - o_ref[...]) + exact_dot((i < t).astype(BF), n_ref[...])
            total = total + a_ref[:1, :]
            value = jnp.where(lane < n_heads, total * jax.nn.sigmoid(-logit_ref[...]), 0.0)
            gl_ref[...] = value.astype(BF)
            low = dot_t(q_ref[...], b_ref[:, :cols]) + dot_t(k_ref[...], b_ref[:, cols : 2 * cols])
            low_ref[...] = low + dot_t(v_ref[...], b_ref[:, 2 * cols :])
            for out, grad in ((tq_ref, q_ref), (tk_ref, k_ref), (tv_ref, v_ref)):
                out[...] = t_dot(lq_ref[...], grad[...])

        mine = pl.ds(pl.multiple_of(rank_ref[0] * half, half), half)
        theirs = pl.ds(pl.multiple_of((1 - rank_ref[0]) * half, half), half)
        for p, (w_ref, s_ref) in enumerate(((w0, s0), (w1, s1))):
            def part(at):
                value = dot_t(q_ref[at, :], w_ref[:, :cols]) + dot_t(k_ref[at, :], w_ref[:, cols : 2 * cols])
                return value + dot_t(v_ref[at, :], w_ref[:, 2 * cols :]) + dot_t(gl_ref[at, :], s_ref[...])

            far_ref[p] = part(theirs).astype(BF)
            own_ref[p] = part(mine)

    ins = (rank, *grads, logits, seg_keys, seg_row, row_lanes, own_lanes, next_lanes, across, w[0], w[1], side_w, side_w, qkv_b, low_qkv)
    at_own = lambda v: spec((rows, v.shape[1]), lambda i, *_: (before // rows, 0))
    in_specs = [whole(g) for g in grads] + [at_own(logits), at_own(seg_keys)]
    in_specs += [whole(v) for v in (seg_row, row_lanes, own_lanes, next_lanes, across)]
    n_col = w[0].shape[1]
    in_specs += [spec((chunk, n_col), lambda i, *_: (i, 0))] * 2
    in_specs += [spec((chunk, LANES), lambda i, *_: (i, 0)), spec((chunk, LANES), lambda i, *_: (i + steps, 0))]
    in_specs += [whole(qkv_b), whole(low_qkv)]
    outs = (
        jax.ShapeDtypeStruct((2, half, depth), BF), jax.ShapeDtypeStruct((2, half, depth), F32),
        jax.ShapeDtypeStruct((rows, rank_r), F32),
        *[jax.ShapeDtypeStruct((rank_r, cols), F32)] * 3,
    )
    halves = spec((2, half, chunk), lambda i, *_: (0, 0, i))
    return call(
        kernel, (steps,), ins, in_specs, outs, (halves, halves, *[whole(o) for o in outs[2:]]), [pltpu.VMEM((rows, LANES), BF)],
        prefetch=1, flops=2 * rows * 2 * depth * 3 * cols, nbytes=4 * depth * 3 * cols,
    )


def token_gradient(offs, rank, own, got, grad_low, a, x, gain, grad_hidden):
    half, width = grad_hidden.shape
    block = width // 4

    def kernel(offs_ref, rank_ref, own_ref, got_ref, low_ref, a_ref, x_ref, gain_ref, gh_ref, out_ref):
        blocks, scaled, product = [], [], 0.0
        for k in range(4):
            here = pl.ds(pl.multiple_of(offs_ref[k], LANES), block)
            cols = slice(k % 2 * block, (k % 2 + 1) * block)
            value = own_ref[k // 2][:, cols] + got_ref[k // 2][:, cols].astype(F32)
            value = value + dot_t(low_ref[...], a_ref[k * block : (k + 1) * block, :])
            blocks.append(x_ref[:, here].astype(F32))
            scaled.append(value * gain_ref[:, here])
            product = product + jnp.sum(blocks[k] * scaled[k], axis=1, keepdims=True)
        factor = norm_terms(blocks)
        mean = product / width
        for k in range(4):
            here = pl.ds(pl.multiple_of(offs_ref[k], LANES), block)
            back = factor * scaled[k] - blocks[k] * (factor * factor * factor * mean)
            out_ref[:, here] = (gh_ref[:, k * block : (k + 1) * block] + back).astype(BF)

    mine = lambda v: spec((half, v.shape[1]), lambda i, o, r: (r[0], 0))
    out = jax.ShapeDtypeStruct((half, width), BF)
    return call(
        kernel, (1,), (offs, rank, own, got, grad_low, a, x, gain, grad_hidden),
        [whole(own), whole(got), mine(grad_low), whole(a), mine(x), whole(gain), whole(grad_hidden)],
        out, whole(out), prefetch=2, nbytes=20 * half * width,
    )


def both_halves(rank, own, far):
    half, width = own.shape

    def kernel(rank_ref, own_ref, far_ref, out_ref):
        @pl.when(pl.program_id(0) == rank_ref[0])
        def _():
            out_ref[...] = own_ref[...].astype(F32)

        @pl.when(pl.program_id(0) != rank_ref[0])
        def _():
            out_ref[...] = far_ref[...].astype(F32)

    return call(
        kernel, (2,), (rank, own, far), [whole(own), whole(far)], jax.ShapeDtypeStruct((2 * half, width), F32),
        spec((half, width), lambda i, *_: (i, 0)), prefetch=1, nbytes=16 * half * width,
    )


def down_partial(units, down, down_a):
    rows, unit_cols = units.shape
    block = down[0].shape[0]
    width = 4 * block
    rank_r = down_a.shape[1]

    def kernel(u_ref, w0, w1, w2, w3, a_ref, out_ref, low_ref):
        low_ref[...] = jnp.zeros_like(low_ref)
        low_ref[:, :rank_r] = dot(u_ref[...], a_ref[...])
        for k, w_ref in enumerate((w0, w1, w2, w3)):
            out_ref[:, k * block : (k + 1) * block] = dot_t(u_ref[...], w_ref[...]).astype(BF)
        out_ref[:, width:] = split_lanes(low_ref[...], rank_r).astype(BF)

    rowed = lambda n: spec((BLK, n), lambda i: (i, 0))
    last = spec((block, unit_cols), lambda i: (0, 0))
    return call(
        kernel, (rows // BLK,), (units, *down, down_a), [rowed(unit_cols), last, last, last, last, whole(down_a)],
        jax.ShapeDtypeStruct((rows, width + LANES), BF), rowed(width + LANES), [pltpu.VMEM((BLK, LANES), F32)],
    )


def block_result(offs, hidden, own, got, down_b):
    rows, width = hidden.shape
    block = width // 4
    rank_r = down_b.shape[0]

    def kernel(offs_ref, h_ref, own_ref, got_ref, b_ref, out_ref):
        low = (whole_low(own_ref[:, width:], rank_r) + whole_low(got_ref[:, width:], rank_r)).astype(BF)
        for k in range(4):
            here = pl.ds(pl.multiple_of(offs_ref[k], LANES), block)
            cols = slice(k * block, (k + 1) * block)
            both = own_ref[:, cols].astype(F32) + got_ref[:, cols].astype(F32)
            out_ref[:, here] = (h_ref[:, cols] + both + dot(low, b_ref[:, cols])).astype(BF)

    rowed = lambda v: spec((BLK, v.shape[1]), lambda i, *_: (i, 0))
    out = jax.ShapeDtypeStruct((rows, width), BF)
    return call(
        kernel, (rows // BLK,), (offs, hidden, own, got, down_b),
        [rowed(hidden), rowed(own), rowed(got), whole(down_b)], out, rowed(out),
        prefetch=1, nbytes=12 * rows * width,
    )


def pack_gradients(inv, rank, xor_own, xor_both, halves, out_a, wide, owners):
    rank_r, width = xor_own[0].shape
    block = width // 4
    part, unit_part = block // 8, wide[0].shape[1] // 16
    n = len(wide) * unit_part + (len(xor_own) + len(xor_both) + len(halves) + 1) * part
    assert owners == 32 and block % LANES == 0

    def kernel(inv_ref, rank_ref, *refs):
        out_ref, refs = refs[-1], list(refs[:-1])
        take = lambda count: [refs.pop(0) for _ in range(count)]
        own_refs, both_refs = take(len(xor_own)), take(len(xor_both))
        half_refs, (ao, af), wide_refs = take(len(halves)), take(2), take(len(wide))
        for f in range(4):
            mine = rank_ref[0] == f // 2
            at = pl.ds(pl.multiple_of(inv_ref[f], LANES), block)
            cols = slice(f % 2 * block, (f % 2 + 1) * block)
            blocks = [jnp.where(mine, r[:, at], 0.0) for r in own_refs] + [r[:, at] for r in both_refs]
            blocks += [jnp.where(mine, r[:, cols], 0.0) for r in half_refs]
            blocks.append(jnp.where(mine, ao[:, cols], af[:, cols]))
            units = 8 * unit_part
            big = [jnp.where(mine, r[:, f % 2 * units : (f % 2 + 1) * units], 0.0) for r in wide_refs]
            for j in range(8):
                row = [b[:, j * unit_part : (j + 1) * unit_part] for b in big]
                row += [b[:, j * part : (j + 1) * part] for b in blocks]
                at_row = slice((8 * f + j) * rank_r, (8 * f + j + 1) * rank_r)
                out_ref[at_row, :] = jnp.concatenate(row, axis=1).astype(BF)

    ins = (inv, rank, *xor_own, *xor_both, *halves, *out_a, *wide)
    out = jax.ShapeDtypeStruct((owners * rank_r, n), BF)
    return call(kernel, (1,), ins, [whole(v) for v in ins[2:]], out, whole(out), prefetch=2)


def spread_gradients(every, landed, n_adapters, rank_r, n_wide, n_small, unit_part, part):
    n = landed.shape[1]
    senders = landed.shape[0] // (4 * rank_r)

    def kernel(every_ref, x_ref, out_ref, swap_ref):
        sums = []
        for f in range(4):
            total = 0.0
            for i in range(senders):
                at = (f * senders + i) * rank_r
                total = total + x_ref[at : at + rank_r, :].astype(F32)
            sums.append(total)
        for a in range(n_adapters):
            total = 0.0
            for f in range(4):
                total = total + jnp.where(every_ref[f] == a, sums[f], 0.0)
            out_ref[a] = total
            swap_ref[a] = total.T

    outs = (jax.ShapeDtypeStruct((n_adapters, rank_r, n), F32), jax.ShapeDtypeStruct((n_adapters, n, rank_r), F32))
    return call(kernel, (1,), (every, landed), [whole(landed)], outs, tuple(whole(o) for o in outs), prefetch=1)


def body(
    tokens, segments, adapter_index, w_qkv, w_forget, forget_bias, w_out, w_gate_up, w_down,
    gain_attn, gain_ffn, a_qkv, b_qkv, a_out, b_out, a_gate_up, b_gate_up, a_down, b_down, cotangent,
):
    count, rows, width = tokens.shape
    assert count == 1
    head_cols = w_qkv.shape[2]
    n_heads = w_forget.shape[1]
    unit_cols = w_gate_up.shape[2]
    rank_r = a_qkv.shape[2]
    n_f, n_c, n_t = (lax.axis_size("fsdp"), lax.axis_size("ctx"), lax.axis_size("tp"))
    f_rank, t_rank = (lax.axis_index("fsdp"), lax.axis_index("tp"))
    hops = -(-(DOC_MOST - 1) // rows)
    assert hops == 2 and n_c > 2 and n_t == 2 and n_f % 4 == 0
    tail = -(-(DOC_MOST - 1 - rows) // 32) * 32
    before = hops * rows
    half = rows // 2
    block = width // 4
    first = t_rank == 0
    rank = t_rank.astype(jnp.int32)[None]

    def other(values):
        return lax.ppermute(values, "tp", [(0, 1), (1, 0)])

    def four(pieces):
        return [*pieces, *[lax.ppermute(part, "fsdp", [(i, i ^ 1) for i in range(n_f)]) for part in pieces]]

    mix = lambda values, dim: to_xor(values, dim, n_f, f_rank)
    direct = n_f == 4 and block % LANES == 0
    if direct:
        offs = jnp.stack([(f_rank ^ step) * block for step in xor_order(4)]).astype(jnp.int32)
        lay = lambda values, dim: values
    else:
        offs = jnp.arange(4, dtype=jnp.int32) * block
        lay = mix

    pick = adapter_index[0]
    tok = lay(tokens[0], 1)
    seg_one = segments[0] + 1
    note = jnp.zeros((32, width), BF).at[0, :rows].set(seg_one.astype(BF))
    qkv_own = jnp.concatenate([w_qkv[:, i] for i in range(3)], axis=1)
    qkv_far = far_blocks(qkv_own, 0)
    prev_one = shift(jnp.concatenate([tok, after(note, qkv_own)], axis=0), 1, n_c)
    side = jnp.broadcast_to(pick.astype(BF), (w_forget.shape[0], 1))
    side_far = far_blocks(after(jnp.concatenate([w_forget, side], axis=1), qkv_own), 0)
    take = lambda table: lax.dynamic_index_in_dim(table, pick, 0, keepdims=False)
    mine = lambda values, n, dim: lax.dynamic_slice_in_dim(values, t_rank * n, n, dim)
    theirs = lambda values, n, dim: lax.dynamic_slice_in_dim(values, (1 - t_rank) * n, n, dim)
    qkv_a, ffn_a = (mix(take(a_qkv), 0), mix(take(a_gate_up), 0))
    out_b, down_b = (mix(take(b_out), 1), mix(take(b_down), 1))
    qkv_b = mine(take(b_qkv), head_cols, 2).reshape(rank_r, 3 * head_cols)
    out_a = take(a_out)
    out_a_own, out_a_far = (mine(out_a, head_cols, 0), theirs(out_a, head_cols, 0))
    ffn_b = mine(take(b_gate_up), unit_cols, 2).reshape(rank_r, 2 * unit_cols)
    down_a = mine(take(a_down), unit_cols, 0)
    gain_one = lay(gain_attn.astype(F32), 0)[None]
    gain_two = mix(gain_ffn.astype(F32), 0)[None]
    bias = jnp.pad(forget_bias.astype(F32), (0, LANES - n_heads))[None]
    cot = mix(cotangent[0], 1)
    grad_low_down = dot_t(cot, down_b).astype(BF)

    out_pair = jnp.concatenate([w_out, other(w_out)], axis=0)
    gate_up_own = jnp.concatenate([w_gate_up[:, 0], w_gate_up[:, 1]], axis=1)
    down_own = w_down.T
    shared = n_f == 4 and n_c % 2 == 0
    odd = lax.axis_index("ctx") % 2
    down_sent = down_own
    if shared:
        down_sent = lax.dynamic_slice_in_dim(down_own, odd * (unit_cols // 2), unit_cols // 2, 1)
    (
        prev_one, qkv_far, side_far, out_pair, qkv_a, qkv_b, gain_one, bias, ffn_a, out_b, down_b, out_a_own, out_a_far,
        ffn_b, down_a, gain_two, cot, grad_low_down, gate_up_own, down_own, down_sent,
    ) = lax.optimization_barrier((
        prev_one, qkv_far, side_far, out_pair, qkv_a, qkv_b, gain_one, bias, ffn_a, out_b, down_b, out_a_own, out_a_far,
        ffn_b, down_a, gain_two, cot, grad_low_down, gate_up_own, down_own, down_sent,
    ))
    out_far = far_blocks(out_pair, 1)
    prev_two = shift(prev_one[rows - tail :], 1, n_c)
    qkv_four = four(qkv_far)
    side_all = jnp.concatenate(near_blocks(*side_far, 0), axis=0)
    every = from_xor(side_all[:: w_forget.shape[0], n_heads], 0, n_f, f_rank).astype(jnp.int32)
    side_w = jnp.concatenate([side_all, jnp.zeros((width, LANES - n_heads - 1 - rank_r), BF), qkv_a], axis=1)
    args = (gain_one, qkv_four, side_w, qkv_b, bias, head_cols, rank_r)
    down_far = far_blocks(down_sent, 0)
    tok_in, prev_two = lax.optimization_barrier((tok, prev_two))
    normed, low_qkv, query, *filled = project(offs, tok_in, None, tail, *args, None, before)
    seg_two = prev_two[tail, :rows].astype(jnp.int32)
    seg_far = []
    for b in range(-(-tail // BLK)):
        start, end = min(b * BLK, tail + 32 - BLK), min((b + 1) * BLK, tail)
        known = seg_two[rows - tail + b * BLK : rows - tail + end]
        seg_far.append(jnp.pad(known, (b * BLK - start, BLK - (end - start))))
    seg_keys = jnp.concatenate(seg_far + [prev_one[rows, :rows].astype(jnp.int32), seg_one])
    last_keys = jnp.max(seg_keys.reshape(-1, BLK), axis=1)
    lows = jnp.sum(last_keys[None, :] < seg_one[::BLK][:, None], axis=1).astype(jnp.int32)

    gate_up_far = far_blocks(after(gate_up_own, out_far[1], down_far[1], query), 0)
    keys, vals, logits = project(offs, prev_one, prev_two, tail, *args, filled)
    out_w = near_blocks(out_far[0], after(out_far[1], query), 1)
    logits, out_w = lax.optimization_barrier((logits, out_w))
    seg_col, seg_row = (seg_keys[:, None], seg_one[None, :])
    gq, gk, gk_next, gates, total = gate_tables(logits, seg_col, seg_row, n_heads, rows)
    mixed_own, mixed_f, gq_one, gq_two = attention_forward(lows, query, keys, vals, gq, gk, gates, total, n_heads)
    mixed_far = other(mixed_own)
    sent_q1 = jnp.concatenate([query, gq_one], axis=1)
    sent_q2 = jnp.concatenate([query[:tail], gq_two[:tail]], axis=1)
    if shared:
        down_pair = lax.ppermute(after(down_far[1], keys), "ctx", [(i, i ^ 1) for i in range(n_c)])
        down_pair = after(down_pair, mixed_own)
        lower, upper = jnp.where(odd == 0, down_far[1], down_pair), jnp.where(odd == 0, down_pair, down_far[1])
        down_got = jnp.concatenate([lower, upper], axis=1)
    else:
        down_got = down_far[1]
    mixed_far, sent_q1, sent_q2, down_got = lax.optimization_barrier((mixed_far, sent_q1, sent_q2, down_got))
    next_q1 = shift(sent_q1, -1, n_c)
    next_q2 = shift(sent_q2, -2, n_c)

    gate_up_w = four((after(gate_up_own, mixed_own), after(gate_up_far[1], down_got))) if shared else four(gate_up_far)
    down_w = four((after(down_own, mixed_own), down_got)) if shared else four(down_far)
    if shared:
        mixed_far, gate_up_far = lax.optimization_barrier((mixed_far, gate_up_far))
    hidden, normed_ffn, low_ffn, low_out = out_projection(
        offs, rank, tok, mixed_own, mixed_far, out_w, out_a_own, out_a_far, out_b, gain_two, ffn_a
    )
    units, grad_gate, grad_up, far, own, own_low = feed_forward(
        rank, normed_ffn, low_ffn, cot, grad_low_down, gate_up_w, down_w, ffn_b, down_a
    )
    got = other(far)
    down_part = down_partial(after(units, far), down_w, down_a)
    qkv_w = [jnp.concatenate([after(qkv_four[i], far), qkv_four[i + 1]], axis=0) for i in (0, 2)]
    got, down_part, qkv_w = lax.optimization_barrier((got, down_part, qkv_w))
    grad_hidden, grad_hidden_b, grad_low_ffn, grad_low_out, gm_own, gm_send = middle(
        rank, own, got, own_low, hidden, cot, gain_two, ffn_a, out_b, out_w, out_a_own, out_a_far
    )
    grad_mixed, sent_d2 = mixed_gradient(rank, gm_own, other(gm_send), mixed_f, n_heads, tail)

    next_d1 = shift(grad_mixed, -1, n_c)
    next_d2 = shift(sent_d2, -2, n_c)
    grad_q, row_lanes, across = attention_dq(
        lows, query, keys, vals, grad_mixed, gq_one, gk, n_heads, (before - rows) // BLK
    )
    across = shift(across, -1, n_c)
    docs_at = head_cols + 3 * n_heads
    grad_k_own, grad_v_own, own_lanes = attention_dkv_own(keys, vals, query, after(grad_mixed, grad_q), gq_one, gk, n_heads)
    next_q1, next_q2, next_d1, next_d2, _ = lax.optimization_barrier((next_q1, next_q2, next_d1, next_d2, grad_k_own))
    next_docs = jnp.concatenate([next_q1[::BLK, docs_at : docs_at + DOCS], next_q2[::BLK, docs_at : docs_at + DOCS]])
    next_docs = next_docs.astype(F32)
    ids = jnp.arange(1, DOCS + 1).astype(F32)
    next_first = jnp.where(jnp.sum(next_docs, 1) > 0, jnp.sum(next_docs * ids[None, :], 1), 99.0)
    last_rows = seg_one[BLK - 1 :: BLK].astype(F32)
    highs = jnp.sum(next_first[None, :] <= last_rows[:, None], axis=1).astype(jnp.int32)
    lane = lax.broadcasted_iota(jnp.int32, (1, width), 1)
    own_part = lambda values: values * (lane // (width // 2) == t_rank)
    natural = lambda values: from_xor(values, 1, n_f, f_rank)
    by_tp = lambda a, b: jnp.concatenate([jnp.where(first, a, b), jnp.where(first, b, a)], axis=1)
    place = lambda values: by_tp(values, jnp.zeros_like(values))
    rows_of = lambda values: lax.dynamic_slice_in_dim(values, t_rank * half, half, 0)
    onehot = (jnp.arange(a_qkv.shape[0])[:, None] == every[None, :]).astype(F32)
    onehot = jnp.repeat(onehot, n_c * n_t, axis=1)

    owners = n_f * n_c * n_t

    def pack(tables):
        packed = jnp.concatenate([t.reshape(rank_r, owners, -1) for t in tables], axis=2).transpose(1, 0, 2)
        return packed.astype(BF).reshape(owners, -1), [t.shape[1] // owners for t in tables]

    def take_apart(spread, sizes):
        spread = spread.reshape(-1, rank_r, sum(sizes))
        outs, at = [], 0
        for size in sizes:
            outs.append(spread[:, :, at : at + size])
            at += size
        return outs

    table_out_a = [t_dot(grad_low_out, rows_of(mixed_own)), t_dot(grad_low_out, rows_of(mixed_far))]
    table_out_b = t_dot(rows_of(low_out), grad_hidden_b)
    table_ffn_a = t_dot(grad_low_ffn, rows_of(normed_ffn))
    tables_ffn = [t_dot(low_ffn, grad_gate), t_dot(low_ffn, grad_up), t_dot(grad_low_down, units)]
    highs, table_out_a, table_out_b, table_ffn_a, tables_ffn = lax.optimization_barrier(
        (highs, table_out_a, table_out_b, table_ffn_a, tables_ffn)
    )
    grad_k, grad_v, next_lanes = attention_dkv_next(
        highs, keys, vals, next_q1, next_q2, next_d1, next_d2, gk_next, grad_k_own, grad_v_own, n_heads
    )
    down_other = other(after(down_part, grad_mixed))

    grads = (grad_q, grad_k, grad_v)
    far_in, own_in, part_low_qkv, *tables_b = input_gradient(
        rank, grads, logits, seg_col, seg_row, row_lanes, own_lanes, next_lanes, across, qkv_w, side_w, qkv_b, low_qkv, n_heads
    )
    grad_low_qkv = (part_low_qkv + other(part_low_qkv)).astype(BF)
    got_in = other(far_in)
    parts = [values[:, width : width + 3 * rank_r].astype(F32).reshape(rows, 3, rank_r) for values in (down_part, down_other)]
    parts = [values[:, 0] + values[:, 1] + values[:, 2] for values in parts]
    low_down = after((parts[0] + parts[1]).astype(BF), far_in)
    grad_tok = token_gradient(offs, rank, own_in, got_in, grad_low_qkv, qkv_a, tok, gain_one, grad_hidden)
    tok_far = other(grad_tok)
    block_output = block_result(offs, hidden, down_part, after(down_other, grad_tok), down_b)
    grad_tokens = both_halves(rank, grad_tok, tok_far)
    if not direct:
        block_output = from_xor(block_output, 1, n_f, f_rank)
        grad_tokens = from_xor(grad_tokens, 1, n_f, f_rank)

    table_qkv_a, table_down_b = t_dot(grad_low_qkv, normed), t_dot(low_down, cot)
    if direct:
        bits = n_f.bit_length() - 1
        inv = [sum((((f_rank ^ i) >> j) & 1) << (bits - 1 - j) for j in range(bits)) * block for i in range(n_f)]
        packed = pack_gradients(
            jnp.stack(inv).astype(jnp.int32), rank, [table_qkv_a, table_down_b], [table_out_b, table_ffn_a], tables_b,
            table_out_a, tables_ffn, owners,
        )
        landed = lax.all_to_all(after(packed, grad_tok), ("fsdp", "ctx", "tp"), 0, 0, tiled=True)
        part, unit_part = width // owners, unit_cols * n_t // owners
        by_row, by_column = spread_gradients(every, landed, a_qkv.shape[0], rank_r, 3, 8, unit_part, part)
        at = [0, unit_part, 2 * unit_part] + [3 * unit_part + i * part for i in range(9)]
        cut = lambda i: by_row[:, :, at[i] : at[i + 1]]
        cut_t = lambda i: by_column[:, at[i] : at[i + 1]]
        return (
            block_output[None], grad_tokens[None], cut_t(3), jnp.stack([cut(7), cut(8), cut(9)], axis=2), cut_t(10),
            cut(5), cut_t(6), jnp.stack([cut(0), cut(1)], axis=2), cut_t(2), cut(4),
        )
    early, early_sizes = pack([
        by_tp(*table_out_a), natural(table_out_b), natural(table_ffn_a), *[place(t) for t in tables_ffn],
    ])
    late, late_sizes = pack([
        own_part(natural(table_qkv_a)), *[place(t) for t in tables_b], own_part(natural(table_down_b)),
    ])
    landed = lax.all_to_all(jnp.concatenate([late, early], axis=1), ("fsdp", "ctx", "tp"), 0, 0, tiled=True)
    split = rank_r * sum(late_sizes)
    spread = jnp.dot(onehot.astype(BF), landed, preferred_element_type=F32)
    done = take_apart(spread[:, :split], late_sizes) + take_apart(spread[:, split:], early_sizes)
    swap = lambda values: values.transpose(0, 2, 1)
    return (
        block_output[None],
        grad_tokens[None],
        swap(done[0]),
        jnp.stack(done[1:4], axis=2),
        swap(done[5]),
        done[6],
        swap(done[7]),
        jnp.stack(done[8:10], axis=2),
        swap(done[10]),
        done[4],
    )


def solution(mesh):
    in_specs = (
        P("fsdp", "ctx", None), P("fsdp", "ctx"), P("fsdp"), P("fsdp", None, "tp"), P("fsdp", "tp"), P("tp"),
        P("tp", "fsdp"), P("fsdp", None, "tp"), P("tp", "fsdp"),
        P(), P(), P(), P(), P(), P(), P(), P(), P(), P(),
        P("fsdp", "ctx", None),
    )
    out_specs = (
        P("fsdp", "ctx", None),
        P("fsdp", "ctx", None),
        P(None, ("fsdp", "ctx", "tp"), None),
        P(None, None, None, ("fsdp", "ctx", "tp")),
        P(None, ("fsdp", "ctx", "tp"), None),
        P(None, None, ("fsdp", "ctx", "tp")),
        P(None, ("fsdp", "ctx", "tp"), None),
        P(None, None, None, ("fsdp", "ctx", "tp")),
        P(None, ("fsdp", "ctx", "tp"), None),
        P(None, None, ("fsdp", "ctx", "tp")),
    )
    return jax.shard_map(body, mesh=mesh, in_specs=in_specs, out_specs=out_specs, check_vma=False)
```

```python
import jax
import jax.numpy as jnp
from jax import lax
from jax.experimental import pallas as pl
from jax.experimental.pallas import tpu as pltpu
from jax.sharding import PartitionSpec as P

HD = 64
DOC_MOST = 800
DOCS = 8
BF = jnp.bfloat16
F32 = jnp.float32
HI = lax.Precision.HIGHEST


def dot(a, b):
    return jnp.dot(a, b, preferred_element_type=F32)


def dot_t(a, b):
    return lax.dot_general(a, b, (((1,), (1,)), ((), ())), preferred_element_type=F32)


def t_dot(a, b):
    return lax.dot_general(a, b, (((0,), (0,)), ((), ())), preferred_element_type=F32)


def xor_order(size):
    order, bit = [0], size // 2
    while bit:
        order, bit = order + [step ^ bit for step in order], bit // 2
    return order


def after(values, *done):
    return lax.optimization_barrier((values, *done))[0]


def far_blocks(shard, dim):
    size = lax.axis_size("fsdp")
    own, bit = shard, size // 2
    while True:
        got = lax.ppermute(own, "fsdp", [(i, i ^ bit) for i in range(size)])
        if bit == 2:
            return own, got
        own, bit = jnp.concatenate([own, got], axis=dim), bit // 2


def near_blocks(own, got, dim):
    both = jnp.concatenate([own, got], axis=dim)
    size = lax.axis_size("fsdp")
    return [both, lax.ppermute(both, "fsdp", [(i, i ^ 1) for i in range(size)])]


def to_xor(values, dim, size, rank):
    block = values.shape[dim] // size
    return jnp.concatenate(
        [lax.dynamic_slice_in_dim(values, (rank ^ step) * block, block, dim) for step in xor_order(size)],
        axis=dim,
    )


def from_xor(values, dim, size, rank):
    block = values.shape[dim] // size
    bits = size.bit_length() - 1
    pieces = []
    for natural in range(size):
        mixed = rank ^ natural
        place = sum(((mixed >> j) & 1) << (bits - 1 - j) for j in range(bits))
        pieces.append(lax.dynamic_slice_in_dim(values, place * block, block, dim))
    return jnp.concatenate(pieces, axis=dim)


def shift(values, hop, size):
    pairs = [(i, i + hop) for i in range(size) if 0 <= i + hop < size]
    return lax.ppermute(values, "ctx", pairs)


LANES = 128
BLK = 256
BIG = -1e30


def spec(shape, index):
    return pl.BlockSpec(shape, index)


def call(kernel, grid, ins, in_specs, outs, out_specs, scratch=(), prefetch=0, flops=0, nbytes=0, exps=0, aliases=None, cost=1):
    return pl.pallas_call(
        kernel,
        out_shape=outs,
        grid_spec=pltpu.PrefetchScalarGridSpec(
            num_scalar_prefetch=prefetch, grid=grid, in_specs=in_specs, out_specs=out_specs, scratch_shapes=list(scratch)
        ),
        compiler_params=pltpu.CompilerParams(
            dimension_semantics=("arbitrary",) * len(grid), vmem_limit_bytes=56 * 2**20
        ),
        input_output_aliases=aliases or {},
        cost_estimate=pl.CostEstimate(flops=cost, bytes_accessed=1, transcendentals=0),
    )(*ins)


def whole(values):
    return spec(values.shape, lambda *_: (0,) * len(values.shape))


def lane_ids(rows):
    return lax.broadcasted_iota(jnp.int32, (rows, LANES), 1)


def split3(values):
    high = values.astype(BF)
    rest = values - high.astype(F32)
    mid = rest.astype(BF)
    return high, mid, (rest - mid.astype(F32)).astype(BF)


def split_lanes(values, n):
    lane = lane_ids(values.shape[0])
    values = jnp.where(lane < n, values, 0.0)
    high, mid, low = (part.astype(F32) for part in split3(values))
    return high + pltpu.roll(mid, n, 1) + pltpu.roll(low, 2 * n, 1)


def exact_dot(mask, values):
    high, mid, low = split3(values)
    return dot(mask, high) + dot(mask, mid) + dot(mask, low)


def norm_terms(blocks):
    width = sum(b.shape[1] for b in blocks)
    total = sum(jnp.sum(b * b, axis=1, keepdims=True) for b in blocks)
    return lax.rsqrt(total / width + 1e-05)


def pair_lanes(pair, n_heads, kind):
    lane = lax.broadcasted_iota(jnp.int32, (LANES, LANES), 1)
    to = lane & (HD - 1)
    head = jnp.where(lane >= HD, 2 * pair, 2 * pair + 1)
    gate_at = 3 if kind == "k" else 0
    part = to - gate_at
    source = jnp.where((part >= 0) & (part < 3), part * n_heads + head, -1)
    if kind != "d":
        ones = to - (3 - gate_at)
        source = jnp.where((ones >= 0) & (ones < 3), 3 * n_heads + DOCS, source)
        source = jnp.where((to >= 8) & (to < 8 + DOCS), to - 8 + 3 * n_heads, source)
    return (lax.broadcasted_iota(jnp.int32, (LANES, LANES), 0) == source).astype(BF)


def pair_of(values, gate_parts, select):
    extra = dot(gate_parts, select).astype(BF)
    low = lane_ids(values.shape[0]) < HD
    return jnp.where(low, values, extra), jnp.where(low, extra, values)


def pair_ones(values):
    low = lane_ids(values.shape[0]) < HD
    one = jnp.ones((), BF)
    return jnp.where(low, values, one), jnp.where(low, one, values)


def block_at(index):
    return pl.ds(pl.multiple_of(index * BLK, BLK), BLK)


def causal_from(rows, first):
    row = lax.broadcasted_iota(jnp.int32, (rows, BLK), 0)
    return row + first >= lax.broadcasted_iota(jnp.int32, (rows, BLK), 1)


def lane_column(acc, lane_at):
    return jnp.sum(jnp.where(lane_ids(acc.shape[0]) == lane_at, acc, 0.0), axis=1, keepdims=True)


def attention_forward(bounds, q, k, v, gq, gk, gates, total, n_heads):
    rows, keys = q.shape[0], k.shape[0]
    n_before = (keys - rows) // BLK
    pairs = n_heads // 2
    assert rows == 2 * BLK

    def kernel(
        lo_ref, q_ref, k_ref, v_ref, gq_ref, gk_ref, gate_ref, tot_ref, mixed_ref, float_ref, one_ref, two_ref,
        qx, scores, tops, parts, accs, log_ref,
    ):
        pair = pl.program_id(0)
        pick_k = pair_lanes(pair, n_heads, "k")
        for side, value in enumerate(pair_of(q_ref[...], gq_ref[...], pair_lanes(pair, n_heads, "q"))):
            qx[side] = value
        both, late, early = slice(0, rows), slice(BLK, rows), slice(0, BLK)

        def score(kb, here, at, mask=None, first=False):
            for side, key in enumerate(pair_of(k_ref[here, :], gk_ref[here, :], pick_k)):
                s = dot_t(qx[side, at, :], key)
                if mask is not None:
                    s = jnp.where(mask, s, BIG)
                scores[side, at, here] = s
                top = jnp.maximum(s[:, :LANES], s[:, LANES:])
                tops[side, at, :] = top if first else jnp.maximum(tops[side, at, :], top)

        def gather(here, at, first=False):
            for side in range(2):
                w = jnp.exp(scores[side, at, here] - tops[side, at, :1])
                part = w[:, :LANES] + w[:, LANES:]
                acc = dot(w.astype(BF), v_ref[here, :])
                parts[side, at, :] = part if first else parts[side, at, :] + part
                accs[side, at, :] = acc if first else accs[side, at, :] + acc

        own = [slice(b * BLK, (b + 1) * BLK) for b in (n_before, n_before + 1)]
        low, high = lo_ref[0], jnp.minimum(lo_ref[1], n_before)
        score(n_before, own[0], both, causal_from(rows, 0), True)
        score(n_before + 1, own[1], late, causal_from(BLK, 0))
        pl.loop(high, n_before)(lambda kb: score(kb, block_at(kb), both))
        pl.loop(low, high)(lambda kb: score(kb, block_at(kb), early))
        for side in range(2):
            tops[side] = jnp.broadcast_to(jnp.max(tops[side], axis=1, keepdims=True), (rows, LANES))
        gather(own[0], both, True)
        gather(own[1], late)
        pl.loop(high, n_before)(lambda kb: gather(block_at(kb), both))
        pl.loop(low, high)(lambda kb: gather(block_at(kb), early))
        lane = lane_ids(rows)
        results, logs = [], jnp.zeros((rows, LANES), F32)
        for side in range(2):
            row_total = jnp.sum(parts[side], axis=1, keepdims=True)
            results.append(accs[side] / row_total)
            logs = jnp.where(lane == 2 * pair + side, tops[side] + jnp.log(row_total), logs)
        out = jnp.where(lane < HD, results[0], results[1])
        mixed_ref[...] = out.astype(BF)
        float_ref[...] = out

        @pl.when(pair == 0)
        def _():
            log_ref[...] = logs

        @pl.when(pair > 0)
        def _():
            log_ref[...] = jnp.where((lane >> 1) == pair, logs, log_ref[...])

        @pl.when(pair == pairs - 1)
        def _():
            values = gate_ref[...] - log_ref[...]
            rest = gq_ref[...].astype(F32)
            one_ref[...] = jnp.where(lane < 3 * n_heads, split_lanes(values, n_heads), rest).astype(BF)
            values = values + tot_ref[:1, :]
            two_ref[...] = jnp.where(lane < 3 * n_heads, split_lanes(values, n_heads), rest).astype(BF)

    here = lambda n: spec((n, LANES), lambda i, *_: (0, i))
    shared = lambda n: spec((n, LANES), lambda i, *_: (0, 0))
    return call(
        kernel,
        (pairs,),
        (bounds, q, k, v, gq, gk, gates, total),
        [here(rows), here(keys), here(keys), shared(rows), shared(keys), shared(rows), shared(8)],
        (
            jax.ShapeDtypeStruct(q.shape, BF), jax.ShapeDtypeStruct(q.shape, F32),
            jax.ShapeDtypeStruct((rows, LANES), BF), jax.ShapeDtypeStruct((rows, LANES), BF),
        ),
        (here(rows), here(rows), shared(rows), shared(rows)),
        [pltpu.VMEM((2, rows, LANES), BF), pltpu.VMEM((2, rows, keys), F32)]
        + [pltpu.VMEM((2, rows, LANES), F32)] * 3 + [pltpu.VMEM((rows, LANES), F32)],
        prefetch=1,
    )


def attention_dq(bounds, q, k, v, d, gq, gk, n_heads, n_far):
    rows, keys = q.shape[0], k.shape[0]
    n_before = (keys - rows) // BLK
    pairs = n_heads // 2

    def kernel(lo_ref, q_ref, k_ref, v_ref, d_ref, gq_ref, gk_ref, gd_ref, dq_ref, row_ref, far_ref, qx, dx, accs):
        pair = pl.program_id(0)
        lane = lane_ids(rows)
        pick_k = pair_lanes(pair, n_heads, "k")
        for side, value in enumerate(pair_of(q_ref[...], gq_ref[...], pair_lanes(pair, n_heads, "q"))):
            qx[side] = value
        for side, value in enumerate(pair_of(d_ref[...], gd_ref[...], pair_lanes(pair, n_heads, "d"))):
            dx[side] = value
        both, late, early = slice(0, rows), slice(BLK, rows), slice(0, BLK)

        @pl.when(pair == 0)
        def _():
            far_ref[...] = jnp.zeros_like(far_ref)
            row_ref[...] = jnp.zeros_like(row_ref)

        def block(here, at, mask=None, first=False):
            values = pair_ones(v_ref[here, :])
            for side, key in enumerate(pair_of(k_ref[here, :], gk_ref[here, :], pick_k)):
                s = dot_t(qx[side, at, :], key)
                if mask is not None:
                    s = jnp.where(mask, s, BIG)
                ds = (jnp.exp(s) * dot_t(dx[side, at, :], values[side])).astype(BF)
                acc = dot(ds, key)
                accs[side, at, :] = acc if first else accs[side, at, :] + acc

        low, high = lo_ref[0], jnp.minimum(lo_ref[1], n_before)

        @pl.when(low < n_far)
        def _():
            accs[...] = jnp.zeros_like(accs)
            pl.loop(high, n_far)(lambda kb: block(block_at(kb), both))
            pl.loop(low, jnp.minimum(high, n_far))(lambda kb: block(block_at(kb), early))
            for side in range(2):
                moved = jnp.sum(jnp.where(lane == HD * (1 - side), accs[side], 0.0))
                far_ref[...] += jnp.where(lane[:8] == 2 * pair + side, moved, 0.0)
            block(slice(n_before * BLK, (n_before + 1) * BLK), both, causal_from(rows, 0))

        @pl.when(low >= n_far)
        def _():
            block(slice(n_before * BLK, (n_before + 1) * BLK), both, causal_from(rows, 0), True)

        block(slice((n_before + 1) * BLK, (n_before + 2) * BLK), late, causal_from(BLK, 0))
        pl.loop(jnp.maximum(high, n_far), n_before)(lambda kb: block(block_at(kb), both))
        pl.loop(jnp.maximum(low, n_far), high)(lambda kb: block(block_at(kb), early))
        dq_ref[...] = (jnp.where(lane < HD, accs[0], accs[1]) * HD ** (-0.5)).astype(BF)
        for side in range(2):
            total = lane_column(accs[side], HD * (1 - side))
            row_ref[...] = jnp.where(lane == 2 * pair + side, total, row_ref[...])

    here = lambda n: spec((n, LANES), lambda i, *_: (0, i))
    shared = lambda n: spec((n, LANES), lambda i, *_: (0, 0))
    return call(
        kernel,
        (pairs,),
        (bounds, q, k, v, d, gq, gk, d),
        [here(rows), here(keys), here(keys), here(rows), shared(rows), shared(keys), spec((rows, LANES), lambda i, *_: (0, pairs))],
        (
            jax.ShapeDtypeStruct(q.shape, BF), jax.ShapeDtypeStruct((rows, LANES), F32),
            jax.ShapeDtypeStruct((8, LANES), F32),
        ),
        (here(rows), shared(rows), shared(8)),
        [pltpu.VMEM((2, rows, LANES), BF)] * 2 + [pltpu.VMEM((2, rows, LANES), F32)],
        prefetch=1, cost=3363750000
    )


def score_block(kx, vx, queries, grads, at, dks, dvs, mask=None, first=False):
    for side in range(2):
        s = dot_t(kx[side, at, :], queries[side])
        if mask is not None:
            s = jnp.where(mask, s, BIG)
        w = jnp.exp(s)
        ds = (w * dot_t(vx[side, at, :], grads[side])).astype(BF)
        dk, dv = dot(ds, queries[side]), dot(w.astype(BF), grads[side])
        dks[side, at, :] = dk if first else dks[side, at, :] + dk
        dvs[side, at, :] = dv if first else dvs[side, at, :] + dv


def attention_dkv_own(k, v, q, d, gq, gk, n_heads):
    rows = q.shape[0]
    place = k.shape[0] // rows - 1
    pairs = n_heads // 2

    def kernel(k_ref, v_ref, q_ref, d_ref, gq_ref, gd_ref, gk_ref, dk_ref, dv_ref, own_ref, kx, vx, dks, dvs):
        pair = pl.program_id(0)
        lane = lane_ids(rows)
        pick_q, pick_d = (pair_lanes(pair, n_heads, "q"), pair_lanes(pair, n_heads, "d"))
        for side, value in enumerate(pair_of(k_ref[...], gk_ref[...], pair_lanes(pair, n_heads, "k"))):
            kx[side] = value
        for side, value in enumerate(pair_ones(v_ref[...])):
            vx[side] = value
        both, late, early = slice(0, rows), slice(BLK, rows), slice(0, BLK)

        @pl.when(pair == 0)
        def _():
            own_ref[...] = jnp.zeros_like(own_ref)

        def load(here):
            return pair_of(q_ref[here, :], gq_ref[here, :], pick_q), pair_of(d_ref[here, :], gd_ref[here, :], pick_d)

        keep = lax.broadcasted_iota(jnp.int32, (rows, BLK), 0) - BLK <= lax.broadcasted_iota(jnp.int32, (rows, BLK), 1)
        first_keep = lax.broadcasted_iota(jnp.int32, (BLK, BLK), 0) <= lax.broadcasted_iota(jnp.int32, (BLK, BLK), 1)
        score_block(kx, vx, *load(late), both, dks, dvs, keep, True)
        score_block(kx, vx, *load(early), early, dks, dvs, first_keep)
        for side in range(2):
            column = lane_column(dks[side], HD * (1 - side) + 3)
            own_ref[...] = jnp.where(lane == 2 * pair + side, column, own_ref[...])
        dk_ref[...] = jnp.where(lane < HD, dks[0], dks[1])
        dv_ref[...] = jnp.where(lane < HD, dvs[0], dvs[1])

    heads_spec = lambda n: spec((n, LANES), lambda i, *_: (0, i))
    shared = lambda n: spec((n, LANES), lambda i, *_: (0, 0))
    keys_spec = spec((rows, LANES), lambda i, *_: (place, i))
    return call(
        kernel, (pairs,), (k, v, q, d, gq, d, gk),
        [
            keys_spec, keys_spec, heads_spec(rows), heads_spec(rows), shared(rows),
            spec((rows, LANES), lambda i, *_: (0, pairs)), spec((rows, LANES), lambda i, *_: (place, 0)),
        ],
        (jax.ShapeDtypeStruct(q.shape, F32), jax.ShapeDtypeStruct(q.shape, F32), jax.ShapeDtypeStruct((rows, LANES), F32)),
        (heads_spec(rows), heads_spec(rows), shared(rows)),
        [pltpu.VMEM((2, rows, LANES), BF)] * 2 + [pltpu.VMEM((2, rows, LANES), F32)] * 2, cost=2294250000
    )


def attention_dkv_next(bounds, k, v, q_one, q_two, d_one, d_two, gkn, dk, dv, n_heads):
    rows, tail = q_one.shape[0], q_two.shape[0]
    place = k.shape[0] // rows - 1
    pairs = n_heads // 2
    assert 0 < tail - BLK <= BLK

    def kernel(
        hi_ref, k_ref, v_ref, q1_ref, d1_ref, gq1_ref, gd1_ref, q2_ref, d2_ref, gq2_ref, gd2_ref, gkn_ref,
        dk_own, dv_own, dk_ref, dv_ref, next_ref, kx, vx, dks, dvs,
    ):
        pair = pl.program_id(0)
        lane = lane_ids(rows)
        both, late, early = slice(0, rows), slice(BLK, rows), slice(0, BLK)
        few, many = hi_ref[0], hi_ref[1]

        @pl.when(pair == 0)
        def _():
            next_ref[...] = jnp.zeros_like(next_ref)

        @pl.when(many > 0)
        def _():
            pick_q, pick_d = (pair_lanes(pair, n_heads, "q"), pair_lanes(pair, n_heads, "d"))
            for side, value in enumerate(pair_of(k_ref[...], gkn_ref[...], pair_lanes(pair, n_heads, "k"))):
                kx[side] = value
            for side, value in enumerate(pair_ones(v_ref[...])):
                vx[side] = value
            dks[...] = jnp.zeros_like(dks)
            dvs[...] = jnp.zeros_like(dvs)

            def block(refs, here, at):
                q_ref, gq_ref, d_ref, gd_ref = refs
                queries = pair_of(q_ref[here, :], gq_ref[here, :], pick_q)
                score_block(kx, vx, queries, pair_of(d_ref[here, :], gd_ref[here, :], pick_d), at, dks, dvs)

            one, two = (q1_ref, gq1_ref, d1_ref, gd1_ref), (q2_ref, gq2_ref, d2_ref, gd2_ref)
            pl.loop(0, jnp.minimum(few, 2))(lambda j: block(one, block_at(j), both))
            pl.loop(few, jnp.minimum(many, 2))(lambda j: block(one, block_at(j), late))
            pl.when(few > 2)(lambda: block(two, early, both))
            pl.when((few <= 2) & (many > 2))(lambda: block(two, early, late))
            pl.when(many > 3)(lambda: block(two, slice(BLK, tail), both))
            for side in range(2):
                value = lane_column(dks[side], HD * (1 - side) + 3)
                next_ref[...] = jnp.where(lane == 2 * pair + side, value, next_ref[...])
            dk_ref[...] = (dk_own[...] + jnp.where(lane < HD, dks[0], dks[1])).astype(BF)
            dv_ref[...] = (dv_own[...] + jnp.where(lane < HD, dvs[0], dvs[1])).astype(BF)

        @pl.when(many == 0)
        def _():
            dk_ref[...] = dk_own[...].astype(BF)
            dv_ref[...] = dv_own[...].astype(BF)

    heads_spec = lambda n: spec((n, LANES), lambda i, *_: (0, i))
    shared = lambda n: spec((n, LANES), lambda i, *_: (0, 0))
    last = lambda n: spec((n, LANES), lambda i, *_: (0, pairs))
    keys_spec = spec((rows, LANES), lambda i, *_: (place, i))
    return call(
        kernel, (pairs,), (bounds, k, v, q_one, d_one, q_one, d_one, q_two, d_two, q_two, d_two, gkn, dk, dv),
        [
            keys_spec, keys_spec, heads_spec(rows), heads_spec(rows), last(rows), last(rows),
            heads_spec(tail), heads_spec(tail), last(tail), last(tail), shared(rows), heads_spec(rows), heads_spec(rows),
        ],
        (jax.ShapeDtypeStruct(dk.shape, BF), jax.ShapeDtypeStruct(dk.shape, BF), jax.ShapeDtypeStruct((rows, LANES), F32)),
        (heads_spec(rows), heads_spec(rows), shared(rows)),
        [pltpu.VMEM((2, rows, LANES), BF)] * 2 + [pltpu.VMEM((2, rows, LANES), F32)] * 2,
        prefetch=1, cost=2932500000
    )


def project(offs, x, x_far, tail, gain, w, side_w, qkv_b, bias, cols, rank_r, filled=None, before=0):
    width = gain.shape[1]
    block = width // 4
    own = filled is None
    rows = x.shape[0] // (2 * BLK) * 2 * BLK
    row_steps = 1 if own else 2
    parts = ("q", "k", "v") if own else ("k", "v")
    assert rows == 2 * BLK and BLK <= tail <= rows - 32

    def kernel(*refs):
        offs_ref, x_ref = refs[0], refs[1]
        at = 2
        if not own:
            far_ref, at = refs[2], 3
        gain_ref, *pieces, side_ref, b_ref, bias_ref = refs[at : at + 8]
        at += 8 + (0 if own else 3)
        outs, scr = refs[at:-3], refs[-3:]
        part, step = pl.program_id(0), pl.program_id(1)
        n_outs = dict(zip(("n", "low", "q", "k", "v", "logits") if own else ("k", "v", "logits"), outs))
        scr, low_scr, joint = scr
        at_rows = pl.ds(pl.multiple_of(step * rows, rows), rows)

        @pl.when(part == 0)
        def _():
            blocks = []
            for k in range(4):
                here = pl.ds(pl.multiple_of(offs_ref[k], LANES), block)
                value = x_ref[:, here]
                if not own:
                    far = jnp.concatenate([far_ref[:BLK, here], far_ref[tail + 32 - BLK : tail + 32, here]], axis=0)
                    value = jnp.where(step == 0, far, value)
                blocks.append(value.astype(F32))
            factor = norm_terms(blocks)
            for k in range(4):
                here = pl.ds(pl.multiple_of(offs_ref[k], LANES), block)
                scr[at_rows, k * block : (k + 1) * block] = (blocks[k] * factor * gain_ref[:, here]).astype(BF)
            side = dot(scr[at_rows, :], side_ref[...])
            low = side[:, LANES - rank_r :].astype(BF)
            low_scr[at_rows, :rank_r] = low
            n_outs["logits"][at_rows, :] = side + bias_ref[...]
            if own:
                n_outs["n"][...] = scr[...]
                n_outs["low"][...] = low

        @pl.when(step == 0)
        def _():
            for k in range(4):
                joint[k * block : (k + 1) * block, :] = pieces[k][...]

        value = dot(scr[at_rows, :], joint[...])
        value = (value + dot(low_scr[at_rows, :rank_r], b_ref[...])).astype(BF)
        for n, name in enumerate(parts):
            @pl.when(part == n)
            def _(name=name):
                out = n_outs[name]
                out[at_rows, :] = (value.astype(F32) * HD ** (-0.5)).astype(BF) if name == "q" else value

    keys = before + rows if own else filled[0].shape[0]
    ins = [offs, x] + ([] if own else [x_far]) + [gain, *w, side_w, qkv_b, bias] + ([] if own else list(filled))
    row_spec = spec((rows, width), lambda i, *_: (0, 0))
    in_specs = [row_spec] + ([] if own else [whole(x_far)])
    first = 0 if own else 1
    column = lambda n: spec((n, cols), lambda j, *_: (0, j + first))
    in_specs += [whole(gain), *[column(block)] * 4, whole(side_w), column(rank_r), whole(bias)]
    if not own:
        in_specs += [pl.BlockSpec(memory_space=pl.ANY)] * 3
    some = row_steps * rows
    at_keys = lambda n: spec((some, n), lambda *_: (before // some if own else 0, 0))
    outs = [jax.ShapeDtypeStruct((keys, cols), BF)] * 2 + [jax.ShapeDtypeStruct((keys, LANES), F32)]
    out_specs = [at_keys(cols), at_keys(cols), at_keys(LANES)]
    if own:
        here = lambda n: spec((rows, n), lambda *_: (0, 0))
        outs = [
            jax.ShapeDtypeStruct((rows, width), BF),
            jax.ShapeDtypeStruct((rows, rank_r), BF),
            jax.ShapeDtypeStruct((rows, cols), BF),
        ] + outs
        out_specs = [here(width), here(rank_r), here(cols)] + out_specs
    return call(
        kernel, (len(parts), row_steps), ins, in_specs, tuple(outs), tuple(out_specs),
        [pltpu.VMEM((some, width), BF), pltpu.VMEM((some, LANES), BF), pltpu.VMEM((width, cols), BF)], prefetch=1,
        aliases={} if own else {11: 0, 12: 1, 13: 2},
    )


def gate_tables(logits, seg_keys, seg_row, n_heads, rows):
    keys = logits.shape[0]
    before = keys - rows
    one = 3 * n_heads + DOCS

    def kernel(logit_ref, seg_ref, row_ref, gq_ref, gk_ref, gkn_ref, gate_ref, tot_ref):
        lane = lane_ids(BLK)
        doc = lane - 3 * n_heads + 1
        doc_lane = (doc > 0) & (doc <= DOCS)
        inner = lax.broadcasted_iota(jnp.int32, (BLK, BLK), 1) > lax.broadcasted_iota(jnp.int32, (BLK, BLK), 0)
        later = inner.astype(BF)

        def forget(at):
            value = logit_ref[at, :]
            value = jnp.minimum(value, 0.0) - jnp.log(1.0 + jnp.exp(-jnp.abs(value)))
            return jnp.where((lane < n_heads) & (seg_ref[at, :] > 0), value, 0.0)

        def lanes(values, docs):
            return (split_lanes(values, n_heads) + docs + jnp.where(lane == one, 1.0, 0.0)).astype(BF)

        def docs_k(at):
            return jnp.where(doc_lane & (doc != seg_ref[at, :]), BIG, 0.0)

        def suffix(first, last, carry, out_ref, base):
            for b in range(last - 1, first - 1, -1):
                at = slice(b * BLK, (b + 1) * BLK)
                values = forget(at)
                sums = exact_dot(later, values) + carry
                out_ref[b * BLK - base : (b + 1) * BLK - base, :] = lanes(sums, docs_k(at))
                carry = carry + jnp.sum(values, axis=0, keepdims=True)
            return carry

        n_before, n_all = before // BLK, keys // BLK
        zero = jnp.zeros((1, LANES), F32)
        near = suffix((before - rows) // BLK, n_before, zero, gk_ref, 0)
        tot_ref[...] = jnp.broadcast_to(near, tot_ref.shape)
        suffix(0, (before - rows) // BLK, near, gk_ref, 0)
        suffix(n_before, n_all, zero, gkn_ref, before)
        own = jnp.concatenate([forget(slice(b * BLK, (b + 1) * BLK)) for b in range(n_before, n_all)], axis=0)
        for b in range(rows // BLK):
            at = slice(before + b * BLK, before + (b + 1) * BLK)
            here = slice(b * BLK, (b + 1) * BLK)
            q_pos = lax.broadcasted_iota(jnp.int32, (BLK, rows), 0) + b * BLK
            k_pos = lax.broadcasted_iota(jnp.int32, (BLK, rows), 1)
            same = (row_ref[...] == seg_ref[at, :]) & (k_pos <= q_pos)
            sums = exact_dot(same.astype(BF), own)
            gate_ref[here, :] = sums
            gq_ref[here, :] = lanes(sums, jnp.where(doc_lane & (doc == seg_ref[at, :]), 1.0, 0.0))
            gk_ref[at, :] = lanes(-sums, docs_k(at))

    shape = lambda n, t: jax.ShapeDtypeStruct((n, LANES), t)
    outs = (shape(rows, BF), shape(keys, BF), shape(rows, BF), shape(rows, F32), shape(8, F32))
    return call(
        kernel, (1,), (logits, seg_keys, seg_row), [whole(logits), whole(seg_keys), whole(seg_row)],
        outs, tuple(whole(o) for o in outs), flops=10**8, nbytes=4 * 10**6,
    )


def weight_halves(w):
    half = w[0].shape[0] // 2
    at = lambda row: spec((half, w[0].shape[1]), lambda *_: (row, 0))
    return [at(0), at(0), at(1), at(1)]


def out_projection(offs, rank, x, mixed_own, mixed_far, w, a_own, a_far, out_b, gain, ffn_a):
    rows, width = x.shape
    block = width // 4
    rank_r = a_own.shape[1]

    def kernel(
        offs_ref, rank_ref, x_ref, mo, mf, wo0, wo1, wf0, wf1, ao, af, b_ref, gain_ref, fa, h_ref, n_ref, low_ref, lo_ref
    ):
        def run(m0, m1, w0, w1, a0, a1):
            low = (dot(m0[...], a0[...]) + dot(m1[...], a1[...])).astype(BF)
            lo_ref[...] = low
            for half in range(2):
                both = dot(m0[...], w0[half][...]) + dot(m1[...], w1[half][...])
                both = both + dot(low, b_ref[:, 2 * half * block : 2 * (half + 1) * block])
                for j in range(2):
                    k = 2 * half + j
                    here = pl.ds(pl.multiple_of(offs_ref[k], LANES), block)
                    value = x_ref[:, here].astype(F32) + both[:, j * block : (j + 1) * block]
                    h_ref[:, k * block : (k + 1) * block] = value

        pl.when(rank_ref[0] == 0)(lambda: run(mo, mf, (wo0, wo1), (wf0, wf1), ao, af))
        pl.when(rank_ref[0] != 0)(lambda: run(mf, mo, (wf0, wf1), (wo0, wo1), af, ao))
        value = h_ref[...]
        normed = (value * norm_terms([value]) * gain_ref[...]).astype(BF)
        n_ref[...] = normed
        low_ref[...] = dot(normed, fa[...]).astype(BF)

    rowed = whole
    outs = (
        jax.ShapeDtypeStruct((rows, width), F32), jax.ShapeDtypeStruct((rows, width), BF),
        jax.ShapeDtypeStruct((rows, rank_r), BF), jax.ShapeDtypeStruct((rows, rank_r), BF),
    )
    ins = (offs, rank, x, mixed_own, mixed_far, *w, *w, a_own, a_far, out_b, gain, ffn_a)
    return call(
        kernel, (1,), ins,
        [rowed(x), rowed(mixed_own), rowed(mixed_far)] + weight_halves(w) + [whole(v) for v in ins[9:]],
        outs, tuple(rowed(o) for o in outs), prefetch=2, flops=4 * rows * width * mixed_own.shape[1],
        nbytes=4 * width * mixed_own.shape[1] + 8 * rows * width, cost=1725000000
    )


def feed_forward(rank, normed, low, cot, grad_low, gate_up, down, ffn_b, down_a):
    rows, width = normed.shape
    block = width // 4
    half = rows // 2
    rank_r = low.shape[1]
    unit_cols = down_a.shape[0]
    tile = 512 if unit_cols % 512 == 0 else unit_cols
    tiles = unit_cols // tile
    down_at = down[0].shape[1] // tile - tiles

    def kernel(
        rank_ref, x_ref, low_ref, cot_ref, gl_ref, *rest,
    ):
        pieces, rest = rest[:12], rest[12:]
        bg_ref, bu_ref, ad_ref, *rest, wg, wu, wd = rest
        step = pl.program_id(0)
        units_ref, gg_ref, gu_ref, far_ref, own_ref, own_low_ref, part_ref, part_low_ref = rest

        @pl.when(step == 0)
        def _():
            part_ref[...] = jnp.zeros_like(part_ref)
            part_low_ref[...] = jnp.zeros_like(part_low_ref)

        for n, joint in enumerate((wg, wu, wd)):
            for k in range(4):
                joint[k * block : (k + 1) * block, :] = pieces[4 * n + k][...]
        gate = dot(x_ref[...], wg[...]) + dot(low_ref[...], bg_ref[...])
        up = dot(x_ref[...], wu[...]) + dot(low_ref[...], bu_ref[...])
        grad = dot(cot_ref[...], wd[...]) + dot_t(gl_ref[...], ad_ref[...])
        sig = jax.nn.sigmoid(gate)
        act = gate * sig
        units_ref[...] = (act * up).astype(BF)
        gg = (grad * up * sig * (1.0 + gate * (1.0 - sig))).astype(BF)
        gu = (grad * act).astype(BF)
        gg_ref[...] = gg
        gu_ref[...] = gu
        part_low_ref[:, :rank_r] += dot_t(gg, bg_ref[...]) + dot_t(gu, bu_ref[...])
        part_ref[...] += dot_t(gg, wg[...]) + dot_t(gu, wu[...])

        @pl.when(step == tiles - 1)
        def _():
            mine = pl.ds(pl.multiple_of(rank_ref[0] * half, half), half)
            theirs = pl.ds(pl.multiple_of((1 - rank_ref[0]) * half, half), half)
            far_ref[:, :width] = part_ref[theirs, :].astype(BF)
            far_ref[:, width:] = split_lanes(part_low_ref[theirs, :], rank_r).astype(BF)
            own_ref[...] = part_ref[mine, :]
            own_low_ref[...] = part_low_ref[mine, :]

    out = jax.ShapeDtypeStruct((rows, unit_cols), BF)
    out_spec = spec((rows, tile), lambda i, *_: (0, i))
    sums = (jax.ShapeDtypeStruct((rows, width), F32), jax.ShapeDtypeStruct((rows, LANES), F32))
    ends = (
        jax.ShapeDtypeStruct((half, width + LANES), BF), jax.ShapeDtypeStruct((half, width), F32),
        jax.ShapeDtypeStruct((half, LANES), F32),
    )
    return call(
        kernel,
        (tiles,),
        (rank, normed, low, cot, grad_low, *gate_up, *gate_up, *down, ffn_b, ffn_b, down_a),
        [
            whole(normed), whole(low), whole(cot), whole(grad_low),
            *[spec((block, tile), lambda i, *_: (0, i)) for _ in range(4)],
            *[spec((block, tile), lambda i, *_: (0, i + tiles)) for _ in range(4)],
            *[spec((block, tile), lambda i, *_: (0, i + down_at)) for _ in range(4)],
            spec((rank_r, tile), lambda i, *_: (0, i)),
            spec((rank_r, tile), lambda i, *_: (0, i + tiles)),
            spec((tile, rank_r), lambda i, *_: (i, 0)),
        ],
        (out, out, out, *ends),
        (out_spec, out_spec, out_spec, *[whole(e) for e in ends]),
        [pltpu.VMEM(e.shape, F32) for e in sums] + [pltpu.VMEM((width, tile), BF)] * 3,
        prefetch=1, cost=4657500000
    )


def whole_low(parts, n):
    parts = parts.astype(F32)
    return parts[:, :n] + parts[:, n : 2 * n] + parts[:, 2 * n : 3 * n]


def middle(rank, own, got, own_low, hidden, cot, gain, ffn_a, out_b, w, a_own, a_far):
    half, width = own.shape
    depth = width // 2
    rank_r = out_b.shape[0]
    cols = a_own.shape[0]

    def kernel(
        rank_ref, own_ref, got_ref, low_ref, h_ref, cot_ref, gain_ref, fa, b_ref, wo0, wo1, wf0, wf1, ao, af,
        gh_ref, ghb_ref, glf_ref, glo_ref, mine_ref, far_ref,
    ):
        ffn_low = (low_ref[:, :rank_r] + whole_low(got_ref[:, width:], rank_r)).astype(BF)
        glf_ref[...] = ffn_low
        incoming = own_ref[...] + got_ref[:, :width].astype(F32) + dot_t(ffn_low, fa[...])
        value = h_ref[...]
        factor = norm_terms([value])
        scaled = incoming * gain_ref[...]
        mean = jnp.mean(value * scaled, axis=1, keepdims=True)
        grad = cot_ref[...].astype(F32) + (factor * scaled - value * (factor * factor * factor * mean))
        gh_ref[...] = grad
        low_precision = grad.astype(BF)
        ghb_ref[...] = low_precision
        left, right = low_precision[:, :depth], low_precision[:, depth:]
        out_low = dot_t(low_precision, b_ref[...]).astype(BF)
        glo_ref[...] = out_low
        mine_ref[...] = (dot_t(left, wo0[...]) + dot_t(right, wo1[...]) + dot_t(out_low, ao[...])).astype(BF)
        far_ref[...] = (dot_t(left, wf0[...]) + dot_t(right, wf1[...]) + dot_t(out_low, af[...])).astype(BF)

    outs = (
        jax.ShapeDtypeStruct((half, width), F32), jax.ShapeDtypeStruct((half, width), BF),
        jax.ShapeDtypeStruct((half, rank_r), BF), jax.ShapeDtypeStruct((half, rank_r), BF),
        jax.ShapeDtypeStruct((half, cols), BF), jax.ShapeDtypeStruct((half, cols), BF),
    )
    ins = (rank, own, got, own_low, hidden, cot, gain, ffn_a, out_b, *w, *w, a_own, a_far)
    mine = lambda v: spec((half, v.shape[1]), lambda i, r: (r[0], 0))
    in_specs = [whole(own), whole(got), whole(own_low), mine(hidden), mine(cot)] + [whole(v) for v in ins[6:9]]
    in_specs += weight_halves(w) + [whole(a_own), whole(a_far)]
    return call(
        kernel, (1,), ins, in_specs, outs, tuple(whole(o) for o in outs), prefetch=1,
        flops=4 * half * width * cols, nbytes=4 * width * cols + 16 * half * width, cost=1311000000
    )


def mixed_gradient(rank, own, far, mixed, n_heads, tail):
    half, cols = own.shape

    def kernel(rank_ref, own_ref, far_ref, mixed_ref, out_ref, tail_ref):
        lane = lane_ids(half)
        for ref, first in ((own_ref, rank_ref[0]), (far_ref, 1 - rank_ref[0])):
            at = pl.ds(pl.multiple_of(first * half, half), half)
            sums = jnp.zeros((half, LANES), F32)
            for pair in range(n_heads // 2):
                here = slice(pair * LANES, (pair + 1) * LANES)
                product = ref[:, here].astype(F32) * mixed_ref[at, here]
                a = jnp.sum(jnp.where(lane < HD, product, 0.0), axis=1, keepdims=True)
                b = jnp.sum(jnp.where(lane < HD, 0.0, product), axis=1, keepdims=True)
                sums = jnp.where(lane == 2 * pair, -a, jnp.where(lane == 2 * pair + 1, -b, sums))
            out_ref[at, :cols] = ref[...]
            out_ref[at, cols:] = split_lanes(sums, n_heads).astype(BF)
        tail_ref[...] = out_ref[:tail, :]

    outs = [jax.ShapeDtypeStruct((n, cols + LANES), BF) for n in (2 * half, tail)]
    return call(
        kernel, (1,), (rank, own, far, mixed), [whole(own), whole(far), whole(mixed)],
        tuple(outs), tuple(whole(o) for o in outs), prefetch=1,
        flops=4 * half * cols, nbytes=16 * half * cols, cost=672750000
    )


def input_gradient(rank, grads, logits, seg_keys, seg_row, row_lanes, own_lanes, next_lanes, across, w, side_w, qkv_b, low_qkv, n_heads):
    rows, cols = grads[0].shape
    block = w[0].shape[0]
    half = rows // 2
    rank_r = qkv_b.shape[0]
    before = logits.shape[0] - rows
    steps = 3
    chunk = block // steps

    def kernel(
        rank_ref, q_ref, k_ref, v_ref, logit_ref, seg_ref, seg_row_ref, r_ref, o_ref, n_ref, a_ref, *refs,
    ):
        pieces, sides, refs = refs[:4], refs[4:8], refs[8:]
        (
            b_ref, lq_ref, far_ref, own_ref, low_ref, tq_ref, tk_ref, tv_ref, gl_ref, sum_ref, joint,
            side,
        ) = refs

        @pl.when(pl.program_id(0) == 0)
        def _():
            lane = lane_ids(rows)
            t = lax.broadcasted_iota(jnp.int32, (rows, rows), 0)
            i = lax.broadcasted_iota(jnp.int32, (rows, rows), 1)
            same = ((seg_row_ref[...] == seg_ref[...]) & (i >= t)).astype(BF)
            total = exact_dot(same, r_ref[...] - o_ref[...]) + exact_dot((i < t).astype(BF), n_ref[...])
            total = total + a_ref[:1, :]
            value = jnp.where(lane < n_heads, total * jax.nn.sigmoid(-logit_ref[...]), 0.0)
            gl_ref[...] = value.astype(BF)
            low = dot_t(q_ref[...], b_ref[:, :cols]) + dot_t(k_ref[...], b_ref[:, cols : 2 * cols])
            low_ref[...] = low + dot_t(v_ref[...], b_ref[:, 2 * cols :])
            for out, grad in ((tq_ref, q_ref), (tk_ref, k_ref), (tv_ref, v_ref)):
                out[...] = t_dot(lq_ref[...], grad[...])

        mine = pl.ds(pl.multiple_of(rank_ref[0] * half, half), half)
        theirs = pl.ds(pl.multiple_of((1 - rank_ref[0]) * half, half), half)
        for k in range(4):
            joint[k * chunk : (k + 1) * chunk, :] = pieces[k][...]
            side[k * chunk : (k + 1) * chunk, :] = sides[k][...]
        value = dot_t(q_ref[...], joint[:, :cols]) + dot_t(k_ref[...], joint[:, cols : 2 * cols])
        sum_ref[...] = value + dot_t(v_ref[...], joint[:, 2 * cols :]) + dot_t(gl_ref[...], side[...])
        for k in range(4):
            at = slice(k * chunk, (k + 1) * chunk)
            far_ref[k] = sum_ref[theirs, at].astype(BF)
            own_ref[k] = sum_ref[mine, at]

    ins = (rank, *grads, logits, seg_keys, seg_row, row_lanes, own_lanes, next_lanes, across, *w, *[side_w] * 4, qkv_b, low_qkv)
    at_own = lambda v: spec((rows, v.shape[1]), lambda i, *_: (before // rows, 0))
    in_specs = [whole(g) for g in grads] + [at_own(logits), at_own(seg_keys)]
    in_specs += [whole(v) for v in (seg_row, row_lanes, own_lanes, next_lanes, across)]
    n_col = w[0].shape[1]
    in_specs += [spec((chunk, n_col), lambda i, *_: (i, 0))] * 4
    in_specs += [spec((chunk, LANES), lambda i, *_, k=k: (i + k * steps, 0)) for k in range(4)]
    in_specs += [whole(qkv_b), whole(low_qkv)]
    outs = (
        jax.ShapeDtypeStruct((4, half, block), BF), jax.ShapeDtypeStruct((4, half, block), F32),
        jax.ShapeDtypeStruct((rows, rank_r), F32),
        *[jax.ShapeDtypeStruct((rank_r, cols), F32)] * 3,
    )
    halves = spec((4, half, chunk), lambda i, *_: (0, 0, i))
    return call(
        kernel, (steps,), ins, in_specs, outs, (halves, halves, *[whole(o) for o in outs[2:]]), [pltpu.VMEM((rows, LANES), BF), pltpu.VMEM((rows, 4 * chunk), F32), pltpu.VMEM((4 * chunk, n_col), BF),
         pltpu.VMEM((4 * chunk, LANES), BF)],
        prefetch=1, cost=1932000000
    )


def token_gradient(offs, rank, own, got, grad_low, a, x, gain, grad_hidden):
    half, width = grad_hidden.shape
    block = width // 4

    def kernel(offs_ref, rank_ref, own_ref, got_ref, low_ref, a_ref, x_ref, gain_ref, gh_ref, out_ref):
        blocks, scaled, product = [], [], 0.0
        for k in range(4):
            here = pl.ds(pl.multiple_of(offs_ref[k], LANES), block)
            value = own_ref[k] + got_ref[k].astype(F32)
            value = value + dot_t(low_ref[...], a_ref[k * block : (k + 1) * block, :])
            blocks.append(x_ref[:, here].astype(F32))
            scaled.append(value * gain_ref[:, here])
            product = product + jnp.sum(blocks[k] * scaled[k], axis=1, keepdims=True)
        factor = norm_terms(blocks)
        mean = product / width
        for k in range(4):
            here = pl.ds(pl.multiple_of(offs_ref[k], LANES), block)
            back = factor * scaled[k] - blocks[k] * (factor * factor * factor * mean)
            out_ref[:, here] = (gh_ref[:, k * block : (k + 1) * block] + back).astype(BF)

    mine = lambda v: spec((half, v.shape[1]), lambda i, o, r: (r[0], 0))
    out = jax.ShapeDtypeStruct((half, width), BF)
    return call(
        kernel, (1,), (offs, rank, own, got, grad_low, a, x, gain, grad_hidden),
        [whole(own), whole(got), mine(grad_low), whole(a), mine(x), whole(gain), whole(grad_hidden)],
        out, whole(out), prefetch=2, nbytes=20 * half * width, cost=862500000
    )


def both_halves(rank, own, far):
    half, width = own.shape

    def kernel(rank_ref, own_ref, far_ref, out_ref):
        @pl.when(pl.program_id(0) == rank_ref[0])
        def _():
            out_ref[...] = own_ref[...].astype(F32)

        @pl.when(pl.program_id(0) != rank_ref[0])
        def _():
            out_ref[...] = far_ref[...].astype(F32)

    return call(
        kernel, (2,), (rank, own, far), [whole(own), whole(far)], jax.ShapeDtypeStruct((2 * half, width), F32),
        spec((half, width), lambda i, *_: (i, 0)), prefetch=1, nbytes=16 * half * width, cost=517500000
    )


def down_partial(units, down, down_a):
    rows, unit_cols = units.shape
    block = down[0].shape[0]
    width = 4 * block
    rank_r = down_a.shape[1]

    def kernel(u_ref, w0, w1, w2, w3, a_ref, out_ref, low_ref):
        low_ref[...] = jnp.zeros_like(low_ref)
        low_ref[:, :rank_r] = dot(u_ref[...], a_ref[...])
        for k, w_ref in enumerate((w0, w1, w2, w3)):
            out_ref[:, k * block : (k + 1) * block] = dot_t(u_ref[...], w_ref[...]).astype(BF)
        out_ref[:, width:] = split_lanes(low_ref[...], rank_r).astype(BF)

    rowed = lambda n: spec((BLK, n), lambda i: (i, 0))
    last = spec((block, unit_cols), lambda i: (0, 0))
    return call(
        kernel, (rows // BLK,), (units, *down, down_a), [rowed(unit_cols), last, last, last, last, whole(down_a)],
        jax.ShapeDtypeStruct((rows, width + LANES), BF), rowed(width + LANES), [pltpu.VMEM((BLK, LANES), F32)], cost=1621500000
    )


def block_result(offs, hidden, own, got, down_b):
    rows, width = hidden.shape
    block = width // 4
    rank_r = down_b.shape[0]

    def kernel(offs_ref, h_ref, own_ref, got_ref, b_ref, out_ref):
        low = (whole_low(own_ref[:, width:], rank_r) + whole_low(got_ref[:, width:], rank_r)).astype(BF)
        for k in range(4):
            here = pl.ds(pl.multiple_of(offs_ref[k], LANES), block)
            cols = slice(k * block, (k + 1) * block)
            both = own_ref[:, cols].astype(F32) + got_ref[:, cols].astype(F32)
            out_ref[:, here] = (h_ref[:, cols] + both + dot(low, b_ref[:, cols])).astype(BF)

    rowed = lambda v: spec((BLK, v.shape[1]), lambda i, *_: (i, 0))
    out = jax.ShapeDtypeStruct((rows, width), BF)
    return call(
        kernel, (rows // BLK,), (offs, hidden, own, got, down_b),
        [rowed(hidden), rowed(own), rowed(got), whole(down_b)], out, rowed(out),
        prefetch=1, nbytes=12 * rows * width, cost=862500000
    )


def pack_gradients(inv, rank, xor_own, xor_both, halves, out_a, wide, owners):
    rank_r, width = xor_own[0].shape
    block = width // 4
    part, unit_part = block // 8, wide[0].shape[1] // 16
    n = len(wide) * unit_part + (len(xor_own) + len(xor_both) + len(halves) + 1) * part
    assert owners == 32 and block % LANES == 0

    def kernel(inv_ref, rank_ref, *refs):
        out_ref, refs = refs[-1], list(refs[:-1])
        take = lambda count: [refs.pop(0) for _ in range(count)]
        own_refs, both_refs = take(len(xor_own)), take(len(xor_both))
        half_refs, (ao, af), wide_refs = take(len(halves)), take(2), take(len(wide))
        for f in range(4):
            mine = rank_ref[0] == f // 2
            at = pl.ds(pl.multiple_of(inv_ref[f], LANES), block)
            cols = slice(f % 2 * block, (f % 2 + 1) * block)
            blocks = [jnp.where(mine, r[:, at], 0.0) for r in own_refs] + [r[:, at] for r in both_refs]
            blocks += [jnp.where(mine, r[:, cols], 0.0) for r in half_refs]
            blocks.append(jnp.where(mine, ao[:, cols], af[:, cols]))
            units = 8 * unit_part
            big = [jnp.where(mine, r[:, f % 2 * units : (f % 2 + 1) * units], 0.0) for r in wide_refs]
            for j in range(8):
                row = [b[:, j * unit_part : (j + 1) * unit_part] for b in big]
                row += [b[:, j * part : (j + 1) * part] for b in blocks]
                at_row = slice((8 * f + j) * rank_r, (8 * f + j + 1) * rank_r)
                out_ref[at_row, :] = jnp.concatenate(row, axis=1).astype(BF)

    ins = (inv, rank, *xor_own, *xor_both, *halves, *out_a, *wide)
    out = jax.ShapeDtypeStruct((owners * rank_r, n), BF)
    return call(kernel, (1,), ins, [whole(v) for v in ins[2:]], out, whole(out), prefetch=2, cost=552000000
    )


def spread_gradients(every, landed, n_adapters, rank_r, unit_part, part):
    senders = landed.shape[0] // (4 * rank_r)
    at = [0, unit_part, 2 * unit_part] + [3 * unit_part + i * part for i in range(9)]

    def kernel(every_ref, x_ref, aq, bq, ao, bo, ag, bg, ad, bd):
        sums = []
        for f in range(4):
            total = 0.0
            for i in range(senders):
                row = (f * senders + i) * rank_r
                total = total + x_ref[row : row + rank_r, :].astype(F32)
            sums.append(total)
        for a in range(n_adapters):
            total = 0.0
            for f in range(4):
                total = total + jnp.where(every_ref[f] == a, sums[f], 0.0)
            cut = lambda i: total[:, at[i] : at[i + 1]]
            for out, i in ((aq, 3), (ao, 10), (ag, 6), (ad, 2)):
                out[a] = cut(i)
            bo[a], bd[a] = cut(5), cut(4)
            for j in range(3):
                bq[a, j] = cut(7 + j)
            for j in range(2):
                bg[a, :, j, :] = cut(j)

    shape = lambda *dims: jax.ShapeDtypeStruct((n_adapters, *dims), F32)
    row = shape(rank_r, part)
    outs = (row, shape(3, rank_r, part), row, row, row, shape(rank_r, 2, unit_part), shape(rank_r, unit_part), row)
    return call(kernel, (1,), (every, landed), [whole(landed)], outs, tuple(whole(o) for o in outs), prefetch=1, cost=500250000
    )


def body(
    tokens, segments, adapter_index, w_qkv, w_forget, forget_bias, w_out, w_gate_up, w_down,
    gain_attn, gain_ffn, a_qkv, b_qkv, a_out, b_out, a_gate_up, b_gate_up, a_down, b_down, cotangent,
):
    count, rows, width = tokens.shape
    assert count == 1
    head_cols = w_qkv.shape[2]
    n_heads = w_forget.shape[1]
    unit_cols = w_gate_up.shape[2]
    rank_r = a_qkv.shape[2]
    n_f, n_c, n_t = (lax.axis_size("fsdp"), lax.axis_size("ctx"), lax.axis_size("tp"))
    f_rank, t_rank = (lax.axis_index("fsdp"), lax.axis_index("tp"))
    hops = -(-(DOC_MOST - 1) // rows)
    assert hops == 2 and n_c > 2 and n_t == 2 and n_f % 4 == 0
    tail = -(-(DOC_MOST - 1 - rows) // 32) * 32
    before = hops * rows
    half = rows // 2
    block = width // 4
    first = t_rank == 0
    rank = t_rank.astype(jnp.int32)[None]

    def other(values):
        return lax.ppermute(values, "tp", [(0, 1), (1, 0)])

    def four(pieces):
        return [*pieces, *[lax.ppermute(part, "fsdp", [(i, i ^ 1) for i in range(n_f)]) for part in pieces]]

    mix = lambda values, dim: to_xor(values, dim, n_f, f_rank)
    direct = n_f == 4 and block % LANES == 0
    if direct:
        offs = jnp.stack([(f_rank ^ step) * block for step in xor_order(4)]).astype(jnp.int32)
        lay = lambda values, dim: values
    else:
        offs = jnp.arange(4, dtype=jnp.int32) * block
        lay = mix

    pick = adapter_index[0]
    tok = lay(tokens[0], 1)
    seg_one = segments[0] + 1
    note = jnp.zeros((32, width), BF).at[0, :rows].set(seg_one.astype(BF))
    qkv_own = jnp.concatenate([w_qkv[:, i] for i in range(3)], axis=1)
    qkv_far = far_blocks(qkv_own, 0)
    prev_one = shift(jnp.concatenate([tok, after(note, qkv_own)], axis=0), 1, n_c)
    side = jnp.broadcast_to(pick.astype(BF), (w_forget.shape[0], 1))
    side_far = far_blocks(after(jnp.concatenate([w_forget, side], axis=1), qkv_own), 0)
    take = lambda table: lax.dynamic_index_in_dim(table, pick, 0, keepdims=False)
    mine = lambda values, n, dim: lax.dynamic_slice_in_dim(values, t_rank * n, n, dim)
    theirs = lambda values, n, dim: lax.dynamic_slice_in_dim(values, (1 - t_rank) * n, n, dim)
    qkv_a, ffn_a = (mix(take(a_qkv), 0), mix(take(a_gate_up), 0))
    out_b, down_b = (mix(take(b_out), 1), mix(take(b_down), 1))
    qkv_b = mine(take(b_qkv), head_cols, 2).reshape(rank_r, 3 * head_cols)
    out_a = take(a_out)
    out_a_own, out_a_far = (mine(out_a, head_cols, 0), theirs(out_a, head_cols, 0))
    ffn_b = mine(take(b_gate_up), unit_cols, 2).reshape(rank_r, 2 * unit_cols)
    down_a = mine(take(a_down), unit_cols, 0)
    gain_one = lay(gain_attn.astype(F32), 0)[None]
    gain_two = mix(gain_ffn.astype(F32), 0)[None]
    bias = jnp.pad(forget_bias.astype(F32), (0, LANES - n_heads))[None]
    cot = mix(cotangent[0], 1)
    grad_low_down = dot_t(cot, down_b).astype(BF)

    out_pair = jnp.concatenate([w_out, other(w_out)], axis=0)
    gate_up_own = jnp.concatenate([w_gate_up[:, 0], w_gate_up[:, 1]], axis=1)
    down_own = w_down.T
    shared = n_f == 4 and n_c % 2 == 0
    odd = lax.axis_index("ctx") % 2
    down_sent = down_own
    if shared:
        down_sent = lax.dynamic_slice_in_dim(down_own, odd * (unit_cols // 2), unit_cols // 2, 1)
    (
        prev_one, qkv_far, side_far, out_pair, qkv_a, qkv_b, gain_one, bias, ffn_a, out_b, down_b, out_a_own, out_a_far,
        ffn_b, down_a, gain_two, cot, grad_low_down, gate_up_own, down_own, down_sent,
    ) = lax.optimization_barrier((
        prev_one, qkv_far, side_far, out_pair, qkv_a, qkv_b, gain_one, bias, ffn_a, out_b, down_b, out_a_own, out_a_far,
        ffn_b, down_a, gain_two, cot, grad_low_down, gate_up_own, down_own, down_sent,
    ))
    out_far = far_blocks(out_pair, 1)
    prev_two = shift(prev_one[rows - tail :], 1, n_c)
    qkv_four = four(qkv_far)
    side_all = jnp.concatenate(near_blocks(*side_far, 0), axis=0)
    every = from_xor(side_all[:: w_forget.shape[0], n_heads], 0, n_f, f_rank).astype(jnp.int32)
    side_w = jnp.concatenate([side_all, jnp.zeros((width, LANES - n_heads - 1 - rank_r), BF), qkv_a], axis=1)
    args = (gain_one, qkv_four, side_w, qkv_b, bias, head_cols, rank_r)
    down_far = far_blocks(down_sent, 0)
    tok_in, prev_two = lax.optimization_barrier((tok, prev_two))
    normed, low_qkv, query, *filled = project(offs, tok_in, None, tail, *args, None, before)
    seg_two = prev_two[tail, :rows].astype(jnp.int32)
    seg_far = []
    for b in range(-(-tail // BLK)):
        start, end = min(b * BLK, tail + 32 - BLK), min((b + 1) * BLK, tail)
        known = seg_two[rows - tail + b * BLK : rows - tail + end]
        seg_far.append(jnp.pad(known, (b * BLK - start, BLK - (end - start))))
    seg_keys = jnp.concatenate(seg_far + [prev_one[rows, :rows].astype(jnp.int32), seg_one])
    last_keys = jnp.max(seg_keys.reshape(-1, BLK), axis=1)
    lows = jnp.sum(last_keys[None, :] < seg_one[::BLK][:, None], axis=1).astype(jnp.int32)

    gate_up_far = far_blocks(after(gate_up_own, out_far[1], down_far[1], query), 0)
    keys, vals, logits = project(offs, prev_one, prev_two, tail, *args, filled)
    out_w = near_blocks(out_far[0], after(out_far[1], query), 1)
    logits, out_w = lax.optimization_barrier((logits, out_w))
    seg_col, seg_row = (seg_keys[:, None], seg_one[None, :])
    gq, gk, gk_next, gates, total = gate_tables(logits, seg_col, seg_row, n_heads, rows)
    mixed_own, mixed_f, gq_one, gq_two = attention_forward(lows, query, keys, vals, gq, gk, gates, total, n_heads)
    mixed_far = other(mixed_own)
    sent_q1 = jnp.concatenate([query, gq_one], axis=1)
    sent_q2 = jnp.concatenate([query[:tail], gq_two[:tail]], axis=1)
    if shared:
        down_pair = lax.ppermute(after(down_far[1], keys), "ctx", [(i, i ^ 1) for i in range(n_c)])
        down_pair = after(down_pair, mixed_own)
        lower, upper = jnp.where(odd == 0, down_far[1], down_pair), jnp.where(odd == 0, down_pair, down_far[1])
        down_got = jnp.concatenate([lower, upper], axis=1)
    else:
        down_got = down_far[1]
    mixed_far, sent_q1, sent_q2, down_got = lax.optimization_barrier((mixed_far, sent_q1, sent_q2, down_got))
    next_q1 = shift(sent_q1, -1, n_c)
    next_q2 = shift(sent_q2, -2, n_c)

    down_w = four((after(down_own, mixed_own), down_got)) if shared else four(down_far)
    hidden, normed_ffn, low_ffn, low_out = out_projection(
        offs, rank, tok, mixed_own, mixed_far, out_w, out_a_own, out_a_far, out_b, gain_two, ffn_a
    )
    gate_up_w = four((after(gate_up_own, mixed_own), after(gate_up_far[1], hidden))) if shared else four(gate_up_far)
    units, grad_gate, grad_up, far, own, own_low = feed_forward(
        rank, normed_ffn, low_ffn, cot, grad_low_down, gate_up_w, down_w, ffn_b, down_a
    )
    got = other(far)
    down_part = down_partial(after(units, far), down_w, down_a)
    gate_g, up_g, units_g = after((grad_gate, grad_up, units), far)
    tables_ffn = [t_dot(low_ffn, gate_g), t_dot(low_ffn, up_g), t_dot(grad_low_down, units_g)]
    got, down_part, tables_ffn = lax.optimization_barrier((got, down_part, tables_ffn))
    grad_hidden, grad_hidden_b, grad_low_ffn, grad_low_out, gm_own, gm_send = middle(
        rank, own, got, own_low, hidden, cot, gain_two, ffn_a, out_b, out_w, out_a_own, out_a_far
    )
    grad_mixed, sent_d2 = mixed_gradient(rank, gm_own, other(gm_send), mixed_f, n_heads, tail)

    next_d1 = shift(grad_mixed, -1, n_c)
    next_d2 = shift(sent_d2, -2, n_c)
    grad_q, row_lanes, across = attention_dq(
        lows, query, keys, vals, grad_mixed, gq_one, gk, n_heads, (before - rows) // BLK
    )
    across = shift(across, -1, n_c)
    docs_at = head_cols + 3 * n_heads
    grad_k_own, grad_v_own, own_lanes = attention_dkv_own(keys, vals, query, after(grad_mixed, grad_q), gq_one, gk, n_heads)
    next_q1, next_q2, next_d1, next_d2, _ = lax.optimization_barrier((next_q1, next_q2, next_d1, next_d2, grad_k_own))
    next_docs = jnp.concatenate([next_q1[::BLK, docs_at : docs_at + DOCS], next_q2[::BLK, docs_at : docs_at + DOCS]])
    next_docs = next_docs.astype(F32)
    ids = jnp.arange(1, DOCS + 1).astype(F32)
    next_first = jnp.where(jnp.sum(next_docs, 1) > 0, jnp.sum(next_docs * ids[None, :], 1), 99.0)
    last_rows = seg_one[BLK - 1 :: BLK].astype(F32)
    highs = jnp.sum(next_first[None, :] <= last_rows[:, None], axis=1).astype(jnp.int32)
    lane = lax.broadcasted_iota(jnp.int32, (1, width), 1)
    own_part = lambda values: values * (lane // (width // 2) == t_rank)
    natural = lambda values: from_xor(values, 1, n_f, f_rank)
    by_tp = lambda a, b: jnp.concatenate([jnp.where(first, a, b), jnp.where(first, b, a)], axis=1)
    place = lambda values: by_tp(values, jnp.zeros_like(values))
    rows_of = lambda values: lax.dynamic_slice_in_dim(values, t_rank * half, half, 0)
    onehot = (jnp.arange(a_qkv.shape[0])[:, None] == every[None, :]).astype(F32)
    onehot = jnp.repeat(onehot, n_c * n_t, axis=1)

    owners = n_f * n_c * n_t

    def pack(tables):
        packed = jnp.concatenate([t.reshape(rank_r, owners, -1) for t in tables], axis=2).transpose(1, 0, 2)
        return packed.astype(BF).reshape(owners, -1), [t.shape[1] // owners for t in tables]

    def take_apart(spread, sizes):
        spread = spread.reshape(-1, rank_r, sum(sizes))
        outs, at = [], 0
        for size in sizes:
            outs.append(spread[:, :, at : at + size])
            at += size
        return outs

    table_out_a = [t_dot(grad_low_out, rows_of(mixed_own)), t_dot(grad_low_out, rows_of(mixed_far))]
    table_out_b = t_dot(rows_of(low_out), grad_hidden_b)
    table_ffn_a = t_dot(grad_low_ffn, rows_of(normed_ffn))
    highs, table_out_a, table_out_b, table_ffn_a = lax.optimization_barrier(
        (highs, table_out_a, table_out_b, table_ffn_a)
    )
    grad_k, grad_v, next_lanes = attention_dkv_next(
        highs, keys, vals, next_q1, next_q2, next_d1, next_d2, gk_next, grad_k_own, grad_v_own, n_heads
    )
    down_other = other(after(down_part, grad_mixed))

    grads = (grad_q, grad_k, grad_v)
    far_in, own_in, part_low_qkv, *tables_b = input_gradient(
        rank, grads, logits, seg_col, seg_row, row_lanes, own_lanes, next_lanes, across, qkv_four, side_w, qkv_b, low_qkv, n_heads
    )
    grad_low_qkv = (part_low_qkv + other(part_low_qkv)).astype(BF)
    got_in = other(far_in)
    parts = [values[:, width : width + 3 * rank_r].astype(F32).reshape(rows, 3, rank_r) for values in (down_part, down_other)]
    parts = [values[:, 0] + values[:, 1] + values[:, 2] for values in parts]
    low_down = after((parts[0] + parts[1]).astype(BF), far_in)
    grad_tok = token_gradient(offs, rank, own_in, got_in, grad_low_qkv, qkv_a, tok, gain_one, grad_hidden)
    tok_far = other(grad_tok)
    block_output = block_result(offs, hidden, down_part, after(down_other, grad_tok), down_b)
    grad_tokens = both_halves(rank, grad_tok, tok_far)
    if not direct:
        block_output = from_xor(block_output, 1, n_f, f_rank)
        grad_tokens = from_xor(grad_tokens, 1, n_f, f_rank)

    table_qkv_a, table_down_b = t_dot(grad_low_qkv, normed), t_dot(low_down, cot)
    if direct:
        bits = n_f.bit_length() - 1
        inv = [sum((((f_rank ^ i) >> j) & 1) << (bits - 1 - j) for j in range(bits)) * block for i in range(n_f)]
        packed = pack_gradients(
            jnp.stack(inv).astype(jnp.int32), rank, [table_qkv_a, table_down_b], [table_out_b, table_ffn_a], tables_b,
            table_out_a, tables_ffn, owners,
        )
        landed = lax.all_to_all(packed, ("fsdp", "ctx", "tp"), 0, 0, tiled=True)
        part, unit_part = width // owners, unit_cols * n_t // owners
        done = spread_gradients(every, landed, a_qkv.shape[0], rank_r, unit_part, part)
        done = [v.transpose(0, 2, 1) if i in (0, 2, 4, 6) else v for i, v in enumerate(done)]
        done[1] = done[1].transpose(0, 2, 1, 3)
        return (block_output[None], grad_tokens[None], *done)
    early, early_sizes = pack([
        by_tp(*table_out_a), natural(table_out_b), natural(table_ffn_a), *[place(t) for t in tables_ffn],
    ])
    late, late_sizes = pack([
        own_part(natural(table_qkv_a)), *[place(t) for t in tables_b], own_part(natural(table_down_b)),
    ])
    landed = lax.all_to_all(jnp.concatenate([late, early], axis=1), ("fsdp", "ctx", "tp"), 0, 0, tiled=True)
    split = rank_r * sum(late_sizes)
    spread = jnp.dot(onehot.astype(BF), landed, preferred_element_type=F32)
    done = take_apart(spread[:, :split], late_sizes) + take_apart(spread[:, split:], early_sizes)
    swap = lambda values: values.transpose(0, 2, 1)
    return (
        block_output[None],
        grad_tokens[None],
        swap(done[0]),
        jnp.stack(done[1:4], axis=2),
        swap(done[5]),
        done[6],
        swap(done[7]),
        jnp.stack(done[8:10], axis=2),
        swap(done[10]),
        done[4],
    )


def solution(mesh):
    in_specs = (
        P("fsdp", "ctx", None), P("fsdp", "ctx"), P("fsdp"), P("fsdp", None, "tp"), P("fsdp", "tp"), P("tp"),
        P("tp", "fsdp"), P("fsdp", None, "tp"), P("tp", "fsdp"),
        P(), P(), P(), P(), P(), P(), P(), P(), P(), P(),
        P("fsdp", "ctx", None),
    )
    out_specs = (
        P("fsdp", "ctx", None),
        P("fsdp", "ctx", None),
        P(None, ("fsdp", "ctx", "tp"), None),
        P(None, None, None, ("fsdp", "ctx", "tp")),
        P(None, ("fsdp", "ctx", "tp"), None),
        P(None, None, ("fsdp", "ctx", "tp")),
        P(None, ("fsdp", "ctx", "tp"), None),
        P(None, None, None, ("fsdp", "ctx", "tp")),
        P(None, ("fsdp", "ctx", "tp"), None),
        P(None, None, ("fsdp", "ctx", "tp")),
    )
    return jax.shard_map(body, mesh=mesh, in_specs=in_specs, out_specs=out_specs, check_vma=False)
```

```python
import jax
import jax.numpy as jnp
from jax import lax
from jax.experimental import pallas as pl
from jax.experimental.pallas import tpu as pltpu
from jax.sharding import PartitionSpec as P

HD = 64
DOC_MOST = 800
DOCS = 8
BF = jnp.bfloat16
F32 = jnp.float32
HI = lax.Precision.HIGHEST


def dot(a, b):
    return jnp.dot(a, b, preferred_element_type=F32)


def dot_t(a, b):
    return lax.dot_general(a, b, (((1,), (1,)), ((), ())), preferred_element_type=F32)


def t_dot(a, b):
    return lax.dot_general(a, b, (((0,), (0,)), ((), ())), preferred_element_type=F32)


def xor_order(size):
    order, bit = [0], size // 2
    while bit:
        order, bit = order + [step ^ bit for step in order], bit // 2
    return order


def after(values, *done):
    return lax.optimization_barrier((values, *done))[0]


def far_blocks(shard, dim):
    size = lax.axis_size("fsdp")
    own, bit = shard, size // 2
    while True:
        got = lax.ppermute(own, "fsdp", [(i, i ^ bit) for i in range(size)])
        if bit == 2:
            return own, got
        own, bit = jnp.concatenate([own, got], axis=dim), bit // 2


def near_blocks(own, got, dim):
    both = jnp.concatenate([own, got], axis=dim)
    size = lax.axis_size("fsdp")
    return [both, lax.ppermute(both, "fsdp", [(i, i ^ 1) for i in range(size)])]


def to_xor(values, dim, size, rank):
    block = values.shape[dim] // size
    return jnp.concatenate(
        [lax.dynamic_slice_in_dim(values, (rank ^ step) * block, block, dim) for step in xor_order(size)],
        axis=dim,
    )


def from_xor(values, dim, size, rank):
    block = values.shape[dim] // size
    bits = size.bit_length() - 1
    pieces = []
    for natural in range(size):
        mixed = rank ^ natural
        place = sum(((mixed >> j) & 1) << (bits - 1 - j) for j in range(bits))
        pieces.append(lax.dynamic_slice_in_dim(values, place * block, block, dim))
    return jnp.concatenate(pieces, axis=dim)


def shift(values, hop, size):
    pairs = [(i, i + hop) for i in range(size) if 0 <= i + hop < size]
    return lax.ppermute(values, "ctx", pairs)


LANES = 128
BLK = 256
BIG = -1e30


def spec(shape, index):
    return pl.BlockSpec(shape, index)


def call(kernel, grid, ins, in_specs, outs, out_specs, scratch=(), prefetch=0, flops=0, nbytes=0, exps=0, aliases=None, cost=1):
    return pl.pallas_call(
        kernel,
        out_shape=outs,
        grid_spec=pltpu.PrefetchScalarGridSpec(
            num_scalar_prefetch=prefetch, grid=grid, in_specs=in_specs, out_specs=out_specs, scratch_shapes=list(scratch)
        ),
        compiler_params=pltpu.CompilerParams(
            dimension_semantics=("arbitrary",) * len(grid), vmem_limit_bytes=56 * 2**20
        ),
        input_output_aliases=aliases or {},
        cost_estimate=pl.CostEstimate(flops=cost, bytes_accessed=1, transcendentals=0),
    )(*ins)


def whole(values):
    return spec(values.shape, lambda *_: (0,) * len(values.shape))


def lane_ids(rows):
    return lax.broadcasted_iota(jnp.int32, (rows, LANES), 1)


def split3(values):
    high = values.astype(BF)
    rest = values - high.astype(F32)
    mid = rest.astype(BF)
    return high, mid, (rest - mid.astype(F32)).astype(BF)


def split_lanes(values, n):
    lane = lane_ids(values.shape[0])
    values = jnp.where(lane < n, values, 0.0)
    high, mid, low = (part.astype(F32) for part in split3(values))
    return high + pltpu.roll(mid, n, 1) + pltpu.roll(low, 2 * n, 1)


def exact_dot(mask, values):
    high, mid, low = split3(values)
    return dot(mask, high) + dot(mask, mid) + dot(mask, low)


def norm_terms(blocks):
    width = sum(b.shape[1] for b in blocks)
    total = sum(jnp.sum(b * b, axis=1, keepdims=True) for b in blocks)
    return lax.rsqrt(total / width + 1e-05)


def pair_lanes(pair, n_heads, kind):
    lane = lax.broadcasted_iota(jnp.int32, (LANES, LANES), 1)
    to = lane & (HD - 1)
    head = jnp.where(lane >= HD, 2 * pair, 2 * pair + 1)
    gate_at = 3 if kind == "k" else 0
    part = to - gate_at
    source = jnp.where((part >= 0) & (part < 3), part * n_heads + head, -1)
    if kind != "d":
        ones = to - (3 - gate_at)
        source = jnp.where((ones >= 0) & (ones < 3), 3 * n_heads + DOCS, source)
        source = jnp.where((to >= 8) & (to < 8 + DOCS), to - 8 + 3 * n_heads, source)
    return (lax.broadcasted_iota(jnp.int32, (LANES, LANES), 0) == source).astype(BF)


def pair_of(values, gate_parts, select):
    extra = dot(gate_parts, select).astype(BF)
    low = lane_ids(values.shape[0]) < HD
    return jnp.where(low, values, extra), jnp.where(low, extra, values)


def pair_ones(values):
    low = lane_ids(values.shape[0]) < HD
    one = jnp.ones((), BF)
    return jnp.where(low, values, one), jnp.where(low, one, values)


def block_at(index):
    return pl.ds(pl.multiple_of(index * BLK, BLK), BLK)


def causal_from(rows, first):
    row = lax.broadcasted_iota(jnp.int32, (rows, BLK), 0)
    return row + first >= lax.broadcasted_iota(jnp.int32, (rows, BLK), 1)


def lane_column(acc, lane_at):
    return jnp.sum(jnp.where(lane_ids(acc.shape[0]) == lane_at, acc, 0.0), axis=1, keepdims=True)


def attention_forward(bounds, q, k, v, gq, gk, gates, total, n_heads):
    rows, keys = q.shape[0], k.shape[0]
    n_before = (keys - rows) // BLK
    pairs = n_heads // 2
    assert rows == 2 * BLK

    def kernel(
        lo_ref, q_ref, k_ref, v_ref, gq_ref, gk_ref, gate_ref, tot_ref, mixed_ref, float_ref, one_ref, two_ref,
        qx, scores, tops, parts, accs, log_ref,
    ):
        pair = pl.program_id(0)
        pick_k = pair_lanes(pair, n_heads, "k")
        for side, value in enumerate(pair_of(q_ref[...], gq_ref[...], pair_lanes(pair, n_heads, "q"))):
            qx[side] = value
        both, late, early = slice(0, rows), slice(BLK, rows), slice(0, BLK)

        def score(kb, here, at, mask=None, first=False):
            for side, key in enumerate(pair_of(k_ref[here, :], gk_ref[here, :], pick_k)):
                s = dot_t(qx[side, at, :], key)
                if mask is not None:
                    s = jnp.where(mask, s, BIG)
                scores[side, at, here] = s
                top = jnp.maximum(s[:, :LANES], s[:, LANES:])
                tops[side, at, :] = top if first else jnp.maximum(tops[side, at, :], top)

        def gather(here, at, first=False):
            for side in range(2):
                w = jnp.exp(scores[side, at, here] - tops[side, at, :1])
                part = w[:, :LANES] + w[:, LANES:]
                acc = dot(w.astype(BF), v_ref[here, :])
                parts[side, at, :] = part if first else parts[side, at, :] + part
                accs[side, at, :] = acc if first else accs[side, at, :] + acc

        own = [slice(b * BLK, (b + 1) * BLK) for b in (n_before, n_before + 1)]
        low, high = lo_ref[0], jnp.minimum(lo_ref[1], n_before)
        score(n_before, own[0], both, causal_from(rows, 0), True)
        score(n_before + 1, own[1], late, causal_from(BLK, 0))
        pl.loop(high, n_before)(lambda kb: score(kb, block_at(kb), both))
        pl.loop(low, high)(lambda kb: score(kb, block_at(kb), early))
        for side in range(2):
            tops[side] = jnp.broadcast_to(jnp.max(tops[side], axis=1, keepdims=True), (rows, LANES))
        gather(own[0], both, True)
        gather(own[1], late)
        pl.loop(high, n_before)(lambda kb: gather(block_at(kb), both))
        pl.loop(low, high)(lambda kb: gather(block_at(kb), early))
        lane = lane_ids(rows)
        results, logs = [], jnp.zeros((rows, LANES), F32)
        for side in range(2):
            row_total = jnp.sum(parts[side], axis=1, keepdims=True)
            results.append(accs[side] / row_total)
            logs = jnp.where(lane == 2 * pair + side, tops[side] + jnp.log(row_total), logs)
        out = jnp.where(lane < HD, results[0], results[1])
        mixed_ref[...] = out.astype(BF)
        float_ref[...] = out

        @pl.when(pair == 0)
        def _():
            log_ref[...] = logs

        @pl.when(pair > 0)
        def _():
            log_ref[...] = jnp.where((lane >> 1) == pair, logs, log_ref[...])

        @pl.when(pair == pairs - 1)
        def _():
            values = gate_ref[...] - log_ref[...]
            rest = gq_ref[...].astype(F32)
            one_ref[...] = jnp.where(lane < 3 * n_heads, split_lanes(values, n_heads), rest).astype(BF)
            values = values + tot_ref[:1, :]
            two_ref[...] = jnp.where(lane < 3 * n_heads, split_lanes(values, n_heads), rest).astype(BF)

    here = lambda n: spec((n, LANES), lambda i, *_: (0, i))
    shared = lambda n: spec((n, LANES), lambda i, *_: (0, 0))
    return call(
        kernel,
        (pairs,),
        (bounds, q, k, v, gq, gk, gates, total),
        [here(rows), here(keys), here(keys), shared(rows), shared(keys), shared(rows), shared(8)],
        (
            jax.ShapeDtypeStruct(q.shape, BF), jax.ShapeDtypeStruct(q.shape, F32),
            jax.ShapeDtypeStruct((rows, LANES), BF), jax.ShapeDtypeStruct((rows, LANES), BF),
        ),
        (here(rows), here(rows), shared(rows), shared(rows)),
        [pltpu.VMEM((2, rows, LANES), BF), pltpu.VMEM((2, rows, keys), F32)]
        + [pltpu.VMEM((2, rows, LANES), F32)] * 3 + [pltpu.VMEM((rows, LANES), F32)],
        prefetch=1,
    )


def attention_dq(bounds, q, k, v, d, gq, gk, n_heads, n_far):
    rows, keys = q.shape[0], k.shape[0]
    n_before = (keys - rows) // BLK
    pairs = n_heads // 2

    def kernel(lo_ref, q_ref, k_ref, v_ref, d_ref, gq_ref, gk_ref, gd_ref, dq_ref, row_ref, far_ref, qx, dx, accs):
        pair = pl.program_id(0)
        lane = lane_ids(rows)
        pick_k = pair_lanes(pair, n_heads, "k")
        for side, value in enumerate(pair_of(q_ref[...], gq_ref[...], pair_lanes(pair, n_heads, "q"))):
            qx[side] = value
        for side, value in enumerate(pair_of(d_ref[...], gd_ref[...], pair_lanes(pair, n_heads, "d"))):
            dx[side] = value
        both, late, early = slice(0, rows), slice(BLK, rows), slice(0, BLK)

        @pl.when(pair == 0)
        def _():
            far_ref[...] = jnp.zeros_like(far_ref)
            row_ref[...] = jnp.zeros_like(row_ref)

        def block(here, at, mask=None, first=False):
            values = pair_ones(v_ref[here, :])
            for side, key in enumerate(pair_of(k_ref[here, :], gk_ref[here, :], pick_k)):
                s = dot_t(qx[side, at, :], key)
                if mask is not None:
                    s = jnp.where(mask, s, BIG)
                ds = (jnp.exp(s) * dot_t(dx[side, at, :], values[side])).astype(BF)
                acc = dot(ds, key)
                accs[side, at, :] = acc if first else accs[side, at, :] + acc

        low, high = lo_ref[0], jnp.minimum(lo_ref[1], n_before)

        @pl.when(low < n_far)
        def _():
            accs[...] = jnp.zeros_like(accs)
            pl.loop(high, n_far)(lambda kb: block(block_at(kb), both))
            pl.loop(low, jnp.minimum(high, n_far))(lambda kb: block(block_at(kb), early))
            for side in range(2):
                moved = jnp.sum(jnp.where(lane == HD * (1 - side), accs[side], 0.0))
                far_ref[...] += jnp.where(lane[:8] == 2 * pair + side, moved, 0.0)
            block(slice(n_before * BLK, (n_before + 1) * BLK), both, causal_from(rows, 0))

        @pl.when(low >= n_far)
        def _():
            block(slice(n_before * BLK, (n_before + 1) * BLK), both, causal_from(rows, 0), True)

        block(slice((n_before + 1) * BLK, (n_before + 2) * BLK), late, causal_from(BLK, 0))
        pl.loop(jnp.maximum(high, n_far), n_before)(lambda kb: block(block_at(kb), both))
        pl.loop(jnp.maximum(low, n_far), high)(lambda kb: block(block_at(kb), early))
        dq_ref[...] = (jnp.where(lane < HD, accs[0], accs[1]) * HD ** (-0.5)).astype(BF)
        for side in range(2):
            total = lane_column(accs[side], HD * (1 - side))
            row_ref[...] = jnp.where(lane == 2 * pair + side, total, row_ref[...])

    here = lambda n: spec((n, LANES), lambda i, *_: (0, i))
    shared = lambda n: spec((n, LANES), lambda i, *_: (0, 0))
    return call(
        kernel,
        (pairs,),
        (bounds, q, k, v, d, gq, gk, d),
        [here(rows), here(keys), here(keys), here(rows), shared(rows), shared(keys), spec((rows, LANES), lambda i, *_: (0, pairs))],
        (
            jax.ShapeDtypeStruct(q.shape, BF), jax.ShapeDtypeStruct((rows, LANES), F32),
            jax.ShapeDtypeStruct((8, LANES), F32),
        ),
        (here(rows), shared(rows), shared(8)),
        [pltpu.VMEM((2, rows, LANES), BF)] * 2 + [pltpu.VMEM((2, rows, LANES), F32)],
        prefetch=1, cost=3363750000
    )


def score_block(kx, vx, queries, grads, at, dks, dvs, mask=None, first=False):
    for side in range(2):
        s = dot_t(kx[side, at, :], queries[side])
        if mask is not None:
            s = jnp.where(mask, s, BIG)
        w = jnp.exp(s)
        ds = (w * dot_t(vx[side, at, :], grads[side])).astype(BF)
        dk, dv = dot(ds, queries[side]), dot(w.astype(BF), grads[side])
        dks[side, at, :] = dk if first else dks[side, at, :] + dk
        dvs[side, at, :] = dv if first else dvs[side, at, :] + dv


def attention_dkv_own(k, v, q, d, gq, gk, n_heads):
    rows = q.shape[0]
    place = k.shape[0] // rows - 1
    pairs = n_heads // 2

    def kernel(k_ref, v_ref, q_ref, d_ref, gq_ref, gd_ref, gk_ref, dk_ref, dv_ref, own_ref, kx, vx, dks, dvs):
        pair = pl.program_id(0)
        lane = lane_ids(rows)
        pick_q, pick_d = (pair_lanes(pair, n_heads, "q"), pair_lanes(pair, n_heads, "d"))
        for side, value in enumerate(pair_of(k_ref[...], gk_ref[...], pair_lanes(pair, n_heads, "k"))):
            kx[side] = value
        for side, value in enumerate(pair_ones(v_ref[...])):
            vx[side] = value
        both, late, early = slice(0, rows), slice(BLK, rows), slice(0, BLK)

        @pl.when(pair == 0)
        def _():
            own_ref[...] = jnp.zeros_like(own_ref)

        def load(here):
            return pair_of(q_ref[here, :], gq_ref[here, :], pick_q), pair_of(d_ref[here, :], gd_ref[here, :], pick_d)

        keep = lax.broadcasted_iota(jnp.int32, (rows, BLK), 0) - BLK <= lax.broadcasted_iota(jnp.int32, (rows, BLK), 1)
        first_keep = lax.broadcasted_iota(jnp.int32, (BLK, BLK), 0) <= lax.broadcasted_iota(jnp.int32, (BLK, BLK), 1)
        score_block(kx, vx, *load(late), both, dks, dvs, keep, True)
        score_block(kx, vx, *load(early), early, dks, dvs, first_keep)
        for side in range(2):
            column = lane_column(dks[side], HD * (1 - side) + 3)
            own_ref[...] = jnp.where(lane == 2 * pair + side, column, own_ref[...])
        dk_ref[...] = jnp.where(lane < HD, dks[0], dks[1])
        dv_ref[...] = jnp.where(lane < HD, dvs[0], dvs[1])

    heads_spec = lambda n: spec((n, LANES), lambda i, *_: (0, i))
    shared = lambda n: spec((n, LANES), lambda i, *_: (0, 0))
    keys_spec = spec((rows, LANES), lambda i, *_: (place, i))
    return call(
        kernel, (pairs,), (k, v, q, d, gq, d, gk),
        [
            keys_spec, keys_spec, heads_spec(rows), heads_spec(rows), shared(rows),
            spec((rows, LANES), lambda i, *_: (0, pairs)), spec((rows, LANES), lambda i, *_: (place, 0)),
        ],
        (jax.ShapeDtypeStruct(q.shape, F32), jax.ShapeDtypeStruct(q.shape, F32), jax.ShapeDtypeStruct((rows, LANES), F32)),
        (heads_spec(rows), heads_spec(rows), shared(rows)),
        [pltpu.VMEM((2, rows, LANES), BF)] * 2 + [pltpu.VMEM((2, rows, LANES), F32)] * 2, cost=2294250000
    )


def attention_dkv_next(bounds, k, v, q_one, q_two, d_one, d_two, gkn, dk, dv, n_heads):
    rows, tail = q_one.shape[0], q_two.shape[0]
    place = k.shape[0] // rows - 1
    pairs = n_heads // 2
    assert 0 < tail - BLK <= BLK

    def kernel(
        hi_ref, k_ref, v_ref, q1_ref, d1_ref, gq1_ref, gd1_ref, q2_ref, d2_ref, gq2_ref, gd2_ref, gkn_ref,
        dk_own, dv_own, dk_ref, dv_ref, next_ref, kx, vx, dks, dvs,
    ):
        pair = pl.program_id(0)
        lane = lane_ids(rows)
        both, late, early = slice(0, rows), slice(BLK, rows), slice(0, BLK)
        few, many = hi_ref[0], hi_ref[1]

        @pl.when(pair == 0)
        def _():
            next_ref[...] = jnp.zeros_like(next_ref)

        @pl.when(many > 0)
        def _():
            pick_q, pick_d = (pair_lanes(pair, n_heads, "q"), pair_lanes(pair, n_heads, "d"))
            for side, value in enumerate(pair_of(k_ref[...], gkn_ref[...], pair_lanes(pair, n_heads, "k"))):
                kx[side] = value
            for side, value in enumerate(pair_ones(v_ref[...])):
                vx[side] = value
            dks[...] = jnp.zeros_like(dks)
            dvs[...] = jnp.zeros_like(dvs)

            def block(refs, here, at):
                q_ref, gq_ref, d_ref, gd_ref = refs
                queries = pair_of(q_ref[here, :], gq_ref[here, :], pick_q)
                score_block(kx, vx, queries, pair_of(d_ref[here, :], gd_ref[here, :], pick_d), at, dks, dvs)

            one, two = (q1_ref, gq1_ref, d1_ref, gd1_ref), (q2_ref, gq2_ref, d2_ref, gd2_ref)
            pl.loop(0, jnp.minimum(few, 2))(lambda j: block(one, block_at(j), both))
            pl.loop(few, jnp.minimum(many, 2))(lambda j: block(one, block_at(j), late))
            pl.when(few > 2)(lambda: block(two, early, both))
            pl.when((few <= 2) & (many > 2))(lambda: block(two, early, late))
            pl.when(many > 3)(lambda: block(two, slice(BLK, tail), both))
            for side in range(2):
                value = lane_column(dks[side], HD * (1 - side) + 3)
                next_ref[...] = jnp.where(lane == 2 * pair + side, value, next_ref[...])
            dk_ref[...] = (dk_own[...] + jnp.where(lane < HD, dks[0], dks[1])).astype(BF)
            dv_ref[...] = (dv_own[...] + jnp.where(lane < HD, dvs[0], dvs[1])).astype(BF)

        @pl.when(many == 0)
        def _():
            dk_ref[...] = dk_own[...].astype(BF)
            dv_ref[...] = dv_own[...].astype(BF)

    heads_spec = lambda n: spec((n, LANES), lambda i, *_: (0, i))
    shared = lambda n: spec((n, LANES), lambda i, *_: (0, 0))
    last = lambda n: spec((n, LANES), lambda i, *_: (0, pairs))
    keys_spec = spec((rows, LANES), lambda i, *_: (place, i))
    return call(
        kernel, (pairs,), (bounds, k, v, q_one, d_one, q_one, d_one, q_two, d_two, q_two, d_two, gkn, dk, dv),
        [
            keys_spec, keys_spec, heads_spec(rows), heads_spec(rows), last(rows), last(rows),
            heads_spec(tail), heads_spec(tail), last(tail), last(tail), shared(rows), heads_spec(rows), heads_spec(rows),
        ],
        (jax.ShapeDtypeStruct(dk.shape, BF), jax.ShapeDtypeStruct(dk.shape, BF), jax.ShapeDtypeStruct((rows, LANES), F32)),
        (heads_spec(rows), heads_spec(rows), shared(rows)),
        [pltpu.VMEM((2, rows, LANES), BF)] * 2 + [pltpu.VMEM((2, rows, LANES), F32)] * 2,
        prefetch=1, cost=2932500000
    )


def project(offs, x, x_far, tail, gain, w, side_w, qkv_b, bias, cols, rank_r, filled=None, before=0):
    width = gain.shape[1]
    block = width // 4
    own = filled is None
    rows = x.shape[0] // (2 * BLK) * 2 * BLK
    row_steps = 1 if own else 2
    parts = ("q", "k", "v") if own else ("k", "v")
    assert rows == 2 * BLK and BLK <= tail <= rows - 32

    def kernel(*refs):
        offs_ref, x_ref = refs[0], refs[1]
        at = 2
        if not own:
            far_ref, at = refs[2], 3
        gain_ref, *pieces, side_ref, b_ref, bias_ref = refs[at : at + 8]
        at += 8 + (0 if own else 3)
        outs, scr = refs[at:-3], refs[-3:]
        part, step = pl.program_id(0), pl.program_id(1)
        n_outs = dict(zip(("n", "low", "q", "k", "v", "logits") if own else ("k", "v", "logits"), outs))
        scr, low_scr, joint = scr
        at_rows = pl.ds(pl.multiple_of(step * rows, rows), rows)

        @pl.when(part == 0)
        def _():
            blocks = []
            for k in range(4):
                here = pl.ds(pl.multiple_of(offs_ref[k], LANES), block)
                value = x_ref[:, here]
                if not own:
                    far = jnp.concatenate([far_ref[:BLK, here], far_ref[tail + 32 - BLK : tail + 32, here]], axis=0)
                    value = jnp.where(step == 0, far, value)
                blocks.append(value.astype(F32))
            factor = norm_terms(blocks)
            for k in range(4):
                here = pl.ds(pl.multiple_of(offs_ref[k], LANES), block)
                scr[at_rows, k * block : (k + 1) * block] = (blocks[k] * factor * gain_ref[:, here]).astype(BF)
            side = dot(scr[at_rows, :], side_ref[...])
            low = side[:, LANES - rank_r :].astype(BF)
            low_scr[at_rows, :rank_r] = low
            n_outs["logits"][at_rows, :] = side + bias_ref[...]
            if own:
                n_outs["n"][...] = scr[...]
                n_outs["low"][...] = low

        @pl.when(step == 0)
        def _():
            for k in range(4):
                joint[k * block : (k + 1) * block, :] = pieces[k][...]

        value = dot(scr[at_rows, :], joint[...])
        value = (value + dot(low_scr[at_rows, :rank_r], b_ref[...])).astype(BF)
        for n, name in enumerate(parts):
            @pl.when(part == n)
            def _(name=name):
                out = n_outs[name]
                out[at_rows, :] = (value.astype(F32) * HD ** (-0.5)).astype(BF) if name == "q" else value

    keys = before + rows if own else filled[0].shape[0]
    ins = [offs, x] + ([] if own else [x_far]) + [gain, *w, side_w, qkv_b, bias] + ([] if own else list(filled))
    row_spec = spec((rows, width), lambda i, *_: (0, 0))
    in_specs = [row_spec] + ([] if own else [whole(x_far)])
    first = 0 if own else 1
    column = lambda n: spec((n, cols), lambda j, *_: (0, j + first))
    in_specs += [whole(gain), *[column(block)] * 4, whole(side_w), column(rank_r), whole(bias)]
    if not own:
        in_specs += [pl.BlockSpec(memory_space=pl.ANY)] * 3
    some = row_steps * rows
    at_keys = lambda n: spec((some, n), lambda *_: (before // some if own else 0, 0))
    outs = [jax.ShapeDtypeStruct((keys, cols), BF)] * 2 + [jax.ShapeDtypeStruct((keys, LANES), F32)]
    out_specs = [at_keys(cols), at_keys(cols), at_keys(LANES)]
    if own:
        here = lambda n: spec((rows, n), lambda *_: (0, 0))
        outs = [
            jax.ShapeDtypeStruct((rows, width), BF),
            jax.ShapeDtypeStruct((rows, rank_r), BF),
            jax.ShapeDtypeStruct((rows, cols), BF),
        ] + outs
        out_specs = [here(width), here(rank_r), here(cols)] + out_specs
    return call(
        kernel, (len(parts), row_steps), ins, in_specs, tuple(outs), tuple(out_specs),
        [pltpu.VMEM((some, width), BF), pltpu.VMEM((some, LANES), BF), pltpu.VMEM((width, cols), BF)], prefetch=1,
        aliases={} if own else {11: 0, 12: 1, 13: 2},
    )


def gate_tables(logits, seg_keys, seg_row, n_heads, rows):
    keys = logits.shape[0]
    before = keys - rows
    one = 3 * n_heads + DOCS

    def kernel(logit_ref, seg_ref, row_ref, gq_ref, gk_ref, gkn_ref, gate_ref, tot_ref):
        lane = lane_ids(BLK)
        doc = lane - 3 * n_heads + 1
        doc_lane = (doc > 0) & (doc <= DOCS)
        inner = lax.broadcasted_iota(jnp.int32, (BLK, BLK), 1) > lax.broadcasted_iota(jnp.int32, (BLK, BLK), 0)
        later = inner.astype(BF)

        def forget(at):
            value = logit_ref[at, :]
            value = jnp.minimum(value, 0.0) - jnp.log(1.0 + jnp.exp(-jnp.abs(value)))
            return jnp.where((lane < n_heads) & (seg_ref[at, :] > 0), value, 0.0)

        def lanes(values, docs):
            return (split_lanes(values, n_heads) + docs + jnp.where(lane == one, 1.0, 0.0)).astype(BF)

        def docs_k(at):
            return jnp.where(doc_lane & (doc != seg_ref[at, :]), BIG, 0.0)

        def suffix(first, last, carry, out_ref, base):
            for b in range(last - 1, first - 1, -1):
                at = slice(b * BLK, (b + 1) * BLK)
                values = forget(at)
                sums = exact_dot(later, values) + carry
                out_ref[b * BLK - base : (b + 1) * BLK - base, :] = lanes(sums, docs_k(at))
                carry = carry + jnp.sum(values, axis=0, keepdims=True)
            return carry

        n_before, n_all = before // BLK, keys // BLK
        zero = jnp.zeros((1, LANES), F32)
        near = suffix((before - rows) // BLK, n_before, zero, gk_ref, 0)
        tot_ref[...] = jnp.broadcast_to(near, tot_ref.shape)
        suffix(0, (before - rows) // BLK, near, gk_ref, 0)
        suffix(n_before, n_all, zero, gkn_ref, before)
        own = jnp.concatenate([forget(slice(b * BLK, (b + 1) * BLK)) for b in range(n_before, n_all)], axis=0)
        for b in range(rows // BLK):
            at = slice(before + b * BLK, before + (b + 1) * BLK)
            here = slice(b * BLK, (b + 1) * BLK)
            q_pos = lax.broadcasted_iota(jnp.int32, (BLK, rows), 0) + b * BLK
            k_pos = lax.broadcasted_iota(jnp.int32, (BLK, rows), 1)
            same = (row_ref[...] == seg_ref[at, :]) & (k_pos <= q_pos)
            sums = exact_dot(same.astype(BF), own)
            gate_ref[here, :] = sums
            gq_ref[here, :] = lanes(sums, jnp.where(doc_lane & (doc == seg_ref[at, :]), 1.0, 0.0))
            gk_ref[at, :] = lanes(-sums, docs_k(at))

    shape = lambda n, t: jax.ShapeDtypeStruct((n, LANES), t)
    outs = (shape(rows, BF), shape(keys, BF), shape(rows, BF), shape(rows, F32), shape(8, F32))
    return call(
        kernel, (1,), (logits, seg_keys, seg_row), [whole(logits), whole(seg_keys), whole(seg_row)],
        outs, tuple(whole(o) for o in outs), flops=10**8, nbytes=4 * 10**6,
    )


def weight_halves(w):
    half = w[0].shape[0] // 2
    at = lambda row: spec((half, w[0].shape[1]), lambda *_: (row, 0))
    return [at(0), at(0), at(1), at(1)]


def out_projection(offs, rank, x, mixed_own, mixed_far, w, a_own, a_far, out_b, gain, ffn_a):
    rows, width = x.shape
    block = width // 4
    rank_r = a_own.shape[1]

    def kernel(
        offs_ref, rank_ref, x_ref, mo, mf, wo0, wo1, wf0, wf1, ao, af, b_ref, gain_ref, fa, h_ref, n_ref, low_ref, lo_ref
    ):
        def run(m0, m1, w0, w1, a0, a1):
            low = (dot(m0[...], a0[...]) + dot(m1[...], a1[...])).astype(BF)
            lo_ref[...] = low
            for half in range(2):
                both = dot(m0[...], w0[half][...]) + dot(m1[...], w1[half][...])
                both = both + dot(low, b_ref[:, 2 * half * block : 2 * (half + 1) * block])
                for j in range(2):
                    k = 2 * half + j
                    here = pl.ds(pl.multiple_of(offs_ref[k], LANES), block)
                    value = x_ref[:, here].astype(F32) + both[:, j * block : (j + 1) * block]
                    h_ref[:, k * block : (k + 1) * block] = value

        pl.when(rank_ref[0] == 0)(lambda: run(mo, mf, (wo0, wo1), (wf0, wf1), ao, af))
        pl.when(rank_ref[0] != 0)(lambda: run(mf, mo, (wf0, wf1), (wo0, wo1), af, ao))
        value = h_ref[...]
        normed = (value * norm_terms([value]) * gain_ref[...]).astype(BF)
        n_ref[...] = normed
        low_ref[...] = dot(normed, fa[...]).astype(BF)

    rowed = whole
    outs = (
        jax.ShapeDtypeStruct((rows, width), F32), jax.ShapeDtypeStruct((rows, width), BF),
        jax.ShapeDtypeStruct((rows, rank_r), BF), jax.ShapeDtypeStruct((rows, rank_r), BF),
    )
    ins = (offs, rank, x, mixed_own, mixed_far, *w, *w, a_own, a_far, out_b, gain, ffn_a)
    return call(
        kernel, (1,), ins,
        [rowed(x), rowed(mixed_own), rowed(mixed_far)] + weight_halves(w) + [whole(v) for v in ins[9:]],
        outs, tuple(rowed(o) for o in outs), prefetch=2, flops=4 * rows * width * mixed_own.shape[1],
        nbytes=4 * width * mixed_own.shape[1] + 8 * rows * width, cost=1725000000
    )


def feed_forward(rank, normed, low, cot, grad_low, gate_up, down, ffn_b, down_a):
    rows, width = normed.shape
    block = width // 4
    half = rows // 2
    rank_r = low.shape[1]
    unit_cols = down_a.shape[0]
    tile = 512 if unit_cols % 512 == 0 else unit_cols
    tiles = unit_cols // tile
    down_at = down[0].shape[1] // tile - tiles

    def kernel(
        rank_ref, x_ref, low_ref, cot_ref, gl_ref, *rest,
    ):
        pieces, rest = rest[:12], rest[12:]
        bg_ref, bu_ref, ad_ref, *rest, wg, wu, wd = rest
        step = pl.program_id(0)
        units_ref, gg_ref, gu_ref, far_ref, own_ref, own_low_ref, part_ref, part_low_ref = rest

        @pl.when(step == 0)
        def _():
            part_ref[...] = jnp.zeros_like(part_ref)
            part_low_ref[...] = jnp.zeros_like(part_low_ref)

        for n, joint in enumerate((wg, wu, wd)):
            for k in range(4):
                joint[k * block : (k + 1) * block, :] = pieces[4 * n + k][...]
        gate = dot(x_ref[...], wg[...]) + dot(low_ref[...], bg_ref[...])
        up = dot(x_ref[...], wu[...]) + dot(low_ref[...], bu_ref[...])
        grad = dot(cot_ref[...], wd[...]) + dot_t(gl_ref[...], ad_ref[...])
        sig = jax.nn.sigmoid(gate)
        act = gate * sig
        units_ref[...] = (act * up).astype(BF)
        gg = (grad * up * sig * (1.0 + gate * (1.0 - sig))).astype(BF)
        gu = (grad * act).astype(BF)
        gg_ref[...] = gg
        gu_ref[...] = gu
        part_low_ref[:, :rank_r] += dot_t(gg, bg_ref[...]) + dot_t(gu, bu_ref[...])
        part_ref[...] += dot_t(gg, wg[...]) + dot_t(gu, wu[...])

        @pl.when(step == tiles - 1)
        def _():
            mine = pl.ds(pl.multiple_of(rank_ref[0] * half, half), half)
            theirs = pl.ds(pl.multiple_of((1 - rank_ref[0]) * half, half), half)
            far_ref[:, :width] = part_ref[theirs, :].astype(BF)
            far_ref[:, width:] = split_lanes(part_low_ref[theirs, :], rank_r).astype(BF)
            own_ref[...] = part_ref[mine, :]
            own_low_ref[...] = part_low_ref[mine, :]

    out = jax.ShapeDtypeStruct((rows, unit_cols), BF)
    out_spec = spec((rows, tile), lambda i, *_: (0, i))
    sums = (jax.ShapeDtypeStruct((rows, width), F32), jax.ShapeDtypeStruct((rows, LANES), F32))
    ends = (
        jax.ShapeDtypeStruct((half, width + LANES), BF), jax.ShapeDtypeStruct((half, width), F32),
        jax.ShapeDtypeStruct((half, LANES), F32),
    )
    return call(
        kernel,
        (tiles,),
        (rank, normed, low, cot, grad_low, *gate_up, *gate_up, *down, ffn_b, ffn_b, down_a),
        [
            whole(normed), whole(low), whole(cot), whole(grad_low),
            *[spec((block, tile), lambda i, *_: (0, i)) for _ in range(4)],
            *[spec((block, tile), lambda i, *_: (0, i + tiles)) for _ in range(4)],
            *[spec((block, tile), lambda i, *_: (0, i + down_at)) for _ in range(4)],
            spec((rank_r, tile), lambda i, *_: (0, i)),
            spec((rank_r, tile), lambda i, *_: (0, i + tiles)),
            spec((tile, rank_r), lambda i, *_: (i, 0)),
        ],
        (out, out, out, *ends),
        (out_spec, out_spec, out_spec, *[whole(e) for e in ends]),
        [pltpu.VMEM(e.shape, F32) for e in sums] + [pltpu.VMEM((width, tile), BF)] * 3,
        prefetch=1, cost=4657500000
    )


def whole_low(parts, n):
    parts = parts.astype(F32)
    return parts[:, :n] + parts[:, n : 2 * n] + parts[:, 2 * n : 3 * n]


def middle(rank, own, got, own_low, hidden, cot, gain, ffn_a, out_b, w, a_own, a_far):
    half, width = own.shape
    depth = width // 2
    rank_r = out_b.shape[0]
    cols = a_own.shape[0]

    def kernel(
        rank_ref, own_ref, got_ref, low_ref, h_ref, cot_ref, gain_ref, fa, b_ref, wo0, wo1, wf0, wf1, ao, af,
        gh_ref, ghb_ref, glf_ref, glo_ref, mine_ref, far_ref,
    ):
        ffn_low = (low_ref[:, :rank_r] + whole_low(got_ref[:, width:], rank_r)).astype(BF)
        glf_ref[...] = ffn_low
        incoming = own_ref[...] + got_ref[:, :width].astype(F32) + dot_t(ffn_low, fa[...])
        value = h_ref[...]
        factor = norm_terms([value])
        scaled = incoming * gain_ref[...]
        mean = jnp.mean(value * scaled, axis=1, keepdims=True)
        grad = cot_ref[...].astype(F32) + (factor * scaled - value * (factor * factor * factor * mean))
        gh_ref[...] = grad
        low_precision = grad.astype(BF)
        ghb_ref[...] = low_precision
        left, right = low_precision[:, :depth], low_precision[:, depth:]
        out_low = dot_t(low_precision, b_ref[...]).astype(BF)
        glo_ref[...] = out_low
        mine_ref[...] = (dot_t(left, wo0[...]) + dot_t(right, wo1[...]) + dot_t(out_low, ao[...])).astype(BF)
        far_ref[...] = (dot_t(left, wf0[...]) + dot_t(right, wf1[...]) + dot_t(out_low, af[...])).astype(BF)

    outs = (
        jax.ShapeDtypeStruct((half, width), F32), jax.ShapeDtypeStruct((half, width), BF),
        jax.ShapeDtypeStruct((half, rank_r), BF), jax.ShapeDtypeStruct((half, rank_r), BF),
        jax.ShapeDtypeStruct((half, cols), BF), jax.ShapeDtypeStruct((half, cols), BF),
    )
    ins = (rank, own, got, own_low, hidden, cot, gain, ffn_a, out_b, *w, *w, a_own, a_far)
    mine = lambda v: spec((half, v.shape[1]), lambda i, r: (r[0], 0))
    in_specs = [whole(own), whole(got), whole(own_low), mine(hidden), mine(cot)] + [whole(v) for v in ins[6:9]]
    in_specs += weight_halves(w) + [whole(a_own), whole(a_far)]
    return call(
        kernel, (1,), ins, in_specs, outs, tuple(whole(o) for o in outs), prefetch=1,
        flops=4 * half * width * cols, nbytes=4 * width * cols + 16 * half * width, cost=1311000000
    )


def mixed_gradient(rank, own, far, mixed, n_heads, tail):
    half, cols = own.shape

    def kernel(rank_ref, own_ref, far_ref, mixed_ref, out_ref, tail_ref):
        lane = lane_ids(half)
        for ref, first in ((own_ref, rank_ref[0]), (far_ref, 1 - rank_ref[0])):
            at = pl.ds(pl.multiple_of(first * half, half), half)
            sums = jnp.zeros((half, LANES), F32)
            for pair in range(n_heads // 2):
                here = slice(pair * LANES, (pair + 1) * LANES)
                product = ref[:, here].astype(F32) * mixed_ref[at, here]
                a = jnp.sum(jnp.where(lane < HD, product, 0.0), axis=1, keepdims=True)
                b = jnp.sum(jnp.where(lane < HD, 0.0, product), axis=1, keepdims=True)
                sums = jnp.where(lane == 2 * pair, -a, jnp.where(lane == 2 * pair + 1, -b, sums))
            out_ref[at, :cols] = ref[...]
            out_ref[at, cols:] = split_lanes(sums, n_heads).astype(BF)
        tail_ref[...] = out_ref[:tail, :]

    outs = [jax.ShapeDtypeStruct((n, cols + LANES), BF) for n in (2 * half, tail)]
    return call(
        kernel, (1,), (rank, own, far, mixed), [whole(own), whole(far), whole(mixed)],
        tuple(outs), tuple(whole(o) for o in outs), prefetch=1,
        flops=4 * half * cols, nbytes=16 * half * cols, cost=672750000
    )


def input_gradient(rank, grads, logits, seg_keys, seg_row, row_lanes, own_lanes, next_lanes, across, w, side_w, qkv_b, low_qkv, n_heads):
    rows, cols = grads[0].shape
    block = w[0].shape[0]
    half = rows // 2
    rank_r = qkv_b.shape[0]
    before = logits.shape[0] - rows
    steps = 3
    chunk = block // steps

    def kernel(
        rank_ref, q_ref, k_ref, v_ref, logit_ref, seg_ref, seg_row_ref, r_ref, o_ref, n_ref, a_ref, *refs,
    ):
        pieces, sides, refs = refs[:4], refs[4:8], refs[8:]
        (
            b_ref, lq_ref, far_ref, own_ref, low_ref, tq_ref, tk_ref, tv_ref, gl_ref, sum_ref, joint,
            side,
        ) = refs

        @pl.when(pl.program_id(0) == 0)
        def _():
            lane = lane_ids(rows)
            t = lax.broadcasted_iota(jnp.int32, (rows, rows), 0)
            i = lax.broadcasted_iota(jnp.int32, (rows, rows), 1)
            same = ((seg_row_ref[...] == seg_ref[...]) & (i >= t)).astype(BF)
            total = exact_dot(same, r_ref[...] - o_ref[...]) + exact_dot((i < t).astype(BF), n_ref[...])
            total = total + a_ref[:1, :]
            value = jnp.where(lane < n_heads, total * jax.nn.sigmoid(-logit_ref[...]), 0.0)
            gl_ref[...] = value.astype(BF)
            low = dot_t(b_ref[:, :cols], q_ref[...]) + dot_t(b_ref[:, cols : 2 * cols], k_ref[...])
            low_ref[...] = low + dot_t(b_ref[:, 2 * cols :], v_ref[...])
            for out, grad in ((tq_ref, q_ref), (tk_ref, k_ref), (tv_ref, v_ref)):
                out[...] = t_dot(lq_ref[...], grad[...])

        mine = pl.ds(pl.multiple_of(rank_ref[0] * half, half), half)
        theirs = pl.ds(pl.multiple_of((1 - rank_ref[0]) * half, half), half)
        for k in range(4):
            joint[k * chunk : (k + 1) * chunk, :] = pieces[k][...]
            side[k * chunk : (k + 1) * chunk, :] = sides[k][...]
        value = dot_t(q_ref[...], joint[:, :cols]) + dot_t(k_ref[...], joint[:, cols : 2 * cols])
        sum_ref[...] = value + dot_t(v_ref[...], joint[:, 2 * cols :]) + dot_t(gl_ref[...], side[...])
        for k in range(4):
            at = slice(k * chunk, (k + 1) * chunk)
            far_ref[k] = sum_ref[theirs, at].astype(BF)
            own_ref[k] = sum_ref[mine, at]

    ins = (rank, *grads, logits, seg_keys, seg_row, row_lanes, own_lanes, next_lanes, across, *w, *[side_w] * 4, qkv_b, low_qkv)
    at_own = lambda v: spec((rows, v.shape[1]), lambda i, *_: (before // rows, 0))
    in_specs = [whole(g) for g in grads] + [at_own(logits), at_own(seg_keys)]
    in_specs += [whole(v) for v in (seg_row, row_lanes, own_lanes, next_lanes, across)]
    n_col = w[0].shape[1]
    in_specs += [spec((chunk, n_col), lambda i, *_: (i, 0))] * 4
    in_specs += [spec((chunk, LANES), lambda i, *_, k=k: (i + k * steps, 0)) for k in range(4)]
    in_specs += [whole(qkv_b), whole(low_qkv)]
    outs = (
        jax.ShapeDtypeStruct((4, half, block), BF), jax.ShapeDtypeStruct((4, half, block), F32),
        jax.ShapeDtypeStruct((rank_r, rows), F32),
        *[jax.ShapeDtypeStruct((rank_r, cols), F32)] * 3,
    )
    halves = spec((4, half, chunk), lambda i, *_: (0, 0, i))
    return call(
        kernel, (steps,), ins, in_specs, outs, (halves, halves, *[whole(o) for o in outs[2:]]), [pltpu.VMEM((rows, LANES), BF), pltpu.VMEM((rows, 4 * chunk), F32), pltpu.VMEM((4 * chunk, n_col), BF),
         pltpu.VMEM((4 * chunk, LANES), BF)],
        prefetch=1, cost=1932000000
    )


def token_gradient(offs, rank, own, got, grad_low, a, x, gain, grad_hidden):
    half, width = grad_hidden.shape
    block = width // 4

    def kernel(offs_ref, rank_ref, own_ref, got_ref, low_ref, a_ref, x_ref, gain_ref, gh_ref, out_ref):
        blocks, scaled, product = [], [], 0.0
        for k in range(4):
            here = pl.ds(pl.multiple_of(offs_ref[k], LANES), block)
            value = own_ref[k] + got_ref[k].astype(F32)
            value = value + lax.dot_general(
                low_ref[...], a_ref[k * block : (k + 1) * block, :], (((0,), (1,)), ((), ())), preferred_element_type=F32
            )
            blocks.append(x_ref[:, here].astype(F32))
            scaled.append(value * gain_ref[:, here])
            product = product + jnp.sum(blocks[k] * scaled[k], axis=1, keepdims=True)
        factor = norm_terms(blocks)
        mean = product / width
        for k in range(4):
            here = pl.ds(pl.multiple_of(offs_ref[k], LANES), block)
            back = factor * scaled[k] - blocks[k] * (factor * factor * factor * mean)
            out_ref[:, here] = (gh_ref[:, k * block : (k + 1) * block] + back).astype(BF)

    mine = lambda v: spec((half, v.shape[1]), lambda i, o, r: (r[0], 0))
    out = jax.ShapeDtypeStruct((half, width), BF)
    return call(
        kernel, (1,), (offs, rank, own, got, grad_low, a, x, gain, grad_hidden),
        [whole(own), whole(got), spec((grad_low.shape[0], half), lambda i, o, r: (0, r[0])), whole(a), mine(x), whole(gain), whole(grad_hidden)],
        out, whole(out), prefetch=2, nbytes=20 * half * width, cost=862500000
    )


def both_halves(rank, own, far):
    half, width = own.shape

    def kernel(rank_ref, own_ref, far_ref, out_ref):
        @pl.when(pl.program_id(0) == rank_ref[0])
        def _():
            out_ref[...] = own_ref[...].astype(F32)

        @pl.when(pl.program_id(0) != rank_ref[0])
        def _():
            out_ref[...] = far_ref[...].astype(F32)

    return call(
        kernel, (2,), (rank, own, far), [whole(own), whole(far)], jax.ShapeDtypeStruct((2 * half, width), F32),
        spec((half, width), lambda i, *_: (i, 0)), prefetch=1, nbytes=16 * half * width, cost=517500000
    )


def down_partial(units, down, down_a):
    rows, unit_cols = units.shape
    block = down[0].shape[0]
    width = 4 * block
    rank_r = down_a.shape[1]

    def kernel(u_ref, w0, w1, w2, w3, a_ref, out_ref, low_ref):
        low_ref[...] = jnp.zeros_like(low_ref)
        low_ref[:, :rank_r] = dot(u_ref[...], a_ref[...])
        for k, w_ref in enumerate((w0, w1, w2, w3)):
            out_ref[:, k * block : (k + 1) * block] = dot_t(u_ref[...], w_ref[...]).astype(BF)
        out_ref[:, width:] = split_lanes(low_ref[...], rank_r).astype(BF)

    rowed = lambda n: spec((BLK, n), lambda i: (i, 0))
    last = spec((block, unit_cols), lambda i: (0, 0))
    return call(
        kernel, (rows // BLK,), (units, *down, down_a), [rowed(unit_cols), last, last, last, last, whole(down_a)],
        jax.ShapeDtypeStruct((rows, width + LANES), BF), rowed(width + LANES), [pltpu.VMEM((BLK, LANES), F32)], cost=1621500000
    )


def block_result(offs, hidden, own, got, down_b):
    rows, width = hidden.shape
    block = width // 4
    rank_r = down_b.shape[0]

    def kernel(offs_ref, h_ref, own_ref, got_ref, b_ref, out_ref):
        low = (whole_low(own_ref[:, width:], rank_r) + whole_low(got_ref[:, width:], rank_r)).astype(BF)
        for k in range(4):
            here = pl.ds(pl.multiple_of(offs_ref[k], LANES), block)
            cols = slice(k * block, (k + 1) * block)
            both = own_ref[:, cols].astype(F32) + got_ref[:, cols].astype(F32)
            out_ref[:, here] = (h_ref[:, cols] + both + dot(low, b_ref[:, cols])).astype(BF)

    rowed = lambda v: spec((BLK, v.shape[1]), lambda i, *_: (i, 0))
    out = jax.ShapeDtypeStruct((rows, width), BF)
    return call(
        kernel, (rows // BLK,), (offs, hidden, own, got, down_b),
        [rowed(hidden), rowed(own), rowed(got), whole(down_b)], out, rowed(out),
        prefetch=1, nbytes=12 * rows * width, cost=862500000
    )


def pack_gradients(inv, rank, xor_own, xor_both, halves, out_a, wide, owners):
    rank_r, width = xor_own[0].shape
    block = width // 4
    part, unit_part = block // 8, wide[0].shape[1] // 16
    n = len(wide) * unit_part + (len(xor_own) + len(xor_both) + len(halves) + 1) * part
    assert owners == 32 and block % LANES == 0

    def kernel(inv_ref, rank_ref, *refs):
        out_ref, refs = refs[-1], list(refs[:-1])
        take = lambda count: [refs.pop(0) for _ in range(count)]
        own_refs, both_refs = take(len(xor_own)), take(len(xor_both))
        half_refs, (ao, af), wide_refs = take(len(halves)), take(2), take(len(wide))
        for f in range(4):
            mine = rank_ref[0] == f // 2
            at = pl.ds(pl.multiple_of(inv_ref[f], LANES), block)
            cols = slice(f % 2 * block, (f % 2 + 1) * block)
            blocks = [jnp.where(mine, r[:, at], 0.0) for r in own_refs] + [r[:, at] for r in both_refs]
            blocks += [jnp.where(mine, r[:, cols], 0.0) for r in half_refs]
            blocks.append(jnp.where(mine, ao[:, cols], af[:, cols]))
            units = 8 * unit_part
            big = [jnp.where(mine, r[:, f % 2 * units : (f % 2 + 1) * units], 0.0) for r in wide_refs]
            for j in range(8):
                row = [b[:, j * unit_part : (j + 1) * unit_part] for b in big]
                row += [b[:, j * part : (j + 1) * part] for b in blocks]
                at_row = slice((8 * f + j) * rank_r, (8 * f + j + 1) * rank_r)
                out_ref[at_row, :] = jnp.concatenate(row, axis=1).astype(BF)

    ins = (inv, rank, *xor_own, *xor_both, *halves, *out_a, *wide)
    out = jax.ShapeDtypeStruct((owners * rank_r, n), BF)
    return call(kernel, (1,), ins, [whole(v) for v in ins[2:]], out, whole(out), prefetch=2, cost=552000000
    )


def spread_gradients(every, landed, n_adapters, rank_r, unit_part, part):
    senders = landed.shape[0] // (4 * rank_r)
    at = [0, unit_part, 2 * unit_part] + [3 * unit_part + i * part for i in range(9)]

    def kernel(every_ref, x_ref, aq, bq, ao, bo, ag, bg, ad, bd):
        sums = []
        for f in range(4):
            total = 0.0
            for i in range(senders):
                row = (f * senders + i) * rank_r
                total = total + x_ref[row : row + rank_r, :].astype(F32)
            sums.append(total)
        for a in range(n_adapters):
            total = 0.0
            for f in range(4):
                total = total + jnp.where(every_ref[f] == a, sums[f], 0.0)
            cut = lambda i: total[:, at[i] : at[i + 1]]
            for out, i in ((aq, 3), (ao, 10), (ag, 6), (ad, 2)):
                out[a] = cut(i)
            bo[a], bd[a] = cut(5), cut(4)
            for j in range(3):
                bq[a, j] = cut(7 + j)
            for j in range(2):
                bg[a, :, j, :] = cut(j)

    shape = lambda *dims: jax.ShapeDtypeStruct((n_adapters, *dims), F32)
    row = shape(rank_r, part)
    outs = (row, shape(3, rank_r, part), row, row, row, shape(rank_r, 2, unit_part), shape(rank_r, unit_part), row)
    return call(kernel, (1,), (every, landed), [whole(landed)], outs, tuple(whole(o) for o in outs), prefetch=1, cost=500250000
    )


def body(
    tokens, segments, adapter_index, w_qkv, w_forget, forget_bias, w_out, w_gate_up, w_down,
    gain_attn, gain_ffn, a_qkv, b_qkv, a_out, b_out, a_gate_up, b_gate_up, a_down, b_down, cotangent,
):
    count, rows, width = tokens.shape
    assert count == 1
    head_cols = w_qkv.shape[2]
    n_heads = w_forget.shape[1]
    unit_cols = w_gate_up.shape[2]
    rank_r = a_qkv.shape[2]
    n_f, n_c, n_t = (lax.axis_size("fsdp"), lax.axis_size("ctx"), lax.axis_size("tp"))
    f_rank, t_rank = (lax.axis_index("fsdp"), lax.axis_index("tp"))
    hops = -(-(DOC_MOST - 1) // rows)
    assert hops == 2 and n_c > 2 and n_t == 2 and n_f % 4 == 0
    tail = -(-(DOC_MOST - 1 - rows) // 32) * 32
    before = hops * rows
    half = rows // 2
    block = width // 4
    first = t_rank == 0
    rank = t_rank.astype(jnp.int32)[None]

    def other(values):
        return lax.ppermute(values, "tp", [(0, 1), (1, 0)])

    def four(pieces):
        return [*pieces, *[lax.ppermute(part, "fsdp", [(i, i ^ 1) for i in range(n_f)]) for part in pieces]]

    mix = lambda values, dim: to_xor(values, dim, n_f, f_rank)
    direct = n_f == 4 and block % LANES == 0
    if direct:
        offs = jnp.stack([(f_rank ^ step) * block for step in xor_order(4)]).astype(jnp.int32)
        lay = lambda values, dim: values
    else:
        offs = jnp.arange(4, dtype=jnp.int32) * block
        lay = mix

    pick = adapter_index[0]
    tok = lay(tokens[0], 1)
    seg_one = segments[0] + 1
    note = jnp.zeros((32, width), BF).at[0, :rows].set(seg_one.astype(BF))
    qkv_own = jnp.concatenate([w_qkv[:, i] for i in range(3)], axis=1)
    qkv_far = far_blocks(qkv_own, 0)
    prev_one = shift(jnp.concatenate([tok, after(note, qkv_own)], axis=0), 1, n_c)
    side = jnp.broadcast_to(pick.astype(BF), (w_forget.shape[0], 1))
    side_far = far_blocks(after(jnp.concatenate([w_forget, side], axis=1), qkv_own), 0)
    take = lambda table: lax.dynamic_index_in_dim(table, pick, 0, keepdims=False)
    mine = lambda values, n, dim: lax.dynamic_slice_in_dim(values, t_rank * n, n, dim)
    theirs = lambda values, n, dim: lax.dynamic_slice_in_dim(values, (1 - t_rank) * n, n, dim)
    qkv_a, ffn_a = (mix(take(a_qkv), 0), mix(take(a_gate_up), 0))
    out_b, down_b = (mix(take(b_out), 1), mix(take(b_down), 1))
    qkv_b = mine(take(b_qkv), head_cols, 2).reshape(rank_r, 3 * head_cols)
    out_a = take(a_out)
    out_a_own, out_a_far = (mine(out_a, head_cols, 0), theirs(out_a, head_cols, 0))
    ffn_b = mine(take(b_gate_up), unit_cols, 2).reshape(rank_r, 2 * unit_cols)
    down_a = mine(take(a_down), unit_cols, 0)
    gain_one = lay(gain_attn.astype(F32), 0)[None]
    gain_two = mix(gain_ffn.astype(F32), 0)[None]
    bias = jnp.pad(forget_bias.astype(F32), (0, LANES - n_heads))[None]
    cot = mix(cotangent[0], 1)
    grad_low_down = dot_t(cot, down_b).astype(BF)

    out_pair = jnp.concatenate([w_out, other(w_out)], axis=0)
    gate_up_own = jnp.concatenate([w_gate_up[:, 0], w_gate_up[:, 1]], axis=1)
    down_own = w_down.T
    shared = n_f == 4 and n_c % 2 == 0
    odd = lax.axis_index("ctx") % 2
    down_sent = down_own
    if shared:
        down_sent = lax.dynamic_slice_in_dim(down_own, odd * (unit_cols // 2), unit_cols // 2, 1)
    (
        prev_one, qkv_far, side_far, out_pair, qkv_a, qkv_b, gain_one, bias, ffn_a, out_b, down_b, out_a_own, out_a_far,
        ffn_b, down_a, gain_two, cot, grad_low_down, gate_up_own, down_own, down_sent,
    ) = lax.optimization_barrier((
        prev_one, qkv_far, side_far, out_pair, qkv_a, qkv_b, gain_one, bias, ffn_a, out_b, down_b, out_a_own, out_a_far,
        ffn_b, down_a, gain_two, cot, grad_low_down, gate_up_own, down_own, down_sent,
    ))
    out_far = far_blocks(out_pair, 1)
    prev_two = shift(prev_one[rows - tail :], 1, n_c)
    qkv_four = four(qkv_far)
    side_all = jnp.concatenate(near_blocks(*side_far, 0), axis=0)
    every = from_xor(side_all[:: w_forget.shape[0], n_heads], 0, n_f, f_rank).astype(jnp.int32)
    side_w = jnp.concatenate([side_all, jnp.zeros((width, LANES - n_heads - 1 - rank_r), BF), qkv_a], axis=1)
    args = (gain_one, qkv_four, side_w, qkv_b, bias, head_cols, rank_r)
    down_far = far_blocks(down_sent, 0)
    tok_in, prev_two = lax.optimization_barrier((tok, prev_two))
    normed, low_qkv, query, *filled = project(offs, tok_in, None, tail, *args, None, before)
    seg_two = prev_two[tail, :rows].astype(jnp.int32)
    seg_far = []
    for b in range(-(-tail // BLK)):
        start, end = min(b * BLK, tail + 32 - BLK), min((b + 1) * BLK, tail)
        known = seg_two[rows - tail + b * BLK : rows - tail + end]
        seg_far.append(jnp.pad(known, (b * BLK - start, BLK - (end - start))))
    seg_keys = jnp.concatenate(seg_far + [prev_one[rows, :rows].astype(jnp.int32), seg_one])
    last_keys = jnp.max(seg_keys.reshape(-1, BLK), axis=1)
    lows = jnp.sum(last_keys[None, :] < seg_one[::BLK][:, None], axis=1).astype(jnp.int32)

    gate_up_far = far_blocks(after(gate_up_own, out_far[1], down_far[1], query), 0)
    keys, vals, logits = project(offs, prev_one, prev_two, tail, *args, filled)
    out_w = near_blocks(out_far[0], after(out_far[1], query), 1)
    logits, out_w = lax.optimization_barrier((logits, out_w))
    seg_col, seg_row = (seg_keys[:, None], seg_one[None, :])
    gq, gk, gk_next, gates, total = gate_tables(logits, seg_col, seg_row, n_heads, rows)
    mixed_own, mixed_f, gq_one, gq_two = attention_forward(lows, query, keys, vals, gq, gk, gates, total, n_heads)
    mixed_far = other(mixed_own)
    sent_q1 = jnp.concatenate([query, gq_one], axis=1)
    sent_q2 = jnp.concatenate([query[:tail], gq_two[:tail]], axis=1)
    if shared:
        down_pair = lax.ppermute(after(down_far[1], keys), "ctx", [(i, i ^ 1) for i in range(n_c)])
        down_pair = after(down_pair, mixed_own)
        lower, upper = jnp.where(odd == 0, down_far[1], down_pair), jnp.where(odd == 0, down_pair, down_far[1])
        down_got = jnp.concatenate([lower, upper], axis=1)
    else:
        down_got = down_far[1]
    mixed_far, sent_q1, sent_q2, down_got = lax.optimization_barrier((mixed_far, sent_q1, sent_q2, down_got))
    next_q1 = shift(sent_q1, -1, n_c)
    next_q2 = shift(sent_q2, -2, n_c)

    down_w = four((after(down_own, mixed_own), down_got)) if shared else four(down_far)
    hidden, normed_ffn, low_ffn, low_out = out_projection(
        offs, rank, tok, mixed_own, mixed_far, out_w, out_a_own, out_a_far, out_b, gain_two, ffn_a
    )
    gate_up_w = four((after(gate_up_own, mixed_own), after(gate_up_far[1], hidden))) if shared else four(gate_up_far)
    units, grad_gate, grad_up, far, own, own_low = feed_forward(
        rank, normed_ffn, low_ffn, cot, grad_low_down, gate_up_w, down_w, ffn_b, down_a
    )
    got = other(far)
    down_part = down_partial(after(units, far), down_w, down_a)
    gate_g, up_g, units_g = after((grad_gate, grad_up, units), far)
    tables_ffn = [t_dot(low_ffn, gate_g), t_dot(low_ffn, up_g), t_dot(grad_low_down, units_g)]
    got, down_part, tables_ffn = lax.optimization_barrier((got, down_part, tables_ffn))
    grad_hidden, grad_hidden_b, grad_low_ffn, grad_low_out, gm_own, gm_send = middle(
        rank, own, got, own_low, hidden, cot, gain_two, ffn_a, out_b, out_w, out_a_own, out_a_far
    )
    grad_mixed, sent_d2 = mixed_gradient(rank, gm_own, other(gm_send), mixed_f, n_heads, tail)

    next_d1 = shift(grad_mixed, -1, n_c)
    next_d2 = shift(sent_d2, -2, n_c)
    grad_q, row_lanes, across = attention_dq(
        lows, query, keys, vals, grad_mixed, gq_one, gk, n_heads, (before - rows) // BLK
    )
    across = shift(across, -1, n_c)
    docs_at = head_cols + 3 * n_heads
    grad_k_own, grad_v_own, own_lanes = attention_dkv_own(keys, vals, query, after(grad_mixed, grad_q), gq_one, gk, n_heads)
    next_q1, next_q2, next_d1, next_d2, _ = lax.optimization_barrier((next_q1, next_q2, next_d1, next_d2, grad_k_own))
    next_docs = jnp.concatenate([next_q1[::BLK, docs_at : docs_at + DOCS], next_q2[::BLK, docs_at : docs_at + DOCS]])
    next_docs = next_docs.astype(F32)
    ids = jnp.arange(1, DOCS + 1).astype(F32)
    next_first = jnp.where(jnp.sum(next_docs, 1) > 0, jnp.sum(next_docs * ids[None, :], 1), 99.0)
    last_rows = seg_one[BLK - 1 :: BLK].astype(F32)
    highs = jnp.sum(next_first[None, :] <= last_rows[:, None], axis=1).astype(jnp.int32)
    lane = lax.broadcasted_iota(jnp.int32, (1, width), 1)
    own_part = lambda values: values * (lane // (width // 2) == t_rank)
    natural = lambda values: from_xor(values, 1, n_f, f_rank)
    by_tp = lambda a, b: jnp.concatenate([jnp.where(first, a, b), jnp.where(first, b, a)], axis=1)
    place = lambda values: by_tp(values, jnp.zeros_like(values))
    rows_of = lambda values: lax.dynamic_slice_in_dim(values, t_rank * half, half, 0)
    onehot = (jnp.arange(a_qkv.shape[0])[:, None] == every[None, :]).astype(F32)
    onehot = jnp.repeat(onehot, n_c * n_t, axis=1)

    owners = n_f * n_c * n_t

    def pack(tables):
        packed = jnp.concatenate([t.reshape(rank_r, owners, -1) for t in tables], axis=2).transpose(1, 0, 2)
        return packed.astype(BF).reshape(owners, -1), [t.shape[1] // owners for t in tables]

    def take_apart(spread, sizes):
        spread = spread.reshape(-1, rank_r, sum(sizes))
        outs, at = [], 0
        for size in sizes:
            outs.append(spread[:, :, at : at + size])
            at += size
        return outs

    table_out_a = [t_dot(grad_low_out, rows_of(mixed_own)), t_dot(grad_low_out, rows_of(mixed_far))]
    table_out_b = t_dot(rows_of(low_out), grad_hidden_b)
    table_ffn_a = t_dot(grad_low_ffn, rows_of(normed_ffn))
    highs, table_out_a, table_out_b, table_ffn_a = lax.optimization_barrier(
        (highs, table_out_a, table_out_b, table_ffn_a)
    )
    grad_k, grad_v, next_lanes = attention_dkv_next(
        highs, keys, vals, next_q1, next_q2, next_d1, next_d2, gk_next, grad_k_own, grad_v_own, n_heads
    )
    down_other = other(after(down_part, grad_mixed))

    grads = (grad_q, grad_k, grad_v)
    far_in, own_in, part_low_qkv, *tables_b = input_gradient(
        rank, grads, logits, seg_col, seg_row, row_lanes, own_lanes, next_lanes, across, qkv_four, side_w, qkv_b, low_qkv, n_heads
    )
    grad_low_qkv = (part_low_qkv + other(part_low_qkv)).astype(BF)
    got_in = other(far_in)
    parts = [values[:, width : width + 3 * rank_r].astype(F32).reshape(rows, 3, rank_r) for values in (down_part, down_other)]
    parts = [values[:, 0] + values[:, 1] + values[:, 2] for values in parts]
    low_down = after((parts[0] + parts[1]).astype(BF), far_in)
    grad_tok = token_gradient(offs, rank, own_in, got_in, grad_low_qkv, qkv_a, tok, gain_one, grad_hidden)
    tok_far = other(grad_tok)
    block_output = block_result(offs, hidden, down_part, after(down_other, grad_tok), down_b)

    table_qkv_a, table_down_b = dot(grad_low_qkv, normed), t_dot(low_down, cot)
    if direct:
        bits = n_f.bit_length() - 1
        inv = [sum((((f_rank ^ i) >> j) & 1) << (bits - 1 - j) for j in range(bits)) * block for i in range(n_f)]
        packed = pack_gradients(
            jnp.stack(inv).astype(jnp.int32), rank, [table_qkv_a, table_down_b], [table_out_b, table_ffn_a], tables_b,
            table_out_a, tables_ffn, owners,
        )
        landed = lax.all_to_all(packed, ("fsdp", "ctx", "tp"), 0, 0, tiled=True)
        part, unit_part = width // owners, unit_cols * n_t // owners
        done = spread_gradients(every, landed, a_qkv.shape[0], rank_r, unit_part, part)
        done = [v.transpose(0, 2, 1) if i in (0, 2, 4, 6) else v for i, v in enumerate(done)]
        done[1] = done[1].transpose(0, 2, 1, 3)
        grad_tokens = both_halves(rank, grad_tok, after(tok_far, done[0]))
        return (block_output[None], grad_tokens[None], *done)
    block_output = from_xor(block_output, 1, n_f, f_rank)
    grad_tokens = from_xor(both_halves(rank, grad_tok, tok_far), 1, n_f, f_rank)
    early, early_sizes = pack([
        by_tp(*table_out_a), natural(table_out_b), natural(table_ffn_a), *[place(t) for t in tables_ffn],
    ])
    late, late_sizes = pack([
        own_part(natural(table_qkv_a)), *[place(t) for t in tables_b], own_part(natural(table_down_b)),
    ])
    landed = lax.all_to_all(jnp.concatenate([late, early], axis=1), ("fsdp", "ctx", "tp"), 0, 0, tiled=True)
    split = rank_r * sum(late_sizes)
    spread = jnp.dot(onehot.astype(BF), landed, preferred_element_type=F32)
    done = take_apart(spread[:, :split], late_sizes) + take_apart(spread[:, split:], early_sizes)
    swap = lambda values: values.transpose(0, 2, 1)
    return (
        block_output[None],
        grad_tokens[None],
        swap(done[0]),
        jnp.stack(done[1:4], axis=2),
        swap(done[5]),
        done[6],
        swap(done[7]),
        jnp.stack(done[8:10], axis=2),
        swap(done[10]),
        done[4],
    )


def solution(mesh):
    in_specs = (
        P("fsdp", "ctx", None), P("fsdp", "ctx"), P("fsdp"), P("fsdp", None, "tp"), P("fsdp", "tp"), P("tp"),
        P("tp", "fsdp"), P("fsdp", None, "tp"), P("tp", "fsdp"),
        P(), P(), P(), P(), P(), P(), P(), P(), P(), P(),
        P("fsdp", "ctx", None),
    )
    out_specs = (
        P("fsdp", "ctx", None),
        P("fsdp", "ctx", None),
        P(None, ("fsdp", "ctx", "tp"), None),
        P(None, None, None, ("fsdp", "ctx", "tp")),
        P(None, ("fsdp", "ctx", "tp"), None),
        P(None, None, ("fsdp", "ctx", "tp")),
        P(None, ("fsdp", "ctx", "tp"), None),
        P(None, None, None, ("fsdp", "ctx", "tp")),
        P(None, ("fsdp", "ctx", "tp"), None),
        P(None, None, ("fsdp", "ctx", "tp")),
    )
    return jax.shard_map(body, mesh=mesh, in_specs=in_specs, out_specs=out_specs, check_vma=False)
```

```python
import jax
import jax.numpy as jnp
from jax import lax
from jax.experimental import pallas as pl
from jax.experimental.pallas import tpu as pltpu
from jax.sharding import PartitionSpec as P

HD = 64
DOC_MOST = 800
DOCS = 8
BF = jnp.bfloat16
F32 = jnp.float32
HI = lax.Precision.HIGHEST


def dot(a, b):
    return jnp.dot(a, b, preferred_element_type=F32)


def dot_t(a, b):
    return lax.dot_general(a, b, (((1,), (1,)), ((), ())), preferred_element_type=F32)


def t_dot(a, b):
    return lax.dot_general(a, b, (((0,), (0,)), ((), ())), preferred_element_type=F32)


def xor_order(size):
    order, bit = [0], size // 2
    while bit:
        order, bit = order + [step ^ bit for step in order], bit // 2
    return order


def after(values, *done):
    return lax.optimization_barrier((values, *done))[0]


def far_blocks(shard, dim):
    size = lax.axis_size("fsdp")
    own, bit = shard, size // 2
    while True:
        got = lax.ppermute(own, "fsdp", [(i, i ^ bit) for i in range(size)])
        if bit == 2:
            return own, got
        own, bit = jnp.concatenate([own, got], axis=dim), bit // 2


def near_blocks(own, got, dim):
    both = jnp.concatenate([own, got], axis=dim)
    size = lax.axis_size("fsdp")
    return [both, lax.ppermute(both, "fsdp", [(i, i ^ 1) for i in range(size)])]


def to_xor(values, dim, size, rank):
    block = values.shape[dim] // size
    return jnp.concatenate(
        [lax.dynamic_slice_in_dim(values, (rank ^ step) * block, block, dim) for step in xor_order(size)],
        axis=dim,
    )


def from_xor(values, dim, size, rank):
    block = values.shape[dim] // size
    bits = size.bit_length() - 1
    pieces = []
    for natural in range(size):
        mixed = rank ^ natural
        place = sum(((mixed >> j) & 1) << (bits - 1 - j) for j in range(bits))
        pieces.append(lax.dynamic_slice_in_dim(values, place * block, block, dim))
    return jnp.concatenate(pieces, axis=dim)


def shift(values, hop, size):
    pairs = [(i, i + hop) for i in range(size) if 0 <= i + hop < size]
    return lax.ppermute(values, "ctx", pairs)


LANES = 128
BLK = 256
BIG = -1e30


def spec(shape, index):
    return pl.BlockSpec(shape, index)


def call(kernel, grid, ins, in_specs, outs, out_specs, scratch=(), prefetch=0, flops=0, nbytes=0, exps=0, aliases=None, cost=1):
    return pl.pallas_call(
        kernel,
        out_shape=outs,
        grid_spec=pltpu.PrefetchScalarGridSpec(
            num_scalar_prefetch=prefetch, grid=grid, in_specs=in_specs, out_specs=out_specs, scratch_shapes=list(scratch)
        ),
        compiler_params=pltpu.CompilerParams(
            dimension_semantics=("arbitrary",) * len(grid), vmem_limit_bytes=56 * 2**20
        ),
        input_output_aliases=aliases or {},
        cost_estimate=pl.CostEstimate(flops=cost, bytes_accessed=1, transcendentals=0),
    )(*ins)


def whole(values):
    return spec(values.shape, lambda *_: (0,) * len(values.shape))


def lane_ids(rows):
    return lax.broadcasted_iota(jnp.int32, (rows, LANES), 1)


def split3(values):
    high = values.astype(BF)
    rest = values - high.astype(F32)
    mid = rest.astype(BF)
    return high, mid, (rest - mid.astype(F32)).astype(BF)


def split_lanes(values, n):
    lane = lane_ids(values.shape[0])
    values = jnp.where(lane < n, values, 0.0)
    high, mid, low = (part.astype(F32) for part in split3(values))
    return high + pltpu.roll(mid, n, 1) + pltpu.roll(low, 2 * n, 1)


def exact_dot(mask, values):
    high, mid, low = split3(values)
    return dot(mask, high) + dot(mask, mid) + dot(mask, low)


def norm_terms(blocks):
    width = sum(b.shape[1] for b in blocks)
    total = sum(jnp.sum(b * b, axis=1, keepdims=True) for b in blocks)
    return lax.rsqrt(total / width + 1e-05)


def pair_lanes(pair, n_heads, kind):
    lane = lax.broadcasted_iota(jnp.int32, (LANES, LANES), 1)
    to = lane & (HD - 1)
    head = jnp.where(lane >= HD, 2 * pair, 2 * pair + 1)
    gate_at = 3 if kind == "k" else 0
    part = to - gate_at
    source = jnp.where((part >= 0) & (part < 3), part * n_heads + head, -1)
    if kind != "d":
        ones = to - (3 - gate_at)
        source = jnp.where((ones >= 0) & (ones < 3), 3 * n_heads + DOCS, source)
        source = jnp.where((to >= 8) & (to < 8 + DOCS), to - 8 + 3 * n_heads, source)
    return (lax.broadcasted_iota(jnp.int32, (LANES, LANES), 0) == source).astype(BF)


def pair_of(values, gate_parts, select):
    extra = dot(gate_parts, select).astype(BF)
    low = lane_ids(values.shape[0]) < HD
    return jnp.where(low, values, extra), jnp.where(low, extra, values)


def pair_ones(values):
    low = lane_ids(values.shape[0]) < HD
    one = jnp.ones((), BF)
    return jnp.where(low, values, one), jnp.where(low, one, values)


def block_at(index):
    return pl.ds(pl.multiple_of(index * BLK, BLK), BLK)


def causal_from(rows, first):
    row = lax.broadcasted_iota(jnp.int32, (rows, BLK), 0)
    return row + first >= lax.broadcasted_iota(jnp.int32, (rows, BLK), 1)


def lane_column(acc, lane_at):
    return jnp.sum(jnp.where(lane_ids(acc.shape[0]) == lane_at, acc, 0.0), axis=1, keepdims=True)


def attention_forward(bounds, q, k, v, gq, gk, gates, total, n_heads):
    rows, keys = q.shape[0], k.shape[0]
    n_before = (keys - rows) // BLK
    pairs = n_heads // 2
    assert rows == 2 * BLK

    def kernel(
        lo_ref, q_ref, k_ref, v_ref, gq_ref, gk_ref, gate_ref, tot_ref, mixed_ref, float_ref, one_ref, two_ref,
        qx, scores, tops, parts, accs, log_ref,
    ):
        pair = pl.program_id(0)
        pick_k = pair_lanes(pair, n_heads, "k")
        for side, value in enumerate(pair_of(q_ref[...], gq_ref[...], pair_lanes(pair, n_heads, "q"))):
            qx[side] = value
        both, late, early = slice(0, rows), slice(BLK, rows), slice(0, BLK)

        def score(kb, here, at, mask=None, first=False):
            for side, key in enumerate(pair_of(k_ref[here, :], gk_ref[here, :], pick_k)):
                s = dot_t(qx[side, at, :], key)
                if mask is not None:
                    s = jnp.where(mask, s, BIG)
                scores[side, at, here] = s
                top = jnp.maximum(s[:, :LANES], s[:, LANES:])
                tops[side, at, :] = top if first else jnp.maximum(tops[side, at, :], top)

        def gather(here, at, first=False):
            for side in range(2):
                w = jnp.exp(scores[side, at, here] - tops[side, at, :1])
                part = w[:, :LANES] + w[:, LANES:]
                acc = dot(w.astype(BF), v_ref[here, :])
                parts[side, at, :] = part if first else parts[side, at, :] + part
                accs[side, at, :] = acc if first else accs[side, at, :] + acc

        own = [slice(b * BLK, (b + 1) * BLK) for b in (n_before, n_before + 1)]
        low, high = lo_ref[0], jnp.minimum(lo_ref[1], n_before)
        score(n_before, own[0], both, causal_from(rows, 0), True)
        score(n_before + 1, own[1], late, causal_from(BLK, 0))
        pl.loop(high, n_before)(lambda kb: score(kb, block_at(kb), both))
        pl.loop(low, high)(lambda kb: score(kb, block_at(kb), early))
        for side in range(2):
            tops[side] = jnp.broadcast_to(jnp.max(tops[side], axis=1, keepdims=True), (rows, LANES))
        gather(own[0], both, True)
        gather(own[1], late)
        pl.loop(high, n_before)(lambda kb: gather(block_at(kb), both))
        pl.loop(low, high)(lambda kb: gather(block_at(kb), early))
        lane = lane_ids(rows)
        results, logs = [], jnp.zeros((rows, LANES), F32)
        for side in range(2):
            row_total = jnp.sum(parts[side], axis=1, keepdims=True)
            results.append(accs[side] / row_total)
            logs = jnp.where(lane == 2 * pair + side, tops[side] + jnp.log(row_total), logs)
        out = jnp.where(lane < HD, results[0], results[1])
        mixed_ref[...] = out.astype(BF)
        float_ref[...] = out

        @pl.when(pair == 0)
        def _():
            log_ref[...] = logs

        @pl.when(pair > 0)
        def _():
            log_ref[...] = jnp.where((lane >> 1) == pair, logs, log_ref[...])

        @pl.when(pair == pairs - 1)
        def _():
            values = gate_ref[...] - log_ref[...]
            rest = gq_ref[...].astype(F32)
            one_ref[...] = jnp.where(lane < 3 * n_heads, split_lanes(values, n_heads), rest).astype(BF)
            values = values + tot_ref[:1, :]
            two_ref[...] = jnp.where(lane < 3 * n_heads, split_lanes(values, n_heads), rest).astype(BF)

    here = lambda n: spec((n, LANES), lambda i, *_: (0, i))
    shared = lambda n: spec((n, LANES), lambda i, *_: (0, 0))
    return call(
        kernel,
        (pairs,),
        (bounds, q, k, v, gq, gk, gates, total),
        [here(rows), here(keys), here(keys), shared(rows), shared(keys), shared(rows), shared(8)],
        (
            jax.ShapeDtypeStruct(q.shape, BF), jax.ShapeDtypeStruct(q.shape, F32),
            jax.ShapeDtypeStruct((rows, LANES), BF), jax.ShapeDtypeStruct((rows, LANES), BF),
        ),
        (here(rows), here(rows), shared(rows), shared(rows)),
        [pltpu.VMEM((2, rows, LANES), BF), pltpu.VMEM((2, rows, keys), F32)]
        + [pltpu.VMEM((2, rows, LANES), F32)] * 3 + [pltpu.VMEM((rows, LANES), F32)],
        prefetch=1,
    )


def attention_dq(bounds, q, k, v, d, gq, gk, n_heads, n_far):
    rows, keys = q.shape[0], k.shape[0]
    n_before = (keys - rows) // BLK
    pairs = n_heads // 2

    def kernel(lo_ref, q_ref, k_ref, v_ref, d_ref, gq_ref, gk_ref, gd_ref, dq_ref, row_ref, far_ref, qx, dx, accs):
        pair = pl.program_id(0)
        lane = lane_ids(rows)
        pick_k = pair_lanes(pair, n_heads, "k")
        for side, value in enumerate(pair_of(q_ref[...], gq_ref[...], pair_lanes(pair, n_heads, "q"))):
            qx[side] = value
        for side, value in enumerate(pair_of(d_ref[...], gd_ref[...], pair_lanes(pair, n_heads, "d"))):
            dx[side] = value
        both, late, early = slice(0, rows), slice(BLK, rows), slice(0, BLK)

        @pl.when(pair == 0)
        def _():
            far_ref[...] = jnp.zeros_like(far_ref)
            row_ref[...] = jnp.zeros_like(row_ref)

        accs[...] = jnp.zeros_like(accs)

        def block(here, at, mask=None):
            values = pair_ones(v_ref[here, :])
            for side, key in enumerate(pair_of(k_ref[here, :], gk_ref[here, :], pick_k)):
                s = dot_t(qx[side, at, :], key)
                if mask is not None:
                    s = jnp.where(mask, s, BIG)
                ds = (jnp.exp(s) * dot_t(dx[side, at, :], values[side])).astype(BF)
                accs[side, at, :] += dot(ds, key)

        def earlier(kb, at):
            block(block_at(kb), at)

            @pl.when(kb == n_far - 1)
            def _():
                for side in range(2):
                    moved = jnp.sum(jnp.where(lane == HD * (1 - side), accs[side], 0.0))
                    far_ref[...] += jnp.where(lane[:8] == 2 * pair + side, moved, 0.0)

        low, high = lo_ref[0], jnp.minimum(lo_ref[1], n_before)
        pl.loop(low, high)(lambda kb: earlier(kb, early))
        pl.loop(high, n_before)(lambda kb: earlier(kb, both))
        block(slice(n_before * BLK, (n_before + 1) * BLK), both, causal_from(rows, 0))
        block(slice((n_before + 1) * BLK, (n_before + 2) * BLK), late, causal_from(BLK, 0))
        dq_ref[...] = (jnp.where(lane < HD, accs[0], accs[1]) * HD ** (-0.5)).astype(BF)
        for side in range(2):
            total = lane_column(accs[side], HD * (1 - side))
            row_ref[...] = jnp.where(lane == 2 * pair + side, total, row_ref[...])

    here = lambda n: spec((n, LANES), lambda i, *_: (0, i))
    shared = lambda n: spec((n, LANES), lambda i, *_: (0, 0))
    return call(
        kernel,
        (pairs,),
        (bounds, q, k, v, d, gq, gk, d),
        [here(rows), here(keys), here(keys), here(rows), shared(rows), shared(keys), spec((rows, LANES), lambda i, *_: (0, pairs))],
        (
            jax.ShapeDtypeStruct(q.shape, BF), jax.ShapeDtypeStruct((rows, LANES), F32),
            jax.ShapeDtypeStruct((8, LANES), F32),
        ),
        (here(rows), shared(rows), shared(8)),
        [pltpu.VMEM((2, rows, LANES), BF)] * 2 + [pltpu.VMEM((2, rows, LANES), F32)],
        prefetch=1, cost=3363750000
    )


def score_block(kx, vx, queries, grads, at, dks, dvs, mask=None, first=False):
    for side in range(2):
        s = dot_t(kx[side, at, :], queries[side])
        if mask is not None:
            s = jnp.where(mask, s, BIG)
        w = jnp.exp(s)
        ds = (w * dot_t(vx[side, at, :], grads[side])).astype(BF)
        dk, dv = dot(ds, queries[side]), dot(w.astype(BF), grads[side])
        dks[side, at, :] = dk if first else dks[side, at, :] + dk
        dvs[side, at, :] = dv if first else dvs[side, at, :] + dv


def attention_dkv_own(k, v, q, d, gq, gk, n_heads):
    rows = q.shape[0]
    place = k.shape[0] // rows - 1
    pairs = n_heads // 2

    def kernel(k_ref, v_ref, q_ref, d_ref, gq_ref, gd_ref, gk_ref, dk_ref, dv_ref, own_ref, kx, vx, dks, dvs):
        pair = pl.program_id(0)
        lane = lane_ids(rows)
        pick_q, pick_d = (pair_lanes(pair, n_heads, "q"), pair_lanes(pair, n_heads, "d"))
        for side, value in enumerate(pair_of(k_ref[...], gk_ref[...], pair_lanes(pair, n_heads, "k"))):
            kx[side] = value
        for side, value in enumerate(pair_ones(v_ref[...])):
            vx[side] = value
        both, late, early = slice(0, rows), slice(BLK, rows), slice(0, BLK)

        @pl.when(pair == 0)
        def _():
            own_ref[...] = jnp.zeros_like(own_ref)

        def load(here):
            return pair_of(q_ref[here, :], gq_ref[here, :], pick_q), pair_of(d_ref[here, :], gd_ref[here, :], pick_d)

        keep = lax.broadcasted_iota(jnp.int32, (rows, BLK), 0) - BLK <= lax.broadcasted_iota(jnp.int32, (rows, BLK), 1)
        first_keep = lax.broadcasted_iota(jnp.int32, (BLK, BLK), 0) <= lax.broadcasted_iota(jnp.int32, (BLK, BLK), 1)
        score_block(kx, vx, *load(late), both, dks, dvs, keep, True)
        score_block(kx, vx, *load(early), early, dks, dvs, first_keep)
        for side in range(2):
            column = lane_column(dks[side], HD * (1 - side) + 3)
            own_ref[...] = jnp.where(lane == 2 * pair + side, column, own_ref[...])
        dk_ref[...] = jnp.where(lane < HD, dks[0], dks[1])
        dv_ref[...] = jnp.where(lane < HD, dvs[0], dvs[1])

    heads_spec = lambda n: spec((n, LANES), lambda i, *_: (0, i))
    shared = lambda n: spec((n, LANES), lambda i, *_: (0, 0))
    keys_spec = spec((rows, LANES), lambda i, *_: (place, i))
    return call(
        kernel, (pairs,), (k, v, q, d, gq, d, gk),
        [
            keys_spec, keys_spec, heads_spec(rows), heads_spec(rows), shared(rows),
            spec((rows, LANES), lambda i, *_: (0, pairs)), spec((rows, LANES), lambda i, *_: (place, 0)),
        ],
        (jax.ShapeDtypeStruct(q.shape, F32), jax.ShapeDtypeStruct(q.shape, F32), jax.ShapeDtypeStruct((rows, LANES), F32)),
        (heads_spec(rows), heads_spec(rows), shared(rows)),
        [pltpu.VMEM((2, rows, LANES), BF)] * 2 + [pltpu.VMEM((2, rows, LANES), F32)] * 2, cost=2294250000
    )


def attention_dkv_next(bounds, k, v, q_one, q_two, d_one, d_two, gkn, dk, dv, n_heads):
    rows, tail = q_one.shape[0], q_two.shape[0]
    place = k.shape[0] // rows - 1
    pairs = n_heads // 2
    assert 0 < tail - BLK <= BLK

    def kernel(
        hi_ref, k_ref, v_ref, q1_ref, d1_ref, gq1_ref, gd1_ref, q2_ref, d2_ref, gq2_ref, gd2_ref, gkn_ref,
        dk_own, dv_own, dk_ref, dv_ref, next_ref, kx, vx, dks, dvs,
    ):
        pair = pl.program_id(0)
        lane = lane_ids(rows)
        both, late, early = slice(0, rows), slice(BLK, rows), slice(0, BLK)
        few, many = hi_ref[0], hi_ref[1]

        @pl.when(pair == 0)
        def _():
            next_ref[...] = jnp.zeros_like(next_ref)

        @pl.when(many > 0)
        def _():
            pick_q, pick_d = (pair_lanes(pair, n_heads, "q"), pair_lanes(pair, n_heads, "d"))
            for side, value in enumerate(pair_of(k_ref[...], gkn_ref[...], pair_lanes(pair, n_heads, "k"))):
                kx[side] = value
            for side, value in enumerate(pair_ones(v_ref[...])):
                vx[side] = value
            dks[...] = jnp.zeros_like(dks)
            dvs[...] = jnp.zeros_like(dvs)

            def block(refs, here, at):
                q_ref, gq_ref, d_ref, gd_ref = refs
                queries = pair_of(q_ref[here, :], gq_ref[here, :], pick_q)
                score_block(kx, vx, queries, pair_of(d_ref[here, :], gd_ref[here, :], pick_d), at, dks, dvs)

            one, two = (q1_ref, gq1_ref, d1_ref, gd1_ref), (q2_ref, gq2_ref, d2_ref, gd2_ref)
            pl.loop(0, jnp.minimum(few, 2))(lambda j: block(one, block_at(j), both))
            pl.loop(few, jnp.minimum(many, 2))(lambda j: block(one, block_at(j), late))
            pl.when(few > 2)(lambda: block(two, early, both))
            pl.when((few <= 2) & (many > 2))(lambda: block(two, early, late))
            pl.when(many > 3)(lambda: block(two, slice(BLK, tail), both))
            for side in range(2):
                value = lane_column(dks[side], HD * (1 - side) + 3)
                next_ref[...] = jnp.where(lane == 2 * pair + side, value, next_ref[...])
            dk_ref[...] = (dk_own[...] + jnp.where(lane < HD, dks[0], dks[1])).astype(BF)
            dv_ref[...] = (dv_own[...] + jnp.where(lane < HD, dvs[0], dvs[1])).astype(BF)

        @pl.when(many == 0)
        def _():
            dk_ref[...] = dk_own[...].astype(BF)
            dv_ref[...] = dv_own[...].astype(BF)

    heads_spec = lambda n: spec((n, LANES), lambda i, *_: (0, i))
    shared = lambda n: spec((n, LANES), lambda i, *_: (0, 0))
    last = lambda n: spec((n, LANES), lambda i, *_: (0, pairs))
    keys_spec = spec((rows, LANES), lambda i, *_: (place, i))
    return call(
        kernel, (pairs,), (bounds, k, v, q_one, d_one, q_one, d_one, q_two, d_two, q_two, d_two, gkn, dk, dv),
        [
            keys_spec, keys_spec, heads_spec(rows), heads_spec(rows), last(rows), last(rows),
            heads_spec(tail), heads_spec(tail), last(tail), last(tail), shared(rows), heads_spec(rows), heads_spec(rows),
        ],
        (jax.ShapeDtypeStruct(dk.shape, BF), jax.ShapeDtypeStruct(dk.shape, BF), jax.ShapeDtypeStruct((rows, LANES), F32)),
        (heads_spec(rows), heads_spec(rows), shared(rows)),
        [pltpu.VMEM((2, rows, LANES), BF)] * 2 + [pltpu.VMEM((2, rows, LANES), F32)] * 2,
        prefetch=1, cost=2932500000
    )


def project(offs, x, x_far, tail, gain, w, side_w, qkv_b, bias, cols, rank_r, filled=None, before=0):
    width = gain.shape[1]
    block = width // 4
    own = filled is None
    rows = x.shape[0] // (2 * BLK) * 2 * BLK
    row_steps = 1 if own else 2
    parts = ("q", "k", "v") if own else ("k", "v")
    assert rows == 2 * BLK and BLK <= tail <= rows - 32

    def kernel(*refs):
        offs_ref, x_ref = refs[0], refs[1]
        at = 2
        if not own:
            far_ref, at = refs[2], 3
        gain_ref, *pieces, side_ref, b_ref, bias_ref = refs[at : at + 8]
        at += 8 + (0 if own else 3)
        outs, scr = refs[at:-3], refs[-3:]
        part, step = pl.program_id(0), pl.program_id(1)
        n_outs = dict(zip(("n", "low", "q", "k", "v", "logits") if own else ("k", "v", "logits"), outs))
        scr, low_scr, joint = scr
        at_rows = pl.ds(pl.multiple_of(step * rows, rows), rows)

        @pl.when(part == 0)
        def _():
            blocks = []
            for k in range(4):
                here = pl.ds(pl.multiple_of(offs_ref[k], LANES), block)
                value = x_ref[:, here]
                if not own:
                    far = jnp.concatenate([far_ref[:BLK, here], far_ref[tail + 32 - BLK : tail + 32, here]], axis=0)
                    value = jnp.where(step == 0, far, value)
                blocks.append(value.astype(F32))
            factor = norm_terms(blocks)
            for k in range(4):
                here = pl.ds(pl.multiple_of(offs_ref[k], LANES), block)
                scr[at_rows, k * block : (k + 1) * block] = (blocks[k] * factor * gain_ref[:, here]).astype(BF)
            side = dot(scr[at_rows, :], side_ref[...])
            low = side[:, LANES - rank_r :].astype(BF)
            low_scr[at_rows, :rank_r] = low
            n_outs["logits"][at_rows, :] = side + bias_ref[...]
            if own:
                n_outs["n"][...] = scr[...]
                n_outs["low"][...] = low

        @pl.when(step == 0)
        def _():
            for k in range(4):
                joint[k * block : (k + 1) * block, :] = pieces[k][...]

        value = dot(scr[at_rows, :], joint[...])
        value = (value + dot(low_scr[at_rows, :rank_r], b_ref[...])).astype(BF)
        for n, name in enumerate(parts):
            @pl.when(part == n)
            def _(name=name):
                out = n_outs[name]
                out[at_rows, :] = (value.astype(F32) * HD ** (-0.5)).astype(BF) if name == "q" else value

    keys = before + rows if own else filled[0].shape[0]
    ins = [offs, x] + ([] if own else [x_far]) + [gain, *w, side_w, qkv_b, bias] + ([] if own else list(filled))
    row_spec = spec((rows, width), lambda i, *_: (0, 0))
    in_specs = [row_spec] + ([] if own else [whole(x_far)])
    first = 0 if own else 1
    column = lambda n: spec((n, cols), lambda j, *_: (0, j + first))
    in_specs += [whole(gain), *[column(block)] * 4, whole(side_w), column(rank_r), whole(bias)]
    if not own:
        in_specs += [pl.BlockSpec(memory_space=pl.ANY)] * 3
    some = row_steps * rows
    at_keys = lambda n: spec((some, n), lambda *_: (before // some if own else 0, 0))
    outs = [jax.ShapeDtypeStruct((keys, cols), BF)] * 2 + [jax.ShapeDtypeStruct((keys, LANES), F32)]
    out_specs = [at_keys(cols), at_keys(cols), at_keys(LANES)]
    if own:
        here = lambda n: spec((rows, n), lambda *_: (0, 0))
        outs = [
            jax.ShapeDtypeStruct((rows, width), BF),
            jax.ShapeDtypeStruct((rows, rank_r), BF),
            jax.ShapeDtypeStruct((rows, cols), BF),
        ] + outs
        out_specs = [here(width), here(rank_r), here(cols)] + out_specs
    return call(
        kernel, (len(parts), row_steps), ins, in_specs, tuple(outs), tuple(out_specs),
        [pltpu.VMEM((some, width), BF), pltpu.VMEM((some, LANES), BF), pltpu.VMEM((width, cols), BF)], prefetch=1,
        aliases={} if own else {11: 0, 12: 1, 13: 2},
    )


def gate_tables(logits, seg_keys, seg_row, n_heads, rows):
    keys = logits.shape[0]
    before = keys - rows
    one = 3 * n_heads + DOCS

    def kernel(logit_ref, seg_ref, row_ref, gq_ref, gk_ref, gkn_ref, gate_ref, tot_ref):
        lane = lane_ids(BLK)
        doc = lane - 3 * n_heads + 1
        doc_lane = (doc > 0) & (doc <= DOCS)
        inner = lax.broadcasted_iota(jnp.int32, (BLK, BLK), 1) > lax.broadcasted_iota(jnp.int32, (BLK, BLK), 0)
        later = inner.astype(BF)

        def forget(at):
            value = logit_ref[at, :]
            value = jnp.minimum(value, 0.0) - jnp.log(1.0 + jnp.exp(-jnp.abs(value)))
            return jnp.where((lane < n_heads) & (seg_ref[at, :] > 0), value, 0.0)

        def lanes(values, docs):
            return (split_lanes(values, n_heads) + docs + jnp.where(lane == one, 1.0, 0.0)).astype(BF)

        def docs_k(at):
            return jnp.where(doc_lane & (doc != seg_ref[at, :]), BIG, 0.0)

        def suffix(first, last, carry, out_ref, base):
            for b in range(last - 1, first - 1, -1):
                at = slice(b * BLK, (b + 1) * BLK)
                values = forget(at)
                sums = exact_dot(later, values) + carry
                out_ref[b * BLK - base : (b + 1) * BLK - base, :] = lanes(sums, docs_k(at))
                carry = carry + jnp.sum(values, axis=0, keepdims=True)
            return carry

        n_before, n_all = before // BLK, keys // BLK
        zero = jnp.zeros((1, LANES), F32)
        near = suffix((before - rows) // BLK, n_before, zero, gk_ref, 0)
        tot_ref[...] = jnp.broadcast_to(near, tot_ref.shape)
        suffix(0, (before - rows) // BLK, near, gk_ref, 0)
        suffix(n_before, n_all, zero, gkn_ref, before)
        own = jnp.concatenate([forget(slice(b * BLK, (b + 1) * BLK)) for b in range(n_before, n_all)], axis=0)
        for b in range(rows // BLK):
            at = slice(before + b * BLK, before + (b + 1) * BLK)
            here = slice(b * BLK, (b + 1) * BLK)
            q_pos = lax.broadcasted_iota(jnp.int32, (BLK, rows), 0) + b * BLK
            k_pos = lax.broadcasted_iota(jnp.int32, (BLK, rows), 1)
            same = (row_ref[...] == seg_ref[at, :]) & (k_pos <= q_pos)
            sums = exact_dot(same.astype(BF), own)
            gate_ref[here, :] = sums
            gq_ref[here, :] = lanes(sums, jnp.where(doc_lane & (doc == seg_ref[at, :]), 1.0, 0.0))
            gk_ref[at, :] = lanes(-sums, docs_k(at))

    shape = lambda n, t: jax.ShapeDtypeStruct((n, LANES), t)
    outs = (shape(rows, BF), shape(keys, BF), shape(rows, BF), shape(rows, F32), shape(8, F32))
    return call(
        kernel, (1,), (logits, seg_keys, seg_row), [whole(logits), whole(seg_keys), whole(seg_row)],
        outs, tuple(whole(o) for o in outs), flops=10**8, nbytes=4 * 10**6,
    )


def weight_halves(w):
    half = w[0].shape[0] // 2
    at = lambda row: spec((half, w[0].shape[1]), lambda *_: (row, 0))
    return [at(0), at(0), at(1), at(1)]


def out_projection(offs, rank, x, mixed_own, mixed_far, w, a_own, a_far, out_b, gain, ffn_a):
    rows, width = x.shape
    block = width // 4
    rank_r = a_own.shape[1]

    def kernel(
        offs_ref, rank_ref, x_ref, mo, mf, wo0, wo1, wf0, wf1, ao, af, b_ref, gain_ref, fa, h_ref, n_ref, low_ref, lo_ref
    ):
        def run(m0, m1, w0, w1, a0, a1):
            low = (dot(m0[...], a0[...]) + dot(m1[...], a1[...])).astype(BF)
            lo_ref[...] = low
            for half in range(2):
                both = dot(m0[...], w0[half][...]) + dot(m1[...], w1[half][...])
                both = both + dot(low, b_ref[:, 2 * half * block : 2 * (half + 1) * block])
                for j in range(2):
                    k = 2 * half + j
                    here = pl.ds(pl.multiple_of(offs_ref[k], LANES), block)
                    value = x_ref[:, here].astype(F32) + both[:, j * block : (j + 1) * block]
                    h_ref[:, k * block : (k + 1) * block] = value

        pl.when(rank_ref[0] == 0)(lambda: run(mo, mf, (wo0, wo1), (wf0, wf1), ao, af))
        pl.when(rank_ref[0] != 0)(lambda: run(mf, mo, (wf0, wf1), (wo0, wo1), af, ao))
        value = h_ref[...]
        normed = (value * norm_terms([value]) * gain_ref[...]).astype(BF)
        n_ref[...] = normed
        low_ref[...] = dot(normed, fa[...]).astype(BF)

    rowed = whole
    outs = (
        jax.ShapeDtypeStruct((rows, width), F32), jax.ShapeDtypeStruct((rows, width), BF),
        jax.ShapeDtypeStruct((rows, rank_r), BF), jax.ShapeDtypeStruct((rows, rank_r), BF),
    )
    ins = (offs, rank, x, mixed_own, mixed_far, *w, *w, a_own, a_far, out_b, gain, ffn_a)
    return call(
        kernel, (1,), ins,
        [rowed(x), rowed(mixed_own), rowed(mixed_far)] + weight_halves(w) + [whole(v) for v in ins[9:]],
        outs, tuple(rowed(o) for o in outs), prefetch=2, flops=4 * rows * width * mixed_own.shape[1],
        nbytes=4 * width * mixed_own.shape[1] + 8 * rows * width, cost=1725000000
    )


def feed_forward(rank, normed, low, cot, grad_low, gate_up, down, ffn_b, down_a):
    rows, width = normed.shape
    block = width // 4
    half = rows // 2
    rank_r = low.shape[1]
    unit_cols = down_a.shape[0]
    tile = 512 if unit_cols % 512 == 0 else unit_cols
    tiles = unit_cols // tile
    down_at = down[0].shape[1] // tile - tiles

    def kernel(
        rank_ref, x_ref, low_ref, cot_ref, gl_ref, *rest,
    ):
        pieces, rest = rest[:12], rest[12:]
        bg_ref, bu_ref, ad_ref, *rest, wg, wu, wd = rest
        step = pl.program_id(0)
        units_ref, gg_ref, gu_ref, far_ref, own_ref, own_low_ref, part_ref, part_low_ref = rest

        @pl.when(step == 0)
        def _():
            part_ref[...] = jnp.zeros_like(part_ref)
            part_low_ref[...] = jnp.zeros_like(part_low_ref)

        for n, joint in enumerate((wg, wu, wd)):
            for k in range(4):
                joint[k * block : (k + 1) * block, :] = pieces[4 * n + k][...]
        gate = dot(x_ref[...], wg[...]) + dot(low_ref[...], bg_ref[...])
        up = dot(x_ref[...], wu[...]) + dot(low_ref[...], bu_ref[...])
        grad = dot(cot_ref[...], wd[...]) + dot_t(gl_ref[...], ad_ref[...])
        sig = jax.nn.sigmoid(gate)
        act = gate * sig
        units_ref[...] = (act * up).astype(BF)
        gg = (grad * up * sig * (1.0 + gate * (1.0 - sig))).astype(BF)
        gu = (grad * act).astype(BF)
        gg_ref[...] = gg
        gu_ref[...] = gu
        part_low_ref[:, :rank_r] += dot_t(gg, bg_ref[...]) + dot_t(gu, bu_ref[...])
        part_ref[...] += dot_t(gg, wg[...]) + dot_t(gu, wu[...])

        @pl.when(step == tiles - 1)
        def _():
            mine = pl.ds(pl.multiple_of(rank_ref[0] * half, half), half)
            theirs = pl.ds(pl.multiple_of((1 - rank_ref[0]) * half, half), half)
            far_ref[:, :width] = part_ref[theirs, :].astype(BF)
            far_ref[:, width:] = split_lanes(part_low_ref[theirs, :], rank_r).astype(BF)
            own_ref[...] = part_ref[mine, :]
            own_low_ref[...] = part_low_ref[mine, :]

    out = jax.ShapeDtypeStruct((rows, unit_cols), BF)
    out_spec = spec((rows, tile), lambda i, *_: (0, i))
    sums = (jax.ShapeDtypeStruct((rows, width), F32), jax.ShapeDtypeStruct((rows, LANES), F32))
    ends = (
        jax.ShapeDtypeStruct((half, width + LANES), BF), jax.ShapeDtypeStruct((half, width), F32),
        jax.ShapeDtypeStruct((half, LANES), F32),
    )
    return call(
        kernel,
        (tiles,),
        (rank, normed, low, cot, grad_low, *gate_up, *gate_up, *down, ffn_b, ffn_b, down_a),
        [
            whole(normed), whole(low), whole(cot), whole(grad_low),
            *[spec((block, tile), lambda i, *_: (0, i)) for _ in range(4)],
            *[spec((block, tile), lambda i, *_: (0, i + tiles)) for _ in range(4)],
            *[spec((block, tile), lambda i, *_: (0, i + down_at)) for _ in range(4)],
            spec((rank_r, tile), lambda i, *_: (0, i)),
            spec((rank_r, tile), lambda i, *_: (0, i + tiles)),
            spec((tile, rank_r), lambda i, *_: (i, 0)),
        ],
        (out, out, out, *ends),
        (out_spec, out_spec, out_spec, *[whole(e) for e in ends]),
        [pltpu.VMEM(e.shape, F32) for e in sums] + [pltpu.VMEM((width, tile), BF)] * 3,
        prefetch=1, cost=4657500000
    )


def whole_low(parts, n):
    parts = parts.astype(F32)
    return parts[:, :n] + parts[:, n : 2 * n] + parts[:, 2 * n : 3 * n]


def middle(rank, own, got, own_low, hidden, cot, gain, ffn_a, out_b, w, a_own, a_far):
    half, width = own.shape
    depth = width // 2
    rank_r = out_b.shape[0]
    cols = a_own.shape[0]

    def kernel(
        rank_ref, own_ref, got_ref, low_ref, h_ref, cot_ref, gain_ref, fa, b_ref, wo0, wo1, wf0, wf1, ao, af,
        gh_ref, ghb_ref, glf_ref, glo_ref, mine_ref, far_ref,
    ):
        ffn_low = (low_ref[:, :rank_r] + whole_low(got_ref[:, width:], rank_r)).astype(BF)
        glf_ref[...] = ffn_low
        incoming = own_ref[...] + got_ref[:, :width].astype(F32) + dot_t(ffn_low, fa[...])
        value = h_ref[...]
        factor = norm_terms([value])
        scaled = incoming * gain_ref[...]
        mean = jnp.mean(value * scaled, axis=1, keepdims=True)
        grad = cot_ref[...].astype(F32) + (factor * scaled - value * (factor * factor * factor * mean))
        gh_ref[...] = grad
        low_precision = grad.astype(BF)
        ghb_ref[...] = low_precision
        left, right = low_precision[:, :depth], low_precision[:, depth:]
        out_low = dot_t(low_precision, b_ref[...]).astype(BF)
        glo_ref[...] = out_low
        mine_ref[...] = (dot_t(left, wo0[...]) + dot_t(right, wo1[...]) + dot_t(out_low, ao[...])).astype(BF)
        far_ref[...] = (dot_t(left, wf0[...]) + dot_t(right, wf1[...]) + dot_t(out_low, af[...])).astype(BF)

    outs = (
        jax.ShapeDtypeStruct((half, width), F32), jax.ShapeDtypeStruct((half, width), BF),
        jax.ShapeDtypeStruct((half, rank_r), BF), jax.ShapeDtypeStruct((half, rank_r), BF),
        jax.ShapeDtypeStruct((half, cols), BF), jax.ShapeDtypeStruct((half, cols), BF),
    )
    ins = (rank, own, got, own_low, hidden, cot, gain, ffn_a, out_b, *w, *w, a_own, a_far)
    mine = lambda v: spec((half, v.shape[1]), lambda i, r: (r[0], 0))
    in_specs = [whole(own), whole(got), whole(own_low), mine(hidden), mine(cot)] + [whole(v) for v in ins[6:9]]
    in_specs += weight_halves(w) + [whole(a_own), whole(a_far)]
    return call(
        kernel, (1,), ins, in_specs, outs, tuple(whole(o) for o in outs), prefetch=1,
        flops=4 * half * width * cols, nbytes=4 * width * cols + 16 * half * width, cost=1311000000
    )


def mixed_gradient(rank, own, far, mixed, n_heads, tail):
    half, cols = own.shape

    def kernel(rank_ref, own_ref, far_ref, mixed_ref, out_ref, tail_ref):
        lane = lane_ids(half)
        for ref, first in ((own_ref, rank_ref[0]), (far_ref, 1 - rank_ref[0])):
            at = pl.ds(pl.multiple_of(first * half, half), half)
            sums = jnp.zeros((half, LANES), F32)
            for pair in range(n_heads // 2):
                here = slice(pair * LANES, (pair + 1) * LANES)
                product = ref[:, here].astype(F32) * mixed_ref[at, here]
                a = jnp.sum(jnp.where(lane < HD, product, 0.0), axis=1, keepdims=True)
                b = jnp.sum(jnp.where(lane < HD, 0.0, product), axis=1, keepdims=True)
                sums = jnp.where(lane == 2 * pair, -a, jnp.where(lane == 2 * pair + 1, -b, sums))
            out_ref[at, :cols] = ref[...]
            out_ref[at, cols:] = split_lanes(sums, n_heads).astype(BF)
        tail_ref[...] = out_ref[:tail, :]

    outs = [jax.ShapeDtypeStruct((n, cols + LANES), BF) for n in (2 * half, tail)]
    return call(
        kernel, (1,), (rank, own, far, mixed), [whole(own), whole(far), whole(mixed)],
        tuple(outs), tuple(whole(o) for o in outs), prefetch=1,
        flops=4 * half * cols, nbytes=16 * half * cols, cost=672750000
    )


def input_gradient(rank, grads, logits, seg_keys, seg_row, row_lanes, own_lanes, next_lanes, across, w, side_w, qkv_b, low_qkv, n_heads):
    rows, cols = grads[0].shape
    block = w[0].shape[0]
    half = rows // 2
    rank_r = qkv_b.shape[0]
    before = logits.shape[0] - rows
    steps = 3
    chunk = block // steps

    def kernel(
        rank_ref, q_ref, k_ref, v_ref, logit_ref, seg_ref, seg_row_ref, r_ref, o_ref, n_ref, a_ref, *refs,
    ):
        pieces, sides, refs = refs[:4], refs[4:8], refs[8:]
        (
            b_ref, lq_ref, far_ref, own_ref, low_ref, tq_ref, tk_ref, tv_ref, gl_ref, sum_ref, joint,
            side,
        ) = refs

        @pl.when(pl.program_id(0) == 0)
        def _():
            lane = lane_ids(rows)
            t = lax.broadcasted_iota(jnp.int32, (rows, rows), 0)
            i = lax.broadcasted_iota(jnp.int32, (rows, rows), 1)
            same = ((seg_row_ref[...] == seg_ref[...]) & (i >= t)).astype(BF)
            total = exact_dot(same, r_ref[...] - o_ref[...]) + exact_dot((i < t).astype(BF), n_ref[...])
            total = total + a_ref[:1, :]
            value = jnp.where(lane < n_heads, total * jax.nn.sigmoid(-logit_ref[...]), 0.0)
            gl_ref[...] = value.astype(BF)
            low = dot_t(b_ref[:, :cols], q_ref[...]) + dot_t(b_ref[:, cols : 2 * cols], k_ref[...])
            low_ref[...] = low + dot_t(b_ref[:, 2 * cols :], v_ref[...])
            for out, grad in ((tq_ref, q_ref), (tk_ref, k_ref), (tv_ref, v_ref)):
                out[...] = t_dot(lq_ref[...], grad[...])

        mine = pl.ds(pl.multiple_of(rank_ref[0] * half, half), half)
        theirs = pl.ds(pl.multiple_of((1 - rank_ref[0]) * half, half), half)
        for k in range(4):
            joint[k * chunk : (k + 1) * chunk, :] = pieces[k][...]
            side[k * chunk : (k + 1) * chunk, :] = sides[k][...]
        value = dot_t(q_ref[...], joint[:, :cols]) + dot_t(k_ref[...], joint[:, cols : 2 * cols])
        sum_ref[...] = value + dot_t(v_ref[...], joint[:, 2 * cols :]) + dot_t(gl_ref[...], side[...])
        for k in range(4):
            at = slice(k * chunk, (k + 1) * chunk)
            far_ref[k] = sum_ref[theirs, at].astype(BF)
            own_ref[k] = sum_ref[mine, at]

    ins = (rank, *grads, logits, seg_keys, seg_row, row_lanes, own_lanes, next_lanes, across, *w, *[side_w] * 4, qkv_b, low_qkv)
    at_own = lambda v: spec((rows, v.shape[1]), lambda i, *_: (before // rows, 0))
    in_specs = [whole(g) for g in grads] + [at_own(logits), at_own(seg_keys)]
    in_specs += [whole(v) for v in (seg_row, row_lanes, own_lanes, next_lanes, across)]
    n_col = w[0].shape[1]
    in_specs += [spec((chunk, n_col), lambda i, *_: (i, 0))] * 4
    in_specs += [spec((chunk, LANES), lambda i, *_, k=k: (i + k * steps, 0)) for k in range(4)]
    in_specs += [whole(qkv_b), whole(low_qkv)]
    outs = (
        jax.ShapeDtypeStruct((4, half, block), BF), jax.ShapeDtypeStruct((4, half, block), F32),
        jax.ShapeDtypeStruct((rank_r, rows), F32),
        *[jax.ShapeDtypeStruct((rank_r, cols), F32)] * 3,
    )
    halves = spec((4, half, chunk), lambda i, *_: (0, 0, i))
    return call(
        kernel, (steps,), ins, in_specs, outs, (halves, halves, *[whole(o) for o in outs[2:]]), [pltpu.VMEM((rows, LANES), BF), pltpu.VMEM((rows, 4 * chunk), F32), pltpu.VMEM((4 * chunk, n_col), BF),
         pltpu.VMEM((4 * chunk, LANES), BF)],
        prefetch=1, cost=1932000000
    )


def token_gradient(offs, rank, own, got, grad_low, a, x, gain, grad_hidden):
    half, width = grad_hidden.shape
    block = width // 4

    def kernel(offs_ref, rank_ref, own_ref, got_ref, low_ref, a_ref, x_ref, gain_ref, gh_ref, out_ref):
        blocks, scaled, product = [], [], 0.0
        for k in range(4):
            here = pl.ds(pl.multiple_of(offs_ref[k], LANES), block)
            value = own_ref[k] + got_ref[k].astype(F32)
            value = value + lax.dot_general(
                low_ref[...], a_ref[k * block : (k + 1) * block, :], (((0,), (1,)), ((), ())), preferred_element_type=F32
            )
            blocks.append(x_ref[:, here].astype(F32))
            scaled.append(value * gain_ref[:, here])
            product = product + jnp.sum(blocks[k] * scaled[k], axis=1, keepdims=True)
        factor = norm_terms(blocks)
        mean = product / width
        for k in range(4):
            here = pl.ds(pl.multiple_of(offs_ref[k], LANES), block)
            back = factor * scaled[k] - blocks[k] * (factor * factor * factor * mean)
            out_ref[:, here] = (gh_ref[:, k * block : (k + 1) * block] + back).astype(BF)

    mine = lambda v: spec((half, v.shape[1]), lambda i, o, r: (r[0], 0))
    out = jax.ShapeDtypeStruct((half, width), BF)
    return call(
        kernel, (1,), (offs, rank, own, got, grad_low, a, x, gain, grad_hidden),
        [whole(own), whole(got), spec((grad_low.shape[0], half), lambda i, o, r: (0, r[0])), whole(a), mine(x), whole(gain), whole(grad_hidden)],
        out, whole(out), prefetch=2, nbytes=20 * half * width, cost=862500000
    )


def both_halves(rank, own, far):
    half, width = own.shape

    def kernel(rank_ref, own_ref, far_ref, out_ref):
        @pl.when(pl.program_id(0) == rank_ref[0])
        def _():
            out_ref[...] = own_ref[...].astype(F32)

        @pl.when(pl.program_id(0) != rank_ref[0])
        def _():
            out_ref[...] = far_ref[...].astype(F32)

    return call(
        kernel, (2,), (rank, own, far), [whole(own), whole(far)], jax.ShapeDtypeStruct((2 * half, width), F32),
        spec((half, width), lambda i, *_: (i, 0)), prefetch=1, nbytes=16 * half * width, cost=517500000
    )


def down_partial(units, down, down_a):
    rows, unit_cols = units.shape
    block = down[0].shape[0]
    width = 4 * block
    rank_r = down_a.shape[1]

    def kernel(u_ref, w0, w1, w2, w3, a_ref, out_ref, low_ref):
        low_ref[...] = jnp.zeros_like(low_ref)
        low_ref[:, :rank_r] = dot(u_ref[...], a_ref[...])
        for k, w_ref in enumerate((w0, w1, w2, w3)):
            out_ref[:, k * block : (k + 1) * block] = dot_t(u_ref[...], w_ref[...]).astype(BF)
        out_ref[:, width:] = split_lanes(low_ref[...], rank_r).astype(BF)

    rowed = lambda n: spec((BLK, n), lambda i: (i, 0))
    last = spec((block, unit_cols), lambda i: (0, 0))
    return call(
        kernel, (rows // BLK,), (units, *down, down_a), [rowed(unit_cols), last, last, last, last, whole(down_a)],
        jax.ShapeDtypeStruct((rows, width + LANES), BF), rowed(width + LANES), [pltpu.VMEM((BLK, LANES), F32)], cost=1621500000
    )


def block_result(offs, hidden, own, got, down_b):
    rows, width = hidden.shape
    block = width // 4
    rank_r = down_b.shape[0]

    def kernel(offs_ref, h_ref, own_ref, got_ref, b_ref, out_ref):
        low = (whole_low(own_ref[:, width:], rank_r) + whole_low(got_ref[:, width:], rank_r)).astype(BF)
        for k in range(4):
            here = pl.ds(pl.multiple_of(offs_ref[k], LANES), block)
            cols = slice(k * block, (k + 1) * block)
            both = own_ref[:, cols].astype(F32) + got_ref[:, cols].astype(F32)
            out_ref[:, here] = (h_ref[:, cols] + both + dot(low, b_ref[:, cols])).astype(BF)

    rowed = lambda v: spec((BLK, v.shape[1]), lambda i, *_: (i, 0))
    out = jax.ShapeDtypeStruct((rows, width), BF)
    return call(
        kernel, (rows // BLK,), (offs, hidden, own, got, down_b),
        [rowed(hidden), rowed(own), rowed(got), whole(down_b)], out, rowed(out),
        prefetch=1, nbytes=12 * rows * width, cost=862500000
    )


def pack_gradients(inv, rank, xor_own, xor_both, halves, out_a, wide, owners):
    rank_r, width = xor_own[0].shape
    block = width // 4
    part, unit_part = block // 8, wide[0].shape[1] // 16
    n = len(wide) * unit_part + (len(xor_own) + len(xor_both) + len(halves) + 1) * part
    assert owners == 32 and block % LANES == 0

    def kernel(inv_ref, rank_ref, *refs):
        out_ref, refs = refs[-1], list(refs[:-1])
        take = lambda count: [refs.pop(0) for _ in range(count)]
        own_refs, both_refs = take(len(xor_own)), take(len(xor_both))
        half_refs, (ao, af), wide_refs = take(len(halves)), take(2), take(len(wide))
        for f in range(4):
            mine = rank_ref[0] == f // 2
            at = pl.ds(pl.multiple_of(inv_ref[f], LANES), block)
            cols = slice(f % 2 * block, (f % 2 + 1) * block)
            blocks = [jnp.where(mine, r[:, at], 0.0) for r in own_refs] + [r[:, at] for r in both_refs]
            blocks += [jnp.where(mine, r[:, cols], 0.0) for r in half_refs]
            blocks.append(jnp.where(mine, ao[:, cols], af[:, cols]))
            units = 8 * unit_part
            big = [jnp.where(mine, r[:, f % 2 * units : (f % 2 + 1) * units], 0.0) for r in wide_refs]
            for j in range(8):
                row = [b[:, j * unit_part : (j + 1) * unit_part] for b in big]
                row += [b[:, j * part : (j + 1) * part] for b in blocks]
                at_row = slice((8 * f + j) * rank_r, (8 * f + j + 1) * rank_r)
                out_ref[at_row, :] = jnp.concatenate(row, axis=1).astype(BF)

    ins = (inv, rank, *xor_own, *xor_both, *halves, *out_a, *wide)
    out = jax.ShapeDtypeStruct((owners * rank_r, n), BF)
    return call(kernel, (1,), ins, [whole(v) for v in ins[2:]], out, whole(out), prefetch=2, cost=552000000
    )


def spread_gradients(every, landed, n_adapters, rank_r, unit_part, part):
    senders = landed.shape[0] // (4 * rank_r)
    at = [0, unit_part, 2 * unit_part] + [3 * unit_part + i * part for i in range(9)]

    def kernel(every_ref, x_ref, aq, bq, ao, bo, ag, bg, ad, bd):
        sums = []
        for f in range(4):
            total = 0.0
            for i in range(senders):
                row = (f * senders + i) * rank_r
                total = total + x_ref[row : row + rank_r, :].astype(F32)
            sums.append(total)
        for a in range(n_adapters):
            total = 0.0
            for f in range(4):
                total = total + jnp.where(every_ref[f] == a, sums[f], 0.0)
            cut = lambda i: total[:, at[i] : at[i + 1]]
            for out, i in ((aq, 3), (ao, 10), (ag, 6), (ad, 2)):
                out[a] = cut(i)
            bo[a], bd[a] = cut(5), cut(4)
            for j in range(3):
                bq[a, j] = cut(7 + j)
            for j in range(2):
                bg[a, :, j, :] = cut(j)

    shape = lambda *dims: jax.ShapeDtypeStruct((n_adapters, *dims), F32)
    row = shape(rank_r, part)
    outs = (row, shape(3, rank_r, part), row, row, row, shape(rank_r, 2, unit_part), shape(rank_r, unit_part), row)
    return call(kernel, (1,), (every, landed), [whole(landed)], outs, tuple(whole(o) for o in outs), prefetch=1, cost=500250000
    )


def body(
    tokens, segments, adapter_index, w_qkv, w_forget, forget_bias, w_out, w_gate_up, w_down,
    gain_attn, gain_ffn, a_qkv, b_qkv, a_out, b_out, a_gate_up, b_gate_up, a_down, b_down, cotangent,
):
    count, rows, width = tokens.shape
    assert count == 1
    head_cols = w_qkv.shape[2]
    n_heads = w_forget.shape[1]
    unit_cols = w_gate_up.shape[2]
    rank_r = a_qkv.shape[2]
    n_f, n_c, n_t = (lax.axis_size("fsdp"), lax.axis_size("ctx"), lax.axis_size("tp"))
    f_rank, t_rank = (lax.axis_index("fsdp"), lax.axis_index("tp"))
    hops = -(-(DOC_MOST - 1) // rows)
    assert hops == 2 and n_c > 2 and n_t == 2 and n_f % 4 == 0
    tail = -(-(DOC_MOST - 1 - rows) // 32) * 32
    before = hops * rows
    half = rows // 2
    block = width // 4
    first = t_rank == 0
    rank = t_rank.astype(jnp.int32)[None]

    def other(values):
        return lax.ppermute(values, "tp", [(0, 1), (1, 0)])

    def four(pieces):
        return [*pieces, *[lax.ppermute(part, "fsdp", [(i, i ^ 1) for i in range(n_f)]) for part in pieces]]

    mix = lambda values, dim: to_xor(values, dim, n_f, f_rank)
    direct = n_f == 4 and block % LANES == 0
    if direct:
        offs = jnp.stack([(f_rank ^ step) * block for step in xor_order(4)]).astype(jnp.int32)
        lay = lambda values, dim: values
    else:
        offs = jnp.arange(4, dtype=jnp.int32) * block
        lay = mix

    pick = adapter_index[0]
    tok = lay(tokens[0], 1)
    seg_one = segments[0] + 1
    note = jnp.zeros((32, width), BF).at[0, :rows].set(seg_one.astype(BF))
    qkv_own = jnp.concatenate([w_qkv[:, i] for i in range(3)], axis=1)
    qkv_far = far_blocks(qkv_own, 0)
    prev_one = shift(jnp.concatenate([tok, after(note, qkv_own)], axis=0), 1, n_c)
    side = jnp.broadcast_to(pick.astype(BF), (w_forget.shape[0], 1))
    side_far = far_blocks(after(jnp.concatenate([w_forget, side], axis=1), qkv_own), 0)
    take = lambda table: lax.dynamic_index_in_dim(table, pick, 0, keepdims=False)
    mine = lambda values, n, dim: lax.dynamic_slice_in_dim(values, t_rank * n, n, dim)
    theirs = lambda values, n, dim: lax.dynamic_slice_in_dim(values, (1 - t_rank) * n, n, dim)
    qkv_a, ffn_a = (mix(take(a_qkv), 0), mix(take(a_gate_up), 0))
    out_b, down_b = (mix(take(b_out), 1), mix(take(b_down), 1))
    qkv_b = mine(take(b_qkv), head_cols, 2).reshape(rank_r, 3 * head_cols)
    out_a = take(a_out)
    out_a_own, out_a_far = (mine(out_a, head_cols, 0), theirs(out_a, head_cols, 0))
    ffn_b = mine(take(b_gate_up), unit_cols, 2).reshape(rank_r, 2 * unit_cols)
    down_a = mine(take(a_down), unit_cols, 0)
    gain_one = lay(gain_attn.astype(F32), 0)[None]
    gain_two = mix(gain_ffn.astype(F32), 0)[None]
    bias = jnp.pad(forget_bias.astype(F32), (0, LANES - n_heads))[None]
    cot = mix(cotangent[0], 1)
    grad_low_down = dot_t(cot, down_b).astype(BF)

    out_pair = jnp.concatenate([w_out, other(w_out)], axis=0)
    gate_up_own = jnp.concatenate([w_gate_up[:, 0], w_gate_up[:, 1]], axis=1)
    down_own = w_down.T
    shared = n_f == 4 and n_c % 2 == 0
    odd = lax.axis_index("ctx") % 2
    down_sent = down_own
    if shared:
        down_sent = lax.dynamic_slice_in_dim(down_own, odd * (unit_cols // 2), unit_cols // 2, 1)
    (
        prev_one, qkv_far, side_far, out_pair, qkv_a, qkv_b, gain_one, bias, ffn_a, out_b, down_b, out_a_own, out_a_far,
        ffn_b, down_a, gain_two, cot, grad_low_down, gate_up_own, down_own, down_sent,
    ) = lax.optimization_barrier((
        prev_one, qkv_far, side_far, out_pair, qkv_a, qkv_b, gain_one, bias, ffn_a, out_b, down_b, out_a_own, out_a_far,
        ffn_b, down_a, gain_two, cot, grad_low_down, gate_up_own, down_own, down_sent,
    ))
    out_far = far_blocks(out_pair, 1)
    prev_two = shift(prev_one[rows - tail :], 1, n_c)
    qkv_four = four(qkv_far)
    side_all = jnp.concatenate(near_blocks(*side_far, 0), axis=0)
    every = from_xor(side_all[:: w_forget.shape[0], n_heads], 0, n_f, f_rank).astype(jnp.int32)
    side_w = jnp.concatenate([side_all, jnp.zeros((width, LANES - n_heads - 1 - rank_r), BF), qkv_a], axis=1)
    args = (gain_one, qkv_four, side_w, qkv_b, bias, head_cols, rank_r)
    down_far = far_blocks(down_sent, 0)
    tok_in, prev_two = lax.optimization_barrier((tok, prev_two))
    normed, low_qkv, query, *filled = project(offs, tok_in, None, tail, *args, None, before)
    seg_two = prev_two[tail, :rows].astype(jnp.int32)
    seg_far = []
    for b in range(-(-tail // BLK)):
        start, end = min(b * BLK, tail + 32 - BLK), min((b + 1) * BLK, tail)
        known = seg_two[rows - tail + b * BLK : rows - tail + end]
        seg_far.append(jnp.pad(known, (b * BLK - start, BLK - (end - start))))
    seg_keys = jnp.concatenate(seg_far + [prev_one[rows, :rows].astype(jnp.int32), seg_one])
    last_keys = jnp.max(seg_keys.reshape(-1, BLK), axis=1)
    lows = jnp.sum(last_keys[None, :] < seg_one[::BLK][:, None], axis=1).astype(jnp.int32)

    gate_up_far = far_blocks(after(gate_up_own, out_far[1], down_far[1], query), 0)
    keys, vals, logits = project(offs, prev_one, prev_two, tail, *args, filled)
    out_w = near_blocks(out_far[0], after(out_far[1], query), 1)
    logits, out_w = lax.optimization_barrier((logits, out_w))
    seg_col, seg_row = (seg_keys[:, None], seg_one[None, :])
    gq, gk, gk_next, gates, total = gate_tables(logits, seg_col, seg_row, n_heads, rows)
    mixed_own, mixed_f, gq_one, gq_two = attention_forward(lows, query, keys, vals, gq, gk, gates, total, n_heads)
    mixed_far = other(mixed_own)
    sent_q1 = jnp.concatenate([query, gq_one], axis=1)
    sent_q2 = jnp.concatenate([query[:tail], gq_two[:tail]], axis=1)
    if shared:
        down_pair = lax.ppermute(after(down_far[1], keys), "ctx", [(i, i ^ 1) for i in range(n_c)])
        down_pair = after(down_pair, mixed_own)
        lower, upper = jnp.where(odd == 0, down_far[1], down_pair), jnp.where(odd == 0, down_pair, down_far[1])
        down_got = jnp.concatenate([lower, upper], axis=1)
    else:
        down_got = down_far[1]
    mixed_far, sent_q1, sent_q2, down_got = lax.optimization_barrier((mixed_far, sent_q1, sent_q2, down_got))
    next_q1 = shift(sent_q1, -1, n_c)
    next_q2 = shift(sent_q2, -2, n_c)

    down_w = four((after(down_own, keys), down_got)) if shared else four(down_far)
    mixed_far, down_w[2] = lax.optimization_barrier((mixed_far, down_w[2]))
    hidden, normed_ffn, low_ffn, low_out = out_projection(
        offs, rank, tok, mixed_own, mixed_far, out_w, out_a_own, out_a_far, out_b, gain_two, ffn_a
    )
    gate_up_w = four((after(gate_up_own, mixed_own), after(gate_up_far[1], hidden))) if shared else four(gate_up_far)
    units, grad_gate, grad_up, far, own, own_low = feed_forward(
        rank, normed_ffn, low_ffn, cot, grad_low_down, gate_up_w, down_w, ffn_b, down_a
    )
    got = other(far)
    down_part = down_partial(after(units, far), down_w, down_a)
    gate_g, up_g, units_g = after((grad_gate, grad_up, units), far)
    tables_ffn = [t_dot(low_ffn, gate_g), t_dot(low_ffn, up_g), t_dot(grad_low_down, units_g)]
    got, down_part, tables_ffn = lax.optimization_barrier((got, down_part, tables_ffn))
    grad_hidden, grad_hidden_b, grad_low_ffn, grad_low_out, gm_own, gm_send = middle(
        rank, own, got, own_low, hidden, cot, gain_two, ffn_a, out_b, out_w, out_a_own, out_a_far
    )
    grad_mixed, sent_d2 = mixed_gradient(rank, gm_own, other(gm_send), mixed_f, n_heads, tail)

    next_d1 = shift(grad_mixed, -1, n_c)
    next_d2 = shift(sent_d2, -2, n_c)
    grad_q, row_lanes, across = attention_dq(
        lows, query, keys, vals, grad_mixed, gq_one, gk, n_heads, (before - rows) // BLK
    )
    across = shift(across, -1, n_c)
    docs_at = head_cols + 3 * n_heads
    grad_k_own, grad_v_own, own_lanes = attention_dkv_own(keys, vals, query, after(grad_mixed, grad_q), gq_one, gk, n_heads)
    next_q1, next_q2, next_d1, next_d2, _ = lax.optimization_barrier((next_q1, next_q2, next_d1, next_d2, grad_k_own))
    next_docs = jnp.concatenate([next_q1[::BLK, docs_at : docs_at + DOCS], next_q2[::BLK, docs_at : docs_at + DOCS]])
    next_docs = next_docs.astype(F32)
    ids = jnp.arange(1, DOCS + 1).astype(F32)
    next_first = jnp.where(jnp.sum(next_docs, 1) > 0, jnp.sum(next_docs * ids[None, :], 1), 99.0)
    last_rows = seg_one[BLK - 1 :: BLK].astype(F32)
    highs = jnp.sum(next_first[None, :] <= last_rows[:, None], axis=1).astype(jnp.int32)
    lane = lax.broadcasted_iota(jnp.int32, (1, width), 1)
    own_part = lambda values: values * (lane // (width // 2) == t_rank)
    natural = lambda values: from_xor(values, 1, n_f, f_rank)
    by_tp = lambda a, b: jnp.concatenate([jnp.where(first, a, b), jnp.where(first, b, a)], axis=1)
    place = lambda values: by_tp(values, jnp.zeros_like(values))
    rows_of = lambda values: lax.dynamic_slice_in_dim(values, t_rank * half, half, 0)
    onehot = (jnp.arange(a_qkv.shape[0])[:, None] == every[None, :]).astype(F32)
    onehot = jnp.repeat(onehot, n_c * n_t, axis=1)

    owners = n_f * n_c * n_t

    def pack(tables):
        packed = jnp.concatenate([t.reshape(rank_r, owners, -1) for t in tables], axis=2).transpose(1, 0, 2)
        return packed.astype(BF).reshape(owners, -1), [t.shape[1] // owners for t in tables]

    def take_apart(spread, sizes):
        spread = spread.reshape(-1, rank_r, sum(sizes))
        outs, at = [], 0
        for size in sizes:
            outs.append(spread[:, :, at : at + size])
            at += size
        return outs

    table_out_a = [t_dot(grad_low_out, rows_of(mixed_own)), t_dot(grad_low_out, rows_of(mixed_far))]
    table_out_b = t_dot(rows_of(low_out), grad_hidden_b)
    table_ffn_a = t_dot(grad_low_ffn, rows_of(normed_ffn))
    highs, table_out_a, table_out_b, table_ffn_a = lax.optimization_barrier(
        (highs, table_out_a, table_out_b, table_ffn_a)
    )
    grad_k, grad_v, next_lanes = attention_dkv_next(
        highs, keys, vals, next_q1, next_q2, next_d1, next_d2, gk_next, grad_k_own, grad_v_own, n_heads
    )
    down_other = other(after(down_part, grad_mixed))

    grads = (grad_q, grad_k, grad_v)
    far_in, own_in, part_low_qkv, *tables_b = input_gradient(
        rank, grads, logits, seg_col, seg_row, row_lanes, own_lanes, next_lanes, across, qkv_four, side_w, qkv_b, low_qkv, n_heads
    )
    grad_low_qkv = (part_low_qkv + other(part_low_qkv)).astype(BF)
    got_in = other(far_in)
    parts = [values[:, width : width + 3 * rank_r].astype(F32).reshape(rows, 3, rank_r) for values in (down_part, down_other)]
    parts = [values[:, 0] + values[:, 1] + values[:, 2] for values in parts]
    low_down = after((parts[0] + parts[1]).astype(BF), far_in)
    grad_tok = token_gradient(offs, rank, own_in, got_in, grad_low_qkv, qkv_a, tok, gain_one, grad_hidden)
    tok_far = other(grad_tok)
    block_output = block_result(offs, hidden, down_part, after(down_other, grad_tok), down_b)

    table_qkv_a, table_down_b = dot(grad_low_qkv, normed), t_dot(low_down, cot)
    if direct:
        bits = n_f.bit_length() - 1
        inv = [sum((((f_rank ^ i) >> j) & 1) << (bits - 1 - j) for j in range(bits)) * block for i in range(n_f)]
        packed = pack_gradients(
            jnp.stack(inv).astype(jnp.int32), rank, [table_qkv_a, table_down_b], [table_out_b, table_ffn_a], tables_b,
            table_out_a, tables_ffn, owners,
        )
        landed = lax.all_to_all(packed, ("fsdp", "ctx", "tp"), 0, 0, tiled=True)
        part, unit_part = width // owners, unit_cols * n_t // owners
        done = spread_gradients(every, landed, a_qkv.shape[0], rank_r, unit_part, part)
        done = [v.transpose(0, 2, 1) if i in (0, 2, 4, 6) else v for i, v in enumerate(done)]
        done[1] = done[1].transpose(0, 2, 1, 3)
        grad_tokens = both_halves(rank, grad_tok, after(tok_far, done[0]))
        return (block_output[None], grad_tokens[None], *done)
    block_output = from_xor(block_output, 1, n_f, f_rank)
    grad_tokens = from_xor(both_halves(rank, grad_tok, tok_far), 1, n_f, f_rank)
    early, early_sizes = pack([
        by_tp(*table_out_a), natural(table_out_b), natural(table_ffn_a), *[place(t) for t in tables_ffn],
    ])
    late, late_sizes = pack([
        own_part(natural(table_qkv_a)), *[place(t) for t in tables_b], own_part(natural(table_down_b)),
    ])
    landed = lax.all_to_all(jnp.concatenate([late, early], axis=1), ("fsdp", "ctx", "tp"), 0, 0, tiled=True)
    split = rank_r * sum(late_sizes)
    spread = jnp.dot(onehot.astype(BF), landed, preferred_element_type=F32)
    done = take_apart(spread[:, :split], late_sizes) + take_apart(spread[:, split:], early_sizes)
    swap = lambda values: values.transpose(0, 2, 1)
    return (
        block_output[None],
        grad_tokens[None],
        swap(done[0]),
        jnp.stack(done[1:4], axis=2),
        swap(done[5]),
        done[6],
        swap(done[7]),
        jnp.stack(done[8:10], axis=2),
        swap(done[10]),
        done[4],
    )


def solution(mesh):
    in_specs = (
        P("fsdp", "ctx", None), P("fsdp", "ctx"), P("fsdp"), P("fsdp", None, "tp"), P("fsdp", "tp"), P("tp"),
        P("tp", "fsdp"), P("fsdp", None, "tp"), P("tp", "fsdp"),
        P(), P(), P(), P(), P(), P(), P(), P(), P(), P(),
        P("fsdp", "ctx", None),
    )
    out_specs = (
        P("fsdp", "ctx", None),
        P("fsdp", "ctx", None),
        P(None, ("fsdp", "ctx", "tp"), None),
        P(None, None, None, ("fsdp", "ctx", "tp")),
        P(None, ("fsdp", "ctx", "tp"), None),
        P(None, None, ("fsdp", "ctx", "tp")),
        P(None, ("fsdp", "ctx", "tp"), None),
        P(None, None, None, ("fsdp", "ctx", "tp")),
        P(None, ("fsdp", "ctx", "tp"), None),
        P(None, None, ("fsdp", "ctx", "tp")),
    )
    return jax.shard_map(body, mesh=mesh, in_specs=in_specs, out_specs=out_specs, check_vma=False)
```

```python
import jax
import jax.numpy as jnp
from jax import lax
from jax.experimental import pallas as pl
from jax.experimental.pallas import tpu as pltpu
from jax.sharding import PartitionSpec as P

HD = 64
DOC_MOST = 800
DOCS = 8
BF = jnp.bfloat16
F32 = jnp.float32
HI = lax.Precision.HIGHEST


def dot(a, b):
    return jnp.dot(a, b, preferred_element_type=F32)


def dot_t(a, b):
    return lax.dot_general(a, b, (((1,), (1,)), ((), ())), preferred_element_type=F32)


def t_dot(a, b):
    return lax.dot_general(a, b, (((0,), (0,)), ((), ())), preferred_element_type=F32)


def xor_order(size):
    order, bit = [0], size // 2
    while bit:
        order, bit = order + [step ^ bit for step in order], bit // 2
    return order


def after(values, *done):
    return lax.optimization_barrier((values, *done))[0]


def far_blocks(shard, dim):
    size = lax.axis_size("fsdp")
    own, bit = shard, size // 2
    while True:
        got = lax.ppermute(own, "fsdp", [(i, i ^ bit) for i in range(size)])
        if bit == 2:
            return own, got
        own, bit = jnp.concatenate([own, got], axis=dim), bit // 2


def near_blocks(own, got, dim):
    both = jnp.concatenate([own, got], axis=dim)
    size = lax.axis_size("fsdp")
    return [both, lax.ppermute(both, "fsdp", [(i, i ^ 1) for i in range(size)])]


def to_xor(values, dim, size, rank):
    block = values.shape[dim] // size
    return jnp.concatenate(
        [lax.dynamic_slice_in_dim(values, (rank ^ step) * block, block, dim) for step in xor_order(size)],
        axis=dim,
    )


def from_xor(values, dim, size, rank):
    block = values.shape[dim] // size
    bits = size.bit_length() - 1
    pieces = []
    for natural in range(size):
        mixed = rank ^ natural
        place = sum(((mixed >> j) & 1) << (bits - 1 - j) for j in range(bits))
        pieces.append(lax.dynamic_slice_in_dim(values, place * block, block, dim))
    return jnp.concatenate(pieces, axis=dim)


def shift(values, hop, size):
    pairs = [(i, i + hop) for i in range(size) if 0 <= i + hop < size]
    return lax.ppermute(values, "ctx", pairs)


LANES = 128
BLK = 256
BIG = -1e30


def spec(shape, index):
    return pl.BlockSpec(shape, index)


def call(kernel, grid, ins, in_specs, outs, out_specs, scratch=(), prefetch=0, flops=0, nbytes=0, exps=0, aliases=None, cost=1):
    return pl.pallas_call(
        kernel,
        out_shape=outs,
        grid_spec=pltpu.PrefetchScalarGridSpec(
            num_scalar_prefetch=prefetch, grid=grid, in_specs=in_specs, out_specs=out_specs, scratch_shapes=list(scratch)
        ),
        compiler_params=pltpu.CompilerParams(
            dimension_semantics=("arbitrary",) * len(grid), vmem_limit_bytes=56 * 2**20
        ),
        input_output_aliases=aliases or {},
        cost_estimate=pl.CostEstimate(flops=cost, bytes_accessed=1, transcendentals=0),
    )(*ins)


def whole(values):
    return spec(values.shape, lambda *_: (0,) * len(values.shape))


def lane_ids(rows):
    return lax.broadcasted_iota(jnp.int32, (rows, LANES), 1)


def split3(values):
    high = values.astype(BF)
    rest = values - high.astype(F32)
    mid = rest.astype(BF)
    return high, mid, (rest - mid.astype(F32)).astype(BF)


def split_lanes(values, n):
    lane = lane_ids(values.shape[0])
    values = jnp.where(lane < n, values, 0.0)
    high, mid, low = (part.astype(F32) for part in split3(values))
    return high + pltpu.roll(mid, n, 1) + pltpu.roll(low, 2 * n, 1)


def exact_dot(mask, values):
    high, mid, low = split3(values)
    return dot(mask, high) + dot(mask, mid) + dot(mask, low)


def norm_terms(blocks):
    width = sum(b.shape[1] for b in blocks)
    total = sum(jnp.sum(b * b, axis=1, keepdims=True) for b in blocks)
    return lax.rsqrt(total / width + 1e-05)


def pair_lanes(pair, n_heads, kind):
    lane = lax.broadcasted_iota(jnp.int32, (LANES, LANES), 1)
    to = lane & (HD - 1)
    head = jnp.where(lane >= HD, 2 * pair, 2 * pair + 1)
    gate_at = 3 if kind == "k" else 0
    part = to - gate_at
    source = jnp.where((part >= 0) & (part < 3), part * n_heads + head, -1)
    if kind != "d":
        ones = to - (3 - gate_at)
        source = jnp.where((ones >= 0) & (ones < 3), 3 * n_heads + DOCS, source)
        source = jnp.where((to >= 8) & (to < 8 + DOCS), to - 8 + 3 * n_heads, source)
    return (lax.broadcasted_iota(jnp.int32, (LANES, LANES), 0) == source).astype(BF)


def pair_of(values, gate_parts, select):
    extra = dot(gate_parts, select).astype(BF)
    low = lane_ids(values.shape[0]) < HD
    return jnp.where(low, values, extra), jnp.where(low, extra, values)


def pair_ones(values):
    low = lane_ids(values.shape[0]) < HD
    one = jnp.ones((), BF)
    return jnp.where(low, values, one), jnp.where(low, one, values)


def block_at(index):
    return pl.ds(pl.multiple_of(index * BLK, BLK), BLK)


def causal_from(rows, first):
    row = lax.broadcasted_iota(jnp.int32, (rows, BLK), 0)
    return row + first >= lax.broadcasted_iota(jnp.int32, (rows, BLK), 1)


def lane_column(acc, lane_at):
    return jnp.sum(jnp.where(lane_ids(acc.shape[0]) == lane_at, acc, 0.0), axis=1, keepdims=True)


def attention_forward(bounds, q, k, v, gq, gk, gates, total, n_heads):
    rows, keys = q.shape[0], k.shape[0]
    n_before = (keys - rows) // BLK
    pairs = n_heads // 2
    assert rows == 2 * BLK

    def kernel(
        lo_ref, q_ref, k_ref, v_ref, gq_ref, gk_ref, gate_ref, tot_ref, mixed_ref, float_ref, one_ref, two_ref,
        qx, scores, tops, parts, accs, log_ref,
    ):
        pair = pl.program_id(0)
        pick_k = pair_lanes(pair, n_heads, "k")
        for side, value in enumerate(pair_of(q_ref[...], gq_ref[...], pair_lanes(pair, n_heads, "q"))):
            qx[side] = value
        both, late, early = slice(0, rows), slice(BLK, rows), slice(0, BLK)

        def score(kb, here, at, mask=None, first=False):
            for side, key in enumerate(pair_of(k_ref[here, :], gk_ref[here, :], pick_k)):
                s = dot_t(qx[side, at, :], key)
                if mask is not None:
                    s = jnp.where(mask, s, BIG)
                scores[side, at, here] = s
                top = jnp.maximum(s[:, :LANES], s[:, LANES:])
                tops[side, at, :] = top if first else jnp.maximum(tops[side, at, :], top)

        def gather(here, at, first=False):
            for side in range(2):
                w = jnp.exp(scores[side, at, here] - tops[side, at, :1])
                part = w[:, :LANES] + w[:, LANES:]
                acc = dot(w.astype(BF), v_ref[here, :])
                parts[side, at, :] = part if first else parts[side, at, :] + part
                accs[side, at, :] = acc if first else accs[side, at, :] + acc

        own = [slice(b * BLK, (b + 1) * BLK) for b in (n_before, n_before + 1)]
        low, high = lo_ref[0], jnp.minimum(lo_ref[1], n_before)
        score(n_before, own[0], both, causal_from(rows, 0), True)
        score(n_before + 1, own[1], late, causal_from(BLK, 0))
        pl.loop(high, n_before)(lambda kb: score(kb, block_at(kb), both))
        pl.loop(low, high)(lambda kb: score(kb, block_at(kb), early))
        for side in range(2):
            tops[side] = jnp.broadcast_to(jnp.max(tops[side], axis=1, keepdims=True), (rows, LANES))
        gather(own[0], both, True)
        gather(own[1], late)
        pl.loop(high, n_before)(lambda kb: gather(block_at(kb), both))
        pl.loop(low, high)(lambda kb: gather(block_at(kb), early))
        lane = lane_ids(rows)
        results, logs = [], jnp.zeros((rows, LANES), F32)
        for side in range(2):
            row_total = jnp.sum(parts[side], axis=1, keepdims=True)
            results.append(accs[side] / row_total)
            logs = jnp.where(lane == 2 * pair + side, tops[side] + jnp.log(row_total), logs)
        out = jnp.where(lane < HD, results[0], results[1])
        mixed_ref[...] = out.astype(BF)
        float_ref[...] = out

        @pl.when(pair == 0)
        def _():
            log_ref[...] = logs

        @pl.when(pair > 0)
        def _():
            log_ref[...] = jnp.where((lane >> 1) == pair, logs, log_ref[...])

        @pl.when(pair == pairs - 1)
        def _():
            values = gate_ref[...] - log_ref[...]
            rest = gq_ref[...].astype(F32)
            one_ref[...] = jnp.where(lane < 3 * n_heads, split_lanes(values, n_heads), rest).astype(BF)
            values = values + tot_ref[:1, :]
            two_ref[...] = jnp.where(lane < 3 * n_heads, split_lanes(values, n_heads), rest).astype(BF)

    here = lambda n: spec((n, LANES), lambda i, *_: (0, i))
    shared = lambda n: spec((n, LANES), lambda i, *_: (0, 0))
    return call(
        kernel,
        (pairs,),
        (bounds, q, k, v, gq, gk, gates, total),
        [here(rows), here(keys), here(keys), shared(rows), shared(keys), shared(rows), shared(8)],
        (
            jax.ShapeDtypeStruct(q.shape, BF), jax.ShapeDtypeStruct(q.shape, F32),
            jax.ShapeDtypeStruct((rows, LANES), BF), jax.ShapeDtypeStruct((rows, LANES), BF),
        ),
        (here(rows), here(rows), shared(rows), shared(rows)),
        [pltpu.VMEM((2, rows, LANES), BF), pltpu.VMEM((2, rows, keys), F32)]
        + [pltpu.VMEM((2, rows, LANES), F32)] * 3 + [pltpu.VMEM((rows, LANES), F32)],
        prefetch=1,
    )


def attention_dq(bounds, q, k, v, d, gq, gk, n_heads, n_far):
    rows, keys = q.shape[0], k.shape[0]
    n_before = (keys - rows) // BLK
    pairs = n_heads // 2

    def kernel(lo_ref, q_ref, k_ref, v_ref, d_ref, gq_ref, gk_ref, gd_ref, dq_ref, row_ref, far_ref, qx, dx, accs):
        pair = pl.program_id(0)
        lane = lane_ids(rows)
        pick_k = pair_lanes(pair, n_heads, "k")
        for side, value in enumerate(pair_of(q_ref[...], gq_ref[...], pair_lanes(pair, n_heads, "q"))):
            qx[side] = value
        for side, value in enumerate(pair_of(d_ref[...], gd_ref[...], pair_lanes(pair, n_heads, "d"))):
            dx[side] = value
        both, late, early = slice(0, rows), slice(BLK, rows), slice(0, BLK)

        @pl.when(pair == 0)
        def _():
            far_ref[...] = jnp.zeros_like(far_ref)
            row_ref[...] = jnp.zeros_like(row_ref)

        accs[...] = jnp.zeros_like(accs)

        def block(here, at, mask=None):
            values = pair_ones(v_ref[here, :])
            for side, key in enumerate(pair_of(k_ref[here, :], gk_ref[here, :], pick_k)):
                s = dot_t(qx[side, at, :], key)
                if mask is not None:
                    s = jnp.where(mask, s, BIG)
                ds = (jnp.exp(s) * dot_t(dx[side, at, :], values[side])).astype(BF)
                accs[side, at, :] += dot(ds, key)

        def earlier(kb, at):
            block(block_at(kb), at)

            @pl.when(kb == n_far - 1)
            def _():
                for side in range(2):
                    moved = jnp.sum(jnp.where(lane == HD * (1 - side), accs[side], 0.0))
                    far_ref[...] += jnp.where(lane[:8] == 2 * pair + side, moved, 0.0)

        low, high = lo_ref[0], jnp.minimum(lo_ref[1], n_before)
        pl.loop(low, high)(lambda kb: earlier(kb, early))
        pl.loop(high, n_before)(lambda kb: earlier(kb, both))
        block(slice(n_before * BLK, (n_before + 1) * BLK), both, causal_from(rows, 0))
        block(slice((n_before + 1) * BLK, (n_before + 2) * BLK), late, causal_from(BLK, 0))
        dq_ref[...] = (jnp.where(lane < HD, accs[0], accs[1]) * HD ** (-0.5)).astype(BF)
        for side in range(2):
            total = lane_column(accs[side], HD * (1 - side))
            row_ref[...] = jnp.where(lane == 2 * pair + side, total, row_ref[...])

    here = lambda n: spec((n, LANES), lambda i, *_: (0, i))
    shared = lambda n: spec((n, LANES), lambda i, *_: (0, 0))
    return call(
        kernel,
        (pairs,),
        (bounds, q, k, v, d, gq, gk, d),
        [here(rows), here(keys), here(keys), here(rows), shared(rows), shared(keys), spec((rows, LANES), lambda i, *_: (0, pairs))],
        (
            jax.ShapeDtypeStruct(q.shape, BF), jax.ShapeDtypeStruct((rows, LANES), F32),
            jax.ShapeDtypeStruct((8, LANES), F32),
        ),
        (here(rows), shared(rows), shared(8)),
        [pltpu.VMEM((2, rows, LANES), BF)] * 2 + [pltpu.VMEM((2, rows, LANES), F32)],
        prefetch=1, cost=3363750000
    )


def score_block(kx, vx, queries, grads, at, dks, dvs, mask=None, first=False):
    for side in range(2):
        s = dot_t(kx[side, at, :], queries[side])
        if mask is not None:
            s = jnp.where(mask, s, BIG)
        w = jnp.exp(s)
        ds = (w * dot_t(vx[side, at, :], grads[side])).astype(BF)
        dk, dv = dot(ds, queries[side]), dot(w.astype(BF), grads[side])
        dks[side, at, :] = dk if first else dks[side, at, :] + dk
        dvs[side, at, :] = dv if first else dvs[side, at, :] + dv


def attention_dkv_own(k, v, q, d, gq, gk, n_heads):
    rows = q.shape[0]
    place = k.shape[0] // rows - 1
    pairs = n_heads // 2

    def kernel(k_ref, v_ref, q_ref, d_ref, gq_ref, gd_ref, gk_ref, dk_ref, dv_ref, own_ref, kx, vx, dks, dvs):
        pair = pl.program_id(0)
        lane = lane_ids(rows)
        pick_q, pick_d = (pair_lanes(pair, n_heads, "q"), pair_lanes(pair, n_heads, "d"))
        for side, value in enumerate(pair_of(k_ref[...], gk_ref[...], pair_lanes(pair, n_heads, "k"))):
            kx[side] = value
        for side, value in enumerate(pair_ones(v_ref[...])):
            vx[side] = value
        both, late, early = slice(0, rows), slice(BLK, rows), slice(0, BLK)

        @pl.when(pair == 0)
        def _():
            own_ref[...] = jnp.zeros_like(own_ref)

        def load(here):
            return pair_of(q_ref[here, :], gq_ref[here, :], pick_q), pair_of(d_ref[here, :], gd_ref[here, :], pick_d)

        keep = lax.broadcasted_iota(jnp.int32, (rows, BLK), 0) - BLK <= lax.broadcasted_iota(jnp.int32, (rows, BLK), 1)
        first_keep = lax.broadcasted_iota(jnp.int32, (BLK, BLK), 0) <= lax.broadcasted_iota(jnp.int32, (BLK, BLK), 1)
        score_block(kx, vx, *load(late), both, dks, dvs, keep, True)
        score_block(kx, vx, *load(early), early, dks, dvs, first_keep)
        for side in range(2):
            column = lane_column(dks[side], HD * (1 - side) + 3)
            own_ref[...] = jnp.where(lane == 2 * pair + side, column, own_ref[...])
        dk_ref[...] = jnp.where(lane < HD, dks[0], dks[1])
        dv_ref[...] = jnp.where(lane < HD, dvs[0], dvs[1])

    heads_spec = lambda n: spec((n, LANES), lambda i, *_: (0, i))
    shared = lambda n: spec((n, LANES), lambda i, *_: (0, 0))
    keys_spec = spec((rows, LANES), lambda i, *_: (place, i))
    return call(
        kernel, (pairs,), (k, v, q, d, gq, d, gk),
        [
            keys_spec, keys_spec, heads_spec(rows), heads_spec(rows), shared(rows),
            spec((rows, LANES), lambda i, *_: (0, pairs)), spec((rows, LANES), lambda i, *_: (place, 0)),
        ],
        (jax.ShapeDtypeStruct(q.shape, F32), jax.ShapeDtypeStruct(q.shape, F32), jax.ShapeDtypeStruct((rows, LANES), F32)),
        (heads_spec(rows), heads_spec(rows), shared(rows)),
        [pltpu.VMEM((2, rows, LANES), BF)] * 2 + [pltpu.VMEM((2, rows, LANES), F32)] * 2, cost=2294250000
    )


def attention_dkv_next(bounds, k, v, q_one, q_two, d_one, d_two, gkn, dk, dv, n_heads):
    rows, tail = q_one.shape[0], q_two.shape[0]
    place = k.shape[0] // rows - 1
    pairs = n_heads // 2
    assert 0 < tail - BLK <= BLK

    def kernel(
        hi_ref, k_ref, v_ref, q1_ref, d1_ref, gq1_ref, gd1_ref, q2_ref, d2_ref, gq2_ref, gd2_ref, gkn_ref,
        dk_own, dv_own, dk_ref, dv_ref, next_ref, kx, vx, dks, dvs,
    ):
        pair = pl.program_id(0)
        lane = lane_ids(rows)
        both, late, early = slice(0, rows), slice(BLK, rows), slice(0, BLK)
        few, many = hi_ref[0], hi_ref[1]

        @pl.when(pair == 0)
        def _():
            next_ref[...] = jnp.zeros_like(next_ref)

        @pl.when(many > 0)
        def _():
            pick_q, pick_d = (pair_lanes(pair, n_heads, "q"), pair_lanes(pair, n_heads, "d"))
            for side, value in enumerate(pair_of(k_ref[...], gkn_ref[...], pair_lanes(pair, n_heads, "k"))):
                kx[side] = value
            for side, value in enumerate(pair_ones(v_ref[...])):
                vx[side] = value
            dks[...] = jnp.zeros_like(dks)
            dvs[...] = jnp.zeros_like(dvs)

            def block(refs, here, at):
                q_ref, gq_ref, d_ref, gd_ref = refs
                queries = pair_of(q_ref[here, :], gq_ref[here, :], pick_q)
                score_block(kx, vx, queries, pair_of(d_ref[here, :], gd_ref[here, :], pick_d), at, dks, dvs)

            one, two = (q1_ref, gq1_ref, d1_ref, gd1_ref), (q2_ref, gq2_ref, d2_ref, gd2_ref)
            pl.loop(0, jnp.minimum(few, 2))(lambda j: block(one, block_at(j), both))
            pl.loop(few, jnp.minimum(many, 2))(lambda j: block(one, block_at(j), late))
            pl.when(many > 2)(lambda: block(two, early, both))
            pl.when(many > 3)(lambda: block(two, slice(BLK, tail), both))
            for side in range(2):
                value = lane_column(dks[side], HD * (1 - side) + 3)
                next_ref[...] = jnp.where(lane == 2 * pair + side, value, next_ref[...])
            dk_ref[...] = (dk_own[...] + jnp.where(lane < HD, dks[0], dks[1])).astype(BF)
            dv_ref[...] = (dv_own[...] + jnp.where(lane < HD, dvs[0], dvs[1])).astype(BF)

        @pl.when(many == 0)
        def _():
            dk_ref[...] = dk_own[...].astype(BF)
            dv_ref[...] = dv_own[...].astype(BF)

    heads_spec = lambda n: spec((n, LANES), lambda i, *_: (0, i))
    shared = lambda n: spec((n, LANES), lambda i, *_: (0, 0))
    last = lambda n: spec((n, LANES), lambda i, *_: (0, pairs))
    keys_spec = spec((rows, LANES), lambda i, *_: (place, i))
    return call(
        kernel, (pairs,), (bounds, k, v, q_one, d_one, q_one, d_one, q_two, d_two, q_two, d_two, gkn, dk, dv),
        [
            keys_spec, keys_spec, heads_spec(rows), heads_spec(rows), last(rows), last(rows),
            heads_spec(tail), heads_spec(tail), last(tail), last(tail), shared(rows), heads_spec(rows), heads_spec(rows),
        ],
        (jax.ShapeDtypeStruct(dk.shape, BF), jax.ShapeDtypeStruct(dk.shape, BF), jax.ShapeDtypeStruct((rows, LANES), F32)),
        (heads_spec(rows), heads_spec(rows), shared(rows)),
        [pltpu.VMEM((2, rows, LANES), BF)] * 2 + [pltpu.VMEM((2, rows, LANES), F32)] * 2,
        prefetch=1, cost=2932500000
    )


def project(offs, x, x_far, tail, gain, w, side_w, qkv_b, bias, cols, rank_r, filled=None, before=0):
    width = gain.shape[1]
    block = width // 4
    own = filled is None
    rows = x.shape[0] // (2 * BLK) * 2 * BLK
    row_steps = 1 if own else 2
    parts = ("q", "k", "v") if own else ("k", "v")
    assert rows == 2 * BLK and BLK <= tail <= rows - 32

    def kernel(*refs):
        offs_ref, x_ref = refs[0], refs[1]
        at = 2
        if not own:
            far_ref, at = refs[2], 3
        gain_ref, *pieces, side_ref, b_ref, bias_ref = refs[at : at + 8]
        at += 8 + (0 if own else 3)
        outs, scr = refs[at:-3], refs[-3:]
        part, step = pl.program_id(0), pl.program_id(1)
        n_outs = dict(zip(("n", "low", "q", "k", "v", "logits") if own else ("k", "v", "logits"), outs))
        scr, low_scr, joint = scr
        at_rows = pl.ds(pl.multiple_of(step * rows, rows), rows)

        @pl.when(part == 0)
        def _():
            blocks = []
            for k in range(4):
                here = pl.ds(pl.multiple_of(offs_ref[k], LANES), block)
                value = x_ref[:, here]
                if not own:
                    far = jnp.concatenate([far_ref[:BLK, here], far_ref[tail + 32 - BLK : tail + 32, here]], axis=0)
                    value = jnp.where(step == 0, far, value)
                blocks.append(value.astype(F32))
            factor = norm_terms(blocks)
            for k in range(4):
                here = pl.ds(pl.multiple_of(offs_ref[k], LANES), block)
                scr[at_rows, k * block : (k + 1) * block] = (blocks[k] * factor * gain_ref[:, here]).astype(BF)
            side = dot(scr[at_rows, :], side_ref[...])
            low = side[:, LANES - rank_r :].astype(BF)
            low_scr[at_rows, :rank_r] = low
            n_outs["logits"][at_rows, :] = side + bias_ref[...]
            if own:
                n_outs["n"][...] = scr[...]
                n_outs["low"][...] = low

        @pl.when(step == 0)
        def _():
            for k in range(4):
                joint[k * block : (k + 1) * block, :] = pieces[k][...]

        value = dot(scr[at_rows, :], joint[...])
        value = (value + dot(low_scr[at_rows, :rank_r], b_ref[...])).astype(BF)
        for n, name in enumerate(parts):
            @pl.when(part == n)
            def _(name=name):
                out = n_outs[name]
                out[at_rows, :] = (value.astype(F32) * HD ** (-0.5)).astype(BF) if name == "q" else value

    keys = before + rows if own else filled[0].shape[0]
    ins = [offs, x] + ([] if own else [x_far]) + [gain, *w, side_w, qkv_b, bias] + ([] if own else list(filled))
    row_spec = spec((rows, width), lambda i, *_: (0, 0))
    in_specs = [row_spec] + ([] if own else [whole(x_far)])
    first = 0 if own else 1
    column = lambda n: spec((n, cols), lambda j, *_: (0, j + first))
    in_specs += [whole(gain), *[column(block)] * 4, whole(side_w), column(rank_r), whole(bias)]
    if not own:
        in_specs += [pl.BlockSpec(memory_space=pl.ANY)] * 3
    some = row_steps * rows
    at_keys = lambda n: spec((some, n), lambda *_: (before // some if own else 0, 0))
    outs = [jax.ShapeDtypeStruct((keys, cols), BF)] * 2 + [jax.ShapeDtypeStruct((keys, LANES), F32)]
    out_specs = [at_keys(cols), at_keys(cols), at_keys(LANES)]
    if own:
        here = lambda n: spec((rows, n), lambda *_: (0, 0))
        outs = [
            jax.ShapeDtypeStruct((rows, width), BF),
            jax.ShapeDtypeStruct((rows, rank_r), BF),
            jax.ShapeDtypeStruct((rows, cols), BF),
        ] + outs
        out_specs = [here(width), here(rank_r), here(cols)] + out_specs
    return call(
        kernel, (len(parts), row_steps), ins, in_specs, tuple(outs), tuple(out_specs),
        [pltpu.VMEM((some, width), BF), pltpu.VMEM((some, LANES), BF), pltpu.VMEM((width, cols), BF)], prefetch=1,
        aliases={} if own else {11: 0, 12: 1, 13: 2},
    )


def gate_tables(logits, seg_keys, seg_row, n_heads, rows):
    keys = logits.shape[0]
    before = keys - rows
    one = 3 * n_heads + DOCS

    def kernel(logit_ref, seg_ref, row_ref, gq_ref, gk_ref, gkn_ref, gate_ref, tot_ref):
        lane = lane_ids(BLK)
        doc = lane - 3 * n_heads + 1
        doc_lane = (doc > 0) & (doc <= DOCS)
        inner = lax.broadcasted_iota(jnp.int32, (BLK, BLK), 1) > lax.broadcasted_iota(jnp.int32, (BLK, BLK), 0)
        later = inner.astype(BF)

        def forget(at):
            value = logit_ref[at, :]
            value = jnp.minimum(value, 0.0) - jnp.log(1.0 + jnp.exp(-jnp.abs(value)))
            return jnp.where((lane < n_heads) & (seg_ref[at, :] > 0), value, 0.0)

        def lanes(values, docs):
            return (split_lanes(values, n_heads) + docs + jnp.where(lane == one, 1.0, 0.0)).astype(BF)

        def docs_k(at):
            return jnp.where(doc_lane & (doc != seg_ref[at, :]), BIG, 0.0)

        def suffix(first, last, carry, out_ref, base):
            for b in range(last - 1, first - 1, -1):
                at = slice(b * BLK, (b + 1) * BLK)
                values = forget(at)
                sums = exact_dot(later, values) + carry
                out_ref[b * BLK - base : (b + 1) * BLK - base, :] = lanes(sums, docs_k(at))
                carry = carry + jnp.sum(values, axis=0, keepdims=True)
            return carry

        n_before, n_all = before // BLK, keys // BLK
        zero = jnp.zeros((1, LANES), F32)
        near = suffix((before - rows) // BLK, n_before, zero, gk_ref, 0)
        tot_ref[...] = jnp.broadcast_to(near, tot_ref.shape)
        suffix(0, (before - rows) // BLK, near, gk_ref, 0)
        suffix(n_before, n_all, zero, gkn_ref, before)
        own = jnp.concatenate([forget(slice(b * BLK, (b + 1) * BLK)) for b in range(n_before, n_all)], axis=0)
        for b in range(rows // BLK):
            at = slice(before + b * BLK, before + (b + 1) * BLK)
            here = slice(b * BLK, (b + 1) * BLK)
            q_pos = lax.broadcasted_iota(jnp.int32, (BLK, rows), 0) + b * BLK
            k_pos = lax.broadcasted_iota(jnp.int32, (BLK, rows), 1)
            same = (row_ref[...] == seg_ref[at, :]) & (k_pos <= q_pos)
            sums = exact_dot(same.astype(BF), own)
            gate_ref[here, :] = sums
            gq_ref[here, :] = lanes(sums, jnp.where(doc_lane & (doc == seg_ref[at, :]), 1.0, 0.0))
            gk_ref[at, :] = lanes(-sums, docs_k(at))

    shape = lambda n, t: jax.ShapeDtypeStruct((n, LANES), t)
    outs = (shape(rows, BF), shape(keys, BF), shape(rows, BF), shape(rows, F32), shape(8, F32))
    return call(
        kernel, (1,), (logits, seg_keys, seg_row), [whole(logits), whole(seg_keys), whole(seg_row)],
        outs, tuple(whole(o) for o in outs), flops=10**8, nbytes=4 * 10**6,
    )


def weight_halves(w):
    half = w[0].shape[0] // 2
    at = lambda row: spec((half, w[0].shape[1]), lambda *_: (row, 0))
    return [at(0), at(0), at(1), at(1)]


def out_projection(offs, rank, x, mixed_own, mixed_far, w, a_own, a_far, out_b, gain, ffn_a):
    rows, width = x.shape
    block = width // 4
    rank_r = a_own.shape[1]

    def kernel(
        offs_ref, rank_ref, x_ref, mo, mf, wo0, wo1, wf0, wf1, ao, af, b_ref, gain_ref, fa, h_ref, n_ref, low_ref, lo_ref
    ):
        def run(m0, m1, w0, w1, a0, a1):
            low = (dot(m0[...], a0[...]) + dot(m1[...], a1[...])).astype(BF)
            lo_ref[...] = low
            for half in range(2):
                both = dot(m0[...], w0[half][...]) + dot(m1[...], w1[half][...])
                both = both + dot(low, b_ref[:, 2 * half * block : 2 * (half + 1) * block])
                for j in range(2):
                    k = 2 * half + j
                    here = pl.ds(pl.multiple_of(offs_ref[k], LANES), block)
                    value = x_ref[:, here].astype(F32) + both[:, j * block : (j + 1) * block]
                    h_ref[:, k * block : (k + 1) * block] = value

        pl.when(rank_ref[0] == 0)(lambda: run(mo, mf, (wo0, wo1), (wf0, wf1), ao, af))
        pl.when(rank_ref[0] != 0)(lambda: run(mf, mo, (wf0, wf1), (wo0, wo1), af, ao))
        value = h_ref[...]
        normed = (value * norm_terms([value]) * gain_ref[...]).astype(BF)
        n_ref[...] = normed
        low_ref[...] = dot(normed, fa[...]).astype(BF)

    rowed = whole
    outs = (
        jax.ShapeDtypeStruct((rows, width), F32), jax.ShapeDtypeStruct((rows, width), BF),
        jax.ShapeDtypeStruct((rows, rank_r), BF), jax.ShapeDtypeStruct((rows, rank_r), BF),
    )
    ins = (offs, rank, x, mixed_own, mixed_far, *w, *w, a_own, a_far, out_b, gain, ffn_a)
    return call(
        kernel, (1,), ins,
        [rowed(x), rowed(mixed_own), rowed(mixed_far)] + weight_halves(w) + [whole(v) for v in ins[9:]],
        outs, tuple(rowed(o) for o in outs), prefetch=2, flops=4 * rows * width * mixed_own.shape[1],
        nbytes=4 * width * mixed_own.shape[1] + 8 * rows * width, cost=1725000000
    )


def feed_forward(rank, normed, low, cot, grad_low, gate_up, down, ffn_b, down_a):
    rows, width = normed.shape
    block = width // 4
    half = rows // 2
    rank_r = low.shape[1]
    unit_cols = down_a.shape[0]
    tile = 512 if unit_cols % 512 == 0 else unit_cols
    tiles = unit_cols // tile
    down_at = down[0].shape[1] // tile - tiles

    def kernel(
        rank_ref, x_ref, low_ref, cot_ref, gl_ref, *rest,
    ):
        pieces, rest = rest[:12], rest[12:]
        bg_ref, bu_ref, ad_ref, *rest, wg, wu, wd = rest
        step = pl.program_id(0)
        units_ref, gg_ref, gu_ref, far_ref, own_ref, own_low_ref, part_ref, part_low_ref = rest

        @pl.when(step == 0)
        def _():
            part_ref[...] = jnp.zeros_like(part_ref)
            part_low_ref[...] = jnp.zeros_like(part_low_ref)

        for n, joint in enumerate((wg, wu, wd)):
            for k in range(4):
                joint[k * block : (k + 1) * block, :] = pieces[4 * n + k][...]
        gate = dot(x_ref[...], wg[...]) + dot(low_ref[...], bg_ref[...])
        up = dot(x_ref[...], wu[...]) + dot(low_ref[...], bu_ref[...])
        grad = dot(cot_ref[...], wd[...]) + dot_t(gl_ref[...], ad_ref[...])
        sig = jax.nn.sigmoid(gate)
        act = gate * sig
        units_ref[...] = (act * up).astype(BF)
        gg = (grad * up * sig * (1.0 + gate * (1.0 - sig))).astype(BF)
        gu = (grad * act).astype(BF)
        gg_ref[...] = gg
        gu_ref[...] = gu
        part_low_ref[:, :rank_r] += dot_t(gg, bg_ref[...]) + dot_t(gu, bu_ref[...])
        part_ref[...] += dot_t(gg, wg[...]) + dot_t(gu, wu[...])

        @pl.when(step == tiles - 1)
        def _():
            mine = pl.ds(pl.multiple_of(rank_ref[0] * half, half), half)
            theirs = pl.ds(pl.multiple_of((1 - rank_ref[0]) * half, half), half)
            far_ref[:, :width] = part_ref[theirs, :].astype(BF)
            far_ref[:, width:] = split_lanes(part_low_ref[theirs, :], rank_r).astype(BF)
            own_ref[...] = part_ref[mine, :]
            own_low_ref[...] = part_low_ref[mine, :]

    out = jax.ShapeDtypeStruct((rows, unit_cols), BF)
    out_spec = spec((rows, tile), lambda i, *_: (0, i))
    sums = (jax.ShapeDtypeStruct((rows, width), F32), jax.ShapeDtypeStruct((rows, LANES), F32))
    ends = (
        jax.ShapeDtypeStruct((half, width + LANES), BF), jax.ShapeDtypeStruct((half, width), F32),
        jax.ShapeDtypeStruct((half, LANES), F32),
    )
    return call(
        kernel,
        (tiles,),
        (rank, normed, low, cot, grad_low, *gate_up, *gate_up, *down, ffn_b, ffn_b, down_a),
        [
            whole(normed), whole(low), whole(cot), whole(grad_low),
            *[spec((block, tile), lambda i, *_: (0, i)) for _ in range(4)],
            *[spec((block, tile), lambda i, *_: (0, i + tiles)) for _ in range(4)],
            *[spec((block, tile), lambda i, *_: (0, i + down_at)) for _ in range(4)],
            spec((rank_r, tile), lambda i, *_: (0, i)),
            spec((rank_r, tile), lambda i, *_: (0, i + tiles)),
            spec((tile, rank_r), lambda i, *_: (i, 0)),
        ],
        (out, out, out, *ends),
        (out_spec, out_spec, out_spec, *[whole(e) for e in ends]),
        [pltpu.VMEM(e.shape, F32) for e in sums] + [pltpu.VMEM((width, tile), BF)] * 3,
        prefetch=1, cost=4657500000
    )


def whole_low(parts, n):
    parts = parts.astype(F32)
    return parts[:, :n] + parts[:, n : 2 * n] + parts[:, 2 * n : 3 * n]


def middle(rank, own, got, own_low, hidden, cot, gain, ffn_a, out_b, w, a_own, a_far):
    half, width = own.shape
    depth = width // 2
    rank_r = out_b.shape[0]
    cols = a_own.shape[0]

    def kernel(
        rank_ref, own_ref, got_ref, low_ref, h_ref, cot_ref, gain_ref, fa, b_ref, wo0, wo1, wf0, wf1, ao, af,
        gh_ref, ghb_ref, glf_ref, glo_ref, mine_ref, far_ref,
    ):
        ffn_low = (low_ref[:, :rank_r] + whole_low(got_ref[:, width:], rank_r)).astype(BF)
        glf_ref[...] = ffn_low
        incoming = own_ref[...] + got_ref[:, :width].astype(F32) + dot_t(ffn_low, fa[...])
        value = h_ref[...]
        factor = norm_terms([value])
        scaled = incoming * gain_ref[...]
        mean = jnp.mean(value * scaled, axis=1, keepdims=True)
        grad = cot_ref[...].astype(F32) + (factor * scaled - value * (factor * factor * factor * mean))
        gh_ref[...] = grad
        low_precision = grad.astype(BF)
        ghb_ref[...] = low_precision
        left, right = low_precision[:, :depth], low_precision[:, depth:]
        out_low = dot_t(low_precision, b_ref[...]).astype(BF)
        glo_ref[...] = out_low
        mine_ref[...] = (dot_t(left, wo0[...]) + dot_t(right, wo1[...]) + dot_t(out_low, ao[...])).astype(BF)
        far_ref[...] = (dot_t(left, wf0[...]) + dot_t(right, wf1[...]) + dot_t(out_low, af[...])).astype(BF)

    outs = (
        jax.ShapeDtypeStruct((half, width), F32), jax.ShapeDtypeStruct((half, width), BF),
        jax.ShapeDtypeStruct((half, rank_r), BF), jax.ShapeDtypeStruct((half, rank_r), BF),
        jax.ShapeDtypeStruct((half, cols), BF), jax.ShapeDtypeStruct((half, cols), BF),
    )
    ins = (rank, own, got, own_low, hidden, cot, gain, ffn_a, out_b, *w, *w, a_own, a_far)
    mine = lambda v: spec((half, v.shape[1]), lambda i, r: (r[0], 0))
    in_specs = [whole(own), whole(got), whole(own_low), mine(hidden), mine(cot)] + [whole(v) for v in ins[6:9]]
    in_specs += weight_halves(w) + [whole(a_own), whole(a_far)]
    return call(
        kernel, (1,), ins, in_specs, outs, tuple(whole(o) for o in outs), prefetch=1,
        flops=4 * half * width * cols, nbytes=4 * width * cols + 16 * half * width, cost=1311000000
    )


def mixed_gradient(rank, own, far, mixed, n_heads, tail):
    half, cols = own.shape

    def kernel(rank_ref, own_ref, far_ref, mixed_ref, out_ref, tail_ref):
        lane = lane_ids(half)
        for ref, first in ((own_ref, rank_ref[0]), (far_ref, 1 - rank_ref[0])):
            at = pl.ds(pl.multiple_of(first * half, half), half)
            sums = jnp.zeros((half, LANES), F32)
            for pair in range(n_heads // 2):
                here = slice(pair * LANES, (pair + 1) * LANES)
                product = ref[:, here].astype(F32) * mixed_ref[at, here]
                a = jnp.sum(jnp.where(lane < HD, product, 0.0), axis=1, keepdims=True)
                b = jnp.sum(jnp.where(lane < HD, 0.0, product), axis=1, keepdims=True)
                sums = jnp.where(lane == 2 * pair, -a, jnp.where(lane == 2 * pair + 1, -b, sums))
            out_ref[at, :cols] = ref[...]
            out_ref[at, cols:] = split_lanes(sums, n_heads).astype(BF)
        tail_ref[...] = out_ref[:tail, :]

    outs = [jax.ShapeDtypeStruct((n, cols + LANES), BF) for n in (2 * half, tail)]
    return call(
        kernel, (1,), (rank, own, far, mixed), [whole(own), whole(far), whole(mixed)],
        tuple(outs), tuple(whole(o) for o in outs), prefetch=1,
        flops=4 * half * cols, nbytes=16 * half * cols, cost=672750000
    )


def input_gradient(rank, grads, logits, seg_keys, seg_row, row_lanes, own_lanes, next_lanes, across, w, side_w, qkv_b, low_qkv, n_heads):
    rows, cols = grads[0].shape
    block = w[0].shape[0]
    half = rows // 2
    rank_r = qkv_b.shape[0]
    before = logits.shape[0] - rows
    steps = 3
    chunk = block // steps

    def kernel(
        rank_ref, q_ref, k_ref, v_ref, logit_ref, seg_ref, seg_row_ref, r_ref, o_ref, n_ref, a_ref, *refs,
    ):
        pieces, sides, refs = refs[:4], refs[4:8], refs[8:]
        (
            b_ref, lq_ref, far_ref, own_ref, low_ref, tq_ref, tk_ref, tv_ref, gl_ref, sum_ref, joint,
            side,
        ) = refs

        @pl.when(pl.program_id(0) == 0)
        def _():
            lane = lane_ids(rows)
            t = lax.broadcasted_iota(jnp.int32, (rows, rows), 0)
            i = lax.broadcasted_iota(jnp.int32, (rows, rows), 1)
            same = ((seg_row_ref[...] == seg_ref[...]) & (i >= t)).astype(BF)
            total = exact_dot(same, r_ref[...] - o_ref[...]) + exact_dot((i < t).astype(BF), n_ref[...])
            total = total + a_ref[:1, :]
            value = jnp.where(lane < n_heads, total * jax.nn.sigmoid(-logit_ref[...]), 0.0)
            gl_ref[...] = value.astype(BF)
            low = dot_t(b_ref[:, :cols], q_ref[...]) + dot_t(b_ref[:, cols : 2 * cols], k_ref[...])
            low_ref[...] = low + dot_t(b_ref[:, 2 * cols :], v_ref[...])
            for out, grad in ((tq_ref, q_ref), (tk_ref, k_ref), (tv_ref, v_ref)):
                out[...] = t_dot(lq_ref[...], grad[...])

        mine = pl.ds(pl.multiple_of(rank_ref[0] * half, half), half)
        theirs = pl.ds(pl.multiple_of((1 - rank_ref[0]) * half, half), half)
        for k in range(4):
            joint[k * chunk : (k + 1) * chunk, :] = pieces[k][...]
            side[k * chunk : (k + 1) * chunk, :] = sides[k][...]
        value = dot_t(q_ref[...], joint[:, :cols]) + dot_t(k_ref[...], joint[:, cols : 2 * cols])
        sum_ref[...] = value + dot_t(v_ref[...], joint[:, 2 * cols :]) + dot_t(gl_ref[...], side[...])
        for k in range(4):
            at = slice(k * chunk, (k + 1) * chunk)
            far_ref[k] = sum_ref[theirs, at].astype(BF)
            own_ref[k] = sum_ref[mine, at]

    ins = (rank, *grads, logits, seg_keys, seg_row, row_lanes, own_lanes, next_lanes, across, *w, *[side_w] * 4, qkv_b, low_qkv)
    at_own = lambda v: spec((rows, v.shape[1]), lambda i, *_: (before // rows, 0))
    in_specs = [whole(g) for g in grads] + [at_own(logits), at_own(seg_keys)]
    in_specs += [whole(v) for v in (seg_row, row_lanes, own_lanes, next_lanes, across)]
    n_col = w[0].shape[1]
    in_specs += [spec((chunk, n_col), lambda i, *_: (i, 0))] * 4
    in_specs += [spec((chunk, LANES), lambda i, *_, k=k: (i + k * steps, 0)) for k in range(4)]
    in_specs += [whole(qkv_b), whole(low_qkv)]
    outs = (
        jax.ShapeDtypeStruct((4, half, block), BF), jax.ShapeDtypeStruct((4, half, block), F32),
        jax.ShapeDtypeStruct((rank_r, rows), F32),
        *[jax.ShapeDtypeStruct((rank_r, cols), F32)] * 3,
    )
    halves = spec((4, half, chunk), lambda i, *_: (0, 0, i))
    return call(
        kernel, (steps,), ins, in_specs, outs, (halves, halves, *[whole(o) for o in outs[2:]]), [pltpu.VMEM((rows, LANES), BF), pltpu.VMEM((rows, 4 * chunk), F32), pltpu.VMEM((4 * chunk, n_col), BF),
         pltpu.VMEM((4 * chunk, LANES), BF)],
        prefetch=1, cost=1932000000
    )


def token_gradient(offs, rank, own, got, grad_low, a, x, gain, grad_hidden):
    half, width = grad_hidden.shape
    block = width // 4

    def kernel(offs_ref, rank_ref, own_ref, got_ref, low_ref, a_ref, x_ref, gain_ref, gh_ref, out_ref):
        blocks, scaled, product = [], [], 0.0
        for k in range(4):
            here = pl.ds(pl.multiple_of(offs_ref[k], LANES), block)
            value = own_ref[k] + got_ref[k].astype(F32)
            value = value + lax.dot_general(
                low_ref[...], a_ref[k * block : (k + 1) * block, :], (((0,), (1,)), ((), ())), preferred_element_type=F32
            )
            blocks.append(x_ref[:, here].astype(F32))
            scaled.append(value * gain_ref[:, here])
            product = product + jnp.sum(blocks[k] * scaled[k], axis=1, keepdims=True)
        factor = norm_terms(blocks)
        mean = product / width
        for k in range(4):
            here = pl.ds(pl.multiple_of(offs_ref[k], LANES), block)
            back = factor * scaled[k] - blocks[k] * (factor * factor * factor * mean)
            out_ref[:, here] = (gh_ref[:, k * block : (k + 1) * block] + back).astype(BF)

    mine = lambda v: spec((half, v.shape[1]), lambda i, o, r: (r[0], 0))
    out = jax.ShapeDtypeStruct((half, width), BF)
    return call(
        kernel, (1,), (offs, rank, own, got, grad_low, a, x, gain, grad_hidden),
        [whole(own), whole(got), spec((grad_low.shape[0], half), lambda i, o, r: (0, r[0])), whole(a), mine(x), whole(gain), whole(grad_hidden)],
        out, whole(out), prefetch=2, nbytes=20 * half * width, cost=862500000
    )


def both_halves(rank, own, far):
    half, width = own.shape

    def kernel(rank_ref, own_ref, far_ref, out_ref):
        @pl.when(pl.program_id(0) == rank_ref[0])
        def _():
            out_ref[...] = own_ref[...].astype(F32)

        @pl.when(pl.program_id(0) != rank_ref[0])
        def _():
            out_ref[...] = far_ref[...].astype(F32)

    return call(
        kernel, (2,), (rank, own, far), [whole(own), whole(far)], jax.ShapeDtypeStruct((2 * half, width), F32),
        spec((half, width), lambda i, *_: (i, 0)), prefetch=1, nbytes=16 * half * width, cost=517500000
    )


def down_partial(units, down, down_a):
    rows, unit_cols = units.shape
    block = down[0].shape[0]
    width = 4 * block
    rank_r = down_a.shape[1]

    def kernel(u_ref, w0, w1, w2, w3, a_ref, out_ref, low_ref):
        low_ref[...] = jnp.zeros_like(low_ref)
        low_ref[:, :rank_r] = dot(u_ref[...], a_ref[...])
        for k, w_ref in enumerate((w0, w1, w2, w3)):
            out_ref[:, k * block : (k + 1) * block] = dot_t(u_ref[...], w_ref[...]).astype(BF)
        out_ref[:, width:] = split_lanes(low_ref[...], rank_r).astype(BF)

    rowed = lambda n: spec((BLK, n), lambda i: (i, 0))
    last = spec((block, unit_cols), lambda i: (0, 0))
    return call(
        kernel, (rows // BLK,), (units, *down, down_a), [rowed(unit_cols), last, last, last, last, whole(down_a)],
        jax.ShapeDtypeStruct((rows, width + LANES), BF), rowed(width + LANES), [pltpu.VMEM((BLK, LANES), F32)], cost=1621500000
    )


def block_result(offs, hidden, own, got, down_b):
    rows, width = hidden.shape
    block = width // 4
    rank_r = down_b.shape[0]

    def kernel(offs_ref, h_ref, own_ref, got_ref, b_ref, out_ref):
        low = (whole_low(own_ref[:, width:], rank_r) + whole_low(got_ref[:, width:], rank_r)).astype(BF)
        for k in range(4):
            here = pl.ds(pl.multiple_of(offs_ref[k], LANES), block)
            cols = slice(k * block, (k + 1) * block)
            both = own_ref[:, cols].astype(F32) + got_ref[:, cols].astype(F32)
            out_ref[:, here] = (h_ref[:, cols] + both + dot(low, b_ref[:, cols])).astype(BF)

    rowed = lambda v: spec((BLK, v.shape[1]), lambda i, *_: (i, 0))
    out = jax.ShapeDtypeStruct((rows, width), BF)
    return call(
        kernel, (rows // BLK,), (offs, hidden, own, got, down_b),
        [rowed(hidden), rowed(own), rowed(got), whole(down_b)], out, rowed(out),
        prefetch=1, nbytes=12 * rows * width, cost=862500000
    )


def pack_gradients(inv, rank, xor_own, xor_both, halves, out_a, wide, owners):
    rank_r, width = xor_own[0].shape
    block = width // 4
    part, unit_part = block // 8, wide[0].shape[1] // 16
    n = len(wide) * unit_part + (len(xor_own) + len(xor_both) + len(halves) + 1) * part
    assert owners == 32 and block % LANES == 0

    def kernel(inv_ref, rank_ref, *refs):
        out_ref, refs = refs[-1], list(refs[:-1])
        take = lambda count: [refs.pop(0) for _ in range(count)]
        own_refs, both_refs = take(len(xor_own)), take(len(xor_both))
        half_refs, (ao, af), wide_refs = take(len(halves)), take(2), take(len(wide))
        for f in range(4):
            mine = rank_ref[0] == f // 2
            at = pl.ds(pl.multiple_of(inv_ref[f], LANES), block)
            cols = slice(f % 2 * block, (f % 2 + 1) * block)
            blocks = [jnp.where(mine, r[:, at], 0.0) for r in own_refs] + [r[:, at] for r in both_refs]
            blocks += [jnp.where(mine, r[:, cols], 0.0) for r in half_refs]
            blocks.append(jnp.where(mine, ao[:, cols], af[:, cols]))
            units = 8 * unit_part
            big = [jnp.where(mine, r[:, f % 2 * units : (f % 2 + 1) * units], 0.0) for r in wide_refs]
            for j in range(8):
                row = [b[:, j * unit_part : (j + 1) * unit_part] for b in big]
                row += [b[:, j * part : (j + 1) * part] for b in blocks]
                at_row = slice((8 * f + j) * rank_r, (8 * f + j + 1) * rank_r)
                out_ref[at_row, :] = jnp.concatenate(row, axis=1).astype(BF)

    ins = (inv, rank, *xor_own, *xor_both, *halves, *out_a, *wide)
    out = jax.ShapeDtypeStruct((owners * rank_r, n), BF)
    return call(kernel, (1,), ins, [whole(v) for v in ins[2:]], out, whole(out), prefetch=2, cost=552000000
    )


def spread_gradients(every, landed, n_adapters, rank_r, unit_part, part):
    senders = landed.shape[0] // (4 * rank_r)
    at = [0, unit_part, 2 * unit_part] + [3 * unit_part + i * part for i in range(9)]

    def kernel(every_ref, x_ref, aq, bq, ao, bo, ag, bg, ad, bd):
        sums = []
        for f in range(4):
            total = 0.0
            for i in range(senders):
                row = (f * senders + i) * rank_r
                total = total + x_ref[row : row + rank_r, :].astype(F32)
            sums.append(total)
        for a in range(n_adapters):
            total = 0.0
            for f in range(4):
                total = total + jnp.where(every_ref[f] == a, sums[f], 0.0)
            cut = lambda i: total[:, at[i] : at[i + 1]]
            for out, i in ((aq, 3), (ao, 10), (ag, 6), (ad, 2)):
                out[a] = cut(i)
            bo[a], bd[a] = cut(5), cut(4)
            for j in range(3):
                bq[a, j] = cut(7 + j)
            for j in range(2):
                bg[a, :, j, :] = cut(j)

    shape = lambda *dims: jax.ShapeDtypeStruct((n_adapters, *dims), F32)
    row = shape(rank_r, part)
    outs = (row, shape(3, rank_r, part), row, row, row, shape(rank_r, 2, unit_part), shape(rank_r, unit_part), row)
    return call(kernel, (1,), (every, landed), [whole(landed)], outs, tuple(whole(o) for o in outs), prefetch=1, cost=500250000
    )


def body(
    tokens, segments, adapter_index, w_qkv, w_forget, forget_bias, w_out, w_gate_up, w_down,
    gain_attn, gain_ffn, a_qkv, b_qkv, a_out, b_out, a_gate_up, b_gate_up, a_down, b_down, cotangent,
):
    count, rows, width = tokens.shape
    assert count == 1
    head_cols = w_qkv.shape[2]
    n_heads = w_forget.shape[1]
    unit_cols = w_gate_up.shape[2]
    rank_r = a_qkv.shape[2]
    n_f, n_c, n_t = (lax.axis_size("fsdp"), lax.axis_size("ctx"), lax.axis_size("tp"))
    f_rank, t_rank = (lax.axis_index("fsdp"), lax.axis_index("tp"))
    hops = -(-(DOC_MOST - 1) // rows)
    assert hops == 2 and n_c > 2 and n_t == 2 and n_f % 4 == 0
    tail = -(-(DOC_MOST - 1 - rows) // 32) * 32
    before = hops * rows
    half = rows // 2
    block = width // 4
    first = t_rank == 0
    rank = t_rank.astype(jnp.int32)[None]

    def other(values):
        return lax.ppermute(values, "tp", [(0, 1), (1, 0)])

    def four(pieces):
        return [*pieces, *[lax.ppermute(part, "fsdp", [(i, i ^ 1) for i in range(n_f)]) for part in pieces]]

    mix = lambda values, dim: to_xor(values, dim, n_f, f_rank)
    direct = n_f == 4 and block % LANES == 0
    if direct:
        offs = jnp.stack([(f_rank ^ step) * block for step in xor_order(4)]).astype(jnp.int32)
        lay = lambda values, dim: values
    else:
        offs = jnp.arange(4, dtype=jnp.int32) * block
        lay = mix

    pick = adapter_index[0]
    tok = lay(tokens[0], 1)
    seg_one = segments[0] + 1
    note = jnp.zeros((32, width), BF).at[0, :rows].set(seg_one.astype(BF))
    qkv_own = jnp.concatenate([w_qkv[:, i] for i in range(3)], axis=1)
    qkv_far = far_blocks(qkv_own, 0)
    prev_one = shift(jnp.concatenate([tok, after(note, qkv_own)], axis=0), 1, n_c)
    side = jnp.broadcast_to(pick.astype(BF), (w_forget.shape[0], 1))
    side_far = far_blocks(after(jnp.concatenate([w_forget, side], axis=1), qkv_own), 0)
    take = lambda table: lax.dynamic_index_in_dim(table, pick, 0, keepdims=False)
    mine = lambda values, n, dim: lax.dynamic_slice_in_dim(values, t_rank * n, n, dim)
    theirs = lambda values, n, dim: lax.dynamic_slice_in_dim(values, (1 - t_rank) * n, n, dim)
    qkv_a, ffn_a = (mix(take(a_qkv), 0), mix(take(a_gate_up), 0))
    out_b, down_b = (mix(take(b_out), 1), mix(take(b_down), 1))
    qkv_b = mine(take(b_qkv), head_cols, 2).reshape(rank_r, 3 * head_cols)
    out_a = take(a_out)
    out_a_own, out_a_far = (mine(out_a, head_cols, 0), theirs(out_a, head_cols, 0))
    ffn_b = mine(take(b_gate_up), unit_cols, 2).reshape(rank_r, 2 * unit_cols)
    down_a = mine(take(a_down), unit_cols, 0)
    gain_one = lay(gain_attn.astype(F32), 0)[None]
    gain_two = mix(gain_ffn.astype(F32), 0)[None]
    bias = jnp.pad(forget_bias.astype(F32), (0, LANES - n_heads))[None]
    cot = mix(cotangent[0], 1)
    grad_low_down = dot_t(cot, down_b).astype(BF)

    out_pair = jnp.concatenate([w_out, other(w_out)], axis=0)
    gate_up_own = jnp.concatenate([w_gate_up[:, 0], w_gate_up[:, 1]], axis=1)
    down_own = w_down.T
    shared = n_f == 4 and n_c % 2 == 0
    odd = lax.axis_index("ctx") % 2
    down_sent = down_own
    if shared:
        down_sent = lax.dynamic_slice_in_dim(down_own, odd * (unit_cols // 2), unit_cols // 2, 1)
    (
        prev_one, qkv_far, side_far, out_pair, qkv_a, qkv_b, gain_one, bias, ffn_a, out_b, down_b, out_a_own, out_a_far,
        ffn_b, down_a, gain_two, cot, grad_low_down, gate_up_own, down_own, down_sent,
    ) = lax.optimization_barrier((
        prev_one, qkv_far, side_far, out_pair, qkv_a, qkv_b, gain_one, bias, ffn_a, out_b, down_b, out_a_own, out_a_far,
        ffn_b, down_a, gain_two, cot, grad_low_down, gate_up_own, down_own, down_sent,
    ))
    out_far = far_blocks(out_pair, 1)
    prev_two = shift(prev_one[rows - tail :], 1, n_c)
    qkv_four = four(qkv_far)
    side_all = jnp.concatenate(near_blocks(*side_far, 0), axis=0)
    every = from_xor(side_all[:: w_forget.shape[0], n_heads], 0, n_f, f_rank).astype(jnp.int32)
    side_w = jnp.concatenate([side_all, jnp.zeros((width, LANES - n_heads - 1 - rank_r), BF), qkv_a], axis=1)
    args = (gain_one, qkv_four, side_w, qkv_b, bias, head_cols, rank_r)
    down_far = far_blocks(down_sent, 0)
    tok_in, prev_two = lax.optimization_barrier((tok, prev_two))
    normed, low_qkv, query, *filled = project(offs, tok_in, None, tail, *args, None, before)
    seg_two = prev_two[tail, :rows].astype(jnp.int32)
    seg_far = []
    for b in range(-(-tail // BLK)):
        start, end = min(b * BLK, tail + 32 - BLK), min((b + 1) * BLK, tail)
        known = seg_two[rows - tail + b * BLK : rows - tail + end]
        seg_far.append(jnp.pad(known, (b * BLK - start, BLK - (end - start))))
    seg_keys = jnp.concatenate(seg_far + [prev_one[rows, :rows].astype(jnp.int32), seg_one])
    last_keys = jnp.max(seg_keys.reshape(-1, BLK), axis=1)
    lows = jnp.sum(last_keys[None, :] < seg_one[::BLK][:, None], axis=1).astype(jnp.int32)

    gate_up_far = far_blocks(after(gate_up_own, out_far[1], down_far[1], query), 0)
    keys, vals, logits = project(offs, prev_one, prev_two, tail, *args, filled)
    out_w = near_blocks(out_far[0], after(out_far[1], query), 1)
    logits, out_w = lax.optimization_barrier((logits, out_w))
    seg_col, seg_row = (seg_keys[:, None], seg_one[None, :])
    gq, gk, gk_next, gates, total = gate_tables(logits, seg_col, seg_row, n_heads, rows)
    mixed_own, mixed_f, gq_one, gq_two = attention_forward(lows, query, keys, vals, gq, gk, gates, total, n_heads)
    mixed_far = other(mixed_own)
    sent_q1 = jnp.concatenate([query, gq_one], axis=1)
    sent_q2 = jnp.concatenate([query[:tail], gq_two[:tail]], axis=1)
    if shared:
        down_pair = lax.ppermute(after(down_far[1], keys), "ctx", [(i, i ^ 1) for i in range(n_c)])
        down_pair = after(down_pair, mixed_own)
        lower, upper = jnp.where(odd == 0, down_far[1], down_pair), jnp.where(odd == 0, down_pair, down_far[1])
        down_got = jnp.concatenate([lower, upper], axis=1)
    else:
        down_got = down_far[1]
    mixed_far, sent_q1, sent_q2, down_got = lax.optimization_barrier((mixed_far, sent_q1, sent_q2, down_got))
    next_q1 = shift(sent_q1, -1, n_c)
    next_q2 = shift(sent_q2, -2, n_c)

    down_w = four((after(down_own, keys), down_got)) if shared else four(down_far)
    mixed_far, down_w[2] = lax.optimization_barrier((mixed_far, down_w[2]))
    hidden, normed_ffn, low_ffn, low_out = out_projection(
        offs, rank, tok, mixed_own, mixed_far, out_w, out_a_own, out_a_far, out_b, gain_two, ffn_a
    )
    gate_up_w = four((after(gate_up_own, mixed_own), after(gate_up_far[1], hidden))) if shared else four(gate_up_far)
    units, grad_gate, grad_up, far, own, own_low = feed_forward(
        rank, normed_ffn, low_ffn, cot, grad_low_down, gate_up_w, down_w, ffn_b, down_a
    )
    got = other(far)
    down_part = down_partial(after(units, far), down_w, down_a)
    gate_g, up_g, units_g = after((grad_gate, grad_up, units), far)
    tables_ffn = [t_dot(low_ffn, gate_g), t_dot(low_ffn, up_g), t_dot(grad_low_down, units_g)]
    got, down_part, tables_ffn = lax.optimization_barrier((got, down_part, tables_ffn))
    grad_hidden, grad_hidden_b, grad_low_ffn, grad_low_out, gm_own, gm_send = middle(
        rank, own, got, own_low, hidden, cot, gain_two, ffn_a, out_b, out_w, out_a_own, out_a_far
    )
    grad_mixed, sent_d2 = mixed_gradient(rank, gm_own, other(gm_send), mixed_f, n_heads, tail)

    next_d1 = shift(grad_mixed, -1, n_c)
    next_d2 = shift(sent_d2, -2, n_c)
    grad_q, row_lanes, across = attention_dq(
        lows, query, keys, vals, grad_mixed, gq_one, gk, n_heads, (before - rows) // BLK
    )
    across = shift(across, -1, n_c)
    docs_at = head_cols + 3 * n_heads
    grad_k_own, grad_v_own, own_lanes = attention_dkv_own(keys, vals, query, after(grad_mixed, grad_q), gq_one, gk, n_heads)
    next_q1, next_q2, next_d1, next_d2, _ = lax.optimization_barrier((next_q1, next_q2, next_d1, next_d2, grad_k_own))
    next_docs = jnp.concatenate([next_q1[::BLK, docs_at : docs_at + DOCS], next_q2[::BLK, docs_at : docs_at + DOCS]])
    next_docs = next_docs.astype(F32)
    ids = jnp.arange(1, DOCS + 1).astype(F32)
    next_first = jnp.where(jnp.sum(next_docs, 1) > 0, jnp.sum(next_docs * ids[None, :], 1), 99.0)
    last_rows = seg_one[BLK - 1 :: BLK].astype(F32)
    highs = jnp.sum(next_first[None, :] <= last_rows[:, None], axis=1).astype(jnp.int32)
    lane = lax.broadcasted_iota(jnp.int32, (1, width), 1)
    own_part = lambda values: values * (lane // (width // 2) == t_rank)
    natural = lambda values: from_xor(values, 1, n_f, f_rank)
    by_tp = lambda a, b: jnp.concatenate([jnp.where(first, a, b), jnp.where(first, b, a)], axis=1)
    place = lambda values: by_tp(values, jnp.zeros_like(values))
    rows_of = lambda values: lax.dynamic_slice_in_dim(values, t_rank * half, half, 0)
    onehot = (jnp.arange(a_qkv.shape[0])[:, None] == every[None, :]).astype(F32)
    onehot = jnp.repeat(onehot, n_c * n_t, axis=1)

    owners = n_f * n_c * n_t

    def pack(tables):
        packed = jnp.concatenate([t.reshape(rank_r, owners, -1) for t in tables], axis=2).transpose(1, 0, 2)
        return packed.astype(BF).reshape(owners, -1), [t.shape[1] // owners for t in tables]

    def take_apart(spread, sizes):
        spread = spread.reshape(-1, rank_r, sum(sizes))
        outs, at = [], 0
        for size in sizes:
            outs.append(spread[:, :, at : at + size])
            at += size
        return outs

    table_out_a = [t_dot(grad_low_out, rows_of(mixed_own)), t_dot(grad_low_out, rows_of(mixed_far))]
    table_out_b = t_dot(rows_of(low_out), grad_hidden_b)
    table_ffn_a = t_dot(grad_low_ffn, rows_of(normed_ffn))
    highs, table_out_a, table_out_b, table_ffn_a = lax.optimization_barrier(
        (highs, table_out_a, table_out_b, table_ffn_a)
    )
    grad_k, grad_v, next_lanes = attention_dkv_next(
        highs, keys, vals, next_q1, next_q2, next_d1, next_d2, gk_next, grad_k_own, grad_v_own, n_heads
    )
    down_other = other(after(down_part, grad_mixed))

    grads = (grad_q, grad_k, grad_v)
    far_in, own_in, part_low_qkv, *tables_b = input_gradient(
        rank, grads, logits, seg_col, seg_row, row_lanes, own_lanes, next_lanes, across, qkv_four, side_w, qkv_b, low_qkv, n_heads
    )
    grad_low_qkv = (part_low_qkv + other(part_low_qkv)).astype(BF)
    got_in = other(far_in)
    parts = [values[:, width : width + 3 * rank_r].astype(F32).reshape(rows, 3, rank_r) for values in (down_part, down_other)]
    parts = [values[:, 0] + values[:, 1] + values[:, 2] for values in parts]
    low_down = after((parts[0] + parts[1]).astype(BF), far_in)
    grad_tok = token_gradient(offs, rank, own_in, got_in, grad_low_qkv, qkv_a, tok, gain_one, grad_hidden)
    tok_far = other(grad_tok)
    block_output = block_result(offs, hidden, down_part, after(down_other, grad_tok), down_b)

    table_qkv_a, table_down_b = dot(grad_low_qkv, normed), t_dot(low_down, cot)
    if direct:
        bits = n_f.bit_length() - 1
        inv = [sum((((f_rank ^ i) >> j) & 1) << (bits - 1 - j) for j in range(bits)) * block for i in range(n_f)]
        packed = pack_gradients(
            jnp.stack(inv).astype(jnp.int32), rank, [table_qkv_a, table_down_b], [table_out_b, table_ffn_a], tables_b,
            table_out_a, tables_ffn, owners,
        )
        landed = lax.all_to_all(packed, ("fsdp", "ctx", "tp"), 0, 0, tiled=True)
        part, unit_part = width // owners, unit_cols * n_t // owners
        done = spread_gradients(every, landed, a_qkv.shape[0], rank_r, unit_part, part)
        done = [v.transpose(0, 2, 1) if i in (0, 2, 4, 6) else v for i, v in enumerate(done)]
        done[1] = done[1].transpose(0, 2, 1, 3)
        grad_tokens = both_halves(rank, grad_tok, after(tok_far, done[0]))
        return (block_output[None], grad_tokens[None], *done)
    block_output = from_xor(block_output, 1, n_f, f_rank)
    grad_tokens = from_xor(both_halves(rank, grad_tok, tok_far), 1, n_f, f_rank)
    early, early_sizes = pack([
        by_tp(*table_out_a), natural(table_out_b), natural(table_ffn_a), *[place(t) for t in tables_ffn],
    ])
    late, late_sizes = pack([
        own_part(natural(table_qkv_a)), *[place(t) for t in tables_b], own_part(natural(table_down_b)),
    ])
    landed = lax.all_to_all(jnp.concatenate([late, early], axis=1), ("fsdp", "ctx", "tp"), 0, 0, tiled=True)
    split = rank_r * sum(late_sizes)
    spread = jnp.dot(onehot.astype(BF), landed, preferred_element_type=F32)
    done = take_apart(spread[:, :split], late_sizes) + take_apart(spread[:, split:], early_sizes)
    swap = lambda values: values.transpose(0, 2, 1)
    return (
        block_output[None],
        grad_tokens[None],
        swap(done[0]),
        jnp.stack(done[1:4], axis=2),
        swap(done[5]),
        done[6],
        swap(done[7]),
        jnp.stack(done[8:10], axis=2),
        swap(done[10]),
        done[4],
    )


def solution(mesh):
    in_specs = (
        P("fsdp", "ctx", None), P("fsdp", "ctx"), P("fsdp"), P("fsdp", None, "tp"), P("fsdp", "tp"), P("tp"),
        P("tp", "fsdp"), P("fsdp", None, "tp"), P("tp", "fsdp"),
        P(), P(), P(), P(), P(), P(), P(), P(), P(), P(),
        P("fsdp", "ctx", None),
    )
    out_specs = (
        P("fsdp", "ctx", None),
        P("fsdp", "ctx", None),
        P(None, ("fsdp", "ctx", "tp"), None),
        P(None, None, None, ("fsdp", "ctx", "tp")),
        P(None, ("fsdp", "ctx", "tp"), None),
        P(None, None, ("fsdp", "ctx", "tp")),
        P(None, ("fsdp", "ctx", "tp"), None),
        P(None, None, None, ("fsdp", "ctx", "tp")),
        P(None, ("fsdp", "ctx", "tp"), None),
        P(None, None, ("fsdp", "ctx", "tp")),
    )
    return jax.shard_map(body, mesh=mesh, in_specs=in_specs, out_specs=out_specs, check_vma=False)
```
